32 devices in a mesh: dp: 8 (over y, x, core), tensor: 4 (over z).
Axes of the slice: x: 2, y: 2, z: 4, core: 2. Of those that a mesh axis runs over, the one named last changes fastest.
Arguments:
- inputs: bfloat16 [12608, 512], P(('dp', 'tensor')), may hold values from -6 to 6
- cotangent: bfloat16 [12608, 512], P(('dp', 'tensor')), may hold values from -6 to 6
- routes: int32 [12608, 2], P('dp'), may hold values from 0 to 7, all different within a row
- gain_attn: float32 [512], P(('dp', 'tensor')), may hold values from 0.5 to 1.5
- shift_attn: float32 [512], P(('dp', 'tensor')), may hold values from -3 to 3
- query_w: float32 [512, 512], P(('dp', 'tensor')), may hold values from -0.25 to 0.25
- key_w: float32 [512, 512], P(('dp', 'tensor')), may hold values from -0.25 to 0.25
- value_w: float32 [512, 512], P(('dp', 'tensor')), may hold values from -0.25 to 0.25
- out_w: float32 [512, 512], P(('dp', 'tensor')), may hold values from -1 to 1
- gain_moe: float32 [512], P(('dp', 'tensor')), may hold values from 0.5 to 1.5
- shift_moe: float32 [512], P(('dp', 'tensor')), may hold values from -3 to 3
- router_w: float32 [512, 8], P(('dp', 'tensor')), may hold values from -0.1875 to 0.1875
- expert_in: float32 [8, 512, 2048], P('dp', None, 'tensor'), may hold values from -0.25 to 0.25
- expert_out: float32 [8, 2048, 512], P('dp', 'tensor'), may hold values from -2 to 2
Outputs:
- output_tokens: bfloat16 [12608, 512], P(('dp', 'tensor'))
- grad_inputs: bfloat16 [12608, 512], P(('dp', 'tensor'))
- grad_gain_attn: float32 [512], P(('dp', 'tensor'))
- grad_shift_attn: float32 [512], P(('dp', 'tensor'))
- grad_query_w: float32 [512, 512], P(('dp', 'tensor'))
- grad_key_w: float32 [512, 512], P(('dp', 'tensor'))
- grad_value_w: float32 [512, 512], P(('dp', 'tensor'))
- grad_out_w: float32 [512, 512], P(('dp', 'tensor'))
- grad_gain_moe: float32 [512], P(('dp', 'tensor'))
- grad_shift_moe: float32 [512], P(('dp', 'tensor'))
- grad_router_w: float32 [512, 8], P(('dp', 'tensor'))
- grad_expert_in: float32 [8, 512, 2048], P('dp', None, 'tensor')
- grad_expert_out: float32 [8, 2048, 512], P('dp', 'tensor')
The draws below stay inside these ranges and needn't reach their ends.
Inputs may be any that keep to these rules, and one draw needn't show every extreme that they name: `routes`: each token names two different experts.
All inputs are finite; a program needn't handle non-finite values.
Results may differ from the reference program's by a relative error of at most 0.03.
Values may be sent and summed in bfloat16 or wider, within the bound.
A program may use at most 192 MiB of HBM per device.

```python
import jax
import jax.numpy as jnp
from jax import lax

D = 512
HEADS = 8
FF = 2048
SEQ = 197
EXPERTS = 8
HEAD_DIM = 64
TOK_DEV = 1576
TOKENS = 12608
CAP = 493
N_DP = 8


def levels(own_key, shape, shards, low, top_value):
    gain, own = 1.0, jax.random.fold_in(own_key, 6)
    for axis_at, parts in shards:
        steps = jnp.exp(jax.random.uniform(jax.random.fold_in(own, axis_at), (parts,), jnp.float32, low / len(shards), top_value / len(shards)))
        gain = gain * jnp.repeat(steps, shape[axis_at] // parts).reshape([-1 if axis == axis_at else 1 for axis in range(len(shape))])
    return gain


def picks_of(rng, rows, amount, top, lift):
    sequence = jax.random.permutation(jax.random.fold_in(rng, 1), amount)
    pull = sequence
    for power in range(3):
        pull = pull * pull // amount
    pull = pull * lift // amount
    lots = jax.random.randint(jax.random.fold_in(rng, 2), (rows, amount), 0, 4096) + pull
    sure = jax.random.permutation(jax.random.fold_in(rng, 3), rows)[jnp.arange(amount) % rows]
    lots = jnp.where(jnp.arange(rows)[:, None] == sure[None, :], 1 << 14, lots)
    merit = lots * amount + jnp.arange(amount)
    return lax.top_k(merit.astype(jnp.int32), top)[1].astype(jnp.int32)


def normal_values(own_key, dims, deviation, limit, pieces=(), kind=jnp.bfloat16):
    level = levels(own_key, dims, pieces, -0.22, 0.18) if pieces else 1.0
    drawn = jax.random.normal(own_key, dims, jnp.float32) * deviation * level
    return jnp.minimum(jnp.maximum(drawn, -limit), limit).astype(kind)


def setup_inputs(seed: int = 0) -> dict:
    keys = jax.random.split(jax.random.key(seed), 15)
    return {
        "inputs": normal_values(keys[0], (TOKENS, D), 1.0, 6.0, ((0, 32),)),
        "cotangent": normal_values(keys[1], (TOKENS, D), 1.0, 6.0, ((0, 32),)),
        "routes": picks_of(keys[2], TOKENS, EXPERTS, 2, 2048),
        "gain_attn": jnp.clip(1.0 + 0.1 * jax.random.normal(keys[3], (D,), jnp.float32), 0.5, 1.5),
        "shift_attn": normal_values(keys[4], (D,), 0.5, 3.0, ((0, 32),), jnp.float32),
        "query_w": normal_values(keys[5], (D, D), D ** -0.5, 0.25, ((0, 32),), jnp.float32),
        "key_w": normal_values(keys[6], (D, D), D ** -0.5, 0.25, ((0, 32),), jnp.float32),
        "value_w": normal_values(keys[7], (D, D), D ** -0.5, 0.25, ((0, 32),), jnp.float32),
        "out_w": normal_values(keys[8], (D, D), (D // 16) ** -0.5, 1.0, ((0, 32),), jnp.float32),
        "gain_moe": jnp.clip(1.0 + 0.1 * jax.random.normal(keys[9], (D,), jnp.float32), 0.5, 1.5),
        "shift_moe": normal_values(keys[10], (D,), 0.5, 3.0, ((0, 32),), jnp.float32),
        "router_w": normal_values(keys[11], (D, EXPERTS), (2 * D) ** -0.5, 0.1875, ((0, 32),), jnp.float32),
        "expert_in": normal_values(keys[12], (EXPERTS, D, FF), D ** -0.5, 0.25, ((0, 8), (2, 4)), jnp.float32),
        "expert_out": normal_values(keys[13], (EXPERTS, FF, D), (max(FF // 256, 1)) ** -0.5, 2.0, ((0, 8), (1, 4)), jnp.float32),
    }


@jax.custom_vjp
def low(v):
    return lax.optimization_barrier(v.astype(jnp.bfloat16)).astype(jnp.float32)

@jax.custom_vjp
def low_back(v):
    return v

def low_keep(v):
    return (low(v), None)

def low_pass(kept, grad):
    return (grad,)

def back_keep(v):
    return (v, None)

def back_low(kept, grad):
    return (low(grad),)
low.defvjp(low_keep, low_pass)
low_back.defvjp(back_keep, back_low)

def layer_norm(values, norm_gain, norm_shift):
    centred = values - lax.optimization_barrier(jnp.mean(values, axis=-1, keepdims=True))
    inverse = lax.rsqrt(lax.optimization_barrier(jnp.mean(centred * centred, axis=-1, keepdims=True)) + 1e-06)
    return centred * inverse * norm_gain + norm_shift

def place_pairs(routes_group, experts, capacity):
    tok_count = routes_group.shape[0]
    chosen = jnp.concatenate([routes_group[:, 0], routes_group[:, 1]])
    onehot = (chosen[:, None] == jnp.arange(experts, dtype=jnp.int32)[None, :]).astype(jnp.int32)
    earlier = jnp.cumsum(onehot, axis=0, dtype=jnp.int32) - onehot
    position = lax.optimization_barrier(jnp.sum(earlier * onehot, axis=1, dtype=jnp.int32))
    slot_index = jnp.where(position < capacity, chosen * capacity + position, experts * capacity).astype(jnp.int32)
    owners = jnp.concatenate([jnp.arange(tok_count, dtype=jnp.int32), jnp.arange(tok_count, dtype=jnp.int32)])
    slot_token = jnp.full((experts * capacity + 1,), tok_count, jnp.int32).at[slot_index].set(owners)
    return (slot_index, slot_token[:experts * capacity])

def high_dot(left, right):
    return jnp.dot(left, right, precision=lax.Precision.HIGHEST)

def group_forward(params, inputs, routes_group):
    gain_attn, shift_attn, query_w, key_w, value_w, out_w, gain_moe, shift_moe, router_w, expert_in, expert_out = params
    tok_count = inputs.shape[0]
    images = tok_count // SEQ
    normed = low(layer_norm(inputs, low(gain_attn), low(shift_attn)))
    query_rows = low_back(low(high_dot(normed, low(query_w))))
    key_rows = low_back(low(high_dot(normed, low(key_w))))
    value_rows = low_back(low(high_dot(normed, low(value_w))))
    split_shape = (images, SEQ, HEADS, HEAD_DIM)
    scores = jnp.einsum('bqhd,bkhd->bhqk', query_rows.reshape(split_shape), key_rows.reshape(split_shape), precision=lax.Precision.HIGHEST)
    scores = low_back(scores * HEAD_DIM ** (-0.5))
    attn_probs = low(jax.nn.softmax(scores, axis=-1))
    mixed_heads = jnp.einsum('bhqk,bkhd->bqhd', attn_probs, value_rows.reshape(split_shape), precision=lax.Precision.HIGHEST)
    mixed_heads = low_back(low(mixed_heads.reshape(tok_count, D)))
    attended = low_back(high_dot(mixed_heads, low(out_w)))
    residual = inputs + attended
    moe_normed = low(layer_norm(residual, low(gain_moe), low(shift_moe)))
    logits = low_back(high_dot(moe_normed, low(router_w)))
    router_probs = jax.nn.softmax(logits, axis=-1)
    gate_values = jnp.take_along_axis(router_probs, routes_group, axis=1)
    slot_index, slot_token = place_pairs(routes_group, EXPERTS, CAP)
    padded = jnp.concatenate([moe_normed, jnp.zeros((1, D), jnp.float32)])
    dispatched = padded[slot_token].reshape(EXPERTS, CAP, D)
    hidden = low_back(jnp.einsum('ecd,edf->ecf', dispatched, low(expert_in), precision=lax.Precision.HIGHEST))
    active = low(jax.nn.gelu(hidden, approximate=False))
    returned = low_back(jnp.einsum('ecf,efd->ecd', active, low(expert_out), precision=lax.Precision.HIGHEST))
    flat_rows = jnp.concatenate([returned.reshape(EXPERTS * CAP, D), jnp.zeros((1, D), jnp.float32)])
    per_pair = flat_rows[slot_index]
    combined = gate_values[:, 0:1] * per_pair[:tok_count] + gate_values[:, 1:2] * per_pair[tok_count:]
    return residual + combined

def reference(inputs, cotangent, routes, gain_attn, shift_attn, query_w, key_w, value_w, out_w, gain_moe, shift_moe, router_w, expert_in, expert_out):
    params = (gain_attn, shift_attn, query_w, key_w, value_w, out_w, gain_moe, shift_moe, router_w, expert_in, expert_out)

    def forward(tokens_all, weights_all):
        grouped = tokens_all.reshape(N_DP, TOK_DEV, D)
        route_groups = routes.reshape(N_DP, TOK_DEV, 2)

        def one_group(group_pair):
            return group_forward(weights_all, group_pair[0], group_pair[1])
        outputs = lax.map(jax.checkpoint(one_group), (grouped, route_groups))
        return outputs.reshape(TOKENS, D)
    result, pullback = jax.vjp(forward, inputs.astype(jnp.float32), params)
    grad_tokens, grad_params = pullback(cotangent.astype(jnp.float32))
    return (result.astype(jnp.bfloat16), grad_tokens.astype(jnp.bfloat16), grad_params[0], grad_params[1], grad_params[2], grad_params[3], grad_params[4], grad_params[5], grad_params[6], grad_params[7], grad_params[8], grad_params[9], grad_params[10])
```

```python
from functools import partial

import jax
import jax.numpy as jnp
from jax import lax
from jax.experimental import pallas as pl
from jax.experimental.pallas import tpu as pltpu
from jax.sharding import PartitionSpec as P

SEQ = 197
HEAD_DIM = 64
MESH = pl.DeviceIdType.MESH
F32 = jnp.float32
BF16 = jnp.bfloat16


def ceil_to(value, unit):
    return (value + unit - 1) // unit * unit


def gather_kernel(n_dp, n_t, block_ref, out_ref, own_sem, z_send, z_recv, c_send, c_recv, k_send, k_recv):
    n_chip = n_dp // 2
    dp = lax.axis_index("dp")
    t = lax.axis_index("tensor")
    chip = dp // 2
    core = lax.rem(dp, 2)
    other = chip * 2 + 1 - core
    bar = pltpu.get_barrier_semaphore()
    for k in range(1, n_t):
        pl.semaphore_signal(bar, inc=1, device_id={"tensor": lax.rem(t + k, n_t)}, device_id_type=MESH)
    for k in range(1, n_chip):
        peer = lax.rem(chip + k, n_chip) * 2 + core
        pl.semaphore_signal(bar, inc=1, device_id={"dp": peer}, device_id_type=MESH)
    pl.semaphore_signal(bar, inc=1, device_id={"dp": other}, device_id_type=MESH)
    pl.semaphore_wait(bar, n_t - 1 + n_chip - 1 + 1)

    def z_copy(k):
        return pltpu.make_async_remote_copy(
            src_ref=block_ref,
            dst_ref=out_ref.at[dp, t],
            send_sem=z_send.at[k],
            recv_sem=z_recv.at[k],
            device_id={"tensor": lax.rem(t + k, n_t)},
            device_id_type=MESH,
        )

    def chip_copy(k, j):
        row = lax.rem(t + n_t - j, n_t)
        return pltpu.make_async_remote_copy(
            src_ref=block_ref if j == 0 else out_ref.at[dp, row],
            dst_ref=out_ref.at[dp, row],
            send_sem=c_send.at[k, j],
            recv_sem=c_recv.at[k, j],
            device_id={"dp": lax.rem(chip + k, n_chip) * 2 + core},
            device_id_type=MESH,
        )

    def core_copy(k, j):
        row = lax.rem(t + n_t - j, n_t)
        src = lax.rem(chip + n_chip - k, n_chip) * 2 + core
        return pltpu.make_async_remote_copy(
            src_ref=block_ref if k == 0 and j == 0 else out_ref.at[src, row],
            dst_ref=out_ref.at[src, row],
            send_sem=k_send.at[k, j],
            recv_sem=k_recv.at[k, j],
            device_id={"dp": other},
            device_id_type=MESH,
        )

    copies = []
    for k in range(1, n_t):
        copy = z_copy(k)
        copy.start()
        copies.append(copy)
    own = pltpu.make_async_copy(block_ref, out_ref.at[dp, t], own_sem)
    own.start()
    for j in range(n_t):
        if j > 0:
            z_copy(j).wait_recv()
        for k in range(1, n_chip):
            chip_copy(k, j).start()
        core_copy(0, j).start()
    for j in range(n_t):
        for k in range(1, n_chip):
            chip_copy(k, j).wait_recv()
            core_copy(k, j).start()
    own.wait()
    for k in range(1, n_t):
        z_copy(k).wait_send()
    for j in range(n_t):
        for k in range(1, n_chip):
            chip_copy(k, j).wait_send()
        for k in range(n_chip):
            core_copy(k, j).wait()


def gather_all(block, n_dp, n_t):
    n_chip = n_dp // 2
    dma = pltpu.SemaphoreType.DMA
    return pl.pallas_call(
        partial(gather_kernel, n_dp, n_t),
        out_shape=jax.ShapeDtypeStruct((n_dp, n_t) + block.shape, block.dtype),
        in_specs=[pl.BlockSpec(memory_space=pltpu.VMEM)],
        out_specs=pl.BlockSpec(memory_space=pltpu.VMEM),
        scratch_shapes=[
            dma,
            dma((n_t,)),
            dma((n_t,)),
            dma((n_chip, n_t)),
            dma((n_chip, n_t)),
            dma((n_chip, n_t)),
            dma((n_chip, n_t)),
        ],
        compiler_params=pltpu.CompilerParams(collective_id=0, has_side_effects=True),
    )(block)


def scatter_kernel(
    n_dp, n_t, grads_ref, out_ref, core_in, half, chip_in, part, z_in, k_send, k_recv, c_send, c_recv, z_send, z_recv
):
    n_chip = n_dp // 2
    dp = lax.axis_index("dp")
    t = lax.axis_index("tensor")
    chip = dp // 2
    core = lax.rem(dp, 2)
    other = chip * 2 + 1 - core
    bar = pltpu.get_barrier_semaphore()
    for k in range(1, n_t):
        pl.semaphore_signal(bar, inc=1, device_id={"tensor": lax.rem(t + k, n_t)}, device_id_type=MESH)
    for k in range(1, n_chip):
        peer = lax.rem(chip + k, n_chip) * 2 + core
        pl.semaphore_signal(bar, inc=1, device_id={"dp": peer}, device_id_type=MESH)
    pl.semaphore_signal(bar, inc=1, device_id={"dp": other}, device_id_type=MESH)
    pl.semaphore_wait(bar, n_t - 1 + n_chip - 1 + 1)

    def core_copy(k):
        to = lax.rem(chip + k, n_chip)
        return pltpu.make_async_remote_copy(
            src_ref=grads_ref.at[to * 2 + 1 - core],
            dst_ref=core_in.at[k],
            send_sem=k_send.at[k],
            recv_sem=k_recv.at[k],
            device_id={"dp": other},
            device_id_type=MESH,
        )

    def chip_copy(k):
        return pltpu.make_async_remote_copy(
            src_ref=half.at[k],
            dst_ref=chip_in.at[k],
            send_sem=c_send.at[k],
            recv_sem=c_recv.at[k],
            device_id={"dp": lax.rem(chip + k, n_chip) * 2 + core},
            device_id_type=MESH,
        )

    def z_copy(k):
        return pltpu.make_async_remote_copy(
            src_ref=part.at[k],
            dst_ref=z_in.at[k],
            send_sem=z_send.at[k],
            recv_sem=z_recv.at[k],
            device_id={"tensor": lax.rem(t + k, n_t)},
            device_id_type=MESH,
        )

    order = list(range(1, n_chip)) + [0]
    for k in order:
        core_copy(k).start()
    for k in order:
        core_copy(k).wait_recv()
        to = lax.rem(chip + k, n_chip) * 2 + core
        both = grads_ref[to].astype(F32) + core_in[k].astype(F32)
        half[k] = both.astype(BF16)
        if k > 0:
            chip_copy(k).start()
    for k in range(1, n_chip):
        chip_copy(k).wait_recv()
    for k in list(range(1, n_t)) + [0]:
        row = lax.rem(t + k, n_t)
        to = chip * 2 + core
        total = grads_ref[to, row].astype(F32) + core_in[0, row].astype(F32)
        for c in range(1, n_chip):
            total = total + chip_in[c, row].astype(F32)
        if k > 0:
            part[k] = total.astype(BF16)
            z_copy(k).start()
        else:
            out_ref[...] = total
    for k in range(1, n_t):
        z_copy(k).wait_recv()
        out_ref[...] += z_in[k].astype(F32)
    for k in range(n_chip):
        core_copy(k).wait_send()
    for k in range(1, n_chip):
        chip_copy(k).wait_send()
    for k in range(1, n_t):
        z_copy(k).wait_send()


def scatter_all(grads, n_dp, n_t):
    n_chip = n_dp // 2
    block = grads.shape[2:]
    dma = pltpu.SemaphoreType.DMA
    return pl.pallas_call(
        partial(scatter_kernel, n_dp, n_t),
        out_shape=jax.ShapeDtypeStruct(block, F32),
        in_specs=[pl.BlockSpec(memory_space=pltpu.VMEM)],
        out_specs=pl.BlockSpec(memory_space=pltpu.VMEM),
        scratch_shapes=[
            pltpu.VMEM((n_chip, n_t) + block, BF16),
            pltpu.VMEM((n_chip, n_t) + block, BF16),
            pltpu.VMEM((n_chip, n_t) + block, BF16),
            pltpu.VMEM((n_t,) + block, BF16),
            pltpu.VMEM((n_t,) + block, BF16),
            dma((n_chip,)),
            dma((n_chip,)),
            dma((n_chip,)),
            dma((n_chip,)),
            dma((n_t,)),
            dma((n_t,)),
        ],
        compiler_params=pltpu.CompilerParams(collective_id=1, has_side_effects=True),
    )(grads)


def layer_norm(values, norm_gain, norm_shift):
    centred = values - jnp.mean(values, axis=-1, keepdims=True)
    inverse = lax.rsqrt(jnp.mean(centred * centred, axis=-1, keepdims=True) + 1e-06)
    return centred * inverse * norm_gain + norm_shift


def split_heads(rows, images):
    return rows.reshape(images, SEQ, rows.shape[1] // HEAD_DIM, HEAD_DIM)


def dot_mid(left, right):
    return jnp.dot(left, right, preferred_element_type=F32)


def dot_first(left, right):
    return lax.dot_general(left, right, (((0,), (0,)), ((), ())), preferred_element_type=F32)


def dot_last(left, right):
    return lax.dot_general(left, right, (((1,), (1,)), ((), ())), preferred_element_type=F32)


def route_pairs(routes, t, row_count, experts, capacity):
    tok_count = routes.shape[0]
    ids = jnp.arange(experts, dtype=jnp.int32)[None, :]
    start = t * row_count
    rows = lax.dynamic_slice_in_dim(routes, start, row_count, 0)
    before = (jnp.arange(tok_count, dtype=jnp.int32) < start)[:, None]
    all_first = routes[:, 0:1] == ids
    all_second = routes[:, 1:2] == ids
    base_first = jnp.sum((all_first & before).astype(jnp.int32), axis=0)
    total_first = jnp.sum(all_first.astype(jnp.int32), axis=0)
    base_second = jnp.sum((all_second & before).astype(jnp.int32), axis=0)
    hot_first = rows[:, 0:1] == ids
    hot_second = rows[:, 1:2] == ids
    at = jnp.arange(row_count, dtype=jnp.int32)
    lower = (at[:, None] > at[None, :]).astype(BF16)
    both = jnp.concatenate([hot_first, hot_second], axis=1).astype(BF16)
    earlier = dot_mid(lower, both).astype(jnp.int32)
    own_first = jnp.sum(hot_first.astype(jnp.int32), axis=0)
    rank_first = earlier[:, :experts]
    rank_second = earlier[:, experts:] + own_first
    place_first = rank_first + base_first
    place_second = earlier[:, experts:] + total_first + base_second
    first = jnp.sum(jnp.where(hot_first & (place_first < capacity), rank_first + 1, 0), axis=1) - 1
    second = jnp.sum(jnp.where(hot_second & (place_second < capacity), rank_second + 1, 0), axis=1) - 1
    most = jnp.maximum(jnp.max(first), jnp.max(second)) + 1
    return rows, first, second, most


def slot_masks(route_rows, first, second, base, rooms, experts):
    slots = jnp.arange(experts * rooms, dtype=jnp.int32)[None, :]

    def mask(choice, rank):
        here = rank - base
        ok = (here >= 0) & (here < rooms)
        index = jnp.where(ok, choice * rooms + here, -1)
        return index[:, None] == slots

    return mask(route_rows[:, 0], first), mask(route_rows[:, 1], second)


def exchange(rows):
    return lax.all_to_all(rows, "dp", split_axis=0, concat_axis=0, tiled=True)


def moe_round(masks, gates, moe_low, cotangent, w_in, w_out, experts, rooms):
    first, second = masks
    width = moe_low.shape[1]
    hot = (first | second).astype(BF16)
    dispatched = dot_first(hot, moe_low).astype(BF16)
    slot_gate = jnp.sum(
        jnp.where(first, gates[:, 0:1], 0.0) + jnp.where(second, gates[:, 1:2], 0.0), axis=0
    )
    slot_grad = (slot_gate[:, None] * dot_first(hot, cotangent)).astype(BF16)
    received = exchange(dispatched.reshape(experts, rooms, width)).reshape(experts * rooms, width)
    slot_received = exchange(slot_grad.reshape(experts, rooms, width)).reshape(experts * rooms, width)
    hidden = dot_last(received, w_in)
    active, gelu_pull = jax.vjp(partial(jax.nn.gelu, approximate=False), hidden)
    active = active.astype(BF16)
    returned = dot_mid(active, w_out).astype(BF16)
    grad_outer = dot_first(active, slot_received).astype(BF16)
    grad_active = dot_last(slot_received, w_out)
    grad_hidden = gelu_pull(grad_active)[0].astype(BF16)
    grad_inner = dot_first(grad_hidden, received).astype(BF16)
    grad_dispatch = dot_mid(grad_hidden, w_in).astype(BF16)
    returned = exchange(returned.reshape(experts, rooms, width)).reshape(experts * rooms, width)
    grad_dispatch = exchange(grad_dispatch.reshape(experts, rooms, width)).reshape(experts * rooms, width)
    return returned, grad_dispatch, grad_inner, grad_outer


def combine(masks, gates, cotangent, returned, grad_dispatch):
    first, second = masks
    first_low, second_low = first.astype(BF16), second.astype(BF16)
    first_rows = dot_mid(first_low, returned)
    second_rows = dot_mid(second_low, returned)
    mixed = gates[:, 0:1] * first_rows + gates[:, 1:2] * second_rows
    grad_rows = cotangent.astype(F32)
    gate_grad = jnp.stack(
        [jnp.sum(first_rows * grad_rows, axis=1), jnp.sum(second_rows * grad_rows, axis=1)], axis=1
    )
    token_grad = dot_mid((first | second).astype(BF16), grad_dispatch)
    return mixed, gate_grad, token_grad


def per_device(
    n_dp,
    n_t,
    inputs,
    cotangent,
    routes,
    gain_attn,
    shift_attn,
    query_w,
    key_w,
    value_w,
    out_w,
    gain_moe,
    shift_moe,
    router_w,
    expert_in,
    expert_out,
):
    t = lax.axis_index("tensor")
    shard, width = query_w.shape
    experts = router_w.shape[1]
    tok_count = routes.shape[0]
    row_count = inputs.shape[0]
    images = row_count // SEQ
    capacity = (5 * tok_count + 2 * experts - 1) // (2 * experts)
    rooms = ceil_to((7 * row_count + 2 * experts - 1) // (2 * experts), 16)
    scale = HEAD_DIM ** (-0.5)

    route_rows, first_rank, second_rank, most = route_pairs(routes, t, row_count, experts, capacity)

    w_in = lax.all_gather(expert_in[0].T.astype(BF16), "tensor", axis=0, tiled=True)
    w_out = lax.all_gather(expert_out[0].astype(BF16), "tensor", axis=0, tiled=True)

    small = jnp.concatenate(
        [
            gain_attn[:, None],
            shift_attn[:, None],
            gain_moe[:, None],
            shift_moe[:, None],
            router_w,
            jnp.broadcast_to((most // 16).astype(F32), (shard, 1)),
            jnp.broadcast_to((most % 16).astype(F32), (shard, 1)),
        ],
        axis=1,
    )
    columns = small.shape[1]
    rows_used = 5 * shard
    rows_block = ceil_to(rows_used, 16)
    block = jnp.concatenate(
        [query_w, key_w, value_w, out_w, jnp.pad(small, ((0, rows_block - rows_used), (0, width - columns)))],
        axis=0,
    ).astype(BF16)
    gathered = gather_all(block, n_dp, n_t)

    def whole(at):
        return gathered[:, :, at * shard : (at + 1) * shard, :].reshape(width, width)

    query_low, key_low, value_low, out_low = whole(0), whole(1), whole(2), whole(3)
    small_all = gathered[:, :, 4 * shard : 5 * shard, :128].reshape(width, 128)
    norms = small_all[:, :4].T.astype(F32)
    gain_one, shift_one, gain_two, shift_two = norms[0], norms[1], norms[2], norms[3]
    router_low = small_all[:, 4 : 4 + experts]
    counts = small_all[:, 4 + experts : 6 + experts].astype(F32)
    most_all = jnp.max(counts[:, 0] * 16.0 + counts[:, 1]).astype(jnp.int32)

    token_rows = inputs.astype(F32)
    normed_rows, norm_pull = jax.vjp(layer_norm, token_rows, gain_one, shift_one)
    normed = normed_rows.astype(BF16)
    query_rows = dot_mid(normed, query_low).astype(BF16)
    key_rows = dot_mid(normed, key_low).astype(BF16)
    value_rows = dot_mid(normed, value_low).astype(BF16)
    query_split = split_heads(query_rows, images)
    key_split = split_heads(key_rows, images)
    value_split = split_heads(value_rows, images)
    scores = jnp.einsum("bqhd,bkhd->bhqk", query_split, key_split, preferred_element_type=F32) * scale
    log_total = jax.nn.logsumexp(scores, axis=-1, keepdims=True)
    attn_probs = jnp.exp(scores - log_total).astype(BF16)
    mixed_heads = jnp.einsum("bhqk,bkhd->bqhd", attn_probs, value_split, preferred_element_type=F32)
    mixed_heads = mixed_heads.reshape(row_count, width).astype(BF16)
    attended = dot_mid(mixed_heads, out_low)
    residual = token_rows + attended
    moe_rows, moe_pull = jax.vjp(layer_norm, residual, gain_two, shift_two)
    moe_low = moe_rows.astype(BF16)
    logits = dot_mid(moe_low, router_low)
    probs = jax.nn.softmax(logits, axis=-1)
    expert_ids = jnp.arange(experts, dtype=jnp.int32)[None, :]
    is_first = route_rows[:, 0:1] == expert_ids
    is_second = route_rows[:, 1:2] == expert_ids
    gates = jnp.stack(
        [jnp.sum(jnp.where(is_first, probs, 0.0), axis=1), jnp.sum(jnp.where(is_second, probs, 0.0), axis=1)],
        axis=1,
    )

    masks = slot_masks(route_rows, first_rank, second_rank, 0, rooms, experts)
    returned, grad_dispatch, grad_inner, grad_outer = moe_round(
        masks, gates, moe_low, cotangent, w_in, w_out, experts, rooms
    )
    mixed, gate_grad, token_grad = combine(masks, gates, cotangent, returned, grad_dispatch)

    def more(state):
        def body(carry):
            at, mixed, gate_grad, token_grad, grad_inner, grad_outer = carry
            again = slot_masks(route_rows, first_rank, second_rank, at * rooms, rooms, experts)
            back, back_grad, inner, outer = moe_round(
                again, gates, moe_low, cotangent, w_in, w_out, experts, rooms
            )
            add_mixed, add_gate, add_token = combine(again, gates, cotangent, back, back_grad)
            return (
                at + 1,
                mixed + add_mixed,
                gate_grad + add_gate,
                token_grad + add_token,
                (grad_inner.astype(F32) + inner.astype(F32)).astype(BF16),
                (grad_outer.astype(F32) + outer.astype(F32)).astype(BF16),
            )

        return lax.while_loop(lambda carry: carry[0] * rooms < most_all, body, (jnp.int32(1),) + state)[1:]

    state = (mixed, gate_grad, token_grad, grad_inner, grad_outer)
    state = lax.cond(most_all > rooms, more, lambda same: same, state)
    mixed, gate_grad, token_grad, grad_inner, grad_outer = state

    grad_inner = lax.psum_scatter(grad_inner, "tensor", scatter_dimension=0, tiled=True).astype(F32).T
    grad_outer = lax.psum_scatter(grad_outer, "tensor", scatter_dimension=0, tiled=True).astype(F32)

    output_rows = residual + mixed
    grad_rows = cotangent.astype(F32)
    grad_probs = jnp.where(is_first, gate_grad[:, 0:1], 0.0) + jnp.where(is_second, gate_grad[:, 1:2], 0.0)
    grad_logits = probs * (grad_probs - jnp.sum(probs * grad_probs, axis=1, keepdims=True))
    grad_logits = grad_logits.astype(BF16)
    grad_router = dot_first(moe_low, grad_logits)
    grad_moe = token_grad + dot_last(grad_logits, router_low)
    grad_resid_extra, grad_gain_two, grad_shift_two = moe_pull(grad_moe)
    grad_residual = grad_rows + grad_resid_extra
    grad_attended = grad_residual.astype(BF16)
    grad_out = dot_first(mixed_heads, grad_attended)
    grad_mixed = dot_last(grad_attended, out_low).astype(BF16)
    grad_split = split_heads(grad_mixed, images)
    scores_again = jnp.einsum("bqhd,bkhd->bhqk", query_split, key_split, preferred_element_type=F32) * scale
    probs_again = jnp.exp(scores_again - log_total)
    grad_probs_attn = jnp.einsum("bqhd,bkhd->bhqk", grad_split, value_split, preferred_element_type=F32)
    grad_value = jnp.einsum(
        "bhqk,bqhd->bkhd", probs_again.astype(BF16), grad_split, preferred_element_type=F32
    )
    grad_value = grad_value.reshape(row_count, width).astype(BF16)
    grad_scores = probs_again * (
        grad_probs_attn - jnp.sum(probs_again * grad_probs_attn, axis=-1, keepdims=True)
    )
    grad_scores = grad_scores.astype(BF16)
    grad_query = jnp.einsum("bhqk,bkhd->bqhd", grad_scores, key_split, preferred_element_type=F32) * scale
    grad_query = grad_query.reshape(row_count, width).astype(BF16)
    grad_key = jnp.einsum("bhqk,bqhd->bkhd", grad_scores, query_split, preferred_element_type=F32) * scale
    grad_key = grad_key.reshape(row_count, width).astype(BF16)
    grad_query_w = dot_first(normed, grad_query)
    grad_key_w = dot_first(normed, grad_key)
    grad_value_w = dot_first(normed, grad_value)
    grad_normed = (
        dot_last(grad_query, query_low) + dot_last(grad_key, key_low) + dot_last(grad_value, value_low)
    )
    grad_token_extra, grad_gain_one, grad_shift_one = norm_pull(grad_normed)
    grad_tokens = (grad_residual + grad_token_extra).astype(BF16)

    small_grad = jnp.concatenate(
        [
            grad_gain_one[:, None],
            grad_shift_one[:, None],
            grad_gain_two[:, None],
            grad_shift_two[:, None],
            grad_router,
        ],
        axis=1,
    )
    used = small_grad.shape[1]
    small_grad = jnp.pad(small_grad, ((0, 0), (0, width - used)))
    pieces = [
        piece.astype(BF16).reshape(n_dp, n_t, shard, width)
        for piece in (grad_query_w, grad_key_w, grad_value_w, grad_out, small_grad)
    ]
    if rows_block > rows_used:
        pieces.append(jnp.zeros((n_dp, n_t, rows_block - rows_used, width), BF16))
    summed = scatter_all(jnp.concatenate(pieces, axis=2), n_dp, n_t)
    small_sum = summed[4 * shard : 5 * shard, :used]
    return (
        output_rows.astype(BF16),
        grad_tokens,
        small_sum[:, 0],
        small_sum[:, 1],
        summed[0:shard],
        summed[shard : 2 * shard],
        summed[2 * shard : 3 * shard],
        summed[3 * shard : 4 * shard],
        small_sum[:, 2],
        small_sum[:, 3],
        small_sum[:, 4:used],
        grad_inner[None],
        grad_outer[None],
    )


def solution(mesh):
    every = ("dp", "tensor")
    rows, line = P(every, None), P(every)
    w_in, w_out = P("dp", None, "tensor"), P("dp", "tensor", None)
    return jax.shard_map(
        partial(per_device, mesh.shape["dp"], mesh.shape["tensor"]),
        mesh=mesh,
        in_specs=(rows, rows, P("dp", None), line, line, rows, rows, rows, rows, line, line, rows, w_in, w_out),
        out_specs=(rows, rows, line, line, rows, rows, rows, rows, line, line, rows, w_in, w_out),
        check_vma=False,
    )
```

```python
from functools import partial

import jax
import jax.numpy as jnp
from jax import lax
from jax.experimental import pallas as pl
from jax.experimental.pallas import tpu as pltpu
from jax.sharding import PartitionSpec as P

SEQ = 197
HEAD_DIM = 64
LANES = 128
MESH = pl.DeviceIdType.MESH
F32 = jnp.float32
BF16 = jnp.bfloat16
VMEM = pltpu.VMEM
DMA = pltpu.SemaphoreType.DMA


def ceil_to(value, unit):
    return (value + unit - 1) // unit * unit


def nn(left, right):
    return lax.dot_general(left, right, (((1,), (0,)), ((), ())), preferred_element_type=F32)


def nt(left, right):
    return lax.dot_general(left, right, (((1,), (1,)), ((), ())), preferred_element_type=F32)


def tn(left, right):
    return lax.dot_general(left, right, (((0,), (0,)), ((), ())), preferred_element_type=F32)


def remote(src, dst, send, recv, device):
    return pltpu.make_async_remote_copy(
        src_ref=src, dst_ref=dst, send_sem=send, recv_sem=recv, device_id=device, device_id_type=MESH
    )


def meet(n_dp, n_t, z_too):
    dp = lax.axis_index("dp")
    t = lax.axis_index("tensor")
    bar = pltpu.get_barrier_semaphore()
    for k in range(1, n_dp):
        pl.semaphore_signal(bar, inc=1, device_id={"dp": lax.rem(dp + k, n_dp)}, device_id_type=MESH)
    if z_too:
        for k in range(1, n_t):
            pl.semaphore_signal(bar, inc=1, device_id={"tensor": lax.rem(t + k, n_t)}, device_id_type=MESH)
    pl.semaphore_wait(bar, n_dp - 1 + (n_t - 1 if z_too else 0))


class Gather:
    def __init__(self, n_dp, n_t, block, out, own_sem, z_send, z_recv, c_send, c_recv, k_send, k_recv):
        self.n_t, self.n_chip = n_t, n_dp // 2
        self.block, self.out, self.own_sem = block, out, own_sem
        self.z_sems, self.c_sems, self.k_sems = (z_send, z_recv), (c_send, c_recv), (k_send, k_recv)
        self.dp, self.t = lax.axis_index("dp"), lax.axis_index("tensor")
        self.chip, self.core = self.dp // 2, lax.rem(self.dp, 2)
        self.other = self.chip * 2 + 1 - self.core

    @staticmethod
    def scratch(n_dp, n_t):
        n_chip = n_dp // 2
        pair = [DMA((n_chip, n_t))] * 2
        return [DMA, DMA((n_t,)), DMA((n_t,))] + pair + pair

    def z_copy(self, k):
        send, recv = self.z_sems
        to = lax.rem(self.t + k, self.n_t)
        return remote(self.block, self.out.at[self.dp, self.t], send.at[k], recv.at[k], {"tensor": to})

    def chip_copy(self, k, j):
        send, recv = self.c_sems
        row = lax.rem(self.t + self.n_t - j, self.n_t)
        here = self.out.at[self.dp, row]
        to = lax.rem(self.chip + k, self.n_chip) * 2 + self.core
        return remote(self.block if j == 0 else here, here, send.at[k, j], recv.at[k, j], {"dp": to})

    def core_copy(self, k, j):
        send, recv = self.k_sems
        row = lax.rem(self.t + self.n_t - j, self.n_t)
        src = lax.rem(self.chip + self.n_chip - k, self.n_chip) * 2 + self.core
        here = self.out.at[src, row]
        own = k == 0 and j == 0
        return remote(self.block if own else here, here, send.at[k, j], recv.at[k, j], {"dp": self.other})

    def own_copy(self):
        return pltpu.make_async_copy(self.block, self.out.at[self.dp, self.t], self.own_sem)

    def start(self):
        for k in range(1, self.n_t):
            self.z_copy(k).start()
        self.own_copy().start()
        for k in range(1, self.n_chip):
            self.chip_copy(k, 0).start()
        self.core_copy(0, 0).start()

    def finish(self):
        for j in range(1, self.n_t):
            self.z_copy(j).wait_recv()
            for k in range(1, self.n_chip):
                self.chip_copy(k, j).start()
            self.core_copy(0, j).start()
        for j in range(self.n_t):
            for k in range(1, self.n_chip):
                self.chip_copy(k, j).wait_recv()
                self.core_copy(k, j).start()
        self.own_copy().wait()
        for k in range(1, self.n_t):
            self.z_copy(k).wait_send()
        for j in range(self.n_t):
            for k in range(1, self.n_chip):
                self.chip_copy(k, j).wait_send()
            for k in range(self.n_chip):
                self.core_copy(k, j).wait()


class Scatter:
    def __init__(
        self, n_dp, n_t, grads, out, core_in, half, chip_in, part, z_in, k_send, k_recv, c_send, c_recv, z_send, z_recv
    ):
        self.n_t, self.n_chip = n_t, n_dp // 2
        self.grads, self.out = grads, out
        self.core_in, self.half, self.chip_in, self.part, self.z_in = core_in, half, chip_in, part, z_in
        self.k_sems, self.c_sems, self.z_sems = (k_send, k_recv), (c_send, c_recv), (z_send, z_recv)
        self.dp, self.t = lax.axis_index("dp"), lax.axis_index("tensor")
        self.chip, self.core = self.dp // 2, lax.rem(self.dp, 2)
        self.other = self.chip * 2 + 1 - self.core

    @staticmethod
    def scratch(n_dp, n_t, block):
        n_chip = n_dp // 2
        buffers = [VMEM((n_chip, n_t) + block, BF16)] * 3 + [VMEM((n_t,) + block, BF16)] * 2
        return buffers + [DMA((n_chip,))] * 4 + [DMA((n_t,))] * 2

    def core_copy(self, k):
        to = lax.rem(self.chip + k, self.n_chip)
        src = self.grads.at[to * 2 + 1 - self.core]
        return remote(src, self.core_in.at[k], self.k_sems[0].at[k], self.k_sems[1].at[k], {"dp": self.other})

    def chip_copy(self, k):
        to = lax.rem(self.chip + k, self.n_chip) * 2 + self.core
        return remote(self.half.at[k], self.chip_in.at[k], self.c_sems[0].at[k], self.c_sems[1].at[k], {"dp": to})

    def z_copy(self, k):
        to = lax.rem(self.t + k, self.n_t)
        return remote(self.part.at[k], self.z_in.at[k], self.z_sems[0].at[k], self.z_sems[1].at[k], {"tensor": to})

    def run(self):
        n_chip, n_t = self.n_chip, self.n_t
        order = list(range(1, n_chip)) + [0]
        for k in order:
            self.core_copy(k).start()
        for k in order:
            self.core_copy(k).wait_recv()
            if k > 0:
                to = lax.rem(self.chip + k, n_chip) * 2 + self.core
                self.half[k] = (self.grads[to].astype(F32) + self.core_in[k].astype(F32)).astype(BF16)
                self.chip_copy(k).start()
        for k in range(1, n_chip):
            self.chip_copy(k).wait_recv()
        for k in list(range(1, n_t)) + [0]:
            row = lax.rem(self.t + k, n_t)
            total = self.grads[self.dp, row].astype(F32) + self.core_in[0, row].astype(F32)
            for c in range(1, n_chip):
                total = total + self.chip_in[c, row].astype(F32)
            if k > 0:
                self.part[k] = total.astype(BF16)
                self.z_copy(k).start()
            else:
                self.out[...] = total
        for k in range(1, n_t):
            self.z_copy(k).wait_recv()
            self.out[...] += self.z_in[k].astype(F32)
        for k in range(n_chip):
            self.core_copy(k).wait_send()
        for k in range(1, n_chip):
            self.chip_copy(k).wait_send()
        for k in range(1, n_t):
            self.z_copy(k).wait_send()


def centre(values):
    centred = values - jnp.mean(values, axis=1, keepdims=True)
    inverse = lax.rsqrt(jnp.mean(centred * centred, axis=1, keepdims=True) + 1e-06)
    return centred * inverse, inverse


def norm_back(grad, unit, inverse, gain):
    scaled = grad * gain
    back = inverse * (
        scaled
        - jnp.mean(scaled, axis=1, keepdims=True)
        - unit * jnp.mean(scaled * unit, axis=1, keepdims=True)
    )
    return back, jnp.sum(grad * unit, axis=0, keepdims=True), jnp.sum(grad, axis=0, keepdims=True)


def norm_rows(small):
    pick = lax.broadcasted_iota(jnp.int32, (8, LANES), 0) == lax.broadcasted_iota(jnp.int32, (8, LANES), 1)
    return nt(pick.astype(F32).astype(BF16), small)


def image_bias(rows, padded):
    line = lax.broadcasted_iota(jnp.int32, (padded, padded), 0)
    column = lax.broadcasted_iota(jnp.int32, (padded, padded), 1)
    image_line, image_column = jnp.zeros_like(line), jnp.zeros_like(column)
    for at in range(SEQ, rows + 1, SEQ):
        image_line += (line >= at).astype(jnp.int32)
        image_column += (column >= at).astype(jnp.int32)
    return jnp.where((image_line == image_column) & (column < rows), 0.0, -1e30)


def half_masks():
    lane = lax.broadcasted_iota(jnp.int32, (1, LANES), 1)
    low = (lane < HEAD_DIM).astype(F32)
    return low.astype(BF16), (1.0 - low).astype(BF16)


def soft_scores(query, key, bias):
    scores = nt(query, key) * HEAD_DIM ** (-0.5) + bias
    power = jnp.exp(scores - jnp.max(scores, axis=1, keepdims=True))
    return power * (1.0 / jnp.sum(power, axis=1, keepdims=True))


def router_probs(logits, experts):
    lane = lax.broadcasted_iota(jnp.int32, logits.shape, 1)
    inside = (lane >= 4) & (lane < 4 + experts)
    kept = jnp.where(inside, logits, -1e30)
    power = jnp.where(inside, jnp.exp(kept - jnp.max(kept, axis=1, keepdims=True)), 0.0)
    return power * (1.0 / jnp.sum(power, axis=1, keepdims=True))


def pick_gate(probs, choice):
    lane = lax.broadcasted_iota(jnp.int32, probs.shape, 1)
    return jnp.sum(jnp.where(lane == choice + 4, probs, 0.0), axis=1, keepdims=True)


class Weights:
    def __init__(self, shard, width, gathered=None, whole=None):
        self.shard, self.width, self.gathered, self.whole = shard, width, gathered, whole

    def __call__(self, at):
        if self.whole is not None:
            return self.whole[at]
        part = self.gathered[:, :, at * self.shard : (at + 1) * self.shard, :]
        return part.reshape(self.width, self.width)

    def small(self):
        if self.whole is not None:
            return self.whole[4, :, :LANES]
        part = self.gathered[:, :, 4 * self.shard : 5 * self.shard, :LANES]
        return part.reshape(self.width, LANES)


def forward_kernel(cfg, *refs):
    n_dp, n_t, rows, padded, width, experts, rooms, shard, inside = cfg
    refs = list(refs)

    def take(count):
        got = refs[:count]
        del refs[:count]
        return got

    x_ref, cot_ref, cols_ref, slots_ref, block_ref = take(5)
    gathered, recv_d, recv_s, res_ref, moe_ref, q_ref, k_ref, v_ref, mix_ref, norm_ref, probs_ref = take(11)
    full, cot_full, bias, send_d, send_s, d_send, d_recv, s_send, s_recv = take(9)
    dp = lax.axis_index("dp")
    meet(n_dp, n_t, inside)
    if inside:
        gather = Gather(n_dp, n_t, block_ref, gathered, *refs)
        gather.start()
        weights = Weights(shard, width, gathered=gathered)
    else:
        gathered[...] = jnp.zeros_like(gathered)
        weights = Weights(shard, width, whole=block_ref)

    full[rows - rows % 8 :, :] = jnp.zeros((padded - rows + rows % 8, width), F32)
    full[:rows, :] = x_ref[...].astype(F32)
    cot_full[rows - rows % 8 :, :] = jnp.zeros((padded - rows + rows % 8, width), F32)
    cot_full[:rows, :] = cot_ref[...].astype(F32)
    bias[...] = image_bias(rows, padded)
    unit, _ = centre(full[...])
    norm_ref[...] = unit.astype(BF16)
    if inside:
        gather.finish()

    norms = norm_rows(weights.small())
    unit, _ = centre(full[...])
    normed = (unit * norms[0:1] + norms[1:2]).astype(BF16)
    norm_ref[...] = normed
    q_ref[...] = nn(normed, weights(0)).astype(BF16)
    k_ref[...] = nn(normed, weights(1)).astype(BF16)
    v_ref[...] = nn(normed, weights(2)).astype(BF16)
    low, high = half_masks()

    def heads(j, carry):
        at = pl.ds(pl.multiple_of(j * LANES, LANES), LANES)
        query, key, value = q_ref[:, at], k_ref[:, at], v_ref[:, at]
        first = nn(soft_scores(query * low, key, bias[...]).astype(BF16), value)
        second = nn(soft_scores(query * high, key, bias[...]).astype(BF16), value)
        mix_ref[:, at] = (first * low.astype(F32) + second * high.astype(F32)).astype(BF16)
        return carry

    lax.fori_loop(0, width // LANES, heads, 0)
    residual = full[...] + nn(mix_ref[...], weights(3))
    res_ref[...] = residual
    unit, _ = centre(residual)
    moe = (unit * norms[2:3] + norms[3:4]).astype(BF16)
    moe_ref[...] = moe
    probs = router_probs(nn(moe, weights.small()), experts)
    probs_ref[...] = probs
    cot = cot_full[...]
    full[...] = pick_gate(probs, cols_ref[:, 0:1]) * cot
    cot_full[...] = pick_gate(probs, cols_ref[:, 1:2]) * cot

    def selectors(p):
        slot = lax.broadcasted_iota(jnp.int32, (rooms, padded), 0) + p * rooms
        first = (slot == slots_ref[0:1, :]).astype(F32)
        second = (slot == slots_ref[1:2, :]).astype(F32)
        return first, second

    def d_copy(k):
        to = lax.rem(dp + k, n_dp)
        return remote(send_d.at[to], recv_d.at[dp], d_send.at[k], d_recv.at[k], {"dp": to})

    def s_copy(k):
        to = lax.rem(dp + k, n_dp)
        return remote(send_s.at[to], recv_s.at[dp], s_send.at[k], s_recv.at[k], {"dp": to})

    def dispatch(k, carry):
        to = lax.rem(dp + k, n_dp)
        first, second = selectors(to)
        send_d[to] = nn((first + second).astype(BF16), moe_ref[...]).astype(BF16)

        @pl.when(k > 0)
        def _():
            d_copy(k).start()

        return carry

    def dispatch_grad(k, carry):
        to = lax.rem(dp + k, n_dp)
        first, second = selectors(to)
        rows_grad = nn(first.astype(BF16), full[...].astype(BF16)) + nn(second.astype(BF16), cot_full[...].astype(BF16))
        send_s[to] = rows_grad.astype(BF16)

        @pl.when(k > 0)
        def _():
            s_copy(k).start()

        return carry

    lax.fori_loop(0, n_dp, dispatch, 0)
    lax.fori_loop(0, n_dp, dispatch_grad, 0)
    recv_d[dp] = send_d[dp]
    recv_s[dp] = send_s[dp]
    for k in range(1, n_dp):
        d_copy(k).wait()
    for k in range(1, n_dp):
        s_copy(k).wait()


def forward(cfg, cid, x, cot, cols, slots, block):
    n_dp, n_t, rows, padded, width, experts, rooms, shard, inside = cfg
    rows_block = ceil_to(5 * shard, 16)
    low = jax.ShapeDtypeStruct((padded, width), BF16)
    sent = jax.ShapeDtypeStruct((n_dp, rooms, width), BF16)
    gathered = (n_dp, n_t, rows_block, width) if inside else (1, 1, 16, LANES)
    outs = [jax.ShapeDtypeStruct(gathered, BF16), sent, sent, jax.ShapeDtypeStruct((padded, width), F32)]
    outs += [low] * 6 + [jax.ShapeDtypeStruct((padded, LANES), F32)]
    scratch = [
        VMEM((padded, width), F32),
        VMEM((padded, width), F32),
        VMEM((padded, padded), F32),
        VMEM((n_dp, rooms, width), BF16),
        VMEM((n_dp, rooms, width), BF16),
    ] + [DMA((n_dp,))] * 4
    if inside:
        scratch += Gather.scratch(n_dp, n_t)
    whole = pl.BlockSpec(memory_space=VMEM)
    return pl.pallas_call(
        partial(forward_kernel, cfg),
        out_shape=outs,
        in_specs=[whole] * 5,
        out_specs=[whole] * len(outs),
        scratch_shapes=scratch,
        compiler_params=pltpu.CompilerParams(
            collective_id=cid, has_side_effects=True, vmem_limit_bytes=56 * 2**20
        ),
        name="forward_" + str(rooms),
    )(x, cot, cols, slots, block)


def expert_kernel(chunks, d_ref, s_ref, w_in_ref, w_out_ref, ret_ref, back_ref, g_in_ref, g_out_ref, ret, back, g_in, g_out):
    step = pl.program_id(0)
    rows = d_ref.shape[0]
    chunk = rows // chunks

    @pl.when(step == 0)
    def _():
        ret[...] = jnp.zeros_like(ret)
        back[...] = jnp.zeros_like(back)

    g_in[...] = jnp.zeros_like(g_in)
    g_out[...] = jnp.zeros_like(g_out)
    w_in, w_out = w_in_ref[...], w_out_ref[...]

    def part(c, carry):
        at = pl.ds(pl.multiple_of(c * chunk, 16), chunk)
        took, slot_grad = d_ref[at, :], s_ref[at, :]
        hidden = nt(took, w_in)
        size = jnp.abs(hidden)
        bell = jnp.exp(-0.5 * hidden * hidden)
        near = 1.0 / (1.0 + 0.23164189 * size)
        tail = near * (
            0.127414796 + near * (-0.142248368 + near * (0.7107068705 + near * (-0.7265760135 + near * 0.5307027145)))
        )
        tail = tail * bell
        share = jnp.where(hidden < 0.0, tail, 1.0 - tail)
        active = (hidden * share).astype(BF16)
        slope = share + hidden * bell * 0.3989422804014327
        grad_hidden = (nt(slot_grad, w_out) * slope).astype(BF16)
        ret[at, :] += nn(active, w_out)
        back[at, :] += nn(grad_hidden, w_in)
        g_out[...] += tn(active, slot_grad)
        g_in[...] += tn(grad_hidden, took)
        return carry

    lax.fori_loop(0, chunks, part, 0)
    g_in_ref[...] = g_in[...].astype(BF16)
    g_out_ref[...] = g_out[...].astype(BF16)

    @pl.when(step == pl.num_programs(0) - 1)
    def _():
        ret_ref[...] = ret[...].astype(BF16)
        back_ref[...] = back[...].astype(BF16)


def run_expert(took, slot_grad, w_in, w_out):
    rows, width = took.shape
    hidden = w_in.shape[0]
    block = 256
    chunks = next(c for c in range(max(1, rows // 400), rows + 1) if rows % c == 0 and (rows // c) % 16 == 0)
    whole = pl.BlockSpec((rows, width), lambda i: (0, 0))
    part = pl.BlockSpec((block, width), lambda i: (i, 0))
    low = jax.ShapeDtypeStruct((rows, width), BF16)
    grad = jax.ShapeDtypeStruct((hidden, width), BF16)
    return pl.pallas_call(
        partial(expert_kernel, chunks),
        grid=(hidden // block,),
        out_shape=[low, low, grad, grad],
        in_specs=[whole, whole, part, part],
        out_specs=[whole, whole, part, part],
        scratch_shapes=[
            VMEM((rows, width), F32),
            VMEM((rows, width), F32),
            VMEM((block, width), F32),
            VMEM((block, width), F32),
        ],
        compiler_params=pltpu.CompilerParams(vmem_limit_bytes=56 * 2**20),
        cost_estimate=pl.CostEstimate(
            flops=12 * rows * width * hidden, bytes_accessed=12 * rows * width + 8 * hidden * width, transcendentals=0
        ),
        name="expert_" + str(rows),
    )(took, slot_grad, w_in, w_out)


def backward_kernel(cfg, *refs):
    n_dp, n_t, rows, padded, width, experts, rooms, shard, inside = cfg
    refs = list(refs)

    def take(count):
        got = refs[:count]
        del refs[:count]
        return got

    ret_ref, back_ref, x_ref, cot_ref, cols_ref, weights_ref = take(6)
    res_ref, moe_ref, q_ref, k_ref, v_ref, mix_ref, norm_ref, probs_ref = take(8)
    out_ref, gx_ref, sum_ref = take(3)
    full, cot_full, bias, ret_in, back_in, grads, r_send, r_recv, b_send, b_recv = take(10)
    dq, dk, dv = take(3)
    dp = lax.axis_index("dp")
    meet(n_dp, n_t, inside)

    def r_copy(k):
        to = lax.rem(dp + k, n_dp)
        return remote(ret_ref.at[to], ret_in.at[dp], r_send.at[k], r_recv.at[k], {"dp": to})

    def b_copy(k):
        to = lax.rem(dp + k, n_dp)
        return remote(back_ref.at[to], back_in.at[dp], b_send.at[k], b_recv.at[k], {"dp": to})

    for k in range(1, n_dp):
        r_copy(k).start()
    for k in range(1, n_dp):
        b_copy(k).start()
    ret_in[dp] = ret_ref[dp]
    back_in[dp] = back_ref[dp]
    weights = Weights(shard, width, gathered=weights_ref) if inside else Weights(shard, width, whole=weights_ref)
    tail = rows - rows % 8
    full[tail:, :] = jnp.zeros((padded - tail, width), F32)
    full[:rows, :] = x_ref[...].astype(F32)
    cot_full[tail:, :] = jnp.zeros((padded - tail, width), F32)
    cot_full[:rows, :] = cot_ref[...].astype(F32)
    bias[...] = image_bias(rows, padded)
    norms = norm_rows(weights.small())
    slot_count = n_dp * rooms
    lane = lax.broadcasted_iota(jnp.int32, (padded, slot_count), 1)
    first = (lane == cols_ref[:, 2:3]).astype(F32)
    second = (lane == cols_ref[:, 3:4]).astype(F32)
    both = (first + second).astype(BF16)

    for k in range(1, n_dp):
        r_copy(k).wait()
    returned = ret_in[...].reshape(slot_count, width)
    first_rows = nn(first.astype(BF16), returned)
    second_rows = nn(second.astype(BF16), returned)
    probs = probs_ref[...]
    first_id, second_id = cols_ref[:, 0:1], cols_ref[:, 1:2]
    outcome = res_ref[...] + pick_gate(probs, first_id) * first_rows + pick_gate(probs, second_id) * second_rows
    out_ref[...] = outcome[:rows].astype(BF16)
    cot = cot_full[...]
    first_grad = jnp.sum(first_rows * cot, axis=1, keepdims=True)
    second_grad = jnp.sum(second_rows * cot, axis=1, keepdims=True)
    spot = lax.broadcasted_iota(jnp.int32, probs.shape, 1)
    grad_probs = jnp.where(spot == first_id + 4, first_grad, 0.0) + jnp.where(spot == second_id + 4, second_grad, 0.0)
    grad_logits = (probs * (grad_probs - jnp.sum(probs * grad_probs, axis=1, keepdims=True))).astype(BF16)
    grad_router = tn(moe_ref[...], grad_logits)

    for k in range(1, n_dp):
        b_copy(k).wait()
    grad_moe = nn(both, back_in[...].reshape(slot_count, width)) + nt(grad_logits, weights.small())
    unit, inverse = centre(res_ref[...])
    extra, gain_two, shift_two = norm_back(grad_moe, unit, inverse, norms[2:3])
    grad_residual = cot + extra
    cot_full[...] = grad_residual
    grad_attended = grad_residual.astype(BF16)
    n_all = n_dp * n_t

    def keep(at, value):
        if inside:
            grads[:, :, at * shard : (at + 1) * shard, :] = value.astype(BF16).reshape(n_dp, n_t, shard, width)
        else:
            sum_ref[at] = value

    keep(3, tn(mix_ref[...], grad_attended))
    mix_ref_grad = nt(grad_attended, weights(3)).astype(BF16)
    dq[...] = mix_ref_grad
    low, high = half_masks()
    low_f, high_f = low.astype(F32), high.astype(F32)
    scale = HEAD_DIM ** (-0.5)

    def heads(j, carry):
        at = pl.ds(pl.multiple_of(j * LANES, LANES), LANES)
        query, key, value, grad = q_ref[:, at], k_ref[:, at], v_ref[:, at], dq[:, at]
        for mask, mask_f in ((low, low_f), (high, high_f)):
            probs = soft_scores(query * mask, key, bias[...])
            grad_probs = nt(grad * mask, value)
            grad_scores = probs * (grad_probs - jnp.sum(probs * grad_probs, axis=1, keepdims=True))
            grad_scores = grad_scores.astype(BF16)
            part_v = tn(probs.astype(BF16), grad)
            part_q = nn(grad_scores, key) * scale
            part_k = tn(grad_scores, query) * scale
            if mask is low:
                sum_q, sum_k, sum_v = part_q * mask_f, part_k * mask_f, part_v * mask_f
            else:
                sum_q, sum_k, sum_v = sum_q + part_q * mask_f, sum_k + part_k * mask_f, sum_v + part_v * mask_f
        dq[:, at] = sum_q.astype(BF16)
        dk[:, at] = sum_k.astype(BF16)
        dv[:, at] = sum_v.astype(BF16)
        return carry

    lax.fori_loop(0, width // LANES, heads, 0)
    keep(0, tn(norm_ref[...], dq[...]))
    keep(1, tn(norm_ref[...], dk[...]))
    keep(2, tn(norm_ref[...], dv[...]))
    grad_normed = nt(dq[...], weights(0)) + nt(dk[...], weights(1)) + nt(dv[...], weights(2))
    unit, inverse = centre(full[...])
    extra, gain_one, shift_one = norm_back(grad_normed, unit, inverse, norms[0:1])
    gx_ref[...] = (cot_full[...] + extra)[:rows].astype(BF16)
    line = lax.broadcasted_iota(jnp.int32, (8, width), 0)
    small_rows = (
        jnp.where(line == 0, gain_one, 0.0)
        + jnp.where(line == 1, shift_one, 0.0)
        + jnp.where(line == 2, gain_two, 0.0)
        + jnp.where(line == 3, shift_two, 0.0)
    )
    pick = lax.broadcasted_iota(jnp.int32, (8, LANES), 0) == lax.broadcasted_iota(jnp.int32, (8, LANES), 1)
    small = grad_router + tn(small_rows.astype(BF16), pick.astype(F32).astype(BF16))
    if inside:
        at = slice(4 * shard, 5 * shard)
        grads[:, :, at, :LANES] = small.astype(BF16).reshape(n_dp, n_t, shard, LANES)
        grads[:, :, at, LANES:] = jnp.zeros((n_dp, n_t, shard, width - LANES), BF16)
        Scatter(n_dp, n_t, grads, sum_ref, *refs).run()
    else:
        sum_ref[4] = jnp.zeros((width, width), F32)
        sum_ref[4, :, :LANES] = small


def backward(cfg, cid, *args):
    n_dp, n_t, rows, padded, width, experts, rooms, shard, inside = cfg
    rows_block = ceil_to(5 * shard, 16)
    total = (rows_block, width) if inside else (5, width, width)
    outs = [jax.ShapeDtypeStruct((rows, width), BF16)] * 2 + [jax.ShapeDtypeStruct(total, F32)]
    scratch = [
        VMEM((padded, width), F32),
        VMEM((padded, width), F32),
        VMEM((padded, padded), F32),
        VMEM((n_dp, rooms, width), BF16),
        VMEM((n_dp, rooms, width), BF16),
        VMEM((n_dp, n_t, rows_block, width) if inside else (1, 1, 16, LANES), BF16),
    ]
    scratch += [DMA((n_dp,))] * 4 + [VMEM((padded, width), BF16)] * 3
    if inside:
        scratch += Scatter.scratch(n_dp, n_t, (rows_block, width))
    whole = pl.BlockSpec(memory_space=VMEM)
    return pl.pallas_call(
        partial(backward_kernel, cfg),
        out_shape=outs,
        in_specs=[whole] * len(args),
        out_specs=[whole] * len(outs),
        scratch_shapes=scratch,
        compiler_params=pltpu.CompilerParams(
            collective_id=cid, has_side_effects=True, vmem_limit_bytes=56 * 2**20
        ),
        name="backward_" + str(rooms),
    )(*args)


def route_pairs(routes, t, row_count, experts, capacity):
    tok_count = routes.shape[0]
    ids = jnp.arange(experts, dtype=jnp.int32)[None, :]
    start = t * row_count
    rows = lax.dynamic_slice_in_dim(routes, start, row_count, 0)
    before = (jnp.arange(tok_count, dtype=jnp.int32) < start)[:, None]
    all_first = routes[:, 0:1] == ids
    all_second = routes[:, 1:2] == ids
    base_first = jnp.sum((all_first & before).astype(jnp.int32), axis=0)
    total_first = jnp.sum(all_first.astype(jnp.int32), axis=0)
    base_second = jnp.sum((all_second & before).astype(jnp.int32), axis=0)
    hot_first = rows[:, 0:1] == ids
    hot_second = rows[:, 1:2] == ids
    at = jnp.arange(row_count, dtype=jnp.int32)
    lower = (at[:, None] > at[None, :]).astype(BF16)
    both = jnp.concatenate([hot_first, hot_second], axis=1).astype(BF16)
    earlier = nn(lower, both).astype(jnp.int32)
    own_first = jnp.sum(hot_first.astype(jnp.int32), axis=0)
    rank_first = earlier[:, :experts]
    rank_second = earlier[:, experts:] + own_first
    place_first = rank_first + base_first
    place_second = earlier[:, experts:] + total_first + base_second
    first = jnp.sum(jnp.where(hot_first & (place_first < capacity), rank_first + 1, 0), axis=1) - 1
    second = jnp.sum(jnp.where(hot_second & (place_second < capacity), rank_second + 1, 0), axis=1) - 1
    most = jnp.maximum(jnp.max(first), jnp.max(second)) + 1
    return rows, first, second, most


def per_device(
    n_dp,
    n_t,
    inputs,
    cotangent,
    routes,
    gain_attn,
    shift_attn,
    query_w,
    key_w,
    value_w,
    out_w,
    gain_moe,
    shift_moe,
    router_w,
    expert_in,
    expert_out,
):
    t = lax.axis_index("tensor")
    shard, width = query_w.shape
    experts = router_w.shape[1]
    tok_count = routes.shape[0]
    rows = inputs.shape[0]
    padded = ceil_to(rows, 16)
    capacity = (5 * tok_count + 2 * experts - 1) // (2 * experts)
    inside = shard % 16 == 0
    every = ("dp", "tensor")

    route_rows, first_rank, second_rank, most = route_pairs(routes, t, rows, experts, capacity)

    w_in = lax.all_gather(expert_in[0].T.astype(BF16), "tensor", axis=0, tiled=True)
    w_out = lax.all_gather(expert_out[0].astype(BF16), "tensor", axis=0, tiled=True)

    small = jnp.concatenate(
        [
            gain_attn[:, None],
            shift_attn[:, None],
            gain_moe[:, None],
            shift_moe[:, None],
            router_w,
            jnp.broadcast_to((most // 16).astype(F32), (shard, 1)),
            jnp.broadcast_to((most % 16).astype(F32), (shard, 1)),
        ],
        axis=1,
    )
    small = jnp.pad(small, ((0, 0), (0, width - small.shape[1])))
    if inside:
        block = jnp.concatenate([query_w, key_w, value_w, out_w, small], axis=0).astype(BF16)
    else:
        stack = jnp.stack([query_w, key_w, value_w, out_w, small]).astype(BF16)
        block = lax.all_gather(stack, every, axis=1, tiled=True)

    def program(rooms, cids):
        cfg = (n_dp, n_t, rows, padded, width, experts, rooms, shard, inside)

        def slot(choice, rank):
            return jnp.where((rank >= 0) & (rank < rooms), choice * rooms + rank, -1)

        slots = jnp.stack([slot(route_rows[:, 0], first_rank), slot(route_rows[:, 1], second_rank)])
        slots = jnp.pad(slots, ((0, 0), (0, padded - rows)), constant_values=-1)
        cols = jnp.concatenate([jnp.pad(route_rows, ((0, padded - rows), (0, 0))), slots.T], axis=1)

        def first_half():
            return forward(cfg, cids[0], inputs, cotangent, cols, slots, block)

        def second_half(kept):
            gathered, took, slot_grad = kept[0], kept[1], kept[2]
            returned, back, grad_inner, grad_outer = run_expert(
                took.reshape(n_dp * rooms, width), slot_grad.reshape(n_dp * rooms, width), w_in, w_out
            )
            grad_inner = lax.psum_scatter(grad_inner, "tensor", scatter_dimension=0, tiled=True).astype(F32).T
            grad_outer = lax.psum_scatter(grad_outer, "tensor", scatter_dimension=0, tiled=True).astype(F32)
            output_rows, grad_tokens, summed = backward(
                cfg,
                cids[1],
                returned.reshape(n_dp, rooms, width),
                back.reshape(n_dp, rooms, width),
                inputs,
                cotangent,
                cols,
                gathered if inside else block,
                *kept[3:],
            )
            if not inside:
                summed = lax.psum_scatter(summed, every, scatter_dimension=1, tiled=True).reshape(5 * shard, width)
            return output_rows, grad_tokens, summed, grad_inner, grad_outer

        return first_half, second_half

    most_rooms = ceil_to(rows, 16)
    rooms = min(ceil_to((7 * rows + 2 * experts - 1) // (2 * experts), 16), most_rooms)
    first_half, second_half = program(rooms, (0, 1))
    kept = first_half()
    small_all = kept[0][:, :, 4 * shard : 5 * shard, :LANES] if inside else block[4][:, :LANES]
    counts = small_all[..., 4 + experts : 6 + experts].astype(F32)
    most_all = jnp.max(counts[..., 0] * 16.0 + counts[..., 1]).astype(jnp.int32)

    def again(_):
        first_again, second_again = program(most_rooms, (2, 3))
        return second_again(first_again())

    output_rows, grad_tokens, summed, grad_inner, grad_outer = lax.cond(most_all > rooms, again, second_half, kept)
    small_sum = summed[4 * shard : 5 * shard]
    return (
        output_rows,
        grad_tokens,
        small_sum[:, 0],
        small_sum[:, 1],
        summed[0:shard],
        summed[shard : 2 * shard],
        summed[2 * shard : 3 * shard],
        summed[3 * shard : 4 * shard],
        small_sum[:, 2],
        small_sum[:, 3],
        small_sum[:, 4 : 4 + experts],
        grad_inner[None],
        grad_outer[None],
    )


def solution(mesh):
    every = ("dp", "tensor")
    rows, line = P(every, None), P(every)
    w_in, w_out = P("dp", None, "tensor"), P("dp", "tensor", None)
    return jax.shard_map(
        partial(per_device, mesh.shape["dp"], mesh.shape["tensor"]),
        mesh=mesh,
        in_specs=(rows, rows, P("dp", None), line, line, rows, rows, rows, rows, line, line, rows, w_in, w_out),
        out_specs=(rows, rows, line, line, rows, rows, rows, rows, line, line, rows, w_in, w_out),
        check_vma=False,
    )
```

```python
from functools import partial

import jax
import jax.numpy as jnp
from jax import lax
from jax.experimental import pallas as pl
from jax.experimental.pallas import tpu as pltpu
from jax.sharding import PartitionSpec as P

SEQ = 197
HEAD_DIM = 64
LANES = 128
MESH = pl.DeviceIdType.MESH
F32 = jnp.float32
BF16 = jnp.bfloat16
VMEM = pltpu.VMEM
DMA = pltpu.SemaphoreType.DMA


def ceil_to(value, unit):
    return (value + unit - 1) // unit * unit


def nn(left, right):
    return lax.dot_general(left, right, (((1,), (0,)), ((), ())), preferred_element_type=F32)


def nt(left, right):
    return lax.dot_general(left, right, (((1,), (1,)), ((), ())), preferred_element_type=F32)


def tn(left, right):
    return lax.dot_general(left, right, (((0,), (0,)), ((), ())), preferred_element_type=F32)


def remote(src, dst, send, recv, device):
    return pltpu.make_async_remote_copy(
        src_ref=src, dst_ref=dst, send_sem=send, recv_sem=recv, device_id=device, device_id_type=MESH
    )


def meet(n_dp, n_t, z_too):
    dp = lax.axis_index("dp")
    t = lax.axis_index("tensor")
    bar = pltpu.get_barrier_semaphore()
    for k in range(1, n_dp):
        pl.semaphore_signal(bar, inc=1, device_id={"dp": lax.rem(dp + k, n_dp)}, device_id_type=MESH)
    if z_too:
        for k in range(1, n_t):
            pl.semaphore_signal(bar, inc=1, device_id={"tensor": lax.rem(t + k, n_t)}, device_id_type=MESH)
    pl.semaphore_wait(bar, n_dp - 1 + (n_t - 1 if z_too else 0))


class Gather:
    def __init__(self, n_dp, n_t, block, out, own_sem, z_send, z_recv, c_send, c_recv, k_send, k_recv):
        self.n_t, self.n_chip = n_t, n_dp // 2
        self.block, self.out, self.own_sem = block, out, own_sem
        self.z_sems, self.c_sems, self.k_sems = (z_send, z_recv), (c_send, c_recv), (k_send, k_recv)
        self.dp, self.t = lax.axis_index("dp"), lax.axis_index("tensor")
        self.chip, self.core = self.dp // 2, lax.rem(self.dp, 2)
        self.other = self.chip * 2 + 1 - self.core

    @staticmethod
    def scratch(n_dp, n_t):
        n_chip = n_dp // 2
        pair = [DMA((n_chip, n_t))] * 2
        return [DMA, DMA((n_t,)), DMA((n_t,))] + pair + pair

    def z_copy(self, k):
        send, recv = self.z_sems
        to = lax.rem(self.t + k, self.n_t)
        return remote(self.block, self.out.at[self.dp, self.t], send.at[k], recv.at[k], {"tensor": to})

    def chip_copy(self, k, j):
        send, recv = self.c_sems
        row = lax.rem(self.t + self.n_t - j, self.n_t)
        here = self.out.at[self.dp, row]
        to = lax.rem(self.chip + k, self.n_chip) * 2 + self.core
        return remote(self.block if j == 0 else here, here, send.at[k, j], recv.at[k, j], {"dp": to})

    def core_copy(self, k, j):
        send, recv = self.k_sems
        row = lax.rem(self.t + self.n_t - j, self.n_t)
        src = lax.rem(self.chip + self.n_chip - k, self.n_chip) * 2 + self.core
        here = self.out.at[src, row]
        own = k == 0 and j == 0
        return remote(self.block if own else here, here, send.at[k, j], recv.at[k, j], {"dp": self.other})

    def own_copy(self):
        return pltpu.make_async_copy(self.block, self.out.at[self.dp, self.t], self.own_sem)

    def start(self):
        for k in range(1, self.n_t):
            self.z_copy(k).start()
        self.own_copy().start()
        for k in range(1, self.n_chip):
            self.chip_copy(k, 0).start()
        self.core_copy(0, 0).start()

    def finish(self):
        for j in range(1, self.n_t):
            self.z_copy(j).wait_recv()
            for k in range(1, self.n_chip):
                self.chip_copy(k, j).start()
            self.core_copy(0, j).start()
        for j in range(self.n_t):
            for k in range(1, self.n_chip):
                self.chip_copy(k, j).wait_recv()
                self.core_copy(k, j).start()
        self.own_copy().wait()
        for k in range(1, self.n_t):
            self.z_copy(k).wait_send()
        for j in range(self.n_t):
            for k in range(1, self.n_chip):
                self.chip_copy(k, j).wait_send()
            for k in range(self.n_chip):
                self.core_copy(k, j).wait()


class Scatter:
    def __init__(
        self, n_dp, n_t, grads, out, core_in, half, chip_in, part, z_in, k_send, k_recv, c_send, c_recv, z_send, z_recv
    ):
        self.n_t, self.n_chip = n_t, n_dp // 2
        self.grads, self.out = grads, out
        self.core_in, self.half, self.chip_in, self.part, self.z_in = core_in, half, chip_in, part, z_in
        self.k_sems, self.c_sems, self.z_sems = (k_send, k_recv), (c_send, c_recv), (z_send, z_recv)
        self.dp, self.t = lax.axis_index("dp"), lax.axis_index("tensor")
        self.chip, self.core = self.dp // 2, lax.rem(self.dp, 2)
        self.other = self.chip * 2 + 1 - self.core

    @staticmethod
    def scratch(n_dp, n_t, block):
        n_chip = n_dp // 2
        buffers = [VMEM((n_chip, n_t) + block, BF16)] * 3 + [VMEM((n_t,) + block, BF16)] * 2
        return buffers + [DMA((n_chip,))] * 4 + [DMA((n_t,))] * 2

    def core_copy(self, k):
        to = lax.rem(self.chip + k, self.n_chip)
        src = self.grads.at[to * 2 + 1 - self.core]
        return remote(src, self.core_in.at[k], self.k_sems[0].at[k], self.k_sems[1].at[k], {"dp": self.other})

    def chip_copy(self, k):
        to = lax.rem(self.chip + k, self.n_chip) * 2 + self.core
        return remote(self.half.at[k], self.chip_in.at[k], self.c_sems[0].at[k], self.c_sems[1].at[k], {"dp": to})

    def z_copy(self, k):
        to = lax.rem(self.t + k, self.n_t)
        return remote(self.part.at[k], self.z_in.at[k], self.z_sems[0].at[k], self.z_sems[1].at[k], {"tensor": to})

    def run(self):
        n_chip, n_t = self.n_chip, self.n_t
        order = list(range(1, n_chip)) + [0]
        for k in order:
            self.core_copy(k).start()
        for k in order:
            self.core_copy(k).wait_recv()
            if k > 0:
                to = lax.rem(self.chip + k, n_chip) * 2 + self.core
                self.half[k] = (self.grads[to].astype(F32) + self.core_in[k].astype(F32)).astype(BF16)
                self.chip_copy(k).start()
        for k in range(1, n_chip):
            self.chip_copy(k).wait_recv()
        for k in list(range(1, n_t)) + [0]:
            row = lax.rem(self.t + k, n_t)
            total = self.grads[self.dp, row].astype(F32) + self.core_in[0, row].astype(F32)
            for c in range(1, n_chip):
                total = total + self.chip_in[c, row].astype(F32)
            if k > 0:
                self.part[k] = total.astype(BF16)
                self.z_copy(k).start()
            else:
                self.out[...] = total
        for k in range(1, n_t):
            self.z_copy(k).wait_recv()
            self.out[...] += self.z_in[k].astype(F32)
        for k in range(n_chip):
            self.core_copy(k).wait_send()
        for k in range(1, n_chip):
            self.chip_copy(k).wait_send()
        for k in range(1, n_t):
            self.z_copy(k).wait_send()


def centre(values):
    centred = values - jnp.mean(values, axis=1, keepdims=True)
    inverse = lax.rsqrt(jnp.mean(centred * centred, axis=1, keepdims=True) + 1e-06)
    return centred * inverse, inverse


def norm_back(grad, unit, inverse, gain):
    scaled = grad * gain
    back = inverse * (
        scaled
        - jnp.mean(scaled, axis=1, keepdims=True)
        - unit * jnp.mean(scaled * unit, axis=1, keepdims=True)
    )
    return back, jnp.sum(grad * unit, axis=0, keepdims=True), jnp.sum(grad, axis=0, keepdims=True)


def norm_rows(small):
    pick = lax.broadcasted_iota(jnp.int32, (8, LANES), 0) == lax.broadcasted_iota(jnp.int32, (8, LANES), 1)
    return nt(pick.astype(F32).astype(BF16), small)


def image_bias(rows, padded):
    line = lax.broadcasted_iota(jnp.int32, (padded, padded), 0)
    column = lax.broadcasted_iota(jnp.int32, (padded, padded), 1)
    image_line, image_column = jnp.zeros_like(line), jnp.zeros_like(column)
    for at in range(SEQ, rows + 1, SEQ):
        image_line += (line >= at).astype(jnp.int32)
        image_column += (column >= at).astype(jnp.int32)
    return jnp.where((image_line == image_column) & (column < rows), 0.0, -1e30)


def half_masks():
    lane = lax.broadcasted_iota(jnp.int32, (1, LANES), 1)
    low = (lane < HEAD_DIM).astype(F32)
    return low.astype(BF16), (1.0 - low).astype(BF16)


def soft_scores(query, key, bias):
    scores = nt(query, key) * HEAD_DIM ** (-0.5) + bias
    power = jnp.exp(scores - jnp.max(scores, axis=1, keepdims=True))
    return power * (1.0 / jnp.sum(power, axis=1, keepdims=True))


def router_probs(logits, experts):
    lane = lax.broadcasted_iota(jnp.int32, logits.shape, 1)
    inside = (lane >= 4) & (lane < 4 + experts)
    kept = jnp.where(inside, logits, -1e30)
    power = jnp.where(inside, jnp.exp(kept - jnp.max(kept, axis=1, keepdims=True)), 0.0)
    return power * (1.0 / jnp.sum(power, axis=1, keepdims=True))


def pick_gate(probs, choice):
    lane = lax.broadcasted_iota(jnp.int32, probs.shape, 1)
    return jnp.sum(jnp.where(lane == choice + 4, probs, 0.0), axis=1, keepdims=True)


class Weights:
    def __init__(self, shard, width, gathered=None, whole=None):
        self.shard, self.width, self.gathered, self.whole = shard, width, gathered, whole

    def __call__(self, at):
        if self.whole is not None:
            return self.whole[at]
        part = self.gathered[:, :, at * self.shard : (at + 1) * self.shard, :]
        return part.reshape(self.width, self.width)

    def small(self):
        if self.whole is not None:
            return self.whole[4, :, :LANES]
        part = self.gathered[:, :, 4 * self.shard : 5 * self.shard, :LANES]
        return part.reshape(self.width, LANES)


def forward_kernel(cfg, *refs):
    n_dp, n_t, rows, padded, width, experts, rooms, shard, inside = cfg
    refs = list(refs)

    def take(count):
        got = refs[:count]
        del refs[:count]
        return got

    x_ref, cot_ref, cols_ref, slots_ref, block_ref = take(5)
    gathered, recv_d, recv_s, res_ref, moe_ref, q_ref, k_ref, v_ref, mix_ref, norm_ref, probs_ref = take(11)
    full, cot_full, bias, send_d, send_s, d_send, d_recv, s_send, s_recv = take(9)
    dp = lax.axis_index("dp")
    meet(n_dp, n_t, inside)
    if inside:
        gather = Gather(n_dp, n_t, block_ref, gathered, *refs)
        gather.start()
        weights = Weights(shard, width, gathered=gathered)
    else:
        gathered[...] = jnp.zeros_like(gathered)
        weights = Weights(shard, width, whole=block_ref)

    full[rows - rows % 8 :, :] = jnp.zeros((padded - rows + rows % 8, width), F32)
    full[:rows, :] = x_ref[...].astype(F32)
    cot_full[rows - rows % 8 :, :] = jnp.zeros((padded - rows + rows % 8, width), F32)
    cot_full[:rows, :] = cot_ref[...].astype(F32)
    bias[...] = image_bias(rows, padded)
    unit, _ = centre(full[...])
    norm_ref[...] = unit.astype(BF16)
    if inside:
        gather.finish()

    norms = norm_rows(weights.small())
    unit, _ = centre(full[...])
    normed = (unit * norms[0:1] + norms[1:2]).astype(BF16)
    norm_ref[...] = normed
    q_ref[...] = nn(normed, weights(0)).astype(BF16)
    k_ref[...] = nn(normed, weights(1)).astype(BF16)
    v_ref[...] = nn(normed, weights(2)).astype(BF16)
    low, high = half_masks()

    def heads(j, carry):
        at = pl.ds(pl.multiple_of(j * LANES, LANES), LANES)
        query, key, value = q_ref[:, at], k_ref[:, at], v_ref[:, at]
        first = nn(soft_scores(query * low, key, bias[...]).astype(BF16), value)
        second = nn(soft_scores(query * high, key, bias[...]).astype(BF16), value)
        mix_ref[:, at] = (first * low.astype(F32) + second * high.astype(F32)).astype(BF16)
        return carry

    lax.fori_loop(0, width // LANES, heads, 0)
    residual = full[...] + nn(mix_ref[...], weights(3))
    res_ref[...] = residual
    unit, _ = centre(residual)
    moe = (unit * norms[2:3] + norms[3:4]).astype(BF16)
    moe_ref[...] = moe
    probs = router_probs(nn(moe, weights.small()), experts)
    probs_ref[...] = probs
    cot = cot_full[...]
    full[...] = pick_gate(probs, cols_ref[:, 0:1]) * cot
    cot_full[...] = pick_gate(probs, cols_ref[:, 1:2]) * cot

    def selectors(p):
        slot = lax.broadcasted_iota(jnp.int32, (rooms, padded), 0) + p * rooms
        first = (slot == slots_ref[0:1, :]).astype(F32)
        second = (slot == slots_ref[1:2, :]).astype(F32)
        return first, second

    def d_copy(k):
        to = lax.rem(dp + k, n_dp)
        return remote(send_d.at[to], recv_d.at[dp], d_send.at[k], d_recv.at[k], {"dp": to})

    def s_copy(k):
        to = lax.rem(dp + k, n_dp)
        return remote(send_s.at[to], recv_s.at[dp], s_send.at[k], s_recv.at[k], {"dp": to})

    def dispatch(k, carry):
        to = lax.rem(dp + k, n_dp)
        first, second = selectors(to)
        send_d[to] = nn((first + second).astype(BF16), moe_ref[...]).astype(BF16)

        @pl.when(k > 0)
        def _():
            d_copy(k).start()

        return carry

    def dispatch_grad(k, carry):
        to = lax.rem(dp + k, n_dp)
        first, second = selectors(to)
        rows_grad = nn(first.astype(BF16), full[...].astype(BF16)) + nn(second.astype(BF16), cot_full[...].astype(BF16))
        send_s[to] = rows_grad.astype(BF16)

        @pl.when(k > 0)
        def _():
            s_copy(k).start()

        return carry

    lax.fori_loop(0, n_dp, dispatch, 0)
    lax.fori_loop(0, n_dp, dispatch_grad, 0)
    recv_d[dp] = send_d[dp]
    recv_s[dp] = send_s[dp]
    for k in range(1, n_dp):
        d_copy(k).wait()
    for k in range(1, n_dp):
        s_copy(k).wait()


def forward(cfg, cid, x, cot, cols, slots, block):
    n_dp, n_t, rows, padded, width, experts, rooms, shard, inside = cfg
    rows_block = ceil_to(5 * shard, 16)
    low = jax.ShapeDtypeStruct((padded, width), BF16)
    sent = jax.ShapeDtypeStruct((n_dp, rooms, width), BF16)
    gathered = (n_dp, n_t, rows_block, width) if inside else (1, 1, 16, LANES)
    outs = [jax.ShapeDtypeStruct(gathered, BF16), sent, sent, jax.ShapeDtypeStruct((padded, width), F32)]
    outs += [low] * 6 + [jax.ShapeDtypeStruct((padded, LANES), F32)]
    scratch = [
        VMEM((padded, width), F32),
        VMEM((padded, width), F32),
        VMEM((padded, padded), F32),
        VMEM((n_dp, rooms, width), BF16),
        VMEM((n_dp, rooms, width), BF16),
    ] + [DMA((n_dp,))] * 4
    if inside:
        scratch += Gather.scratch(n_dp, n_t)
    whole = pl.BlockSpec(memory_space=VMEM)
    return pl.pallas_call(
        partial(forward_kernel, cfg),
        out_shape=outs,
        in_specs=[whole] * 5,
        out_specs=[whole] * len(outs),
        scratch_shapes=scratch,
        compiler_params=pltpu.CompilerParams(
            collective_id=cid, has_side_effects=True, vmem_limit_bytes=56 * 2**20
        ),
        name="forward_" + str(rooms),
    )(x, cot, cols, slots, block)


def expert_kernel(chunks, d_ref, s_ref, w_in_ref, w_out_ref, ret_ref, back_ref, g_in_ref, g_out_ref, ret, back, g_in, g_out):
    step = pl.program_id(0)
    rows = d_ref.shape[0]
    chunk = rows // chunks

    @pl.when(step == 0)
    def _():
        ret[...] = jnp.zeros_like(ret)
        back[...] = jnp.zeros_like(back)

    g_in[...] = jnp.zeros_like(g_in)
    g_out[...] = jnp.zeros_like(g_out)
    w_in, w_out = w_in_ref[...], w_out_ref[...]

    def part(c, carry):
        at = pl.ds(pl.multiple_of(c * chunk, 16), chunk)
        took, slot_grad = d_ref[at, :], s_ref[at, :]
        hidden = nt(took, w_in)
        size = jnp.abs(hidden)
        bell = jnp.exp(-0.5 * hidden * hidden)
        near = 1.0 / (1.0 + 0.23164189 * size)
        tail = near * (
            0.127414796 + near * (-0.142248368 + near * (0.7107068705 + near * (-0.7265760135 + near * 0.5307027145)))
        )
        tail = tail * bell
        share = jnp.where(hidden < 0.0, tail, 1.0 - tail)
        active = (hidden * share).astype(BF16)
        slope = share + hidden * bell * 0.3989422804014327
        grad_hidden = (nt(slot_grad, w_out) * slope).astype(BF16)
        ret[at, :] += nn(active, w_out)
        back[at, :] += nn(grad_hidden, w_in)
        g_out[...] += tn(active, slot_grad)
        g_in[...] += tn(grad_hidden, took)
        return carry

    lax.fori_loop(0, chunks, part, 0)
    g_in_ref[...] = g_in[...].astype(BF16)
    g_out_ref[...] = g_out[...].astype(BF16)

    @pl.when(step == pl.num_programs(0) - 1)
    def _():
        ret_ref[...] = ret[...].astype(BF16)
        back_ref[...] = back[...].astype(BF16)


def run_expert(took, slot_grad, w_in, w_out):
    rows, width = took.shape
    hidden = w_in.shape[0]
    block = 256
    chunks = next(c for c in range(max(1, rows // 400), rows + 1) if rows % c == 0 and (rows // c) % 16 == 0)
    whole = pl.BlockSpec((rows, width), lambda i: (0, 0))
    part = pl.BlockSpec((block, width), lambda i: (i, 0))
    low = jax.ShapeDtypeStruct((rows, width), BF16)
    grad = jax.ShapeDtypeStruct((hidden, width), BF16)
    return pl.pallas_call(
        partial(expert_kernel, chunks),
        grid=(hidden // block,),
        out_shape=[low, low, grad, grad],
        in_specs=[whole, whole, part, part],
        out_specs=[whole, whole, part, part],
        scratch_shapes=[
            VMEM((rows, width), F32),
            VMEM((rows, width), F32),
            VMEM((block, width), F32),
            VMEM((block, width), F32),
        ],
        compiler_params=pltpu.CompilerParams(vmem_limit_bytes=60 * 2**20),
        cost_estimate=pl.CostEstimate(
            flops=12 * rows * width * hidden, bytes_accessed=12 * rows * width + 8 * hidden * width, transcendentals=0
        ),
        name="expert_" + str(rows),
    )(took, slot_grad, w_in, w_out)


def backward_kernel(cfg, *refs):
    n_dp, n_t, rows, padded, width, experts, rooms, shard, inside = cfg
    refs = list(refs)

    def take(count):
        got = refs[:count]
        del refs[:count]
        return got

    ret_ref, back_ref, x_ref, cot_ref, cols_ref, weights_ref = take(6)
    res_ref, moe_ref, q_ref, k_ref, v_ref, mix_ref, norm_ref, probs_ref = take(8)
    out_ref, gx_ref, sum_ref = take(3)
    full, cot_full, bias, ret_in, back_in, grads, r_send, r_recv, b_send, b_recv = take(10)
    dq, dk, dv = take(3)
    dp = lax.axis_index("dp")
    meet(n_dp, n_t, inside)

    def r_copy(k):
        to = lax.rem(dp + k, n_dp)
        return remote(ret_ref.at[to], ret_in.at[dp], r_send.at[k], r_recv.at[k], {"dp": to})

    def b_copy(k):
        to = lax.rem(dp + k, n_dp)
        return remote(back_ref.at[to], back_in.at[dp], b_send.at[k], b_recv.at[k], {"dp": to})

    for k in range(1, n_dp):
        r_copy(k).start()
    for k in range(1, n_dp):
        b_copy(k).start()
    ret_in[dp] = ret_ref[dp]
    back_in[dp] = back_ref[dp]
    weights = Weights(shard, width, gathered=weights_ref) if inside else Weights(shard, width, whole=weights_ref)
    tail = rows - rows % 8
    full[tail:, :] = jnp.zeros((padded - tail, width), F32)
    full[:rows, :] = x_ref[...].astype(F32)
    cot_full[tail:, :] = jnp.zeros((padded - tail, width), F32)
    cot_full[:rows, :] = cot_ref[...].astype(F32)
    bias[...] = image_bias(rows, padded)
    norms = norm_rows(weights.small())
    slot_count = n_dp * rooms
    lane = lax.broadcasted_iota(jnp.int32, (padded, slot_count), 1)
    first = (lane == cols_ref[:, 2:3]).astype(F32)
    second = (lane == cols_ref[:, 3:4]).astype(F32)
    both = (first + second).astype(BF16)

    for k in range(1, n_dp):
        r_copy(k).wait()
    returned = ret_in[...].reshape(slot_count, width)
    first_rows = nn(first.astype(BF16), returned)
    second_rows = nn(second.astype(BF16), returned)
    probs = probs_ref[...]
    first_id, second_id = cols_ref[:, 0:1], cols_ref[:, 1:2]
    outcome = res_ref[...] + pick_gate(probs, first_id) * first_rows + pick_gate(probs, second_id) * second_rows
    out_ref[...] = outcome[:rows].astype(BF16)
    cot = cot_full[...]
    first_grad = jnp.sum(first_rows * cot, axis=1, keepdims=True)
    second_grad = jnp.sum(second_rows * cot, axis=1, keepdims=True)
    spot = lax.broadcasted_iota(jnp.int32, probs.shape, 1)
    grad_probs = jnp.where(spot == first_id + 4, first_grad, 0.0) + jnp.where(spot == second_id + 4, second_grad, 0.0)
    grad_logits = (probs * (grad_probs - jnp.sum(probs * grad_probs, axis=1, keepdims=True))).astype(BF16)
    grad_router = tn(moe_ref[...], grad_logits)

    for k in range(1, n_dp):
        b_copy(k).wait()
    grad_moe = nn(both, back_in[...].reshape(slot_count, width)) + nt(grad_logits, weights.small())
    unit, inverse = centre(res_ref[...])
    extra, gain_two, shift_two = norm_back(grad_moe, unit, inverse, norms[2:3])
    grad_residual = cot + extra
    cot_full[...] = grad_residual
    grad_attended = grad_residual.astype(BF16)
    n_all = n_dp * n_t

    def keep(at, value):
        if inside:
            grads[:, :, at * shard : (at + 1) * shard, :] = value.astype(BF16).reshape(n_dp, n_t, shard, width)
        else:
            sum_ref[at] = value

    keep(3, tn(mix_ref[...], grad_attended))
    mix_ref_grad = nt(grad_attended, weights(3)).astype(BF16)
    dq[...] = mix_ref_grad
    low, high = half_masks()
    low_f, high_f = low.astype(F32), high.astype(F32)
    scale = HEAD_DIM ** (-0.5)

    def heads(j, carry):
        at = pl.ds(pl.multiple_of(j * LANES, LANES), LANES)
        query, key, value, grad = q_ref[:, at], k_ref[:, at], v_ref[:, at], dq[:, at]
        for mask, mask_f in ((low, low_f), (high, high_f)):
            probs = soft_scores(query * mask, key, bias[...])
            grad_probs = nt(grad * mask, value)
            grad_scores = probs * (grad_probs - jnp.sum(probs * grad_probs, axis=1, keepdims=True))
            grad_scores = grad_scores.astype(BF16)
            part_v = tn(probs.astype(BF16), grad)
            part_q = nn(grad_scores, key) * scale
            part_k = tn(grad_scores, query) * scale
            if mask is low:
                sum_q, sum_k, sum_v = part_q * mask_f, part_k * mask_f, part_v * mask_f
            else:
                sum_q, sum_k, sum_v = sum_q + part_q * mask_f, sum_k + part_k * mask_f, sum_v + part_v * mask_f
        dq[:, at] = sum_q.astype(BF16)
        dk[:, at] = sum_k.astype(BF16)
        dv[:, at] = sum_v.astype(BF16)
        return carry

    lax.fori_loop(0, width // LANES, heads, 0)
    keep(0, tn(norm_ref[...], dq[...]))
    keep(1, tn(norm_ref[...], dk[...]))
    keep(2, tn(norm_ref[...], dv[...]))
    grad_normed = nt(dq[...], weights(0)) + nt(dk[...], weights(1)) + nt(dv[...], weights(2))
    unit, inverse = centre(full[...])
    extra, gain_one, shift_one = norm_back(grad_normed, unit, inverse, norms[0:1])
    gx_ref[...] = (cot_full[...] + extra)[:rows].astype(BF16)
    line = lax.broadcasted_iota(jnp.int32, (8, width), 0)
    small_rows = (
        jnp.where(line == 0, gain_one, 0.0)
        + jnp.where(line == 1, shift_one, 0.0)
        + jnp.where(line == 2, gain_two, 0.0)
        + jnp.where(line == 3, shift_two, 0.0)
    )
    pick = lax.broadcasted_iota(jnp.int32, (8, LANES), 0) == lax.broadcasted_iota(jnp.int32, (8, LANES), 1)
    small = grad_router + tn(small_rows.astype(BF16), pick.astype(F32).astype(BF16))
    if inside:
        at = slice(4 * shard, 5 * shard)
        grads[:, :, at, :LANES] = small.astype(BF16).reshape(n_dp, n_t, shard, LANES)
        grads[:, :, at, LANES:] = jnp.zeros((n_dp, n_t, shard, width - LANES), BF16)
        Scatter(n_dp, n_t, grads, sum_ref, *refs).run()
    else:
        sum_ref[4] = jnp.zeros((width, width), F32)
        sum_ref[4, :, :LANES] = small


def backward(cfg, cid, *args):
    n_dp, n_t, rows, padded, width, experts, rooms, shard, inside = cfg
    rows_block = ceil_to(5 * shard, 16)
    total = (rows_block, width) if inside else (5, width, width)
    outs = [jax.ShapeDtypeStruct((rows, width), BF16)] * 2 + [jax.ShapeDtypeStruct(total, F32)]
    scratch = [
        VMEM((padded, width), F32),
        VMEM((padded, width), F32),
        VMEM((padded, padded), F32),
        VMEM((n_dp, rooms, width), BF16),
        VMEM((n_dp, rooms, width), BF16),
        VMEM((n_dp, n_t, rows_block, width) if inside else (1, 1, 16, LANES), BF16),
    ]
    scratch += [DMA((n_dp,))] * 4 + [VMEM((padded, width), BF16)] * 3
    if inside:
        scratch += Scatter.scratch(n_dp, n_t, (rows_block, width))
    whole = pl.BlockSpec(memory_space=VMEM)
    return pl.pallas_call(
        partial(backward_kernel, cfg),
        out_shape=outs,
        in_specs=[whole] * len(args),
        out_specs=[whole] * len(outs),
        scratch_shapes=scratch,
        compiler_params=pltpu.CompilerParams(
            collective_id=cid, has_side_effects=True, vmem_limit_bytes=56 * 2**20
        ),
        name="backward_" + str(rooms),
    )(*args)


def gelu_parts(hidden):
    bell = jnp.exp(-0.5 * hidden * hidden)
    near = 1.0 / (1.0 + 0.23164189 * jnp.abs(hidden))
    tail = near * (
        0.127414796 + near * (-0.142248368 + near * (0.7107068705 + near * (-0.7265760135 + near * 0.5307027145)))
    )
    tail = tail * bell
    share = jnp.where(hidden < 0.0, tail, 1.0 - tail)
    return hidden * share, share + hidden * bell * 0.3989422804014327


def step_kernel(cfg, *refs):
    n_dp, n_t, rows, padded, width, experts, rooms, shard, inside, hid = cfg
    refs = list(refs)

    def take(count):
        got = refs[:count]
        del refs[:count]
        return got

    x_ref, cot_ref, cols_ref, slots_ref, block_ref, e_in_ref, e_out_ref = take(7)
    out_ref, gx_ref, sum_ref, g_in_ref, g_out_ref, count_ref = take(6)
    gathered, grads, full, cot_full, bias, res, probs_s = take(7)
    moe, q_s, k_s, v_s, mix, norm, dk, dv = take(8)
    send_d, send_s, recv_d, recv_s, ret_in, back_in, act, slope = take(8)
    wi, wo, gi, go, gi_in, go_in = take(6)
    d_send, d_recv, s_send, s_recv, r_send, r_recv, b_send, b_recv = take(8)
    wi_send, wi_recv, wo_send, wo_recv, gi_send, gi_recv, go_send, go_recv, own_sems = take(9)
    dp, t = lax.axis_index("dp"), lax.axis_index("tensor")
    scale = HEAD_DIM ** (-0.5)
    slot_count = n_dp * rooms
    half = min(256, hid)
    wide = min(256, width)

    def dp_copy(src, dst, sems, k):
        to = lax.rem(dp + k, n_dp)
        return remote(src.at[to], dst.at[dp], sems[0].at[k], sems[1].at[k], {"dp": to})

    d_copy = partial(dp_copy, send_d, recv_d, (d_send, d_recv))
    s_copy = partial(dp_copy, send_s, recv_s, (s_send, s_recv))
    r_copy = partial(dp_copy, send_d, ret_in, (r_send, r_recv))
    b_copy = partial(dp_copy, send_s, back_in, (b_send, b_recv))

    def w_copy(w, sems, k):
        to = lax.rem(t + k, n_t)
        return remote(w.at[t], w.at[t], sems[0].at[k], sems[1].at[k], {"tensor": to})

    wi_copy = partial(w_copy, wi, (wi_send, wi_recv))
    wo_copy = partial(w_copy, wo, (wo_send, wo_recv))

    def g_copy(g, g_in, sems, k):
        to = lax.rem(t + k, n_t)
        return remote(g.at[to], g_in.at[k], sems[0].at[k], sems[1].at[k], {"tensor": to})

    gi_copy = partial(g_copy, gi, gi_in, (gi_send, gi_recv))
    go_copy = partial(g_copy, go, go_in, (go_send, go_recv))

    meet(n_dp, n_t, True)
    load_in = pltpu.make_async_copy(e_in_ref, g_in_ref, own_sems.at[0])
    load_out = pltpu.make_async_copy(e_out_ref, g_out_ref, own_sems.at[1])
    load_in.start()
    load_out.start()
    if inside:
        gather = Gather(n_dp, n_t, block_ref, gathered, *refs[: len(Gather.scratch(n_dp, n_t))])
        del refs[: len(Gather.scratch(n_dp, n_t))]
        gather.start()
        weights = Weights(shard, width, gathered=gathered)
    else:
        weights = Weights(shard, width, whole=block_ref)
    load_in.wait()
    wi[t] = g_in_ref[...].astype(BF16)
    for k in range(1, n_t):
        wi_copy(k).start()
    load_out.wait()
    wo[t] = g_out_ref[...].astype(BF16)

    tail = rows - rows % 8
    full[tail:, :] = jnp.zeros((padded - tail, width), F32)
    full[:rows, :] = x_ref[...].astype(F32)
    cot_full[tail:, :] = jnp.zeros((padded - tail, width), F32)
    cot_full[:rows, :] = cot_ref[...].astype(F32)
    bias[...] = image_bias(rows, padded)
    if inside:
        gather.finish()
    for k in range(1, n_t):
        wo_copy(k).start()

    small = weights.small()
    norms = norm_rows(small)
    spot = lax.broadcasted_iota(jnp.int32, small.shape, 1)
    tally = small.astype(F32)
    tally = jnp.where(spot == 4 + experts, tally * 16.0, 0.0) + jnp.where(spot == 5 + experts, tally, 0.0)
    most = jnp.max(jnp.sum(tally, axis=1, keepdims=True), axis=0, keepdims=True)
    count_ref[...] = jnp.broadcast_to(most, count_ref.shape)
    unit, _ = centre(full[...])
    norm[...] = (unit * norms[0:1] + norms[1:2]).astype(BF16)
    q_s[...] = nn(norm[...], weights(0)).astype(BF16)
    k_s[...] = nn(norm[...], weights(1)).astype(BF16)
    v_s[...] = nn(norm[...], weights(2)).astype(BF16)
    low, high = half_masks()
    low_f, high_f = low.astype(F32), high.astype(F32)

    def heads(j, carry):
        at = pl.ds(pl.multiple_of(j * LANES, LANES), LANES)
        query, key, value = q_s[:, at], k_s[:, at], v_s[:, at]
        first = nn(soft_scores(query * low, key, bias[...]).astype(BF16), value)
        second = nn(soft_scores(query * high, key, bias[...]).astype(BF16), value)
        mix[:, at] = (first * low_f + second * high_f).astype(BF16)
        return carry

    lax.fori_loop(0, width // LANES, heads, 0)
    residual = full[...] + nn(mix[...], weights(3))
    res[...] = residual
    unit, _ = centre(residual)
    moe[...] = (unit * norms[2:3] + norms[3:4]).astype(BF16)
    probs_s[...] = router_probs(nn(moe[...], weights.small()), experts)

    def selectors(p):
        slot = lax.broadcasted_iota(jnp.int32, (rooms, padded), 0) + p * rooms
        first = (slot == slots_ref[0:1, :]).astype(F32)
        second = (slot == slots_ref[1:2, :]).astype(F32)
        return first, second

    def dispatch(k, carry):
        to = lax.rem(dp + k, n_dp)
        first, second = selectors(to)
        got = nn((first + second).astype(BF16), moe[...]).astype(BF16)

        @pl.when(k > 0)
        def _():
            send_d[to] = got
            d_copy(k).start()

        @pl.when(k == 0)
        def _():
            recv_d[to] = got

        return carry

    lax.fori_loop(0, n_dp, dispatch, 0)
    cot = cot_full[...]
    q_gate = pick_gate(probs_s[...], cols_ref[:, 0:1])
    k_gate = pick_gate(probs_s[...], cols_ref[:, 1:2])
    dk[...] = (q_gate * cot).astype(BF16)
    dv[...] = (k_gate * cot).astype(BF16)

    def dispatch_grad(k, carry):
        to = lax.rem(dp + k, n_dp)
        first, second = selectors(to)
        got = (nn(first.astype(BF16), dk[...]) + nn(second.astype(BF16), dv[...])).astype(BF16)

        @pl.when(k > 0)
        def _():
            send_s[to] = got
            s_copy(k).start()

        @pl.when(k == 0)
        def _():
            recv_s[to] = got

        return carry

    lax.fori_loop(0, n_dp, dispatch_grad, 0)

    def hidden_units(j, g):
        active, steep = gelu_parts(nn(recv_d[g], wi[j]))
        act[j, g] = active.astype(BF16)
        slope[j, g] = steep.astype(BF16)

    def own_hidden(k, carry):
        @pl.when(k > 0)
        def _():
            d_copy(k).wait_recv()

        hidden_units(t, lax.rem(dp + n_dp - k, n_dp))
        return carry

    lax.fori_loop(0, n_dp, own_hidden, 0)
    for k in range(1, n_t):
        wi_copy(k).wait_recv()

    def other_hidden(i, carry):
        hidden_units(lax.rem(t + 1 + i // n_dp, n_t), lax.rem(i, n_dp))
        return carry

    lax.fori_loop(0, (n_t - 1) * n_dp, other_hidden, 0)

    for k in range(1, n_dp):
        s_copy(k).wait_recv()

    def outer_grad(i, carry):
        k = i // (hid // half)
        j = lax.rem(t + 1 + k, n_t)
        at = pl.ds(pl.multiple_of(lax.rem(i, hid // half) * half, half), half)
        left = act[j, :, :, at].reshape(slot_count, half)
        go[j, at, :] = tn(left, recv_s[...].reshape(slot_count, width)).astype(BF16)

        @pl.when((lax.rem(i, hid // half) == hid // half - 1) & (k < n_t - 1))
        def _():
            go_copy(k + 1).start()

        return carry

    lax.fori_loop(0, n_t * (hid // half), outer_grad, 0)

    for k in range(1, n_t):
        wo_copy(k).wait_recv()
    for k in range(1, n_dp):
        d_copy(k).wait_send()

    def give_back(i, carry):
        k = lax.rem(i + 1, n_dp)
        to = lax.rem(dp + k, n_dp)
        total = nn(act[0, to], wo[0])
        for j in range(1, n_t):
            total = total + nn(act[j, to], wo[j])

        @pl.when(k > 0)
        def _():
            send_d[to] = total.astype(BF16)
            r_copy(k).start()

        @pl.when(k == 0)
        def _():
            ret_in[to] = total.astype(BF16)

        return carry

    lax.fori_loop(0, n_dp, give_back, 0)

    for k in range(1, n_dp):
        s_copy(k).wait_send()

    def hidden_grad(i, carry):
        k = lax.rem(i + 1, n_dp)
        to = lax.rem(dp + k, n_dp)
        total = jnp.zeros((rooms, width), F32)
        for j in range(n_t):
            grad = (nt(recv_s[to], wo[j]) * slope[j, to].astype(F32)).astype(BF16)
            slope[j, to] = grad
            total = total + nt(grad, wi[j])

        @pl.when(k > 0)
        def _():
            send_s[to] = total.astype(BF16)
            b_copy(k).start()

        @pl.when(k == 0)
        def _():
            back_in[to] = total.astype(BF16)

        return carry

    lax.fori_loop(0, n_dp, hidden_grad, 0)

    def inner_grad(i, carry):
        k = i // (width // wide)
        j = lax.rem(t + 1 + k, n_t)
        at = pl.ds(pl.multiple_of(lax.rem(i, width // wide) * wide, wide), wide)
        left = recv_d[:, :, at].reshape(slot_count, wide)
        gi[j, at, :] = tn(left, slope[j].reshape(slot_count, hid)).astype(BF16)

        @pl.when((lax.rem(i, width // wide) == width // wide - 1) & (k < n_t - 1))
        def _():
            gi_copy(k + 1).start()

        return carry

    lax.fori_loop(0, n_t * (width // wide), inner_grad, 0)

    full[...] = jnp.zeros_like(full)
    full[:rows, :] = x_ref[...].astype(F32)
    lane = lax.broadcasted_iota(jnp.int32, (padded, slot_count), 1)
    first = (lane == cols_ref[:, 2:3]).astype(F32)
    second = (lane == cols_ref[:, 3:4]).astype(F32)
    both = (first + second).astype(BF16)
    for k in range(1, n_dp):
        r_copy(k).wait()
    returned = ret_in[...].reshape(slot_count, width)
    first_rows = nn(first.astype(BF16), returned)
    second_rows = nn(second.astype(BF16), returned)
    probs = probs_s[...]
    first_id, second_id = cols_ref[:, 0:1], cols_ref[:, 1:2]
    outcome = res[...] + pick_gate(probs, first_id) * first_rows + pick_gate(probs, second_id) * second_rows
    out_ref[...] = outcome[:rows].astype(BF16)
    cot = cot_full[...]
    first_grad = jnp.sum(first_rows * cot, axis=1, keepdims=True)
    second_grad = jnp.sum(second_rows * cot, axis=1, keepdims=True)
    spot = lax.broadcasted_iota(jnp.int32, probs.shape, 1)
    grad_probs = jnp.where(spot == first_id + 4, first_grad, 0.0) + jnp.where(spot == second_id + 4, second_grad, 0.0)
    grad_logits = (probs * (grad_probs - jnp.sum(probs * grad_probs, axis=1, keepdims=True))).astype(BF16)
    grad_router = tn(moe[...], grad_logits)

    for k in range(1, n_dp):
        b_copy(k).wait()
    grad_moe = nn(both, back_in[...].reshape(slot_count, width)) + nt(grad_logits, weights.small())
    unit, inverse = centre(res[...])
    extra, gain_two, shift_two = norm_back(grad_moe, unit, inverse, norms[2:3])
    grad_residual = cot + extra
    cot_full[...] = grad_residual
    grad_attended = grad_residual.astype(BF16)

    def keep(at, value):
        if inside:
            grads[:, :, at * shard : (at + 1) * shard, :] = value.astype(BF16).reshape(n_dp, n_t, shard, width)
        else:
            sum_ref[at] = value

    keep(3, tn(mix[...], grad_attended))
    dq = mix
    dq[...] = nt(grad_attended, weights(3)).astype(BF16)

    def heads_back(j, carry):
        at = pl.ds(pl.multiple_of(j * LANES, LANES), LANES)
        query, key, value, grad = q_s[:, at], k_s[:, at], v_s[:, at], dq[:, at]
        for mask, mask_f in ((low, low_f), (high, high_f)):
            probs = soft_scores(query * mask, key, bias[...])
            grad_probs = nt(grad * mask, value)
            grad_scores = probs * (grad_probs - jnp.sum(probs * grad_probs, axis=1, keepdims=True))
            grad_scores = grad_scores.astype(BF16)
            part_v = tn(probs.astype(BF16), grad)
            part_q = nn(grad_scores, key) * scale
            part_k = tn(grad_scores, query) * scale
            if mask is low:
                sum_q, sum_k, sum_v = part_q * mask_f, part_k * mask_f, part_v * mask_f
            else:
                sum_q, sum_k, sum_v = sum_q + part_q * mask_f, sum_k + part_k * mask_f, sum_v + part_v * mask_f
        dq[:, at] = sum_q.astype(BF16)
        dk[:, at] = sum_k.astype(BF16)
        dv[:, at] = sum_v.astype(BF16)
        return carry

    lax.fori_loop(0, width // LANES, heads_back, 0)
    keep(0, tn(norm[...], dq[...]))
    keep(1, tn(norm[...], dk[...]))
    keep(2, tn(norm[...], dv[...]))
    grad_normed = nt(dq[...], weights(0)) + nt(dk[...], weights(1)) + nt(dv[...], weights(2))
    unit, inverse = centre(full[...])
    extra, gain_one, shift_one = norm_back(grad_normed, unit, inverse, norms[0:1])
    gx_ref[...] = (cot_full[...] + extra)[:rows].astype(BF16)
    line = lax.broadcasted_iota(jnp.int32, (8, width), 0)
    small_rows = (
        jnp.where(line == 0, gain_one, 0.0)
        + jnp.where(line == 1, shift_one, 0.0)
        + jnp.where(line == 2, gain_two, 0.0)
        + jnp.where(line == 3, shift_two, 0.0)
    )
    pick = lax.broadcasted_iota(jnp.int32, (8, LANES), 0) == lax.broadcasted_iota(jnp.int32, (8, LANES), 1)
    small = grad_router + tn(small_rows.astype(BF16), pick.astype(F32).astype(BF16))
    if inside:
        at = slice(4 * shard, 5 * shard)
        grads[:, :, at, :LANES] = small.astype(BF16).reshape(n_dp, n_t, shard, LANES)
        grads[:, :, at, LANES:] = jnp.zeros((n_dp, n_t, shard, width - LANES), BF16)
        Scatter(n_dp, n_t, grads, sum_ref, *refs).run()
    else:
        sum_ref[4] = jnp.zeros((width, width), F32)
        sum_ref[4, :, :LANES] = small

    for copy, g, g_in, result in ((go_copy, go, go_in, g_out_ref), (gi_copy, gi, gi_in, g_in_ref)):
        total = g[t].astype(F32)
        for k in range(1, n_t):
            copy(k).wait_recv()
            total = total + g_in[k].astype(F32)
        result[...] = total
    for k in range(1, n_t):
        wi_copy(k).wait_send()
        wo_copy(k).wait_send()
        gi_copy(k).wait_send()
        go_copy(k).wait_send()


def run_step(cfg, cid, *args):
    n_dp, n_t, rows, padded, width, experts, rooms, shard, inside, hid = cfg
    rows_block = ceil_to(5 * shard, 16)
    total = (rows_block, width) if inside else (5, width, width)
    outs = [
        jax.ShapeDtypeStruct((rows, width), BF16),
        jax.ShapeDtypeStruct((rows, width), BF16),
        jax.ShapeDtypeStruct(total, F32),
        jax.ShapeDtypeStruct((width, hid), F32),
        jax.ShapeDtypeStruct((hid, width), F32),
        jax.ShapeDtypeStruct((8, LANES), F32),
    ]
    spread = (n_dp, n_t, rows_block, width) if inside else (1, 1, 16, LANES)
    rows_f, rows_b = VMEM((padded, width), F32), VMEM((padded, width), BF16)
    slots_b, units_b = VMEM((n_dp, rooms, width), BF16), VMEM((n_t, n_dp, rooms, hid), BF16)
    in_b, out_b = VMEM((n_t, width, hid), BF16), VMEM((n_t, hid, width), BF16)
    scratch = [VMEM(spread, BF16)] * 2 + [rows_f, rows_f, VMEM((padded, padded), F32), rows_f]
    scratch += [VMEM((padded, LANES), F32)] + [rows_b] * 8 + [slots_b] * 6 + [units_b] * 2
    scratch += [in_b, out_b, in_b, out_b, in_b, out_b]
    scratch += [DMA((n_dp,))] * 8 + [DMA((n_t,))] * 8 + [DMA((2,))]
    if inside:
        scratch += Gather.scratch(n_dp, n_t) + Scatter.scratch(n_dp, n_t, (rows_block, width))
    whole = pl.BlockSpec(memory_space=VMEM)
    anywhere = pl.BlockSpec(memory_space=pl.ANY)
    return pl.pallas_call(
        partial(step_kernel, cfg),
        out_shape=outs,
        in_specs=[whole] * 5 + [anywhere] * 2,
        out_specs=[whole] * len(outs),
        scratch_shapes=scratch,
        compiler_params=pltpu.CompilerParams(
            collective_id=cid, has_side_effects=True, vmem_limit_bytes=60 * 2**20
        ),
        name="step_" + str(rooms),
    )(*args)


def route_pairs(routes, t, row_count, experts, capacity):
    tok_count = routes.shape[0]
    ids = jnp.arange(experts, dtype=jnp.int32)[None, :]
    start = t * row_count
    rows = lax.dynamic_slice_in_dim(routes, start, row_count, 0)
    before = (jnp.arange(tok_count, dtype=jnp.int32) < start)[:, None]
    all_first = routes[:, 0:1] == ids
    all_second = routes[:, 1:2] == ids
    base_first = jnp.sum((all_first & before).astype(jnp.int32), axis=0)
    total_first = jnp.sum(all_first.astype(jnp.int32), axis=0)
    base_second = jnp.sum((all_second & before).astype(jnp.int32), axis=0)
    hot_first = rows[:, 0:1] == ids
    hot_second = rows[:, 1:2] == ids
    at = jnp.arange(row_count, dtype=jnp.int32)
    lower = (at[:, None] > at[None, :]).astype(BF16)
    both = jnp.concatenate([hot_first, hot_second], axis=1).astype(BF16)
    earlier = nn(lower, both).astype(jnp.int32)
    own_first = jnp.sum(hot_first.astype(jnp.int32), axis=0)
    rank_first = earlier[:, :experts]
    rank_second = earlier[:, experts:] + own_first
    place_first = rank_first + base_first
    place_second = earlier[:, experts:] + total_first + base_second
    first = jnp.sum(jnp.where(hot_first & (place_first < capacity), rank_first + 1, 0), axis=1) - 1
    second = jnp.sum(jnp.where(hot_second & (place_second < capacity), rank_second + 1, 0), axis=1) - 1
    most = jnp.maximum(jnp.max(first), jnp.max(second)) + 1
    return rows, first, second, most


def per_device(
    n_dp,
    n_t,
    inputs,
    cotangent,
    routes,
    gain_attn,
    shift_attn,
    query_w,
    key_w,
    value_w,
    out_w,
    gain_moe,
    shift_moe,
    router_w,
    expert_in,
    expert_out,
):
    t = lax.axis_index("tensor")
    shard, width = query_w.shape
    experts = router_w.shape[1]
    tok_count = routes.shape[0]
    rows = inputs.shape[0]
    padded = ceil_to(rows, 16)
    capacity = (5 * tok_count + 2 * experts - 1) // (2 * experts)
    inside = shard % 16 == 0
    every = ("dp", "tensor")

    route_rows, first_rank, second_rank, most = route_pairs(routes, t, rows, experts, capacity)

    small = jnp.concatenate(
        [
            gain_attn[:, None],
            shift_attn[:, None],
            gain_moe[:, None],
            shift_moe[:, None],
            router_w,
            jnp.broadcast_to((most // 16).astype(F32), (shard, 1)),
            jnp.broadcast_to((most % 16).astype(F32), (shard, 1)),
        ],
        axis=1,
    )
    small = jnp.pad(small, ((0, 0), (0, width - small.shape[1])))
    if inside:
        block = jnp.concatenate([query_w, key_w, value_w, out_w, small], axis=0).astype(BF16)
    else:
        stack = jnp.stack([query_w, key_w, value_w, out_w, small]).astype(BF16)
        block = lax.all_gather(stack, every, axis=1, tiled=True)

    hid = expert_in.shape[2]

    def places(rooms):
        def slot(choice, rank):
            return jnp.where((rank >= 0) & (rank < rooms), choice * rooms + rank, -1)

        slots = jnp.stack([slot(route_rows[:, 0], first_rank), slot(route_rows[:, 1], second_rank)])
        slots = jnp.pad(slots, ((0, 0), (0, padded - rows)), constant_values=-1)
        cols = jnp.concatenate([jnp.pad(route_rows, ((0, padded - rows), (0, 0))), slots.T], axis=1)
        return cols, slots

    def finish(summed):
        if inside:
            return summed
        return lax.psum_scatter(summed, every, scatter_dimension=1, tiled=True).reshape(5 * shard, width)

    def slow():
        rooms = ceil_to(rows, 16)
        cfg = (n_dp, n_t, rows, padded, width, experts, rooms, shard, inside)
        cols, slots = places(rooms)
        kept = forward(cfg, 1, inputs, cotangent, cols, slots, block)

        def turn(k):
            return [(i, (i + k) % n_t) for i in range(n_t)]

        both = jnp.stack([expert_in[0].T, expert_out[0]]).astype(BF16)
        parts = [both] + [lax.ppermute(both, "tensor", turn(k)) for k in range(1, n_t)]
        w_in, w_out = (jnp.concatenate([part[i] for part in parts], axis=0) for i in range(2))
        returned, back, grad_inner, grad_outer = run_expert(
            kept[1].reshape(n_dp * rooms, width), kept[2].reshape(n_dp * rooms, width), w_in, w_out
        )
        both = jnp.stack([grad_inner.reshape(n_t, hid, width), grad_outer.reshape(n_t, hid, width)], axis=1)
        total = both[0].astype(F32)
        for k in range(1, n_t):
            total = total + lax.ppermute(both[k], "tensor", turn(-k)).astype(F32)
        output_rows, grad_tokens, summed = backward(
            cfg,
            2,
            returned.reshape(n_dp, rooms, width),
            back.reshape(n_dp, rooms, width),
            inputs,
            cotangent,
            cols,
            kept[0] if inside else block,
            *kept[3:],
        )
        return output_rows, grad_tokens, summed, total[0].T, total[1]

    rooms = min(ceil_to((7 * rows + 2 * experts - 1) // (2 * experts), 16), ceil_to(rows, 16))
    cfg = (n_dp, n_t, rows, padded, width, experts, rooms, shard, inside, hid)
    cols, slots = places(rooms)
    *fast, count = run_step(cfg, 0, inputs, cotangent, cols, slots, block, expert_in[0], expert_out[0])
    state = lax.while_loop(
        lambda state: state[0], lambda state: (False,) + slow(), (count[0, 0] > rooms,) + tuple(fast)
    )
    _, output_rows, grad_tokens, summed, grad_inner, grad_outer = state
    summed = finish(summed)
    small_sum = summed[4 * shard : 5 * shard]
    return (
        output_rows,
        grad_tokens,
        small_sum[:, 0],
        small_sum[:, 1],
        summed[0:shard],
        summed[shard : 2 * shard],
        summed[2 * shard : 3 * shard],
        summed[3 * shard : 4 * shard],
        small_sum[:, 2],
        small_sum[:, 3],
        small_sum[:, 4 : 4 + experts],
        grad_inner[None],
        grad_outer[None],
    )


def solution(mesh):
    every = ("dp", "tensor")
    rows, line = P(every, None), P(every)
    w_in, w_out = P("dp", None, "tensor"), P("dp", "tensor", None)
    return jax.shard_map(
        partial(per_device, mesh.shape["dp"], mesh.shape["tensor"]),
        mesh=mesh,
        in_specs=(rows, rows, P("dp", None), line, line, rows, rows, rows, rows, line, line, rows, w_in, w_out),
        out_specs=(rows, rows, line, line, rows, rows, rows, rows, line, line, rows, w_in, w_out),
        check_vma=False,
    )
```

```python
from functools import partial

import jax
import jax.numpy as jnp
from jax import lax
from jax.experimental import pallas as pl
from jax.experimental.pallas import tpu as pltpu
from jax.sharding import PartitionSpec as P

SEQ = 197
HEAD_DIM = 64
LANES = 128
MESH = pl.DeviceIdType.MESH
F32 = jnp.float32
BF16 = jnp.bfloat16
VMEM = pltpu.VMEM
DMA = pltpu.SemaphoreType.DMA
SMALL, OUT = 3, 4


def ceil_to(value, unit):
    return (value + unit - 1) // unit * unit


def nn(left, right):
    return lax.dot_general(left, right, (((1,), (0,)), ((), ())), preferred_element_type=F32)


def nt(left, right):
    return lax.dot_general(left, right, (((1,), (1,)), ((), ())), preferred_element_type=F32)


def tn(left, right):
    return lax.dot_general(left, right, (((0,), (0,)), ((), ())), preferred_element_type=F32)


def remote(src, dst, send, recv, device):
    return pltpu.make_async_remote_copy(
        src_ref=src, dst_ref=dst, send_sem=send, recv_sem=recv, device_id=device, device_id_type=MESH
    )


def meet(n_dp, n_t, z_too):
    dp = lax.axis_index("dp")
    t = lax.axis_index("tensor")
    bar = pltpu.get_barrier_semaphore()
    for k in range(1, n_dp):
        pl.semaphore_signal(bar, inc=1, device_id={"dp": lax.rem(dp + k, n_dp)}, device_id_type=MESH)
    if z_too:
        for k in range(1, n_t):
            pl.semaphore_signal(bar, inc=1, device_id={"tensor": lax.rem(t + k, n_t)}, device_id_type=MESH)
    pl.semaphore_wait(bar, n_dp - 1 + (n_t - 1 if z_too else 0))


class Gather:
    def __init__(self, n_dp, n_t, first, count, block, out, own_sem, z_send, z_recv, c_send, c_recv, k_send, k_recv):
        self.n_t, self.n_chip = n_t, n_dp // 2
        self.rows = pl.ds(first, count)
        self.block, self.out, self.own_sem = block.at[self.rows], out, own_sem
        self.z_sems, self.c_sems, self.k_sems = (z_send, z_recv), (c_send, c_recv), (k_send, k_recv)
        self.dp, self.t = lax.axis_index("dp"), lax.axis_index("tensor")
        self.chip, self.core = self.dp // 2, lax.rem(self.dp, 2)
        self.other = self.chip * 2 + 1 - self.core

    @staticmethod
    def scratch(n_dp, n_t):
        n_chip = n_dp // 2
        pair = [DMA((n_chip, n_t))] * 2
        return [DMA, DMA((n_t,)), DMA((n_t,))] + pair + pair

    def place(self, dp, t):
        return self.out.at[dp, t, self.rows]

    def z_copy(self, k):
        send, recv = self.z_sems
        to = lax.rem(self.t + k, self.n_t)
        return remote(self.block, self.place(self.dp, self.t), send.at[k], recv.at[k], {"tensor": to})

    def chip_copy(self, k, j):
        send, recv = self.c_sems
        here = self.place(self.dp, lax.rem(self.t + self.n_t - j, self.n_t))
        to = lax.rem(self.chip + k, self.n_chip) * 2 + self.core
        return remote(self.block if j == 0 else here, here, send.at[k, j], recv.at[k, j], {"dp": to})

    def core_copy(self, k, j):
        send, recv = self.k_sems
        src = lax.rem(self.chip + self.n_chip - k, self.n_chip) * 2 + self.core
        here = self.place(src, lax.rem(self.t + self.n_t - j, self.n_t))
        own = k == 0 and j == 0
        return remote(self.block if own else here, here, send.at[k, j], recv.at[k, j], {"dp": self.other})

    def own_copy(self):
        return pltpu.make_async_copy(self.block, self.place(self.dp, self.t), self.own_sem)

    def start(self):
        for k in range(1, self.n_t):
            self.z_copy(k).start()
        self.own_copy().start()
        for k in range(1, self.n_chip):
            self.chip_copy(k, 0).start()
        self.core_copy(0, 0).start()

    def pass_to_chips(self):
        for j in range(1, self.n_t):
            self.z_copy(j).wait_recv()
            for k in range(1, self.n_chip):
                self.chip_copy(k, j).start()
            self.core_copy(0, j).start()

    def pass_to_core(self):
        for j in range(self.n_t):
            for k in range(1, self.n_chip):
                self.chip_copy(k, j).wait_recv()
                self.core_copy(k, j).start()

    def arrive(self):
        self.own_copy().wait()
        for j in range(self.n_t):
            for k in range(self.n_chip):
                self.core_copy(k, j).wait_recv()

    def drain(self):
        for k in range(1, self.n_t):
            self.z_copy(k).wait_send()
        for j in range(self.n_t):
            for k in range(1, self.n_chip):
                self.chip_copy(k, j).wait_send()
            for k in range(self.n_chip):
                self.core_copy(k, j).wait_send()


class Scatter:
    def __init__(
        self, n_dp, n_t, grads, out, core_in, half, chip_in, part, z_in, k_send, k_recv, c_send, c_recv, z_send, z_recv
    ):
        self.n_t, self.n_chip = n_t, n_dp // 2
        self.grads, self.out = grads, out
        self.core_in, self.half, self.chip_in, self.part, self.z_in = core_in, half, chip_in, part, z_in
        self.k_sems, self.c_sems, self.z_sems = (k_send, k_recv), (c_send, c_recv), (z_send, z_recv)
        self.dp, self.t = lax.axis_index("dp"), lax.axis_index("tensor")
        self.chip, self.core = self.dp // 2, lax.rem(self.dp, 2)
        self.other = self.chip * 2 + 1 - self.core

    @staticmethod
    def scratch(n_dp, n_t, block):
        n_chip = n_dp // 2
        buffers = [VMEM((n_chip, n_t) + block, BF16)] + [VMEM((n_chip - 1, n_t) + block, BF16)] * 2
        buffers += [VMEM((n_t - 1,) + block, BF16)] * 2
        return buffers + [DMA((n_chip,))] * 4 + [DMA((n_t,))] * 2

    def core_copy(self, k):
        to = lax.rem(self.chip + k, self.n_chip)
        src = self.grads.at[to * 2 + 1 - self.core]
        return remote(src, self.core_in.at[k], self.k_sems[0].at[k], self.k_sems[1].at[k], {"dp": self.other})

    def chip_copy(self, k):
        to = lax.rem(self.chip + k, self.n_chip) * 2 + self.core
        return remote(self.half.at[k - 1], self.chip_in.at[k - 1], self.c_sems[0].at[k], self.c_sems[1].at[k], {"dp": to})

    def z_copy(self, k):
        to = lax.rem(self.t + k, self.n_t)
        return remote(self.part.at[k - 1], self.z_in.at[k - 1], self.z_sems[0].at[k], self.z_sems[1].at[k], {"tensor": to})

    def run(self, between=None):
        n_chip, n_t = self.n_chip, self.n_t
        order = list(range(1, n_chip)) + [0]
        for k in order:
            self.core_copy(k).start()
        for k in order:
            self.core_copy(k).wait_recv()
            if k > 0:
                to = lax.rem(self.chip + k, n_chip) * 2 + self.core
                self.half[k - 1] = (self.grads[to].astype(F32) + self.core_in[k].astype(F32)).astype(BF16)
                self.chip_copy(k).start()
        if between is not None:
            between()
        for k in range(1, n_chip):
            self.chip_copy(k).wait_recv()
        for k in list(range(1, n_t)) + [0]:
            row = lax.rem(self.t + k, n_t)
            total = self.grads[self.dp, row].astype(F32) + self.core_in[0, row].astype(F32)
            for c in range(1, n_chip):
                total = total + self.chip_in[c - 1, row].astype(F32)
            if k > 0:
                self.part[k - 1] = total.astype(BF16)
                self.z_copy(k).start()
            else:
                self.out[...] = total
        for k in range(1, n_t):
            self.z_copy(k).wait_recv()
            self.out[...] += self.z_in[k - 1].astype(F32)
        for k in range(n_chip):
            self.core_copy(k).wait_send()
        for k in range(1, n_chip):
            self.chip_copy(k).wait_send()
        for k in range(1, n_t):
            self.z_copy(k).wait_send()


class Spread:
    def __init__(self, n_t, parts, send, recv):
        self.n_t, self.t, self.parts, self.send, self.recv = n_t, lax.axis_index("tensor"), parts, send, recv

    @staticmethod
    def scratch(n_t):
        return [DMA((2, n_t)), DMA((n_t,))]

    def hop(self, j, way):
        here = self.parts.at[j]
        return remote(here, here, self.send.at[way, j], self.recv.at[j], {"tensor": self.t + 1 - 2 * way})

    def step(self, s):
        for way, j, in_line, onward in (
            (0, self.t - s, self.t - s >= 0, self.t + 1 < self.n_t),
            (1, self.t + s, self.t + s < self.n_t, self.t > 0),
        ):
            if s > 0:

                @pl.when(in_line)
                def _():
                    self.hop(j, way).wait_recv()

            @pl.when(in_line & onward)
            def _():
                self.hop(j, way).start()

    def drain(self):
        for s in range(self.n_t):

            @pl.when((self.t - s >= 0) & (self.t + 1 < self.n_t))
            def _():
                self.hop(self.t - s, 0).wait_send()

            @pl.when((self.t + s < self.n_t) & (self.t > 0))
            def _():
                self.hop(self.t + s, 1).wait_send()


class Collect:
    def __init__(self, n_t, parts, came, send, recv):
        self.n_t, self.t, self.parts, self.came, self.send, self.recv = (
            n_t,
            lax.axis_index("tensor"),
            parts,
            came,
            send,
            recv,
        )

    @staticmethod
    def scratch(n_t):
        return [DMA((n_t,)), DMA((n_t + 1,))]

    def hop(self, j, way):
        slot = j if way == 0 else jnp.where(j == self.t - 1, self.n_t, j)
        to = self.t + 1 - 2 * way
        return remote(self.parts.at[j], self.came.at[slot], self.send.at[j], self.recv.at[slot], {"tensor": to})

    def wait_slot(self, slot):
        remote(self.parts.at[0], self.came.at[slot], self.send.at[0], self.recv.at[slot], {"tensor": self.t}).wait_recv()

    def begin(self, j):
        @pl.when((self.t == 0) & (j > 0))
        def _():
            self.hop(j, 0).start()

        @pl.when((self.t == self.n_t - 1) & (j < self.n_t - 1))
        def _():
            self.hop(j, 1).start()

    def step(self, e, far):
        if far:
            right, left = self.n_t - 1 - e + self.t, e - self.n_t + 1 + self.t
        else:
            right, left = e - self.t + 2, 2 * self.n_t - 4 - e - self.t
        for way, j, mine in (
            (0, right, (self.t >= 1) & (right <= self.n_t - 1) & (right > self.t)),
            (1, left, (self.t <= self.n_t - 2) & (left >= 0) & (left < self.t)),
        ):

            @pl.when(mine)
            def _():
                self.wait_slot(j)
                self.parts[j] = (self.parts[j].astype(F32) + self.came[j].astype(F32)).astype(BF16)
                self.hop(j, way).start()

    def finish(self, result):
        result[...] = self.parts[self.t].astype(F32)

        @pl.when(self.t > 0)
        def _():
            self.wait_slot(self.t)
            result[...] += self.came[self.t].astype(F32)

        @pl.when(self.t < self.n_t - 1)
        def _():
            self.wait_slot(self.n_t)
            result[...] += self.came[self.n_t].astype(F32)

        for j in range(self.n_t):

            @pl.when(self.t < j)
            def _():
                self.hop(j, 0).wait_send()

            @pl.when(self.t > j)
            def _():
                self.hop(j, 1).wait_send()


def centre(values):
    centred = values - jnp.mean(values, axis=1, keepdims=True)
    inverse = lax.rsqrt(jnp.mean(centred * centred, axis=1, keepdims=True) + 1e-06)
    return centred * inverse, inverse


def norm_back(grad, unit, inverse, gain):
    scaled = grad * gain
    back = inverse * (
        scaled
        - jnp.mean(scaled, axis=1, keepdims=True)
        - unit * jnp.mean(scaled * unit, axis=1, keepdims=True)
    )
    return back, jnp.sum(grad * unit, axis=0, keepdims=True), jnp.sum(grad, axis=0, keepdims=True)


def norm_picks(experts):
    row, lane = (lax.broadcasted_iota(jnp.int32, (8, LANES), axis) for axis in (0, 1))
    return (row + experts == lane).astype(F32).astype(BF16)


def norm_rows(small, experts):
    return nt(norm_picks(experts), small)


def small_grads(experts, grad_router, rows):
    line = lax.broadcasted_iota(jnp.int32, (8, rows[0].shape[1]), 0)
    stack = sum(jnp.where(line == at, row, 0.0) for at, row in enumerate(rows))
    return grad_router + tn(stack.astype(BF16), norm_picks(experts))


def image_bias(rows, padded):
    line = lax.broadcasted_iota(jnp.int32, (padded, padded), 0)
    column = lax.broadcasted_iota(jnp.int32, (padded, padded), 1)
    image_line, image_column = jnp.zeros_like(line), jnp.zeros_like(column)
    for at in range(SEQ, rows + 1, SEQ):
        image_line += (line >= at).astype(jnp.int32)
        image_column += (column >= at).astype(jnp.int32)
    return jnp.where((image_line == image_column) & (column < rows), 0.0, -1e30)


def half_masks():
    lane = lax.broadcasted_iota(jnp.int32, (1, LANES), 1)
    low = (lane < HEAD_DIM).astype(F32)
    return low.astype(BF16), (1.0 - low).astype(BF16)


def soft_scores(query, key, bias):
    scores = nt(query, key) * HEAD_DIM ** (-0.5) + bias
    power = jnp.exp(scores - jnp.max(scores, axis=1, keepdims=True))
    return power * (1.0 / jnp.sum(power, axis=1, keepdims=True))


def router_probs(logits, experts):
    lane = lax.broadcasted_iota(jnp.int32, logits.shape, 1)
    inside = lane < experts
    kept = jnp.where(inside, logits, -1e30)
    power = jnp.where(inside, jnp.exp(kept - jnp.max(kept, axis=1, keepdims=True)), 0.0)
    return power * (1.0 / jnp.sum(power, axis=1, keepdims=True))


def pick_gate(probs, choice):
    lane = lax.broadcasted_iota(jnp.int32, probs.shape, 1)
    return jnp.sum(jnp.where(lane == choice, probs, 0.0), axis=1, keepdims=True)


class Weights:
    def __init__(self, shard, width, gathered=None, whole=None):
        self.shard, self.width, self.gathered, self.whole = shard, width, gathered, whole

    def __call__(self, at):
        if self.whole is not None:
            return self.whole[at]
        part = self.gathered[:, :, at * self.shard : (at + 1) * self.shard, :]
        return part.reshape(self.width, self.width)

    def small(self):
        if self.whole is not None:
            return self.whole[SMALL, :, :LANES]
        part = self.gathered[:, :, SMALL * self.shard : (SMALL + 1) * self.shard, :LANES]
        return part.reshape(self.width, LANES)


def gelu_parts(hidden):
    bell = jnp.exp(-0.5 * hidden * hidden)
    near = 1.0 / (1.0 + 0.23164189 * jnp.abs(hidden))
    tail = near * (
        0.127414796 + near * (-0.142248368 + near * (0.7107068705 + near * (-0.7265760135 + near * 0.5307027145)))
    )
    tail = tail * bell
    share = jnp.where(hidden < 0.0, tail, 1.0 - tail)
    return hidden * share, share + hidden * bell * 0.3989422804014327


def forward_kernel(cfg, *refs):
    n_dp, n_t, rows, padded, width, experts, rooms, shard, inside = cfg
    refs = list(refs)

    def take(count):
        got = refs[:count]
        del refs[:count]
        return got

    x_ref, cot_ref, cols_ref, slots_ref, block_ref = take(5)
    gathered, recv_d, recv_s, res_ref, moe_ref, q_ref, k_ref, v_ref, mix_ref, norm_ref, probs_ref = take(11)
    full, cot_full, bias, send_d, send_s, d_send, d_recv, s_send, s_recv = take(9)
    dp = lax.axis_index("dp")
    meet(n_dp, n_t, inside)
    if inside:
        gather = Gather(n_dp, n_t, 0, block_ref.shape[0], block_ref, gathered, *refs)
        gather.start()
        weights = Weights(shard, width, gathered=gathered)
    else:
        gathered[...] = jnp.zeros_like(gathered)
        weights = Weights(shard, width, whole=block_ref)

    full[rows - rows % 8 :, :] = jnp.zeros((padded - rows + rows % 8, width), F32)
    full[:rows, :] = x_ref[...].astype(F32)
    cot_full[rows - rows % 8 :, :] = jnp.zeros((padded - rows + rows % 8, width), F32)
    cot_full[:rows, :] = cot_ref[...].astype(F32)
    bias[...] = image_bias(rows, padded)
    unit, _ = centre(full[...])
    norm_ref[...] = unit.astype(BF16)
    if inside:
        gather.pass_to_chips()
        gather.pass_to_core()
        gather.arrive()
        gather.drain()

    norms = norm_rows(weights.small(), experts)
    unit, _ = centre(full[...])
    normed = (unit * norms[0:1] + norms[1:2]).astype(BF16)
    norm_ref[...] = normed
    q_ref[...] = nn(normed, weights(0)).astype(BF16)
    k_ref[...] = nn(normed, weights(1)).astype(BF16)
    v_ref[...] = nn(normed, weights(2)).astype(BF16)
    low, high = half_masks()

    def heads(j, carry):
        at = pl.ds(pl.multiple_of(j * LANES, LANES), LANES)
        query, key, value = q_ref[:, at], k_ref[:, at], v_ref[:, at]
        first = nn(soft_scores(query * low, key, bias[...]).astype(BF16), value)
        second = nn(soft_scores(query * high, key, bias[...]).astype(BF16), value)
        mix_ref[:, at] = (first * low.astype(F32) + second * high.astype(F32)).astype(BF16)
        return carry

    lax.fori_loop(0, width // LANES, heads, 0)
    residual = full[...] + nn(mix_ref[...], weights(OUT))
    res_ref[...] = residual
    unit, _ = centre(residual)
    moe = (unit * norms[2:3] + norms[3:4]).astype(BF16)
    moe_ref[...] = moe
    probs = router_probs(nn(moe, weights.small()), experts)
    probs_ref[...] = probs
    cot = cot_full[...]
    full[...] = pick_gate(probs, cols_ref[:, 0:1]) * cot
    cot_full[...] = pick_gate(probs, cols_ref[:, 1:2]) * cot

    def selectors(p):
        slot = lax.broadcasted_iota(jnp.int32, (rooms, padded), 0) + p * rooms
        first = (slot == slots_ref[0:1, :]).astype(F32)
        second = (slot == slots_ref[1:2, :]).astype(F32)
        return first, second

    def d_copy(k):
        to = lax.rem(dp + k, n_dp)
        return remote(send_d.at[to], recv_d.at[dp], d_send.at[k], d_recv.at[k], {"dp": to})

    def s_copy(k):
        to = lax.rem(dp + k, n_dp)
        return remote(send_s.at[to], recv_s.at[dp], s_send.at[k], s_recv.at[k], {"dp": to})

    def dispatch(k, carry):
        to = lax.rem(dp + k, n_dp)
        first, second = selectors(to)
        send_d[to] = nn((first + second).astype(BF16), moe_ref[...]).astype(BF16)

        @pl.when(k > 0)
        def _():
            d_copy(k).start()

        return carry

    def dispatch_grad(k, carry):
        to = lax.rem(dp + k, n_dp)
        first, second = selectors(to)
        rows_grad = nn(first.astype(BF16), full[...].astype(BF16)) + nn(second.astype(BF16), cot_full[...].astype(BF16))
        send_s[to] = rows_grad.astype(BF16)

        @pl.when(k > 0)
        def _():
            s_copy(k).start()

        return carry

    lax.fori_loop(0, n_dp, dispatch, 0)
    lax.fori_loop(0, n_dp, dispatch_grad, 0)
    recv_d[dp] = send_d[dp]
    recv_s[dp] = send_s[dp]
    for k in range(1, n_dp):
        d_copy(k).wait()
    for k in range(1, n_dp):
        s_copy(k).wait()


def forward(cfg, cid, x, cot, cols, slots, block):
    n_dp, n_t, rows, padded, width, experts, rooms, shard, inside = cfg
    rows_block = ceil_to(5 * shard, 16)
    low = jax.ShapeDtypeStruct((padded, width), BF16)
    sent = jax.ShapeDtypeStruct((n_dp, rooms, width), BF16)
    gathered = (n_dp, n_t, rows_block, width) if inside else (1, 1, 16, LANES)
    outs = [jax.ShapeDtypeStruct(gathered, BF16), sent, sent, jax.ShapeDtypeStruct((padded, width), F32)]
    outs += [low] * 6 + [jax.ShapeDtypeStruct((padded, LANES), F32)]
    scratch = [
        VMEM((padded, width), F32),
        VMEM((padded, width), F32),
        VMEM((padded, padded), F32),
        VMEM((n_dp, rooms, width), BF16),
        VMEM((n_dp, rooms, width), BF16),
    ] + [DMA((n_dp,))] * 4
    if inside:
        scratch += Gather.scratch(n_dp, n_t)
    whole = pl.BlockSpec(memory_space=VMEM)
    return pl.pallas_call(
        partial(forward_kernel, cfg),
        out_shape=outs,
        in_specs=[whole] * 5,
        out_specs=[whole] * len(outs),
        scratch_shapes=scratch,
        compiler_params=pltpu.CompilerParams(
            collective_id=cid, has_side_effects=True, vmem_limit_bytes=56 * 2**20
        ),
        name="forward_" + str(rooms),
    )(x, cot, cols, slots, block)


def expert_kernel(chunks, d_ref, s_ref, w_in_ref, w_out_ref, ret_ref, back_ref, g_in_ref, g_out_ref, ret, back, g_in, g_out):
    step = pl.program_id(0)
    rows = d_ref.shape[0]
    chunk = rows // chunks

    @pl.when(step == 0)
    def _():
        ret[...] = jnp.zeros_like(ret)
        back[...] = jnp.zeros_like(back)

    g_in[...] = jnp.zeros_like(g_in)
    g_out[...] = jnp.zeros_like(g_out)
    w_in, w_out = w_in_ref[...], w_out_ref[...]

    def part(c, carry):
        at = pl.ds(pl.multiple_of(c * chunk, 16), chunk)
        took, slot_grad = d_ref[at, :], s_ref[at, :]
        active, slope = gelu_parts(nt(took, w_in))
        active = active.astype(BF16)
        grad_hidden = (nt(slot_grad, w_out) * slope).astype(BF16)
        ret[at, :] += nn(active, w_out)
        back[at, :] += nn(grad_hidden, w_in)
        g_out[...] += tn(active, slot_grad)
        g_in[...] += tn(grad_hidden, took)
        return carry

    lax.fori_loop(0, chunks, part, 0)
    g_in_ref[...] = g_in[...].astype(BF16)
    g_out_ref[...] = g_out[...].astype(BF16)

    @pl.when(step == pl.num_programs(0) - 1)
    def _():
        ret_ref[...] = ret[...].astype(BF16)
        back_ref[...] = back[...].astype(BF16)


def run_expert(took, slot_grad, w_in, w_out):
    rows, width = took.shape
    hidden = w_in.shape[0]
    block = 256
    chunks = next(c for c in range(max(1, rows // 400), rows + 1) if rows % c == 0 and (rows // c) % 16 == 0)
    whole = pl.BlockSpec((rows, width), lambda i: (0, 0))
    part = pl.BlockSpec((block, width), lambda i: (i, 0))
    low = jax.ShapeDtypeStruct((rows, width), BF16)
    grad = jax.ShapeDtypeStruct((hidden, width), BF16)
    return pl.pallas_call(
        partial(expert_kernel, chunks),
        grid=(hidden // block,),
        out_shape=[low, low, grad, grad],
        in_specs=[whole, whole, part, part],
        out_specs=[whole, whole, part, part],
        scratch_shapes=[
            VMEM((rows, width), F32),
            VMEM((rows, width), F32),
            VMEM((block, width), F32),
            VMEM((block, width), F32),
        ],
        compiler_params=pltpu.CompilerParams(vmem_limit_bytes=60 * 2**20),
        cost_estimate=pl.CostEstimate(
            flops=12 * rows * width * hidden, bytes_accessed=12 * rows * width + 8 * hidden * width, transcendentals=0
        ),
        name="expert_" + str(rows),
    )(took, slot_grad, w_in, w_out)


def backward_kernel(cfg, *refs):
    n_dp, n_t, rows, padded, width, experts, rooms, shard, inside = cfg
    refs = list(refs)

    def take(count):
        got = refs[:count]
        del refs[:count]
        return got

    ret_ref, back_ref, x_ref, cot_ref, cols_ref, weights_ref = take(6)
    res_ref, moe_ref, q_ref, k_ref, v_ref, mix_ref, norm_ref, probs_ref = take(8)
    out_ref, gx_ref, sum_ref = take(3)
    full, cot_full, bias, ret_in, back_in, grads, r_send, r_recv, b_send, b_recv = take(10)
    dq, dk, dv = take(3)
    dp = lax.axis_index("dp")
    meet(n_dp, n_t, inside)

    def r_copy(k):
        to = lax.rem(dp + k, n_dp)
        return remote(ret_ref.at[to], ret_in.at[dp], r_send.at[k], r_recv.at[k], {"dp": to})

    def b_copy(k):
        to = lax.rem(dp + k, n_dp)
        return remote(back_ref.at[to], back_in.at[dp], b_send.at[k], b_recv.at[k], {"dp": to})

    for k in range(1, n_dp):
        r_copy(k).start()
    for k in range(1, n_dp):
        b_copy(k).start()
    ret_in[dp] = ret_ref[dp]
    back_in[dp] = back_ref[dp]
    weights = Weights(shard, width, gathered=weights_ref) if inside else Weights(shard, width, whole=weights_ref)
    tail = rows - rows % 8
    full[tail:, :] = jnp.zeros((padded - tail, width), F32)
    full[:rows, :] = x_ref[...].astype(F32)
    cot_full[tail:, :] = jnp.zeros((padded - tail, width), F32)
    cot_full[:rows, :] = cot_ref[...].astype(F32)
    bias[...] = image_bias(rows, padded)
    norms = norm_rows(weights.small(), experts)
    slot_count = n_dp * rooms
    lane = lax.broadcasted_iota(jnp.int32, (padded, slot_count), 1)
    first = (lane == cols_ref[:, 2:3]).astype(F32)
    second = (lane == cols_ref[:, 3:4]).astype(F32)
    both = (first + second).astype(BF16)

    for k in range(1, n_dp):
        r_copy(k).wait()
    returned = ret_in[...].reshape(slot_count, width)
    first_rows = nn(first.astype(BF16), returned)
    second_rows = nn(second.astype(BF16), returned)
    probs = probs_ref[...]
    first_id, second_id = cols_ref[:, 0:1], cols_ref[:, 1:2]
    outcome = res_ref[...] + pick_gate(probs, first_id) * first_rows + pick_gate(probs, second_id) * second_rows
    out_ref[...] = outcome[:rows].astype(BF16)
    cot = cot_full[...]
    first_grad = jnp.sum(first_rows * cot, axis=1, keepdims=True)
    second_grad = jnp.sum(second_rows * cot, axis=1, keepdims=True)
    spot = lax.broadcasted_iota(jnp.int32, probs.shape, 1)
    grad_probs = jnp.where(spot == first_id, first_grad, 0.0) + jnp.where(spot == second_id, second_grad, 0.0)
    grad_logits = (probs * (grad_probs - jnp.sum(probs * grad_probs, axis=1, keepdims=True))).astype(BF16)
    grad_router = tn(moe_ref[...], grad_logits)

    for k in range(1, n_dp):
        b_copy(k).wait()
    grad_moe = nn(both, back_in[...].reshape(slot_count, width)) + nt(grad_logits, weights.small())
    unit, inverse = centre(res_ref[...])
    extra, gain_two, shift_two = norm_back(grad_moe, unit, inverse, norms[2:3])
    grad_residual = cot + extra
    cot_full[...] = grad_residual
    grad_attended = grad_residual.astype(BF16)
    n_all = n_dp * n_t

    def keep(at, value):
        if inside:
            grads[:, :, at * shard : (at + 1) * shard, :] = value.astype(BF16).reshape(n_dp, n_t, shard, width)
        else:
            sum_ref[at] = value

    keep(OUT, tn(mix_ref[...], grad_attended))
    mix_ref_grad = nt(grad_attended, weights(OUT)).astype(BF16)
    dq[...] = mix_ref_grad
    low, high = half_masks()
    low_f, high_f = low.astype(F32), high.astype(F32)
    scale = HEAD_DIM ** (-0.5)

    def heads(j, carry):
        at = pl.ds(pl.multiple_of(j * LANES, LANES), LANES)
        query, key, value, grad = q_ref[:, at], k_ref[:, at], v_ref[:, at], dq[:, at]
        for mask, mask_f in ((low, low_f), (high, high_f)):
            probs = soft_scores(query * mask, key, bias[...])
            grad_probs = nt(grad * mask, value)
            grad_scores = probs * (grad_probs - jnp.sum(probs * grad_probs, axis=1, keepdims=True))
            grad_scores = grad_scores.astype(BF16)
            part_v = tn(probs.astype(BF16), grad)
            part_q = nn(grad_scores, key) * scale
            part_k = tn(grad_scores, query) * scale
            if mask is low:
                sum_q, sum_k, sum_v = part_q * mask_f, part_k * mask_f, part_v * mask_f
            else:
                sum_q, sum_k, sum_v = sum_q + part_q * mask_f, sum_k + part_k * mask_f, sum_v + part_v * mask_f
        dq[:, at] = sum_q.astype(BF16)
        dk[:, at] = sum_k.astype(BF16)
        dv[:, at] = sum_v.astype(BF16)
        return carry

    lax.fori_loop(0, width // LANES, heads, 0)
    keep(0, tn(norm_ref[...], dq[...]))
    keep(1, tn(norm_ref[...], dk[...]))
    keep(2, tn(norm_ref[...], dv[...]))
    grad_normed = nt(dq[...], weights(0)) + nt(dk[...], weights(1)) + nt(dv[...], weights(2))
    unit, inverse = centre(full[...])
    extra, gain_one, shift_one = norm_back(grad_normed, unit, inverse, norms[0:1])
    gx_ref[...] = (cot_full[...] + extra)[:rows].astype(BF16)
    small = small_grads(experts, grad_router, (gain_one, shift_one, gain_two, shift_two))
    if inside:
        at = slice(SMALL * shard, (SMALL + 1) * shard)
        grads[:, :, at, :LANES] = small.astype(BF16).reshape(n_dp, n_t, shard, LANES)
        grads[:, :, at, LANES:] = jnp.zeros((n_dp, n_t, shard, width - LANES), BF16)
        Scatter(n_dp, n_t, grads, sum_ref, *refs).run()
    else:
        sum_ref[SMALL] = jnp.zeros((width, width), F32)
        sum_ref[SMALL, :, :LANES] = small


def backward(cfg, cid, *args):
    n_dp, n_t, rows, padded, width, experts, rooms, shard, inside = cfg
    rows_block = ceil_to(5 * shard, 16)
    total = (rows_block, width) if inside else (5, width, width)
    outs = [jax.ShapeDtypeStruct((rows, width), BF16)] * 2 + [jax.ShapeDtypeStruct(total, F32)]
    scratch = [
        VMEM((padded, width), F32),
        VMEM((padded, width), F32),
        VMEM((padded, padded), F32),
        VMEM((n_dp, rooms, width), BF16),
        VMEM((n_dp, rooms, width), BF16),
        VMEM((n_dp, n_t, rows_block, width) if inside else (1, 1, 16, LANES), BF16),
    ]
    scratch += [DMA((n_dp,))] * 4 + [VMEM((padded, width), BF16)] * 3
    if inside:
        scratch += Scatter.scratch(n_dp, n_t, (rows_block, width))
    whole = pl.BlockSpec(memory_space=VMEM)
    return pl.pallas_call(
        partial(backward_kernel, cfg),
        out_shape=outs,
        in_specs=[whole] * len(args),
        out_specs=[whole] * len(outs),
        scratch_shapes=scratch,
        compiler_params=pltpu.CompilerParams(
            collective_id=cid, has_side_effects=True, vmem_limit_bytes=56 * 2**20
        ),
        name="backward_" + str(rooms),
    )(*args)


def pack_block(refs, block, shard, width, experts):
    q_ref, k_ref, v_ref, o_ref, *line_refs, router_ref = refs
    for at, ref in ((0, q_ref), (1, k_ref), (2, v_ref), (OUT, o_ref)):
        block[at * shard : (at + 1) * shard, :] = ref[...].astype(BF16)
    here = slice(SMALL * shard, (SMALL + 1) * shard)
    block[here, :] = jnp.zeros((shard, width), BF16)
    row, column = (lax.broadcasted_iota(jnp.int32, (shard, shard), axis) for axis in (0, 1))
    lane = lax.broadcasted_iota(jnp.int32, (shard, LANES), 1)
    small = jnp.zeros((shard, LANES), F32)
    for at, ref in enumerate(line_refs):
        upright = jnp.sum(jnp.where(row == column, ref[...], 0.0), axis=1, keepdims=True)
        small = jnp.where(lane == experts + at, upright, small)
    block[here, :LANES] = small.astype(BF16)
    block[here, :experts] = router_ref[...].astype(BF16)


def find_places(cfg, routes_ref, ids, place, turned, over):
    n_dp, n_t, rows, padded, width, experts, rooms, shard, inside, hid = cfg
    t = lax.axis_index("tensor")
    tok_count = routes_ref.shape[0]
    capacity = (5 * tok_count + 2 * experts - 1) // (2 * experts)
    lane = lax.broadcasted_iota(jnp.int32, (tok_count, LANES), 1)
    line = lax.broadcasted_iota(jnp.int32, (tok_count, LANES), 0)
    hot = (lane == routes_ref[:, 0:1]).astype(F32) + (lane == routes_ref[:, 1:2] + experts).astype(F32)
    total = jnp.sum(hot, axis=0, keepdims=True)
    before = jnp.sum(jnp.where(line < t * rows, hot, 0.0), axis=0, keepdims=True)
    ids[...] = jnp.full(ids.shape, LANES, jnp.int32)
    ids[:rows, :] = routes_ref[pl.ds(t * rows, rows), :]
    first_id, second_id = ids[:, 0:1], ids[:, 1:2]
    lane = lax.broadcasted_iota(jnp.int32, (padded, LANES), 1)
    is_first, is_second = lane == first_id, lane == second_id + experts
    hot = is_first.astype(F32) + is_second.astype(F32)
    down, across = (lax.broadcasted_iota(jnp.int32, (padded, padded), axis) for axis in (0, 1))
    rank = nn((down > across).astype(F32).astype(BF16), hot.astype(BF16))
    own = jnp.sum(hot, axis=0, keepdims=True)

    def later(counts):
        counts = pltpu.roll(jnp.broadcast_to(counts, (8, LANES)), experts, 1)[0:1]
        spot = lax.broadcasted_iota(jnp.int32, (1, LANES), 1)
        return jnp.where((spot >= experts) & (spot < 2 * experts), counts, 0.0)

    kept = rank + before + later(total) < capacity
    rank = rank + later(own)

    def slot(choice, mine):
        here = jnp.sum(jnp.where(mine & kept, rank + 1.0, 0.0), axis=1, keepdims=True) - 1.0
        good = (here >= 0.0) & (here < rooms)
        return jnp.where(good, choice.astype(F32) * rooms + here, -1.0), jnp.max(here, axis=0, keepdims=True)

    first_slot, first_most = slot(first_id, is_first)
    second_slot, second_most = slot(second_id, is_second)
    place[...] = jnp.full(place.shape, -1.0, F32)
    place[:padded, :] = jnp.where(lane == 0, first_slot, jnp.where(lane == 1, second_slot, -1.0))
    turned[...] = place[...].T[0:8]
    most = jnp.maximum(first_most, second_most)
    over[...] = jnp.broadcast_to(jnp.where(most >= rooms, 1.0, 0.0), over.shape)


def step_kernel(cfg, *refs):
    n_dp, n_t, rows, padded, width, experts, rooms, shard, inside, hid = cfg
    refs = list(refs)

    def take(count):
        got = refs[:count]
        del refs[:count]
        return got

    x_ref, cot_ref, routes_ref, e_in_ref, e_out_ref = take(5)
    shared = take(9 if inside else 1)
    out_ref, gx_ref, sum_ref, g_in_ref, g_out_ref = take(5)
    block, gathered, grads, full, cot_full, bias, res, probs_s = take(8)
    ids, place, turned, over = take(4)
    moe, q_s, k_s, v_s, mix, norm, dk, dv = take(8)
    send_d, send_s, recv_d, recv_s, ret_in, back_in, act, slope = take(8)
    wi, wo, gi, go, gi_in, go_in = take(6)
    d_send, d_recv, s_send, s_recv, r_send, r_recv, b_send, b_recv, own_sems = take(9)
    wi_spread, wo_spread = Spread(n_t, wi, *take(2)), Spread(n_t, wo, *take(2))
    gi_collect, go_collect = Collect(n_t, gi, gi_in, *take(2)), Collect(n_t, go, go_in, *take(2))
    dp, t = lax.axis_index("dp"), lax.axis_index("tensor")
    scale = HEAD_DIM ** (-0.5)
    slot_count = n_dp * rooms
    half, wide = min(256, hid), min(256, width)
    table = [sorted(range(n_t), key=lambda j: (abs(j - at), j)) for at in range(n_t)]

    def order(p):
        found = jnp.int32(0)
        for at in range(n_t):
            for spot in range(n_t):
                found = found + jnp.where((t == at) & (p == spot), table[at][spot], 0)
        return found

    def dp_copy(src, dst, sems, k):
        to = lax.rem(dp + k, n_dp)
        return remote(src.at[to], dst.at[dp], sems[0].at[k], sems[1].at[k], {"dp": to})

    d_copy = partial(dp_copy, send_d, recv_d, (d_send, d_recv))
    s_copy = partial(dp_copy, send_s, recv_s, (s_send, s_recv))
    r_copy = partial(dp_copy, send_d, ret_in, (r_send, r_recv))
    b_copy = partial(dp_copy, send_s, back_in, (b_send, b_recv))

    meet(n_dp, n_t, True)
    load_in = pltpu.make_async_copy(e_in_ref, g_in_ref, own_sems.at[0])
    load_out = pltpu.make_async_copy(e_out_ref, g_out_ref, own_sems.at[1])
    load_in.start()
    load_out.start()
    if inside:
        pack_block(shared, block, shard, width, experts)
        size = len(Gather.scratch(n_dp, n_t))
        gather_a = Gather(n_dp, n_t, 0, OUT * shard, block, gathered, *take(size))
        gather_b = Gather(n_dp, n_t, OUT * shard, shard, block, gathered, *take(size))
        gather_a.start()
        gather_b.start()
        weights = Weights(shard, width, gathered=gathered)
    else:
        weights = Weights(shard, width, whole=shared[0])
    load_in.wait()
    wi[t] = g_in_ref[...].astype(BF16)
    load_out.wait()
    wo[t] = g_out_ref[...].astype(BF16)
    tail = rows - rows % 8
    full[tail:, :] = jnp.zeros((padded - tail, width), F32)
    full[:rows, :] = x_ref[...].astype(F32)
    cot_full[tail:, :] = jnp.zeros((padded - tail, width), F32)
    cot_full[:rows, :] = cot_ref[...].astype(F32)
    bias[...] = image_bias(rows, padded)
    find_places(cfg, routes_ref, ids, place, turned, over)
    if inside:
        gather_a.pass_to_chips()
    wi_spread.step(0)
    if inside:
        gather_b.pass_to_chips()
        gather_a.pass_to_core()
        gather_a.arrive()
    wi_spread.step(1)
    norms = norm_rows(weights.small(), experts)
    unit, _ = centre(full[...])
    norm[...] = (unit * norms[0:1] + norms[1:2]).astype(BF16)
    q_s[...] = nn(norm[...], weights(0)).astype(BF16)
    k_s[...] = nn(norm[...], weights(1)).astype(BF16)
    v_s[...] = nn(norm[...], weights(2)).astype(BF16)
    if inside:
        gather_b.pass_to_core()
    low, high = half_masks()
    low_f, high_f = low.astype(F32), high.astype(F32)

    def heads(j, carry):
        at = pl.ds(pl.multiple_of(j * LANES, LANES), LANES)
        query, key, value = q_s[:, at], k_s[:, at], v_s[:, at]
        first = nn(soft_scores(query * low, key, bias[...]).astype(BF16), value)
        second = nn(soft_scores(query * high, key, bias[...]).astype(BF16), value)
        mix[:, at] = (first * low_f + second * high_f).astype(BF16)
        return carry

    lax.fori_loop(0, width // LANES, heads, 0)
    if inside:
        gather_b.arrive()
    residual = full[...] + nn(mix[...], weights(OUT))
    res[...] = residual
    unit, _ = centre(residual)
    moe[...] = (unit * norms[2:3] + norms[3:4]).astype(BF16)
    probs_s[...] = router_probs(nn(moe[...], weights.small()), experts)

    def selectors(p):
        slot = lax.broadcasted_iota(jnp.int32, (rooms, padded), 0) + p * rooms
        first = (slot == turned[0:1, :padded].astype(jnp.int32)).astype(F32)
        second = (slot == turned[1:2, :padded].astype(jnp.int32)).astype(F32)
        return first, second

    def dispatch(k, carry):
        to = lax.rem(dp + k, n_dp)
        first, second = selectors(to)
        got = nn((first + second).astype(BF16), moe[...]).astype(BF16)

        @pl.when(k > 0)
        def _():
            send_d[to] = got
            d_copy(k).start()

        @pl.when(k == 0)
        def _():
            recv_d[to] = got

        return carry

    lax.fori_loop(0, n_dp, dispatch, 0)
    if n_t > 2:
        wi_spread.step(2)
    cot = cot_full[...]
    first_id, second_id = ids[:, 0:1], ids[:, 1:2]
    first_gate, second_gate = pick_gate(probs_s[...], first_id), pick_gate(probs_s[...], second_id)
    dk[...] = (first_gate * cot).astype(BF16)
    dv[...] = (second_gate * cot).astype(BF16)

    def dispatch_grad(k, carry):
        to = lax.rem(dp + k, n_dp)
        first, second = selectors(to)
        got = (nn(first.astype(BF16), dk[...]) + nn(second.astype(BF16), dv[...])).astype(BF16)

        @pl.when(k > 0)
        def _():
            send_s[to] = got
            s_copy(k).start()

        @pl.when(k == 0)
        def _():
            recv_s[to] = got

        return carry

    lax.fori_loop(0, n_dp, dispatch_grad, 0)
    wo_spread.step(0)

    def hidden_units(j, g):
        active, steep = gelu_parts(nn(recv_d[g], wi[j]))
        act[j, g] = active.astype(BF16)
        slope[j, g] = steep.astype(BF16)

    def own_hidden(k, carry):
        @pl.when(k > 0)
        def _():
            d_copy(k).wait_recv()

        hidden_units(t, lax.rem(dp + n_dp - k, n_dp))
        return carry

    lax.fori_loop(0, n_dp, own_hidden, 0)
    for s in range(3, n_t):
        wi_spread.step(s)

    def other_hidden(i, carry):
        hidden_units(order(1 + i // n_dp), lax.rem(i, n_dp))
        return carry

    lax.fori_loop(0, (n_t - 1) * n_dp, other_hidden, 0)
    wo_spread.step(1)
    for k in range(1, n_dp):
        s_copy(k).wait_recv()

    def outer_grad(i, carry):
        j = order(n_t - 1 - i // (hid // half))
        at = pl.ds(pl.multiple_of(lax.rem(i, hid // half) * half, half), half)
        left = act[j, :, :, at].reshape(slot_count, half)
        go[j, at, :] = tn(left, recv_s[...].reshape(slot_count, width)).astype(BF16)

        @pl.when(lax.rem(i, hid // half) == hid // half - 1)
        def _():
            go_collect.begin(j)

        return carry

    lax.fori_loop(0, n_t * (hid // half), outer_grad, 0)

    def inner_grads(p, carry):
        j = order(p)

        def hidden_grad(i, inner):
            slope[j, i] = (nt(recv_s[i], wo[j]) * slope[j, i].astype(F32)).astype(BF16)
            return inner

        lax.fori_loop(0, n_dp, hidden_grad, 0)

        def inner_grad(i, inner):
            at = pl.ds(pl.multiple_of(i * wide, wide), wide)
            left = recv_d[:, :, at].reshape(slot_count, wide)
            gi[j, at, :] = tn(left, slope[j].reshape(slot_count, hid)).astype(BF16)
            return inner

        lax.fori_loop(0, width // wide, inner_grad, 0)
        gi_collect.begin(j)
        return carry

    def some_inner(p, carry):
        @pl.when(p == 2)
        def _():
            wo_spread.step(2) if n_t > 2 else None

        @pl.when(p == 3)
        def _():
            go_collect.step(1, True) if n_t > 2 else None
            for s in range(3, n_t):
                wo_spread.step(s)

        return inner_grads(p, carry)

    lax.fori_loop(0, n_t, some_inner, 0)

    for k in range(1, n_dp):
        d_copy(k).wait_send()

    def give_back(i, carry):
        k = lax.rem(i + 1, n_dp)
        to = lax.rem(dp + k, n_dp)
        total = nn(act[0, to], wo[0])
        for j in range(1, n_t):
            total = total + nn(act[j, to], wo[j])

        @pl.when(k > 0)
        def _():
            send_d[to] = total.astype(BF16)
            r_copy(k).start()

        @pl.when(k == 0)
        def _():
            ret_in[to] = total.astype(BF16)

        return carry

    lax.fori_loop(0, n_dp, give_back, 0)
    for e in range(2, n_t - 1):
        go_collect.step(e, True)

    for k in range(1, n_dp):
        s_copy(k).wait_send()

    def give_back_grad(i, carry):
        k = lax.rem(i + 1, n_dp)
        to = lax.rem(dp + k, n_dp)
        total = nt(slope[0, to], wi[0])
        for j in range(1, n_t):
            total = total + nt(slope[j, to], wi[j])

        @pl.when(k > 0)
        def _():
            send_s[to] = total.astype(BF16)
            b_copy(k).start()

        @pl.when(k == 0)
        def _():
            back_in[to] = total.astype(BF16)

        return carry

    lax.fori_loop(0, n_dp, give_back_grad, 0)
    if n_t > 2:
        gi_collect.step(1, False)
    lane = lax.broadcasted_iota(jnp.int32, (padded, slot_count), 1)
    first = (lane == place[:padded, 0:1].astype(jnp.int32)).astype(F32)
    second = (lane == place[:padded, 1:2].astype(jnp.int32)).astype(F32)
    both = (first + second).astype(BF16)
    for k in range(1, n_dp):
        r_copy(k).wait()
    returned = ret_in[...].reshape(slot_count, width)
    first_rows = nn(first.astype(BF16), returned)
    second_rows = nn(second.astype(BF16), returned)
    probs = probs_s[...]
    first_id, second_id = ids[:, 0:1], ids[:, 1:2]
    outcome = res[...] + pick_gate(probs, first_id) * first_rows + pick_gate(probs, second_id) * second_rows
    out_ref[...] = outcome[:rows].astype(BF16)
    cot = cot_full[...]
    first_grad = jnp.sum(first_rows * cot, axis=1, keepdims=True)
    second_grad = jnp.sum(second_rows * cot, axis=1, keepdims=True)
    spot = lax.broadcasted_iota(jnp.int32, probs.shape, 1)
    grad_probs = jnp.where(spot == first_id, first_grad, 0.0) + jnp.where(spot == second_id, second_grad, 0.0)
    grad_logits = (probs * (grad_probs - jnp.sum(probs * grad_probs, axis=1, keepdims=True))).astype(BF16)
    grad_router = tn(moe[...], grad_logits)
    if n_t > 2:
        gi_collect.step(2, False)
    for k in range(1, n_dp):
        b_copy(k).wait()
    grad_moe = nn(both, back_in[...].reshape(slot_count, width)) + nt(grad_logits, weights.small())
    unit, inverse = centre(res[...])
    extra, gain_two, shift_two = norm_back(grad_moe, unit, inverse, norms[2:3])
    grad_residual = cot + extra
    cot_full[...] = grad_residual
    grad_attended = grad_residual.astype(BF16)

    def keep(at, value):
        if inside:
            grads[:, :, at * shard : (at + 1) * shard, :] = value.astype(BF16).reshape(n_dp, n_t, shard, width)
        else:
            sum_ref[at] = value

    keep(OUT, tn(mix[...], grad_attended))
    dq = mix
    dq[...] = nt(grad_attended, weights(OUT)).astype(BF16)

    def heads_back(j, carry):
        at = pl.ds(pl.multiple_of(j * LANES, LANES), LANES)
        query, key, value, grad = q_s[:, at], k_s[:, at], v_s[:, at], dq[:, at]
        for mask, mask_f in ((low, low_f), (high, high_f)):
            probs = soft_scores(query * mask, key, bias[...])
            grad_probs = nt(grad * mask, value)
            grad_scores = probs * (grad_probs - jnp.sum(probs * grad_probs, axis=1, keepdims=True))
            grad_scores = grad_scores.astype(BF16)
            part_v = tn(probs.astype(BF16), grad)
            part_q = nn(grad_scores, key) * scale
            part_k = tn(grad_scores, query) * scale
            if mask is low:
                sum_q, sum_k, sum_v = part_q * mask_f, part_k * mask_f, part_v * mask_f
            else:
                sum_q, sum_k, sum_v = sum_q + part_q * mask_f, sum_k + part_k * mask_f, sum_v + part_v * mask_f
        dq[:, at] = sum_q.astype(BF16)
        dk[:, at] = sum_k.astype(BF16)
        dv[:, at] = sum_v.astype(BF16)
        return carry

    lax.fori_loop(0, width // LANES, heads_back, 0)
    for e in range(3, 2 * n_t - 4):
        gi_collect.step(e, False)
    keep(0, tn(norm[...], dq[...]))
    keep(1, tn(norm[...], dk[...]))
    keep(2, tn(norm[...], dv[...]))
    grad_normed = nt(dq[...], weights(0)) + nt(dk[...], weights(1)) + nt(dv[...], weights(2))
    full[tail:, :] = jnp.zeros((padded - tail, width), F32)
    full[:rows, :] = x_ref[...].astype(F32)
    unit, inverse = centre(full[...])
    extra, gain_one, shift_one = norm_back(grad_normed, unit, inverse, norms[0:1])
    gx_ref[...] = (cot_full[...] + extra)[:rows].astype(BF16)
    small = small_grads(experts, grad_router, (gain_one, shift_one, gain_two, shift_two))
    lane = lax.broadcasted_iota(jnp.int32, small.shape, 1)
    small = jnp.where(lane == experts + 4, over[0:1, :], small)
    if inside:
        at = slice(SMALL * shard, (SMALL + 1) * shard)
        grads[:, :, at, :LANES] = small.astype(BF16).reshape(n_dp, n_t, shard, LANES)
        grads[:, :, at, LANES:] = jnp.zeros((n_dp, n_t, shard, width - LANES), BF16)
        Scatter(n_dp, n_t, grads, sum_ref, *refs).run()
        gather_a.drain()
        gather_b.drain()
    else:
        sum_ref[SMALL] = jnp.zeros((width, width), F32)
        sum_ref[SMALL, :, :LANES] = small
    go_collect.finish(g_out_ref)
    gi_collect.finish(g_in_ref)
    wi_spread.drain()
    wo_spread.drain()


def run_step(cfg, cid, x, cot, routes, e_in, e_out, shared):
    n_dp, n_t, rows, padded, width, experts, rooms, shard, inside, hid = cfg
    rows_block = ceil_to(5 * shard, 16)
    total = (rows_block, width) if inside else (5, width, width)
    outs = [
        jax.ShapeDtypeStruct((rows, width), BF16),
        jax.ShapeDtypeStruct((rows, width), BF16),
        jax.ShapeDtypeStruct(total, F32),
        jax.ShapeDtypeStruct((width, hid), F32),
        jax.ShapeDtypeStruct((hid, width), F32),
    ]
    spread = (n_dp, n_t, rows_block, width) if inside else (1, 1, 16, LANES)
    wide = ceil_to(padded, LANES)
    rows_f, rows_b = VMEM((padded, width), F32), VMEM((padded, width), BF16)
    slots_b, units_b = VMEM((n_dp, rooms, width), BF16), VMEM((n_t, n_dp, rooms, hid), BF16)
    in_b, out_b = (VMEM((n_t,) + shape, BF16) for shape in ((width, hid), (hid, width)))
    in_more, out_more = (VMEM((n_t + 1,) + shape, BF16) for shape in ((width, hid), (hid, width)))
    scratch = [VMEM((rows_block, width), BF16)] + [VMEM(spread, BF16)] * 2
    scratch += [rows_f, rows_f, VMEM((padded, padded), F32), rows_f, VMEM((padded, LANES), F32)]
    scratch += [VMEM((padded, 2), jnp.int32), VMEM((wide, LANES), F32), VMEM((8, wide), F32), VMEM((8, LANES), F32)]
    scratch += [rows_b] * 8 + [slots_b] * 6 + [units_b] * 2
    scratch += [in_b, out_b, in_b, out_b, in_more, out_more]
    scratch += [DMA((n_dp,))] * 8 + [DMA((2,))] + Spread.scratch(n_t) * 2 + Collect.scratch(n_t) * 2
    if inside:
        scratch += Gather.scratch(n_dp, n_t) * 2 + Scatter.scratch(n_dp, n_t, (rows_block, width))
    whole, anywhere = pl.BlockSpec(memory_space=VMEM), pl.BlockSpec(memory_space=pl.ANY)
    return pl.pallas_call(
        partial(step_kernel, cfg),
        out_shape=outs,
        in_specs=[whole] * 3 + [anywhere] * 2 + [whole] * len(shared),
        out_specs=[whole] * len(outs),
        scratch_shapes=scratch,
        compiler_params=pltpu.CompilerParams(
            collective_id=cid, has_side_effects=True, vmem_limit_bytes=60 * 2**20
        ),
        name="step_" + str(rooms),
    )(x, cot, routes, e_in, e_out, *shared)


def lay_kernel(shard, experts, out_ref, gx_ref, sum_ref, in_ref, outer_ref, *outs):
    outs[0][...] = out_ref[...]
    outs[1][...] = gx_ref[...]
    for at, spot in ((0, 4), (1, 5), (2, 6), (OUT, 7)):
        outs[spot][...] = sum_ref[at * shard : (at + 1) * shard, :]
    small = sum_ref[SMALL * shard : (SMALL + 1) * shard, :LANES]
    row, column = (lax.broadcasted_iota(jnp.int32, (shard, shard), axis) for axis in (0, 1))
    for at, spot in enumerate((2, 3, 8, 9)):
        upright = small[:, experts + at : experts + at + 1]
        outs[spot][...] = jnp.sum(jnp.where(row == column, upright, 0.0), axis=0, keepdims=True)
    outs[10][...] = small[:, :experts]
    outs[11][...] = in_ref[...]
    outs[12][...] = outer_ref[...]


def lay_out(shard, experts, *args):
    rows, width = args[0].shape
    line = jax.ShapeDtypeStruct((1, shard), F32)
    square = jax.ShapeDtypeStruct((shard, width), F32)
    outs = [jax.ShapeDtypeStruct((rows, width), BF16)] * 2 + [line] * 2 + [square] * 4 + [line] * 2
    outs += [jax.ShapeDtypeStruct((shard, experts), F32)]
    outs += [jax.ShapeDtypeStruct(arg.shape, F32) for arg in args[3:]]

    def full(shape):
        return pl.BlockSpec(shape, lambda i: (0,) * len(shape))

    return pl.pallas_call(
        partial(lay_kernel, shard, experts),
        grid=(1,),
        out_shape=outs,
        in_specs=[full(arg.shape) for arg in args],
        out_specs=[full(out.shape) for out in outs],
        compiler_params=pltpu.CompilerParams(vmem_limit_bytes=32 * 2**20),
        name="outputs",
    )(*args)


def route_pairs(routes, t, row_count, experts, capacity):
    tok_count = routes.shape[0]
    ids = jnp.arange(experts, dtype=jnp.int32)[None, :]
    start = t * row_count
    rows = lax.dynamic_slice_in_dim(routes, start, row_count, 0)
    before = (jnp.arange(tok_count, dtype=jnp.int32) < start)[:, None]
    all_first = routes[:, 0:1] == ids
    all_second = routes[:, 1:2] == ids
    base_first = jnp.sum((all_first & before).astype(jnp.int32), axis=0)
    total_first = jnp.sum(all_first.astype(jnp.int32), axis=0)
    base_second = jnp.sum((all_second & before).astype(jnp.int32), axis=0)
    hot_first = rows[:, 0:1] == ids
    hot_second = rows[:, 1:2] == ids
    at = jnp.arange(row_count, dtype=jnp.int32)
    lower = (at[:, None] > at[None, :]).astype(BF16)
    both = jnp.concatenate([hot_first, hot_second], axis=1).astype(BF16)
    earlier = nn(lower, both).astype(jnp.int32)
    own_first = jnp.sum(hot_first.astype(jnp.int32), axis=0)
    rank_first = earlier[:, :experts]
    rank_second = earlier[:, experts:] + own_first
    place_first = rank_first + base_first
    place_second = earlier[:, experts:] + total_first + base_second
    first = jnp.sum(jnp.where(hot_first & (place_first < capacity), rank_first + 1, 0), axis=1) - 1
    second = jnp.sum(jnp.where(hot_second & (place_second < capacity), rank_second + 1, 0), axis=1) - 1
    return rows, first, second


def per_device(
    n_dp,
    n_t,
    inputs,
    cotangent,
    routes,
    gain_attn,
    shift_attn,
    query_w,
    key_w,
    value_w,
    out_w,
    gain_moe,
    shift_moe,
    router_w,
    expert_in,
    expert_out,
):
    t = lax.axis_index("tensor")
    shard, width = query_w.shape
    experts = router_w.shape[1]
    tok_count = routes.shape[0]
    rows = inputs.shape[0]
    hid = expert_in.shape[2]
    padded = ceil_to(rows, 16)
    capacity = (5 * tok_count + 2 * experts - 1) // (2 * experts)
    inside = shard % 16 == 0
    every = ("dp", "tensor")
    lines = (gain_attn, shift_attn, gain_moe, shift_moe)

    def stack():
        small = jnp.concatenate([router_w] + [line[:, None] for line in lines], axis=1)
        small = jnp.pad(small, ((0, 0), (0, width - small.shape[1])))
        return jnp.stack([query_w, key_w, value_w, small, out_w]).astype(BF16)

    if inside:
        shared = [query_w, key_w, value_w, out_w] + [line[None, :] for line in lines] + [router_w]
    else:
        shared = [lax.all_gather(stack(), every, axis=1, tiled=True)]

    def finish(results):
        summed = results[2]
        if not inside:
            summed = lax.psum_scatter(summed, every, scatter_dimension=1, tiled=True).reshape(5 * shard, width)
        outs = lay_out(shard, experts, results[0], results[1], summed, *results[3:])
        return tuple(outs)

    def slow(_):
        rooms = ceil_to(rows, 16)
        cfg = (n_dp, n_t, rows, padded, width, experts, rooms, shard, inside)
        route_rows, first_rank, second_rank = route_pairs(routes, t, rows, experts, capacity)

        def slot(choice, rank):
            return jnp.where(rank >= 0, choice * rooms + rank, -1)

        slots = jnp.stack([slot(route_rows[:, 0], first_rank), slot(route_rows[:, 1], second_rank)])
        slots = jnp.pad(slots, ((0, 0), (0, padded - rows)), constant_values=-1)
        cols = jnp.concatenate([jnp.pad(route_rows, ((0, padded - rows), (0, 0))), slots.T], axis=1)
        block = stack().reshape(5 * shard, width) if inside else shared[0]
        kept = forward(cfg, 1, inputs, cotangent, cols, slots, block)

        def turn(k):
            return [(i, (i + k) % n_t) for i in range(n_t)]

        both = jnp.stack([expert_in[0].T, expert_out[0]]).astype(BF16)
        parts = [both] + [lax.ppermute(both, "tensor", turn(k)) for k in range(1, n_t)]
        w_in, w_out = (jnp.concatenate([part[i] for part in parts], axis=0) for i in range(2))
        returned, back, grad_inner, grad_outer = run_expert(
            kept[1].reshape(n_dp * rooms, width), kept[2].reshape(n_dp * rooms, width), w_in, w_out
        )
        both = jnp.stack([grad_inner.reshape(n_t, hid, width), grad_outer.reshape(n_t, hid, width)], axis=1)
        total = both[0].astype(F32)
        for k in range(1, n_t):
            total = total + lax.ppermute(both[k], "tensor", turn(-k)).astype(F32)
        results = backward(
            cfg,
            2,
            returned.reshape(n_dp, rooms, width),
            back.reshape(n_dp, rooms, width),
            inputs,
            cotangent,
            cols,
            kept[0] if inside else block,
            *kept[3:],
        )
        return finish((*results, total[0].T, total[1]))

    rooms = min(ceil_to((7 * rows + 2 * experts - 1) // (2 * experts), 16), ceil_to(rows, 16))
    cfg = (n_dp, n_t, rows, padded, width, experts, rooms, shard, inside, hid)
    fast = run_step(cfg, 0, inputs, cotangent, routes, expert_in[0], expert_out[0], shared)
    if inside:
        crowded = fast[2][SMALL * shard, experts + 4] > 0.5
    else:
        crowded = lax.psum(fast[2][SMALL, 0, experts + 4], every) > 0.5
    outs = lax.cond(crowded, slow, finish, tuple(fast))
    lined = [out.reshape(shard) if at in (2, 3, 8, 9) else out for at, out in enumerate(outs)]
    lined[11], lined[12] = lined[11][None], lined[12][None]
    return tuple(lined)


def solution(mesh):
    every = ("dp", "tensor")
    rows, line = P(every, None), P(every)
    w_in, w_out = P("dp", None, "tensor"), P("dp", "tensor", None)
    return jax.shard_map(
        partial(per_device, mesh.shape["dp"], mesh.shape["tensor"]),
        mesh=mesh,
        in_specs=(rows, rows, P("dp", None), line, line, rows, rows, rows, rows, line, line, rows, w_in, w_out),
        out_specs=(rows, rows, line, line, rows, rows, rows, rows, line, line, rows, w_in, w_out),
        check_vma=False,
    )
```

```python
from functools import partial

import jax
import jax.numpy as jnp
from jax import lax
from jax.experimental import pallas as pl
from jax.experimental.pallas import tpu as pltpu
from jax.sharding import PartitionSpec as P

SEQ = 197
HEAD_DIM = 64
LANES = 128
MESH = pl.DeviceIdType.MESH
F32 = jnp.float32
BF16 = jnp.bfloat16
VMEM = pltpu.VMEM
DMA = pltpu.SemaphoreType.DMA
SMALL, OUT = 3, 4


def ceil_to(value, unit):
    return (value + unit - 1) // unit * unit


def nn(left, right):
    return lax.dot_general(left, right, (((1,), (0,)), ((), ())), preferred_element_type=F32)


def nt(left, right):
    return lax.dot_general(left, right, (((1,), (1,)), ((), ())), preferred_element_type=F32)


def tn(left, right):
    return lax.dot_general(left, right, (((0,), (0,)), ((), ())), preferred_element_type=F32)


def remote(src, dst, send, recv, device):
    return pltpu.make_async_remote_copy(
        src_ref=src, dst_ref=dst, send_sem=send, recv_sem=recv, device_id=device, device_id_type=MESH
    )


def meet(n_dp, n_t, z_too):
    dp = lax.axis_index("dp")
    t = lax.axis_index("tensor")
    bar = pltpu.get_barrier_semaphore()
    for k in range(1, n_dp):
        pl.semaphore_signal(bar, inc=1, device_id={"dp": lax.rem(dp + k, n_dp)}, device_id_type=MESH)
    if z_too:
        for k in range(1, n_t):
            pl.semaphore_signal(bar, inc=1, device_id={"tensor": lax.rem(t + k, n_t)}, device_id_type=MESH)
    pl.semaphore_wait(bar, n_dp - 1 + (n_t - 1 if z_too else 0))


class Gather:
    def __init__(self, n_dp, n_t, first, count, block, out, own_sem, z_send, z_recv, c_send, c_recv, k_send, k_recv):
        self.n_t, self.n_chip = n_t, n_dp // 2
        self.rows = pl.ds(first, count)
        self.block, self.out, self.own_sem = block.at[self.rows], out, own_sem
        self.z_sems, self.c_sems, self.k_sems = (z_send, z_recv), (c_send, c_recv), (k_send, k_recv)
        self.dp, self.t = lax.axis_index("dp"), lax.axis_index("tensor")
        self.chip, self.core = self.dp // 2, lax.rem(self.dp, 2)
        self.other = self.chip * 2 + 1 - self.core

    @staticmethod
    def scratch(n_dp, n_t):
        n_chip = n_dp // 2
        pair = [DMA((n_chip, n_t))] * 2
        return [DMA, DMA((n_t,)), DMA((n_t,))] + pair + pair

    def place(self, dp, t):
        return self.out.at[dp, t, self.rows]

    def z_copy(self, k):
        send, recv = self.z_sems
        to = lax.rem(self.t + k, self.n_t)
        return remote(self.block, self.place(self.dp, self.t), send.at[k], recv.at[k], {"tensor": to})

    def chip_copy(self, k, j):
        send, recv = self.c_sems
        here = self.place(self.dp, lax.rem(self.t + self.n_t - j, self.n_t))
        to = lax.rem(self.chip + k, self.n_chip) * 2 + self.core
        return remote(self.block if j == 0 else here, here, send.at[k, j], recv.at[k, j], {"dp": to})

    def core_copy(self, k, j):
        send, recv = self.k_sems
        src = lax.rem(self.chip + self.n_chip - k, self.n_chip) * 2 + self.core
        here = self.place(src, lax.rem(self.t + self.n_t - j, self.n_t))
        own = k == 0 and j == 0
        return remote(self.block if own else here, here, send.at[k, j], recv.at[k, j], {"dp": self.other})

    def own_copy(self):
        return pltpu.make_async_copy(self.block, self.place(self.dp, self.t), self.own_sem)

    def start(self):
        for k in range(1, self.n_t):
            self.z_copy(k).start()
        self.own_copy().start()
        for k in range(1, self.n_chip):
            self.chip_copy(k, 0).start()
        self.core_copy(0, 0).start()

    def pass_to_chips(self):
        for j in range(1, self.n_t):
            self.z_copy(j).wait_recv()
            for k in range(1, self.n_chip):
                self.chip_copy(k, j).start()
            self.core_copy(0, j).start()

    def pass_to_core(self):
        for j in range(self.n_t):
            for k in range(1, self.n_chip):
                self.chip_copy(k, j).wait_recv()
                self.core_copy(k, j).start()

    def arrive(self):
        self.own_copy().wait()
        for j in range(self.n_t):
            for k in range(self.n_chip):
                self.core_copy(k, j).wait_recv()

    def drain(self):
        for k in range(1, self.n_t):
            self.z_copy(k).wait_send()
        for j in range(self.n_t):
            for k in range(1, self.n_chip):
                self.chip_copy(k, j).wait_send()
            for k in range(self.n_chip):
                self.core_copy(k, j).wait_send()


class Scatter:
    def __init__(
        self, n_dp, n_t, grads, out, core_in, half, chip_in, part, z_in, k_send, k_recv, c_send, c_recv, z_send, z_recv
    ):
        self.n_t, self.n_chip = n_t, n_dp // 2
        self.grads, self.out = grads, out
        self.core_in, self.half, self.chip_in, self.part, self.z_in = core_in, half, chip_in, part, z_in
        self.k_sems, self.c_sems, self.z_sems = (k_send, k_recv), (c_send, c_recv), (z_send, z_recv)
        self.dp, self.t = lax.axis_index("dp"), lax.axis_index("tensor")
        self.chip, self.core = self.dp // 2, lax.rem(self.dp, 2)
        self.other = self.chip * 2 + 1 - self.core

    @staticmethod
    def scratch(n_dp, n_t, block):
        n_chip = n_dp // 2
        buffers = [VMEM((n_chip, n_t) + block, BF16)] + [VMEM((n_chip - 1, n_t) + block, BF16)] * 2
        buffers += [VMEM((n_t - 1,) + block, BF16)] * 2
        return buffers + [DMA((n_chip,))] * 4 + [DMA((n_t,))] * 2

    def core_copy(self, k):
        to = lax.rem(self.chip + k, self.n_chip)
        src = self.grads.at[to * 2 + 1 - self.core]
        return remote(src, self.core_in.at[k], self.k_sems[0].at[k], self.k_sems[1].at[k], {"dp": self.other})

    def chip_copy(self, k):
        to = lax.rem(self.chip + k, self.n_chip) * 2 + self.core
        return remote(self.half.at[k - 1], self.chip_in.at[k - 1], self.c_sems[0].at[k], self.c_sems[1].at[k], {"dp": to})

    def z_copy(self, k):
        to = lax.rem(self.t + k, self.n_t)
        return remote(self.part.at[k - 1], self.z_in.at[k - 1], self.z_sems[0].at[k], self.z_sems[1].at[k], {"tensor": to})

    def run(self, between=None, after=None):
        n_chip, n_t = self.n_chip, self.n_t
        order = list(range(1, n_chip)) + [0]
        for k in order:
            self.core_copy(k).start()
        for k in order:
            self.core_copy(k).wait_recv()
            if k > 0:
                to = lax.rem(self.chip + k, n_chip) * 2 + self.core
                self.half[k - 1] = (self.grads[to].astype(F32) + self.core_in[k].astype(F32)).astype(BF16)
                self.chip_copy(k).start()
        if between is not None:
            between()
        for k in range(1, n_chip):
            self.chip_copy(k).wait_recv()
        for k in list(range(1, n_t)) + [0]:
            row = lax.rem(self.t + k, n_t)
            total = self.grads[self.dp, row].astype(F32) + self.core_in[0, row].astype(F32)
            for c in range(1, n_chip):
                total = total + self.chip_in[c - 1, row].astype(F32)
            if k > 0:
                self.part[k - 1] = total.astype(BF16)
                self.z_copy(k).start()
            else:
                self.out[...] = total
        if after is not None:
            after()
        for k in range(1, n_t):
            self.z_copy(k).wait_recv()
            self.out[...] += self.z_in[k - 1].astype(F32)
        for k in range(n_chip):
            self.core_copy(k).wait_send()
        for k in range(1, n_chip):
            self.chip_copy(k).wait_send()
        for k in range(1, n_t):
            self.z_copy(k).wait_send()


class Reduce:
    def __init__(self, n_dp, n_t, out, grads, core_in, half, chip_in, part, z_in, *sems):
        self.n_t, self.n_chip, self.out = n_t, n_dp // 2, out
        self.grads, self.core_in, self.half = grads, core_in, half
        self.chip_in, self.part, self.z_in = chip_in, part, z_in
        self.k_sems, self.c_sems, self.z_sems = sems[0:2], sems[2:4], sems[4:6]
        self.dp, self.t = lax.axis_index("dp"), lax.axis_index("tensor")
        self.chip, self.core = self.dp // 2, lax.rem(self.dp, 2)
        self.other = self.chip * 2 + 1 - self.core

    @staticmethod
    def scratch(n_dp, n_t, parts, block):
        n_chip = n_dp // 2
        sizes = [(n_dp, n_t), (n_chip, n_t), (n_chip - 1, n_t), (n_chip - 1, n_t), (n_t - 1,), (n_t - 1,)]
        return [VMEM((parts,) + size + block, BF16) for size in sizes] + [DMA((parts, n_chip))] * 4 + [DMA((parts, n_t))] * 2

    def put(self, p, first, value):
        n_dp, n_t = self.n_chip * 2, self.n_t
        count, lanes = value.shape[0] // (n_dp * n_t), value.shape[1]
        self.grads[p, :, :, first : first + count, :] = value.astype(BF16).reshape(n_dp, n_t, count, lanes)

    def core_copy(self, p, k):
        src = self.grads.at[p, lax.rem(self.chip + k, self.n_chip) * 2 + 1 - self.core]
        send, recv = self.k_sems
        return remote(src, self.core_in.at[p, k], send.at[p, k], recv.at[p, k], {"dp": self.other})

    def chip_copy(self, p, k):
        to = lax.rem(self.chip + k, self.n_chip) * 2 + self.core
        send, recv = self.c_sems
        return remote(self.half.at[p, k - 1], self.chip_in.at[p, k - 1], send.at[p, k], recv.at[p, k], {"dp": to})

    def z_copy(self, p, k):
        to = lax.rem(self.t + k, self.n_t)
        send, recv = self.z_sems
        return remote(self.part.at[p, k - 1], self.z_in.at[p, k - 1], send.at[p, k], recv.at[p, k], {"tensor": to})

    def to_core(self, p):
        for k in list(range(1, self.n_chip)) + [0]:
            self.core_copy(p, k).start()

    def to_chips(self, p):
        for k in range(1, self.n_chip):
            self.core_copy(p, k).wait_recv()
            to = lax.rem(self.chip + k, self.n_chip) * 2 + self.core
            self.half[p, k - 1] = (self.grads[p, to].astype(F32) + self.core_in[p, k].astype(F32)).astype(BF16)
            self.chip_copy(p, k).start()

    def to_line(self, p):
        self.core_copy(p, 0).wait_recv()
        for c in range(1, self.n_chip):
            self.chip_copy(p, c).wait_recv()
        for k in list(range(1, self.n_t)) + [0]:
            row = lax.rem(self.t + k, self.n_t)
            total = self.grads[p, self.dp, row].astype(F32) + self.core_in[p, 0, row].astype(F32)
            for c in range(1, self.n_chip):
                total = total + self.chip_in[p, c - 1, row].astype(F32)
            if k > 0:
                self.part[p, k - 1] = total.astype(BF16)
                self.z_copy(p, k).start()
            else:
                self.out(p)[...] = total

    def finish(self, p):
        for k in range(1, self.n_t):
            self.z_copy(p, k).wait()
            self.out(p)[...] += self.z_in[p, k - 1].astype(F32)
        for k in range(self.n_chip):
            self.core_copy(p, k).wait_send()
        for k in range(1, self.n_chip):
            self.chip_copy(p, k).wait_send()


class Spread:
    def __init__(self, n_t, parts, send, recv):
        self.n_t, self.t, self.parts, self.send, self.recv = n_t, lax.axis_index("tensor"), parts, send, recv

    @staticmethod
    def scratch(n_t):
        return [DMA((2, n_t)), DMA((n_t,))]

    def hop(self, j, way):
        here = self.parts.at[j]
        return remote(here, here, self.send.at[way, j], self.recv.at[j], {"tensor": self.t + 1 - 2 * way})

    def step(self, s):
        for way, j, in_line, onward in (
            (0, self.t - s, self.t - s >= 0, self.t + 1 < self.n_t),
            (1, self.t + s, self.t + s < self.n_t, self.t > 0),
        ):
            if s > 0:

                @pl.when(in_line)
                def _():
                    self.hop(j, way).wait_recv()

            @pl.when(in_line & onward)
            def _():
                self.hop(j, way).start()

    def drain(self):
        for s in range(self.n_t):

            @pl.when((self.t - s >= 0) & (self.t + 1 < self.n_t))
            def _():
                self.hop(self.t - s, 0).wait_send()

            @pl.when((self.t + s < self.n_t) & (self.t > 0))
            def _():
                self.hop(self.t + s, 1).wait_send()


class Collect:
    def __init__(self, n_t, parts, came, send, recv):
        self.n_t, self.t, self.parts, self.came, self.send, self.recv = (
            n_t,
            lax.axis_index("tensor"),
            parts,
            came,
            send,
            recv,
        )

    @staticmethod
    def scratch(n_t):
        return [DMA((n_t,)), DMA((n_t + 1,))]

    def hop(self, j, way):
        slot = j if way == 0 else jnp.where(j == self.t - 1, self.n_t, j)
        to = self.t + 1 - 2 * way
        return remote(self.parts.at[j], self.came.at[slot], self.send.at[j], self.recv.at[slot], {"tensor": to})

    def wait_slot(self, slot):
        remote(self.parts.at[0], self.came.at[slot], self.send.at[0], self.recv.at[slot], {"tensor": self.t}).wait_recv()

    def begin(self, j):
        @pl.when((self.t == 0) & (j > 0))
        def _():
            self.hop(j, 0).start()

        @pl.when((self.t == self.n_t - 1) & (j < self.n_t - 1))
        def _():
            self.hop(j, 1).start()

    def step(self, e, far):
        if far:
            right, left = self.n_t - 1 - e + self.t, e - self.n_t + 1 + self.t
        else:
            right, left = e - self.t + 2, 2 * self.n_t - 4 - e - self.t
        for way, j, mine in (
            (0, right, (self.t >= 1) & (right <= self.n_t - 1) & (right > self.t)),
            (1, left, (self.t <= self.n_t - 2) & (left >= 0) & (left < self.t)),
        ):

            @pl.when(mine)
            def _():
                self.wait_slot(j)
                self.parts[j] = (self.parts[j].astype(F32) + self.came[j].astype(F32)).astype(BF16)
                self.hop(j, way).start()

    def finish(self, result):
        result[...] = self.parts[self.t].astype(F32)

        @pl.when(self.t > 0)
        def _():
            self.wait_slot(self.t)
            result[...] += self.came[self.t].astype(F32)

        @pl.when(self.t < self.n_t - 1)
        def _():
            self.wait_slot(self.n_t)
            result[...] += self.came[self.n_t].astype(F32)

        for j in range(self.n_t):

            @pl.when(self.t < j)
            def _():
                self.hop(j, 0).wait_send()

            @pl.when(self.t > j)
            def _():
                self.hop(j, 1).wait_send()


def centre(values):
    centred = values - jnp.mean(values, axis=1, keepdims=True)
    inverse = lax.rsqrt(jnp.mean(centred * centred, axis=1, keepdims=True) + 1e-06)
    return centred * inverse, inverse


def norm_back(grad, unit, inverse, gain):
    scaled = grad * gain
    back = inverse * (
        scaled
        - jnp.mean(scaled, axis=1, keepdims=True)
        - unit * jnp.mean(scaled * unit, axis=1, keepdims=True)
    )
    return back, jnp.sum(grad * unit, axis=0, keepdims=True), jnp.sum(grad, axis=0, keepdims=True)


def norm_picks(experts):
    row, lane = (lax.broadcasted_iota(jnp.int32, (8, LANES), axis) for axis in (0, 1))
    return (row + experts == lane).astype(F32).astype(BF16)


def norm_rows(small, experts):
    return nt(norm_picks(experts), small)


def small_grads(experts, grad_router, rows):
    line = lax.broadcasted_iota(jnp.int32, (8, rows[0].shape[1]), 0)
    stack = sum(jnp.where(line == at, row, 0.0) for at, row in enumerate(rows))
    return grad_router + tn(stack.astype(BF16), norm_picks(experts))


def image_bias(rows, padded):
    line = lax.broadcasted_iota(jnp.int32, (padded, padded), 0)
    column = lax.broadcasted_iota(jnp.int32, (padded, padded), 1)
    image_line, image_column = jnp.zeros_like(line), jnp.zeros_like(column)
    for at in range(SEQ, rows + 1, SEQ):
        image_line += (line >= at).astype(jnp.int32)
        image_column += (column >= at).astype(jnp.int32)
    return jnp.where((image_line == image_column) & (column < rows), 0.0, -1e30)


def half_masks():
    lane = lax.broadcasted_iota(jnp.int32, (1, LANES), 1)
    low = (lane < HEAD_DIM).astype(F32)
    return low.astype(BF16), (1.0 - low).astype(BF16)


def soft_scores(query, key, bias):
    scores = nt(query, key) * HEAD_DIM ** (-0.5) + bias
    power = jnp.exp(scores - jnp.max(scores, axis=1, keepdims=True))
    return power * (1.0 / jnp.sum(power, axis=1, keepdims=True))


def router_probs(logits, experts):
    lane = lax.broadcasted_iota(jnp.int32, logits.shape, 1)
    inside = lane < experts
    kept = jnp.where(inside, logits, -1e30)
    power = jnp.where(inside, jnp.exp(kept - jnp.max(kept, axis=1, keepdims=True)), 0.0)
    return power * (1.0 / jnp.sum(power, axis=1, keepdims=True))


def pick_gate(probs, choice):
    lane = lax.broadcasted_iota(jnp.int32, probs.shape, 1)
    return jnp.sum(jnp.where(lane == choice, probs, 0.0), axis=1, keepdims=True)


class Weights:
    def __init__(self, shard, width, gathered=None, whole=None):
        self.shard, self.width, self.gathered, self.whole = shard, width, gathered, whole

    def __call__(self, at):
        if self.whole is not None:
            return self.whole[at]
        part = self.gathered[:, :, at * self.shard : (at + 1) * self.shard, :]
        return part.reshape(self.width, self.width)

    def small(self):
        if self.whole is not None:
            return self.whole[SMALL, :, :LANES]
        part = self.gathered[:, :, SMALL * self.shard : (SMALL + 1) * self.shard, :LANES]
        return part.reshape(self.width, LANES)


def gelu_parts(hidden):
    bell = jnp.exp(-0.5 * hidden * hidden)
    near = 1.0 / (1.0 + 0.23164189 * jnp.abs(hidden))
    tail = near * (
        0.127414796 + near * (-0.142248368 + near * (0.7107068705 + near * (-0.7265760135 + near * 0.5307027145)))
    )
    tail = tail * bell
    share = jnp.where(hidden < 0.0, tail, 1.0 - tail)
    return hidden * share, share + hidden * bell * 0.3989422804014327


def forward_kernel(cfg, *refs):
    n_dp, n_t, rows, padded, width, experts, rooms, shard, inside = cfg
    refs = list(refs)

    def take(count):
        got = refs[:count]
        del refs[:count]
        return got

    x_ref, cot_ref, cols_ref, slots_ref, block_ref = take(5)
    gathered, recv_d, recv_s, res_ref, moe_ref, q_ref, k_ref, v_ref, mix_ref, norm_ref, probs_ref = take(11)
    full, cot_full, bias, send_d, send_s, d_send, d_recv, s_send, s_recv = take(9)
    dp = lax.axis_index("dp")
    meet(n_dp, n_t, inside)
    if inside:
        gather = Gather(n_dp, n_t, 0, block_ref.shape[0], block_ref, gathered, *refs)
        gather.start()
        weights = Weights(shard, width, gathered=gathered)
    else:
        gathered[...] = jnp.zeros_like(gathered)
        weights = Weights(shard, width, whole=block_ref)

    full[rows - rows % 8 :, :] = jnp.zeros((padded - rows + rows % 8, width), F32)
    full[:rows, :] = x_ref[...].astype(F32)
    cot_full[rows - rows % 8 :, :] = jnp.zeros((padded - rows + rows % 8, width), F32)
    cot_full[:rows, :] = cot_ref[...].astype(F32)
    bias[...] = image_bias(rows, padded)
    unit, _ = centre(full[...])
    norm_ref[...] = unit.astype(BF16)
    if inside:
        gather.pass_to_chips()
        gather.pass_to_core()
        gather.arrive()
        gather.drain()

    norms = norm_rows(weights.small(), experts)
    unit, _ = centre(full[...])
    normed = (unit * norms[0:1] + norms[1:2]).astype(BF16)
    norm_ref[...] = normed
    q_ref[...] = nn(normed, weights(0)).astype(BF16)
    k_ref[...] = nn(normed, weights(1)).astype(BF16)
    v_ref[...] = nn(normed, weights(2)).astype(BF16)
    low, high = half_masks()

    def heads(j, carry):
        at = pl.ds(pl.multiple_of(j * LANES, LANES), LANES)
        query, key, value = q_ref[:, at], k_ref[:, at], v_ref[:, at]
        first = nn(soft_scores(query * low, key, bias[...]).astype(BF16), value)
        second = nn(soft_scores(query * high, key, bias[...]).astype(BF16), value)
        mix_ref[:, at] = (first * low.astype(F32) + second * high.astype(F32)).astype(BF16)
        return carry

    lax.fori_loop(0, width // LANES, heads, 0)
    residual = full[...] + nn(mix_ref[...], weights(OUT))
    res_ref[...] = residual
    unit, _ = centre(residual)
    moe = (unit * norms[2:3] + norms[3:4]).astype(BF16)
    moe_ref[...] = moe
    probs = router_probs(nn(moe, weights.small()), experts)
    probs_ref[...] = probs
    cot = cot_full[...]
    full[...] = pick_gate(probs, cols_ref[:, 0:1]) * cot
    cot_full[...] = pick_gate(probs, cols_ref[:, 1:2]) * cot

    def selectors(p):
        slot = lax.broadcasted_iota(jnp.int32, (rooms, padded), 0) + p * rooms
        first = (slot == slots_ref[0:1, :]).astype(F32)
        second = (slot == slots_ref[1:2, :]).astype(F32)
        return first, second

    def d_copy(k):
        to = lax.rem(dp + k, n_dp)
        return remote(send_d.at[to], recv_d.at[dp], d_send.at[k], d_recv.at[k], {"dp": to})

    def s_copy(k):
        to = lax.rem(dp + k, n_dp)
        return remote(send_s.at[to], recv_s.at[dp], s_send.at[k], s_recv.at[k], {"dp": to})

    def dispatch(k, carry):
        to = lax.rem(dp + k, n_dp)
        first, second = selectors(to)
        send_d[to] = nn((first + second).astype(BF16), moe_ref[...]).astype(BF16)

        @pl.when(k > 0)
        def _():
            d_copy(k).start()

        return carry

    def dispatch_grad(k, carry):
        to = lax.rem(dp + k, n_dp)
        first, second = selectors(to)
        rows_grad = nn(first.astype(BF16), full[...].astype(BF16)) + nn(second.astype(BF16), cot_full[...].astype(BF16))
        send_s[to] = rows_grad.astype(BF16)

        @pl.when(k > 0)
        def _():
            s_copy(k).start()

        return carry

    lax.fori_loop(0, n_dp, dispatch, 0)
    lax.fori_loop(0, n_dp, dispatch_grad, 0)
    recv_d[dp] = send_d[dp]
    recv_s[dp] = send_s[dp]
    for k in range(1, n_dp):
        d_copy(k).wait()
    for k in range(1, n_dp):
        s_copy(k).wait()


def forward(cfg, cid, x, cot, cols, slots, block):
    n_dp, n_t, rows, padded, width, experts, rooms, shard, inside = cfg
    rows_block = ceil_to(5 * shard, 16)
    low = jax.ShapeDtypeStruct((padded, width), BF16)
    sent = jax.ShapeDtypeStruct((n_dp, rooms, width), BF16)
    gathered = (n_dp, n_t, rows_block, width) if inside else (1, 1, 16, LANES)
    outs = [jax.ShapeDtypeStruct(gathered, BF16), sent, sent, jax.ShapeDtypeStruct((padded, width), F32)]
    outs += [low] * 6 + [jax.ShapeDtypeStruct((padded, LANES), F32)]
    scratch = [
        VMEM((padded, width), F32),
        VMEM((padded, width), F32),
        VMEM((padded, padded), F32),
        VMEM((n_dp, rooms, width), BF16),
        VMEM((n_dp, rooms, width), BF16),
    ] + [DMA((n_dp,))] * 4
    if inside:
        scratch += Gather.scratch(n_dp, n_t)
    whole = pl.BlockSpec(memory_space=VMEM)
    return pl.pallas_call(
        partial(forward_kernel, cfg),
        out_shape=outs,
        in_specs=[whole] * 5,
        out_specs=[whole] * len(outs),
        scratch_shapes=scratch,
        compiler_params=pltpu.CompilerParams(
            collective_id=cid, has_side_effects=True, vmem_limit_bytes=56 * 2**20
        ),
        name="forward_" + str(rooms),
    )(x, cot, cols, slots, block)


def expert_kernel(chunks, d_ref, s_ref, w_in_ref, w_out_ref, ret_ref, back_ref, g_in_ref, g_out_ref, ret, back, g_in, g_out):
    step = pl.program_id(0)
    rows = d_ref.shape[0]
    chunk = rows // chunks

    @pl.when(step == 0)
    def _():
        ret[...] = jnp.zeros_like(ret)
        back[...] = jnp.zeros_like(back)

    g_in[...] = jnp.zeros_like(g_in)
    g_out[...] = jnp.zeros_like(g_out)
    w_in, w_out = w_in_ref[...], w_out_ref[...]

    def part(c, carry):
        at = pl.ds(pl.multiple_of(c * chunk, 16), chunk)
        took, slot_grad = d_ref[at, :], s_ref[at, :]
        active, slope = gelu_parts(nt(took, w_in))
        active = active.astype(BF16)
        grad_hidden = (nt(slot_grad, w_out) * slope).astype(BF16)
        ret[at, :] += nn(active, w_out)
        back[at, :] += nn(grad_hidden, w_in)
        g_out[...] += tn(active, slot_grad)
        g_in[...] += tn(grad_hidden, took)
        return carry

    lax.fori_loop(0, chunks, part, 0)
    g_in_ref[...] = g_in[...].astype(BF16)
    g_out_ref[...] = g_out[...].astype(BF16)

    @pl.when(step == pl.num_programs(0) - 1)
    def _():
        ret_ref[...] = ret[...].astype(BF16)
        back_ref[...] = back[...].astype(BF16)


def run_expert(took, slot_grad, w_in, w_out):
    rows, width = took.shape
    hidden = w_in.shape[0]
    block = 256
    chunks = next(c for c in range(max(1, rows // 400), rows + 1) if rows % c == 0 and (rows // c) % 16 == 0)
    whole = pl.BlockSpec((rows, width), lambda i: (0, 0))
    part = pl.BlockSpec((block, width), lambda i: (i, 0))
    low = jax.ShapeDtypeStruct((rows, width), BF16)
    grad = jax.ShapeDtypeStruct((hidden, width), BF16)
    return pl.pallas_call(
        partial(expert_kernel, chunks),
        grid=(hidden // block,),
        out_shape=[low, low, grad, grad],
        in_specs=[whole, whole, part, part],
        out_specs=[whole, whole, part, part],
        scratch_shapes=[
            VMEM((rows, width), F32),
            VMEM((rows, width), F32),
            VMEM((block, width), F32),
            VMEM((block, width), F32),
        ],
        compiler_params=pltpu.CompilerParams(vmem_limit_bytes=60 * 2**20),
        cost_estimate=pl.CostEstimate(
            flops=12 * rows * width * hidden, bytes_accessed=12 * rows * width + 8 * hidden * width, transcendentals=0
        ),
        name="expert_" + str(rows),
    )(took, slot_grad, w_in, w_out)


def backward_kernel(cfg, *refs):
    n_dp, n_t, rows, padded, width, experts, rooms, shard, inside = cfg
    refs = list(refs)

    def take(count):
        got = refs[:count]
        del refs[:count]
        return got

    ret_ref, back_ref, x_ref, cot_ref, cols_ref, weights_ref = take(6)
    res_ref, moe_ref, q_ref, k_ref, v_ref, mix_ref, norm_ref, probs_ref = take(8)
    out_ref, gx_ref, sum_ref = take(3)
    full, cot_full, bias, ret_in, back_in, grads, r_send, r_recv, b_send, b_recv = take(10)
    dq, dk, dv = take(3)
    dp = lax.axis_index("dp")
    meet(n_dp, n_t, inside)

    def r_copy(k):
        to = lax.rem(dp + k, n_dp)
        return remote(ret_ref.at[to], ret_in.at[dp], r_send.at[k], r_recv.at[k], {"dp": to})

    def b_copy(k):
        to = lax.rem(dp + k, n_dp)
        return remote(back_ref.at[to], back_in.at[dp], b_send.at[k], b_recv.at[k], {"dp": to})

    for k in range(1, n_dp):
        r_copy(k).start()
    for k in range(1, n_dp):
        b_copy(k).start()
    ret_in[dp] = ret_ref[dp]
    back_in[dp] = back_ref[dp]
    weights = Weights(shard, width, gathered=weights_ref) if inside else Weights(shard, width, whole=weights_ref)
    tail = rows - rows % 8
    full[tail:, :] = jnp.zeros((padded - tail, width), F32)
    full[:rows, :] = x_ref[...].astype(F32)
    cot_full[tail:, :] = jnp.zeros((padded - tail, width), F32)
    cot_full[:rows, :] = cot_ref[...].astype(F32)
    bias[...] = image_bias(rows, padded)
    norms = norm_rows(weights.small(), experts)
    slot_count = n_dp * rooms
    lane = lax.broadcasted_iota(jnp.int32, (padded, slot_count), 1)
    first = (lane == cols_ref[:, 2:3]).astype(F32)
    second = (lane == cols_ref[:, 3:4]).astype(F32)
    both = (first + second).astype(BF16)

    for k in range(1, n_dp):
        r_copy(k).wait()
    returned = ret_in[...].reshape(slot_count, width)
    first_rows = nn(first.astype(BF16), returned)
    second_rows = nn(second.astype(BF16), returned)
    probs = probs_ref[...]
    first_id, second_id = cols_ref[:, 0:1], cols_ref[:, 1:2]
    outcome = res_ref[...] + pick_gate(probs, first_id) * first_rows + pick_gate(probs, second_id) * second_rows
    out_ref[...] = outcome[:rows].astype(BF16)
    cot = cot_full[...]
    first_grad = jnp.sum(first_rows * cot, axis=1, keepdims=True)
    second_grad = jnp.sum(second_rows * cot, axis=1, keepdims=True)
    spot = lax.broadcasted_iota(jnp.int32, probs.shape, 1)
    grad_probs = jnp.where(spot == first_id, first_grad, 0.0) + jnp.where(spot == second_id, second_grad, 0.0)
    grad_logits = (probs * (grad_probs - jnp.sum(probs * grad_probs, axis=1, keepdims=True))).astype(BF16)
    grad_router = tn(moe_ref[...], grad_logits)

    for k in range(1, n_dp):
        b_copy(k).wait()
    grad_moe = nn(both, back_in[...].reshape(slot_count, width)) + nt(grad_logits, weights.small())
    unit, inverse = centre(res_ref[...])
    extra, gain_two, shift_two = norm_back(grad_moe, unit, inverse, norms[2:3])
    grad_residual = cot + extra
    cot_full[...] = grad_residual
    grad_attended = grad_residual.astype(BF16)
    n_all = n_dp * n_t

    def keep(at, value):
        if inside:
            grads[:, :, at * shard : (at + 1) * shard, :] = value.astype(BF16).reshape(n_dp, n_t, shard, width)
        else:
            sum_ref[at] = value

    keep(OUT, tn(mix_ref[...], grad_attended))
    mix_ref_grad = nt(grad_attended, weights(OUT)).astype(BF16)
    dq[...] = mix_ref_grad
    low, high = half_masks()
    low_f, high_f = low.astype(F32), high.astype(F32)
    scale = HEAD_DIM ** (-0.5)

    def heads(j, carry):
        at = pl.ds(pl.multiple_of(j * LANES, LANES), LANES)
        query, key, value, grad = q_ref[:, at], k_ref[:, at], v_ref[:, at], dq[:, at]
        for mask, mask_f in ((low, low_f), (high, high_f)):
            probs = soft_scores(query * mask, key, bias[...])
            grad_probs = nt(grad * mask, value)
            grad_scores = probs * (grad_probs - jnp.sum(probs * grad_probs, axis=1, keepdims=True))
            grad_scores = grad_scores.astype(BF16)
            part_v = tn(probs.astype(BF16), grad)
            part_q = nn(grad_scores, key) * scale
            part_k = tn(grad_scores, query) * scale
            if mask is low:
                sum_q, sum_k, sum_v = part_q * mask_f, part_k * mask_f, part_v * mask_f
            else:
                sum_q, sum_k, sum_v = sum_q + part_q * mask_f, sum_k + part_k * mask_f, sum_v + part_v * mask_f
        dq[:, at] = sum_q.astype(BF16)
        dk[:, at] = sum_k.astype(BF16)
        dv[:, at] = sum_v.astype(BF16)
        return carry

    lax.fori_loop(0, width // LANES, heads, 0)
    keep(0, tn(norm_ref[...], dq[...]))
    keep(1, tn(norm_ref[...], dk[...]))
    keep(2, tn(norm_ref[...], dv[...]))
    grad_normed = nt(dq[...], weights(0)) + nt(dk[...], weights(1)) + nt(dv[...], weights(2))
    unit, inverse = centre(full[...])
    extra, gain_one, shift_one = norm_back(grad_normed, unit, inverse, norms[0:1])
    gx_ref[...] = (cot_full[...] + extra)[:rows].astype(BF16)
    small = small_grads(experts, grad_router, (gain_one, shift_one, gain_two, shift_two))
    if inside:
        at = slice(SMALL * shard, (SMALL + 1) * shard)
        grads[:, :, at, :LANES] = small.astype(BF16).reshape(n_dp, n_t, shard, LANES)
        grads[:, :, at, LANES:] = jnp.zeros((n_dp, n_t, shard, width - LANES), BF16)
        Scatter(n_dp, n_t, grads, sum_ref, *refs).run()
    else:
        sum_ref[SMALL] = jnp.zeros((width, width), F32)
        sum_ref[SMALL, :, :LANES] = small


def backward(cfg, cid, *args):
    n_dp, n_t, rows, padded, width, experts, rooms, shard, inside = cfg
    rows_block = ceil_to(5 * shard, 16)
    total = (rows_block, width) if inside else (5, width, width)
    outs = [jax.ShapeDtypeStruct((rows, width), BF16)] * 2 + [jax.ShapeDtypeStruct(total, F32)]
    scratch = [
        VMEM((padded, width), F32),
        VMEM((padded, width), F32),
        VMEM((padded, padded), F32),
        VMEM((n_dp, rooms, width), BF16),
        VMEM((n_dp, rooms, width), BF16),
        VMEM((n_dp, n_t, rows_block, width) if inside else (1, 1, 16, LANES), BF16),
    ]
    scratch += [DMA((n_dp,))] * 4 + [VMEM((padded, width), BF16)] * 3
    if inside:
        scratch += Scatter.scratch(n_dp, n_t, (rows_block, width))
    whole = pl.BlockSpec(memory_space=VMEM)
    return pl.pallas_call(
        partial(backward_kernel, cfg),
        out_shape=outs,
        in_specs=[whole] * len(args),
        out_specs=[whole] * len(outs),
        scratch_shapes=scratch,
        compiler_params=pltpu.CompilerParams(
            collective_id=cid, has_side_effects=True, vmem_limit_bytes=56 * 2**20
        ),
        name="backward_" + str(rooms),
    )(*args)


def pack_block(refs, block, shard, width, experts):
    q_ref, k_ref, v_ref, o_ref, router_ref, *line_refs = refs
    for at, ref in ((0, q_ref), (1, k_ref), (2, v_ref), (OUT, o_ref)):
        block[at * shard : (at + 1) * shard, :] = ref[...].astype(BF16)
    here = slice(SMALL * shard, (SMALL + 1) * shard)
    block[here, :] = jnp.zeros((shard, width), BF16)
    row, column = (lax.broadcasted_iota(jnp.int32, (shard, shard), axis) for axis in (0, 1))
    lane = lax.broadcasted_iota(jnp.int32, (shard, LANES), 1)
    small = jnp.zeros((shard, LANES), F32)
    for at in range(experts + len(line_refs)):
        level = router_ref[at : at + 1, :] if at < experts else line_refs[at - experts][...]
        upright = jnp.sum(jnp.where(row == column, level, 0.0), axis=1, keepdims=True)
        small = jnp.where(lane == at, upright, small)
    block[here, :LANES] = small.astype(BF16)


def find_places(cfg, routes_ref, place, turned, over):
    n_dp, n_t, rows, padded, width, experts, rooms, shard, inside, hid = cfg
    t = lax.axis_index("tensor")
    tok_count = routes_ref.shape[1]
    capacity = (5 * tok_count + 2 * experts - 1) // (2 * experts)
    line = lax.broadcasted_iota(jnp.int32, (experts, tok_count), 0)
    lane = lax.broadcasted_iota(jnp.int32, (experts, tok_count), 1)

    def count(row, until):
        hot = (line == routes_ref[row : row + 1, :]) & (lane < until)
        return jnp.sum(hot.astype(F32), axis=1, keepdims=True)

    total = count(0, tok_count)
    before = (count(0, t * rows), count(1, t * rows))
    long = ceil_to(tok_count, LANES)
    wide = turned.shape[1]
    turned[...] = jnp.full(turned.shape, -1.0, F32)
    everyone = jnp.concatenate(
        [routes_ref[...], jnp.full((2, long - tok_count), experts, jnp.int32)], axis=1
    )
    everyone = jnp.concatenate([everyone, everyone, everyone, everyone], axis=0)
    mine = pltpu.roll(everyone, lax.rem(long - t * rows, long), 1)[:, :wide]
    spot = lax.broadcasted_iota(jnp.int32, (8, wide), 1)
    mine = jnp.where(spot < rows, mine, experts)
    line = lax.broadcasted_iota(jnp.int32, (experts, wide), 0)
    first, second = line == mine[0:1], line == mine[1:2]
    down, across = (lax.broadcasted_iota(jnp.int32, (wide, wide), axis) for axis in (0, 1))
    earlier = (down < across).astype(F32).astype(BF16)
    own = jnp.sum(first.astype(F32), axis=1, keepdims=True)
    first_rank = nn(first.astype(F32).astype(BF16), earlier)
    second_rank = nn(second.astype(F32).astype(BF16), earlier)

    def slot(choice, hot, rank, place):
        kept = hot & (place < capacity)
        here = jnp.sum(jnp.where(kept, rank + 1.0, 0.0), axis=0, keepdims=True) - 1.0
        good = (here >= 0.0) & (here < rooms)
        return jnp.where(good, choice.astype(F32) * rooms + here, -1.0), jnp.max(here, axis=1, keepdims=True)

    first_slot, first_most = slot(mine[0:1], first, first_rank, first_rank + before[0])
    second_slot, second_most = slot(mine[1:2], second, second_rank + own, second_rank + total + before[1])
    turned[0:1, :] = first_slot
    turned[1:2, :] = second_slot
    turned[2:3, :] = mine[0:1].astype(F32)
    turned[3:4, :] = mine[1:2].astype(F32)
    place[...] = turned[...].T
    most = jnp.maximum(first_most, second_most)
    over[...] = jnp.broadcast_to(jnp.where(most >= rooms, 1.0, 0.0), over.shape)


def step_kernel(cfg, *refs):
    n_dp, n_t, rows, padded, width, experts, rooms, shard, inside, hid = cfg
    refs = list(refs)

    def take(count):
        got = refs[:count]
        del refs[:count]
        return got

    x_ref, cot_ref, routes_ref, e_in_ref, e_out_ref = take(5)
    shared = take(9 if inside else 1)
    out_ref, gx_ref, sum_ref, g_in_ref, g_out_ref = take(5)
    block, gathered, full, cot_full, bias, res, probs_s = take(7)
    place, turned, over, gate_m, gate_c, gate_s, gate_r, rise_s, rise_r = take(9)
    moe, q_s, k_s, v_s, mix, norm, dk, dv = take(8)
    send_d, send_s, recv_d, recv_s, ret_in, back_in, act, slope = take(8)
    wi, wo, gi, go, gi_in, go_in = take(6)
    d_send, d_recv, s_send, s_recv, r_send, r_recv, b_send, b_recv = take(8)
    f_send, f_recv, e_send, e_recv, own_sems = take(5)
    wi_spread, wo_spread = Spread(n_t, wi, *take(2)), Spread(n_t, wo, *take(2))
    gi_collect, go_collect = Collect(n_t, gi, gi_in, *take(2)), Collect(n_t, go, go_in, *take(2))
    dp, t = lax.axis_index("dp"), lax.axis_index("tensor")
    scale = HEAD_DIM ** (-0.5)
    slot_count = n_dp * rooms
    half, wide = min(256, hid), min(256, width)
    long = gate_m.shape[1]
    early = 2 if hid == width and n_t > 2 else 0
    table = [sorted(range(n_t), key=lambda j: (abs(j - at), j)) for at in range(n_t)]

    def order(p):
        found = jnp.int32(0)
        for at in range(n_t):
            for spot in range(n_t):
                found = found + jnp.where((t == at) & (p == spot), table[at][spot], 0)
        return found

    def dp_copy(src, dst, sems, k):
        to = lax.rem(dp + k, n_dp)
        return remote(src.at[to], dst.at[dp], sems[0].at[k], sems[1].at[k], {"dp": to})

    d_copy = partial(dp_copy, send_d, recv_d, (d_send, d_recv))
    s_copy = partial(dp_copy, send_s, recv_s, (s_send, s_recv))
    r_copy = partial(dp_copy, send_d, ret_in, (r_send, r_recv))
    b_copy = partial(dp_copy, send_s, back_in, (b_send, b_recv))

    f_copy = partial(dp_copy, gate_s, gate_r, (f_send, f_recv))
    e_copy = partial(dp_copy, rise_s, rise_r, (e_send, e_recv))

    def column(at):
        return place[:padded, at : at + 1].astype(jnp.int32)

    meet(n_dp, n_t, True)
    load_in = pltpu.make_async_copy(e_in_ref, g_in_ref, own_sems.at[0])
    load_out = pltpu.make_async_copy(e_out_ref, g_out_ref, own_sems.at[1])
    load_in.start()
    load_out.start()
    if inside:
        pack_block(shared, block, shard, width, experts)
        size = len(Gather.scratch(n_dp, n_t))
        gather_a = Gather(n_dp, n_t, 0, OUT * shard, block, gathered, *take(size))
        gather_b = Gather(n_dp, n_t, OUT * shard, shard, block, gathered, *take(size))
        gather_a.start()
        gather_b.start()
        weights = Weights(shard, width, gathered=gathered)
    else:
        weights = Weights(shard, width, whole=shared[0])
    load_in.wait()
    wi[t] = g_in_ref[...].astype(BF16)
    wi_spread.step(0)
    load_out.wait()
    wo[t] = g_out_ref[...].astype(BF16)
    tail = rows - rows % 8
    full[tail:, :] = jnp.zeros((padded - tail, width), F32)
    full[:rows, :] = x_ref[...].astype(F32)
    cot_full[tail:, :] = jnp.zeros((padded - tail, width), F32)
    cot_full[:rows, :] = cot_ref[...].astype(F32)
    bias[...] = image_bias(rows, padded)
    find_places(cfg, routes_ref, place, turned, over)
    if inside:
        gather_a.pass_to_chips()
        gather_b.pass_to_chips()
        gather_a.pass_to_core()
        gather_a.arrive()
    norms = norm_rows(weights.small(), experts)
    unit, _ = centre(full[...])
    norm[...] = (unit * norms[0:1] + norms[1:2]).astype(BF16)
    q_s[...] = nn(norm[...], weights(0)).astype(BF16)
    k_s[...] = nn(norm[...], weights(1)).astype(BF16)
    v_s[...] = nn(norm[...], weights(2)).astype(BF16)
    if inside:
        gather_b.pass_to_core()
    wi_spread.step(1)
    low, high = half_masks()
    low_f, high_f = low.astype(F32), high.astype(F32)

    def heads(j, carry):
        at = pl.ds(pl.multiple_of(j * LANES, LANES), LANES)
        query, key, value = q_s[:, at], k_s[:, at], v_s[:, at]
        first = nn(soft_scores(query * low, key, bias[...]).astype(BF16), value)
        second = nn(soft_scores(query * high, key, bias[...]).astype(BF16), value)
        mix[:, at] = (first * low_f + second * high_f).astype(BF16)
        return carry

    lax.fori_loop(0, width // LANES, heads, 0)
    if inside:
        gather_b.arrive()
    residual = full[...] + nn(mix[...], weights(OUT))
    res[...] = residual
    unit, _ = centre(residual)
    moe[...] = (unit * norms[2:3] + norms[3:4]).astype(BF16)
    probs_s[...] = router_probs(nn(moe[...], weights.small()), experts)

    spot = lax.broadcasted_iota(jnp.int32, (padded, LANES), 1)
    first_gate, second_gate = pick_gate(probs_s[...], column(2)), pick_gate(probs_s[...], column(3))
    place[:padded, :] = jnp.where(spot == 4, first_gate, jnp.where(spot == 5, second_gate, place[:padded, :]))
    turned[...] = place[...].T
    gate_line = lax.broadcasted_iota(jnp.int32, (8, padded), 0)

    def terms(gate):
        one = gate.astype(BF16).astype(F32)
        two = (gate - one).astype(BF16).astype(F32)
        three = gate - one - two
        stack = jnp.where(gate_line == 0, one, jnp.where(gate_line == 1, two, jnp.where(gate_line == 2, three, 0.0)))
        return stack.astype(BF16)

    first_terms, second_terms = terms(turned[4:5, :padded]), terms(turned[5:6, :padded])
    dk[...] = cot_full[...].astype(BF16)

    def selectors(p):
        slot = lax.broadcasted_iota(jnp.int32, (rooms, padded), 0) + p * rooms
        first = (slot == turned[0:1, :padded].astype(jnp.int32)).astype(F32)
        second = (slot == turned[1:2, :padded].astype(jnp.int32)).astype(F32)
        return first, second

    def dispatch(k, carry):
        to = lax.rem(dp + k, n_dp)
        first, second = selectors(to)
        got = nn((first + second).astype(BF16), moe[...]).astype(BF16)

        @pl.when(k > 0)
        def _():
            send_d[to] = got
            d_copy(k).start()

        @pl.when(k == 0)
        def _():
            recv_d[to] = got

        return carry

    lax.fori_loop(0, n_dp, dispatch, 0)

    def dispatch_grad(k, carry):
        to = lax.rem(dp + k, n_dp)
        first, second = selectors(to)
        got = nn((first + second).astype(BF16), dk[...]).astype(BF16)

        @pl.when(k > 0)
        def _():
            send_s[to] = got

        @pl.when(k == 0)
        def _():
            recv_s[to] = got

        return carry

    lax.fori_loop(0, n_dp, dispatch_grad, 0)
    if n_t > 2:
        wi_spread.step(2)

    def dispatch_gates(k, carry):
        to = lax.rem(dp + k, n_dp)
        first, second = selectors(to)
        gate = nt(first_terms, first.astype(BF16)) + nt(second_terms, second.astype(BF16))
        gate = jnp.sum(gate, axis=0, keepdims=True)

        @pl.when(k > 0)
        def _():
            gate_s[to, :, :rooms] = jnp.broadcast_to(gate, (8, rooms))
            f_copy(k).start()

        @pl.when(k == 0)
        def _():
            gate_r[to, :, :rooms] = jnp.broadcast_to(gate, (8, rooms))

        return carry

    lax.fori_loop(0, n_dp, dispatch_gates, 0)

    def hidden_units(j, g):
        active, steep = gelu_parts(nn(recv_d[g], wi[j]))
        act[j, g] = active.astype(BF16)
        slope[j, g] = steep.astype(BF16)

    def own_hidden(k, carry):
        @pl.when(k > 0)
        def _():
            d_copy(k).wait_recv()

        hidden_units(t, lax.rem(dp + n_dp - k, n_dp))
        return carry

    lax.fori_loop(0, n_dp, own_hidden, 0)
    for k in range(1, n_dp):
        s_copy(k).start()
    wo_spread.step(0)

    def other_hidden(i, carry):
        @pl.when(i == min(2, n_t - 2) * n_dp)
        def _():
            for s in range(3, n_t):
                wi_spread.step(s)

        hidden_units(order(1 + i // n_dp), lax.rem(i, n_dp))
        return carry

    lax.fori_loop(0, (n_t - 1) * n_dp, other_hidden, 0)
    wo_spread.step(1)
    gate_m[...] = jnp.zeros_like(gate_m)
    for k in range(1, n_dp):
        f_copy(k).wait()
    for g in range(n_dp):
        gate_m[g : g + 1, :rooms] = gate_r[g, 0:1, :rooms]
    gate_c[...] = gate_m[...].T
    for k in range(1, n_dp):
        s_copy(k).wait()
    slot_grads = send_s
    room_lane = lax.broadcasted_iota(jnp.int32, (rooms, LANES), 1)

    def slot_grad(g, carry):
        gate = jnp.sum(jnp.where(room_lane == g, gate_c[:rooms, :], 0.0), axis=1, keepdims=True)
        slot_grads[g] = (gate * recv_s[g].astype(F32)).astype(BF16)
        return carry

    lax.fori_loop(0, n_dp, slot_grad, 0)

    def outer_grad(i, carry):
        j = order(n_t - 1 - i // (hid // half))
        at = pl.ds(pl.multiple_of(lax.rem(i, hid // half) * half, half), half)
        left = act[j, :, :, at].reshape(slot_count, half)
        go[j, at, :] = tn(left, slot_grads[...].reshape(slot_count, width)).astype(BF16)

        @pl.when(lax.rem(i, hid // half) == hid // half - 1)
        def _():
            go_collect.begin(j)

        return carry

    lax.fori_loop(0, n_t * (hid // half), outer_grad, 0)

    def hidden_grads(p):
        j = order(p)

        def one(i, inner):
            slope[j, i] = (nt(slot_grads[i], wo[j]) * slope[j, i].astype(F32)).astype(BF16)
            return inner

        lax.fori_loop(0, n_dp, one, 0)

    def inner_grads(p):
        j = order(p)

        def one(i, inner):
            at = pl.ds(pl.multiple_of(i * wide, wide), wide)
            left = recv_d[:, :, at].reshape(slot_count, wide)
            gi[j, at, :] = tn(left, slope[j].reshape(slot_count, hid)).astype(BF16)
            return inner

        lax.fori_loop(0, width // wide, one, 0)

    middle = (t > 0) & (t < n_t - 1)

    def near(p, carry):
        @pl.when((p == 1) & middle)
        def _():
            wo_spread.step(2)

        hidden_grads(p)
        inner_grads(p)
        return carry

    def split(total):
        main = total.astype(BF16)
        return main, (total - main.astype(F32)).astype(BF16)

    if early:
        lax.fori_loop(0, early, near, 0)
        near_a, near_b = order(0), order(1)

        def some_back(g, carry):
            total = nn(act[near_a, g], wo[near_a]) + nn(act[near_b, g], wo[near_b])
            act[near_a, g], act[near_b, g] = split(total)
            total = nt(slope[near_a, g], wi[near_a]) + nt(slope[near_b, g], wi[near_b])
            slope[near_a, g], slope[near_b, g] = split(total)
            return carry

        lax.fori_loop(0, n_dp, some_back, 0)
    if early:

        @pl.when(jnp.logical_not(middle))
        def _():
            wo_spread.step(2)

    elif n_t > 2:
        wo_spread.step(2)
    if n_t > 2:
        go_collect.step(1, True)

    def far(p, carry):
        @pl.when(p == n_t - 1)
        def _():
            for s in range(3, n_t):
                wo_spread.step(s)

        hidden_grads(p)

        @pl.when(p < n_t - 1)
        def _():
            inner_grads(p)

        return carry

    lax.fori_loop(early, n_t, far, 0)
    for k in range(1, n_dp):
        d_copy(k).wait_send()

    def sum_back(rows_of, weights_of, dot, g):
        if early:
            total = rows_of[near_a, g].astype(F32) + rows_of[near_b, g].astype(F32)
        else:
            total = jnp.zeros((rooms, width), F32)
        for p in range(early, n_t):
            j = order(p)
            total = total + dot(rows_of[j, g], weights_of[j])
        return total

    def give_back_grad(i, carry):
        k = lax.rem(i + 1, n_dp)
        to = lax.rem(dp + k, n_dp)
        total = sum_back(slope, wi, nt, to).astype(BF16)

        @pl.when(k > 0)
        def _():
            send_s[to] = total
            b_copy(k).start()

        @pl.when(k == 0)
        def _():
            back_in[to] = total

        return carry

    lax.fori_loop(0, n_dp, give_back_grad, 0)
    inner_grads(n_t - 1)

    def send_inner(p, carry):
        gi_collect.begin(order(n_t - 1 - p))
        return carry

    lax.fori_loop(0, n_t, send_inner, 0)
    gate_c[...] = jnp.zeros_like(gate_c)

    def give_back(i, carry):
        k = lax.rem(i + 1, n_dp)
        to = lax.rem(dp + k, n_dp)
        total = sum_back(act, wo, nn, to)
        rise = jnp.sum(total * recv_s[to].astype(F32), axis=1, keepdims=True)
        gate_c[:rooms, :] = jnp.where(room_lane == to, rise, gate_c[:rooms, :])

        @pl.when(k > 0)
        def _():
            send_d[to] = total.astype(BF16)

        @pl.when(k == 0)
        def _():
            ret_in[to] = total.astype(BF16)

        return carry

    lax.fori_loop(0, n_dp, give_back, 0)
    gate_m[...] = gate_c[...].T
    for g in range(n_dp):
        row = jnp.broadcast_to(gate_m[g : g + 1, :], (8, long))

        @pl.when(dp == g)
        def _():
            rise_r[g] = row

        @pl.when(dp != g)
        def _():
            rise_s[g] = row

    for k in range(1, n_dp):
        e_copy(k).start()
    for k in range(1, n_dp):
        r_copy(k).start()
    for e in range(2, n_t - 1):
        go_collect.step(e, True)
    for k in range(1, n_dp):
        e_copy(k).wait()
    room = lax.broadcasted_iota(jnp.int32, (padded, long), 1)

    slots_of = (column(0), column(1))

    def token_rise(e, carry):
        row = jnp.where(room[0:1] < rooms, rise_r[e, 0:1, :], 0.0)
        parts = []
        for slot, before in zip(slots_of, carry):
            hot = room == jnp.where(slot < (e + 1) * rooms, slot - e * rooms, -1)
            parts.append(before + jnp.sum(jnp.where(hot, row, 0.0), axis=1, keepdims=True))
        return tuple(parts)

    zero = jnp.zeros((padded, 1), F32)
    first_grad, second_grad = lax.fori_loop(0, n_dp, token_rise, (zero, zero))
    probs = probs_s[...]
    spot = lax.broadcasted_iota(jnp.int32, probs.shape, 1)
    grad_probs = jnp.where(spot == column(2), first_grad, 0.0) + jnp.where(spot == column(3), second_grad, 0.0)
    grad_logits = (probs * (grad_probs - jnp.sum(probs * grad_probs, axis=1, keepdims=True))).astype(BF16)
    grad_router = tn(moe[...], grad_logits)
    unit, inverse = centre(res[...])
    lane = lax.broadcasted_iota(jnp.int32, (padded, slot_count), 1)
    both = ((lane == column(0)).astype(F32) + (lane == column(1)).astype(F32)).astype(BF16)
    for k in range(1, n_dp):
        b_copy(k).wait()
    grad_moe = nn(both, back_in[...].reshape(slot_count, width)) + nt(grad_logits, weights.small())
    extra, gain_two, shift_two = norm_back(grad_moe, unit, inverse, norms[2:3])
    grad_residual = cot_full[...] + extra
    cot_full[...] = grad_residual
    grad_attended = grad_residual.astype(BF16)

    pairs = width // LANES
    if inside:
        size = len(Reduce.scratch(n_dp, n_t, 1, (shard, LANES)))
        out_sum = Reduce(n_dp, n_t, lambda p: sum_ref.at[pl.ds(OUT * shard, shard)], *take(size))
        pair_sum = Reduce(
            n_dp, n_t, lambda p: sum_ref.at[pl.ds(0, 3 * shard), pl.ds(pl.multiple_of(p * LANES, LANES), LANES)], *take(size)
        )
        small_sum = Reduce(n_dp, n_t, lambda p: sum_ref.at[pl.ds(SMALL * shard, shard), pl.ds(0, LANES)], *take(size))
        sum_ref[SMALL * shard : (SMALL + 1) * shard, LANES:] = jnp.zeros((shard, width - LANES), F32)
        out_sum.put(0, 0, tn(mix[...], grad_attended))
        out_sum.to_core(0)
    else:
        sum_ref[OUT] = tn(mix[...], grad_attended)
    dq = mix
    dq[...] = nt(grad_attended, weights(OUT)).astype(BF16)

    def heads_back(j, carry):
        at = pl.ds(pl.multiple_of(j * LANES, LANES), LANES)
        query, key, value, grad = q_s[:, at], k_s[:, at], v_s[:, at], dq[:, at]
        for mask, mask_f in ((low, low_f), (high, high_f)):
            probs = soft_scores(query * mask, key, bias[...])
            grad_probs = nt(grad * mask, value)
            grad_scores = probs * (grad_probs - jnp.sum(probs * grad_probs, axis=1, keepdims=True))
            grad_scores = grad_scores.astype(BF16)
            part_v = tn(probs.astype(BF16), grad)
            part_q = nn(grad_scores, key) * scale
            part_k = tn(grad_scores, query) * scale
            if mask is low:
                sum_q, sum_k, sum_v = part_q * mask_f, part_k * mask_f, part_v * mask_f
            else:
                sum_q, sum_k, sum_v = sum_q + part_q * mask_f, sum_k + part_k * mask_f, sum_v + part_v * mask_f
        dq[:, at] = sum_q.astype(BF16)
        dk[:, at] = sum_k.astype(BF16)
        dv[:, at] = sum_v.astype(BF16)
        if inside:
            for spot, ref in enumerate((dq, dk, dv)):
                pair_sum.put(j, spot * shard, tn(norm[...], ref[:, at]))
            pair_sum.to_core(j)

            @pl.when(j == 0)
            def _():
                out_sum.to_chips(0)

            @pl.when(j > 0)
            def _():
                pair_sum.to_chips(j - 1)

            @pl.when(j == 2)
            def _():
                out_sum.to_line(0)

            @pl.when(j > 2)
            def _():
                pair_sum.to_line(j - 3)

        return carry

    if n_t > 2:
        gi_collect.step(1, True)
    lax.fori_loop(0, pairs, heads_back, 0)
    for e in range(2, n_t - 1):
        gi_collect.step(e, True)
    if inside:
        pair_sum.to_chips(pairs - 1)
    else:
        for spot, ref in enumerate((dq, dk, dv)):
            sum_ref[spot] = tn(norm[...], ref[...])
    grad_normed = nt(dq[...], weights(0)) + nt(dk[...], weights(1)) + nt(dv[...], weights(2))
    full[tail:, :] = jnp.zeros((padded - tail, width), F32)
    full[:rows, :] = x_ref[...].astype(F32)
    unit, inverse = centre(full[...])
    extra, gain_one, shift_one = norm_back(grad_normed, unit, inverse, norms[0:1])
    gx_ref[...] = (cot_full[...] + extra)[:rows].astype(BF16)
    small = small_grads(experts, grad_router, (gain_one, shift_one, gain_two, shift_two))
    lane = lax.broadcasted_iota(jnp.int32, small.shape, 1)
    small = jnp.where(lane == experts + 4, over[0:1, :], small)
    def combine():
        for k in range(1, n_dp):
            r_copy(k).wait()
        returned = ret_in[...].reshape(slot_count, width)
        lane = lax.broadcasted_iota(jnp.int32, (padded, slot_count), 1)
        first, second = ((lane == column(at)).astype(F32).astype(BF16) for at in (0, 1))
        first_rows, second_rows = nn(first, returned), nn(second, returned)
        first_gate, second_gate = place[:padded, 4:5], place[:padded, 5:6]
        outcome = res[...] + first_gate * first_rows + second_gate * second_rows
        out_ref[...] = outcome[:rows].astype(BF16)

    if inside:
        small_sum.put(0, 0, small)
        small_sum.to_core(0)
        for p in range(max(pairs - 3, 0), pairs - 1):
            pair_sum.to_line(p)
        small_sum.to_chips(0)
        combine()
        pair_sum.to_line(pairs - 1)
        small_sum.to_line(0)
        out_sum.finish(0)

        def last(p, carry):
            pair_sum.finish(p)
            return carry

        lax.fori_loop(0, pairs, last, 0)
        small_sum.finish(0)
        gather_a.drain()
        gather_b.drain()
    else:
        sum_ref[SMALL] = jnp.zeros((width, width), F32)
        sum_ref[SMALL, :, :LANES] = small
        combine()
    go_collect.finish(g_out_ref)
    gi_collect.finish(g_in_ref)
    wi_spread.drain()
    wo_spread.drain()


def run_step(cfg, cid, x, cot, routes, e_in, e_out, shared):
    n_dp, n_t, rows, padded, width, experts, rooms, shard, inside, hid = cfg
    rows_block = ceil_to(5 * shard, 16)
    total = (rows_block, width) if inside else (5, width, width)
    outs = [
        jax.ShapeDtypeStruct((rows, width), BF16),
        jax.ShapeDtypeStruct((rows, width), BF16),
        jax.ShapeDtypeStruct(total, F32),
        jax.ShapeDtypeStruct((width, hid), F32),
        jax.ShapeDtypeStruct((hid, width), F32),
    ]
    spread = (n_dp, n_t, rows_block, width) if inside else (1, 1, 16, LANES)
    wide, long = ceil_to(padded, LANES), ceil_to(rooms, LANES)
    rows_f, rows_b = VMEM((padded, width), F32), VMEM((padded, width), BF16)
    slots_b, units_b = VMEM((n_dp, rooms, width), BF16), VMEM((n_t, n_dp, rooms, hid), BF16)
    in_b, out_b = (VMEM((n_t,) + shape, BF16) for shape in ((width, hid), (hid, width)))
    in_more, out_more = (VMEM((n_t + 1,) + shape, BF16) for shape in ((width, hid), (hid, width)))
    scratch = [VMEM((rows_block, width), BF16), VMEM(spread, BF16)]
    scratch += [rows_f, rows_f, VMEM((padded, padded), F32), rows_f, VMEM((padded, LANES), F32)]
    scratch += [VMEM((wide, LANES), F32), VMEM((LANES, wide), F32), VMEM((8, LANES), F32)]
    scratch += [VMEM((LANES, long), F32), VMEM((long, LANES), F32)] + [VMEM((n_dp, 8, long), F32)] * 4
    scratch += [rows_b] * 8 + [slots_b] * 6 + [units_b] * 2
    scratch += [in_b, out_b, in_b, out_b, in_more, out_more]
    scratch += [DMA((n_dp,))] * 12 + [DMA((2,))] + Spread.scratch(n_t) * 2 + Collect.scratch(n_t) * 2
    if inside:
        scratch += Gather.scratch(n_dp, n_t) * 2 + Reduce.scratch(n_dp, n_t, 1, (shard, width))
        scratch += Reduce.scratch(n_dp, n_t, width // LANES, (3 * shard, LANES))
        scratch += Reduce.scratch(n_dp, n_t, 1, (shard, LANES))
    whole, anywhere = pl.BlockSpec(memory_space=VMEM), pl.BlockSpec(memory_space=pl.ANY)
    return pl.pallas_call(
        partial(step_kernel, cfg),
        out_shape=outs,
        in_specs=[whole] * 3 + [anywhere] * 2 + [whole] * len(shared),
        out_specs=[whole] * len(outs),
        scratch_shapes=scratch,
        compiler_params=pltpu.CompilerParams(
            collective_id=cid, has_side_effects=True, vmem_limit_bytes=60 * 2**20
        ),
        name="step_" + str(rooms),
    )(x, cot, routes, e_in, e_out, *shared)


def lay_kernel(shard, experts, out_ref, gx_ref, sum_ref, in_ref, outer_ref, *outs):
    outs[0][...] = out_ref[...]
    outs[1][...] = gx_ref[...]
    for at, spot in ((0, 4), (1, 5), (2, 6), (OUT, 7)):
        outs[spot][...] = sum_ref[at * shard : (at + 1) * shard, :]
    small = sum_ref[SMALL * shard : (SMALL + 1) * shard, :LANES]
    row, column = (lax.broadcasted_iota(jnp.int32, (shard, shard), axis) for axis in (0, 1))
    for at, spot in enumerate((2, 3, 8, 9)):
        upright = small[:, experts + at : experts + at + 1]
        outs[spot][...] = jnp.sum(jnp.where(row == column, upright, 0.0), axis=0, keepdims=True)
    for at in range(experts):
        outs[10][at : at + 1, :] = jnp.sum(jnp.where(row == column, small[:, at : at + 1], 0.0), axis=0, keepdims=True)
    outs[11][...] = in_ref[...]
    outs[12][...] = outer_ref[...]


def lay_out(shard, experts, *args):
    rows, width = args[0].shape
    line = jax.ShapeDtypeStruct((1, shard), F32)
    square = jax.ShapeDtypeStruct((shard, width), F32)
    outs = [jax.ShapeDtypeStruct((rows, width), BF16)] * 2 + [line] * 2 + [square] * 4 + [line] * 2
    outs += [jax.ShapeDtypeStruct((experts, shard), F32)]
    outs += [jax.ShapeDtypeStruct(arg.shape, F32) for arg in args[3:]]

    def full(shape):
        return pl.BlockSpec(shape, lambda i: (0,) * len(shape))

    return pl.pallas_call(
        partial(lay_kernel, shard, experts),
        grid=(1,),
        out_shape=outs,
        in_specs=[full(arg.shape) for arg in args],
        out_specs=[full(out.shape) for out in outs],
        compiler_params=pltpu.CompilerParams(vmem_limit_bytes=32 * 2**20),
        name="outputs",
    )(*args)


def route_pairs(routes, t, row_count, experts, capacity):
    tok_count = routes.shape[0]
    ids = jnp.arange(experts, dtype=jnp.int32)[None, :]
    start = t * row_count
    rows = lax.dynamic_slice_in_dim(routes, start, row_count, 0)
    before = (jnp.arange(tok_count, dtype=jnp.int32) < start)[:, None]
    all_first = routes[:, 0:1] == ids
    all_second = routes[:, 1:2] == ids
    base_first = jnp.sum((all_first & before).astype(jnp.int32), axis=0)
    total_first = jnp.sum(all_first.astype(jnp.int32), axis=0)
    base_second = jnp.sum((all_second & before).astype(jnp.int32), axis=0)
    hot_first = rows[:, 0:1] == ids
    hot_second = rows[:, 1:2] == ids
    at = jnp.arange(row_count, dtype=jnp.int32)
    lower = (at[:, None] > at[None, :]).astype(BF16)
    both = jnp.concatenate([hot_first, hot_second], axis=1).astype(BF16)
    earlier = nn(lower, both).astype(jnp.int32)
    own_first = jnp.sum(hot_first.astype(jnp.int32), axis=0)
    rank_first = earlier[:, :experts]
    rank_second = earlier[:, experts:] + own_first
    place_first = rank_first + base_first
    place_second = earlier[:, experts:] + total_first + base_second
    first = jnp.sum(jnp.where(hot_first & (place_first < capacity), rank_first + 1, 0), axis=1) - 1
    second = jnp.sum(jnp.where(hot_second & (place_second < capacity), rank_second + 1, 0), axis=1) - 1
    return rows, first, second


def per_device(
    n_dp,
    n_t,
    inputs,
    cotangent,
    routes,
    gain_attn,
    shift_attn,
    query_w,
    key_w,
    value_w,
    out_w,
    gain_moe,
    shift_moe,
    router_w,
    expert_in,
    expert_out,
):
    t = lax.axis_index("tensor")
    shard, width = query_w.shape
    experts = router_w.shape[1]
    tok_count = routes.shape[0]
    rows = inputs.shape[0]
    hid = expert_in.shape[2]
    padded = ceil_to(rows, 16)
    capacity = (5 * tok_count + 2 * experts - 1) // (2 * experts)
    inside = shard % 16 == 0
    every = ("dp", "tensor")
    lines = (gain_attn, shift_attn, gain_moe, shift_moe)

    def stack():
        small = jnp.concatenate([router_w] + [line[:, None] for line in lines], axis=1)
        small = jnp.pad(small, ((0, 0), (0, width - small.shape[1])))
        return jnp.stack([query_w, key_w, value_w, small, out_w]).astype(BF16)

    if inside:
        shared = [query_w, key_w, value_w, out_w, router_w.T] + [line[None, :] for line in lines]
    else:
        shared = [lax.all_gather(stack(), every, axis=1, tiled=True)]

    def finish(results):
        summed = results[2]
        if not inside:
            summed = lax.psum_scatter(summed, every, scatter_dimension=1, tiled=True).reshape(5 * shard, width)
        outs = lay_out(shard, experts, results[0], results[1], summed, *results[3:])
        return tuple(outs)

    def slow(_):
        rooms = ceil_to(rows, 16)
        cfg = (n_dp, n_t, rows, padded, width, experts, rooms, shard, inside)
        route_rows, first_rank, second_rank = route_pairs(routes, t, rows, experts, capacity)

        def slot(choice, rank):
            return jnp.where(rank >= 0, choice * rooms + rank, -1)

        slots = jnp.stack([slot(route_rows[:, 0], first_rank), slot(route_rows[:, 1], second_rank)])
        slots = jnp.pad(slots, ((0, 0), (0, padded - rows)), constant_values=-1)
        cols = jnp.concatenate([jnp.pad(route_rows, ((0, padded - rows), (0, 0))), slots.T], axis=1)
        block = stack().reshape(5 * shard, width) if inside else shared[0]
        kept = forward(cfg, 1, inputs, cotangent, cols, slots, block)

        def turn(k):
            return [(i, (i + k) % n_t) for i in range(n_t)]

        both = jnp.stack([expert_in[0].T, expert_out[0]]).astype(BF16)
        parts = [both] + [lax.ppermute(both, "tensor", turn(k)) for k in range(1, n_t)]
        w_in, w_out = (jnp.concatenate([part[i] for part in parts], axis=0) for i in range(2))
        returned, back, grad_inner, grad_outer = run_expert(
            kept[1].reshape(n_dp * rooms, width), kept[2].reshape(n_dp * rooms, width), w_in, w_out
        )
        both = jnp.stack([grad_inner.reshape(n_t, hid, width), grad_outer.reshape(n_t, hid, width)], axis=1)
        total = both[0].astype(F32)
        for k in range(1, n_t):
            total = total + lax.ppermute(both[k], "tensor", turn(-k)).astype(F32)
        results = backward(
            cfg,
            2,
            returned.reshape(n_dp, rooms, width),
            back.reshape(n_dp, rooms, width),
            inputs,
            cotangent,
            cols,
            kept[0] if inside else block,
            *kept[3:],
        )
        return finish((*results, total[0].T, total[1]))

    rooms = min(ceil_to((7 * rows + 2 * experts - 1) // (2 * experts), 16), ceil_to(rows, 16))
    cfg = (n_dp, n_t, rows, padded, width, experts, rooms, shard, inside, hid)
    fast = run_step(cfg, 0, inputs, cotangent, routes.T, expert_in[0], expert_out[0], shared)
    if inside:
        crowded = fast[2][SMALL * shard, experts + 4] > 0.5
    else:
        crowded = lax.psum(fast[2][SMALL, 0, experts + 4], every) > 0.5
    outs = lax.cond(crowded, slow, finish, tuple(fast))
    lined = [out.reshape(shard) if at in (2, 3, 8, 9) else out for at, out in enumerate(outs)]
    lined[10], lined[11], lined[12] = lined[10].T, lined[11][None], lined[12][None]
    return tuple(lined)


def solution(mesh):
    every = ("dp", "tensor")
    rows, line = P(every, None), P(every)
    w_in, w_out = P("dp", None, "tensor"), P("dp", "tensor", None)
    return jax.shard_map(
        partial(per_device, mesh.shape["dp"], mesh.shape["tensor"]),
        mesh=mesh,
        in_specs=(rows, rows, P("dp", None), line, line, rows, rows, rows, rows, line, line, rows, w_in, w_out),
        out_specs=(rows, rows, line, line, rows, rows, rows, rows, line, line, rows, w_in, w_out),
        check_vma=False,
    )
```

```python
from functools import partial

import jax
import jax.numpy as jnp
from jax import lax
from jax.experimental import pallas as pl
from jax.experimental.pallas import tpu as pltpu
from jax.sharding import PartitionSpec as P

SEQ = 197
HEAD_DIM = 64
LANES = 128
MESH = pl.DeviceIdType.MESH
F32 = jnp.float32
BF16 = jnp.bfloat16
VMEM = pltpu.VMEM
DMA = pltpu.SemaphoreType.DMA
SMALL, OUT = 3, 4


def ceil_to(value, unit):
    return (value + unit - 1) // unit * unit


def nn(left, right):
    return lax.dot_general(left, right, (((1,), (0,)), ((), ())), preferred_element_type=F32)


def nt(left, right):
    return lax.dot_general(left, right, (((1,), (1,)), ((), ())), preferred_element_type=F32)


def tn(left, right):
    return lax.dot_general(left, right, (((0,), (0,)), ((), ())), preferred_element_type=F32)


def remote(src, dst, send, recv, device):
    return pltpu.make_async_remote_copy(
        src_ref=src, dst_ref=dst, send_sem=send, recv_sem=recv, device_id=device, device_id_type=MESH
    )


def meet(n_dp, n_t, z_too):
    dp = lax.axis_index("dp")
    t = lax.axis_index("tensor")
    bar = pltpu.get_barrier_semaphore()
    for k in range(1, n_dp):
        pl.semaphore_signal(bar, inc=1, device_id={"dp": lax.rem(dp + k, n_dp)}, device_id_type=MESH)
    if z_too:
        for k in range(1, n_t):
            pl.semaphore_signal(bar, inc=1, device_id={"tensor": lax.rem(t + k, n_t)}, device_id_type=MESH)
    pl.semaphore_wait(bar, n_dp - 1 + (n_t - 1 if z_too else 0))


class Gather:
    def __init__(self, n_dp, n_t, first, count, block, out, own_sem, z_send, z_recv, c_send, c_recv, k_send, k_recv):
        self.n_t, self.n_chip = n_t, n_dp // 2
        self.rows = pl.ds(first, count)
        self.block, self.out, self.own_sem = block.at[self.rows], out, own_sem
        self.z_sems, self.c_sems, self.k_sems = (z_send, z_recv), (c_send, c_recv), (k_send, k_recv)
        self.dp, self.t = lax.axis_index("dp"), lax.axis_index("tensor")
        self.chip, self.core = self.dp // 2, lax.rem(self.dp, 2)
        self.other = self.chip * 2 + 1 - self.core

    @staticmethod
    def scratch(n_dp, n_t):
        n_chip = n_dp // 2
        return [DMA, DMA, DMA((n_t,)), DMA, DMA((n_chip, n_t)), DMA, DMA]

    def place(self, dp, t):
        return self.out.at[dp, t, self.rows]

    def z_copy(self, k):
        send, recv = self.z_sems
        to = lax.rem(self.t + k, self.n_t)
        return remote(self.block, self.place(self.dp, self.t), send, recv.at[k], {"tensor": to})

    def chip_copy(self, k, j):
        send, recv = self.c_sems
        here = self.place(self.dp, lax.rem(self.t + self.n_t - j, self.n_t))
        to = lax.rem(self.chip + k, self.n_chip) * 2 + self.core
        return remote(self.block if j == 0 else here, here, send, recv.at[k, j], {"dp": to})

    def core_copy(self, k, j):
        send, recv = self.k_sems
        src = lax.rem(self.chip + self.n_chip - k, self.n_chip) * 2 + self.core
        here = self.place(src, lax.rem(self.t + self.n_t - j, self.n_t))
        own = k == 0 and j == 0
        return remote(self.block if own else here, here, send, recv, {"dp": self.other})

    def own_copy(self):
        return pltpu.make_async_copy(self.block, self.place(self.dp, self.t), self.own_sem)

    def start(self):
        for k in range(1, self.n_t):
            self.z_copy(k).start()
        self.own_copy().start()
        for k in range(1, self.n_chip):
            self.chip_copy(k, 0).start()
        self.core_copy(0, 0).start()

    def pass_to_chips(self):
        for j in range(1, self.n_t):
            self.z_copy(j).wait_recv()
            for k in range(1, self.n_chip):
                self.chip_copy(k, j).start()
            self.core_copy(0, j).start()

    def pass_to_core(self):
        for j in range(self.n_t):
            for k in range(1, self.n_chip):
                self.chip_copy(k, j).wait_recv()
                self.core_copy(k, j).start()

    def arrive(self):
        self.own_copy().wait()
        self.wait_bytes(self.out.at[pl.ds(0, self.n_chip), :, self.rows], self.k_sems[1])

    @staticmethod
    def wait_bytes(part, sem):
        pltpu.make_async_copy(part, part, sem).wait()

    def drain(self):
        self.wait_bytes(self.out.at[0, pl.ds(0, self.n_t - 1), self.rows], self.z_sems[0])
        self.wait_bytes(self.out.at[pl.ds(0, self.n_chip - 1), :, self.rows], self.c_sems[0])
        self.wait_bytes(self.out.at[pl.ds(0, self.n_chip), :, self.rows], self.k_sems[0])


class Scatter:
    def __init__(
        self, n_dp, n_t, grads, out, core_in, half, chip_in, part, z_in, k_send, k_recv, c_send, c_recv, z_send, z_recv
    ):
        self.n_t, self.n_chip = n_t, n_dp // 2
        self.grads, self.out = grads, out
        self.core_in, self.half, self.chip_in, self.part, self.z_in = core_in, half, chip_in, part, z_in
        self.k_sems, self.c_sems, self.z_sems = (k_send, k_recv), (c_send, c_recv), (z_send, z_recv)
        self.dp, self.t = lax.axis_index("dp"), lax.axis_index("tensor")
        self.chip, self.core = self.dp // 2, lax.rem(self.dp, 2)
        self.other = self.chip * 2 + 1 - self.core

    @staticmethod
    def scratch(n_dp, n_t, block):
        n_chip = n_dp // 2
        buffers = [VMEM((n_chip, n_t) + block, BF16)] + [VMEM((n_chip - 1, n_t) + block, BF16)] * 2
        buffers += [VMEM((n_t - 1,) + block, BF16)] * 2
        return buffers + [DMA((n_chip,))] * 4 + [DMA((n_t,))] * 2

    def core_copy(self, k):
        to = lax.rem(self.chip + k, self.n_chip)
        src = self.grads.at[to * 2 + 1 - self.core]
        return remote(src, self.core_in.at[k], self.k_sems[0].at[k], self.k_sems[1].at[k], {"dp": self.other})

    def chip_copy(self, k):
        to = lax.rem(self.chip + k, self.n_chip) * 2 + self.core
        return remote(self.half.at[k - 1], self.chip_in.at[k - 1], self.c_sems[0].at[k], self.c_sems[1].at[k], {"dp": to})

    def z_copy(self, k):
        to = lax.rem(self.t + k, self.n_t)
        return remote(self.part.at[k - 1], self.z_in.at[k - 1], self.z_sems[0].at[k], self.z_sems[1].at[k], {"tensor": to})

    def run(self, between=None, after=None):
        n_chip, n_t = self.n_chip, self.n_t
        order = list(range(1, n_chip)) + [0]
        for k in order:
            self.core_copy(k).start()
        for k in order:
            self.core_copy(k).wait_recv()
            if k > 0:
                to = lax.rem(self.chip + k, n_chip) * 2 + self.core
                self.half[k - 1] = (self.grads[to].astype(F32) + self.core_in[k].astype(F32)).astype(BF16)
                self.chip_copy(k).start()
        if between is not None:
            between()
        for k in range(1, n_chip):
            self.chip_copy(k).wait_recv()
        for k in list(range(1, n_t)) + [0]:
            row = lax.rem(self.t + k, n_t)
            total = self.grads[self.dp, row].astype(F32) + self.core_in[0, row].astype(F32)
            for c in range(1, n_chip):
                total = total + self.chip_in[c - 1, row].astype(F32)
            if k > 0:
                self.part[k - 1] = total.astype(BF16)
                self.z_copy(k).start()
            else:
                self.out[...] = total
        if after is not None:
            after()
        for k in range(1, n_t):
            self.z_copy(k).wait_recv()
            self.out[...] += self.z_in[k - 1].astype(F32)
        for k in range(n_chip):
            self.core_copy(k).wait_send()
        for k in range(1, n_chip):
            self.chip_copy(k).wait_send()
        for k in range(1, n_t):
            self.z_copy(k).wait_send()


class Reduce:
    def __init__(self, n_dp, n_t, out, grads, core_in, half, chip_in, part, z_in, *sems):
        self.n_t, self.n_chip, self.out = n_t, n_dp // 2, out
        self.grads, self.core_in, self.half = grads, core_in, half
        self.chip_in, self.part, self.z_in = chip_in, part, z_in
        self.k_sems, self.c_sems, self.z_sems = sems[0:3], sems[3:5], sems[5:7]
        self.dp, self.t = lax.axis_index("dp"), lax.axis_index("tensor")
        self.chip, self.core = self.dp // 2, lax.rem(self.dp, 2)
        self.other = self.chip * 2 + 1 - self.core

    @staticmethod
    def scratch(n_dp, n_t, parts, block):
        n_chip = n_dp // 2
        sizes = [(n_dp, n_t), (n_chip, n_t), (n_chip - 1, n_t), (n_chip - 1, n_t), (n_t - 1,), (n_t - 1,)]
        return [VMEM((parts,) + size + block, BF16) for size in sizes] + [DMA((parts,))] * 7

    def put(self, p, first, value):
        n_dp, n_t = self.n_chip * 2, self.n_t
        count, lanes = value.shape[0] // (n_dp * n_t), value.shape[1]
        self.grads[p, :, :, first : first + count, :] = value.astype(BF16).reshape(n_dp, n_t, count, lanes)

    def core_copy(self, p, k):
        src = self.grads.at[p, lax.rem(self.chip + k, self.n_chip) * 2 + 1 - self.core]
        send, far, near = self.k_sems
        recv = near if isinstance(k, int) and k == 0 else far
        return remote(src, self.core_in.at[p, k], send.at[p], recv.at[p], {"dp": self.other})

    def chip_copy(self, p, k):
        to = lax.rem(self.chip + k, self.n_chip) * 2 + self.core
        send, recv = self.c_sems
        return remote(self.half.at[p, k - 1], self.chip_in.at[p, k - 1], send.at[p], recv.at[p], {"dp": to})

    def z_copy(self, p, k):
        to = lax.rem(self.t + k, self.n_t)
        send, recv = self.z_sems
        return remote(self.part.at[p, k - 1], self.z_in.at[p, k - 1], send.at[p], recv.at[p], {"tensor": to})

    def to_core(self, p):
        for k in list(range(1, self.n_chip)) + [0]:
            self.core_copy(p, k).start()

    def to_chips(self, p):
        Gather.wait_bytes(self.core_in.at[p, pl.ds(1, self.n_chip - 1)], self.k_sems[1].at[p])
        for k in range(1, self.n_chip):
            to = lax.rem(self.chip + k, self.n_chip) * 2 + self.core
            self.half[p, k - 1] = (self.grads[p, to].astype(F32) + self.core_in[p, k].astype(F32)).astype(BF16)
            self.chip_copy(p, k).start()

    def to_line(self, p):
        self.core_copy(p, 0).wait_recv()
        Gather.wait_bytes(self.chip_in.at[p], self.c_sems[1].at[p])
        for k in list(range(1, self.n_t)) + [0]:
            row = lax.rem(self.t + k, self.n_t)
            total = self.grads[p, self.dp, row].astype(F32) + self.core_in[p, 0, row].astype(F32)
            for c in range(1, self.n_chip):
                total = total + self.chip_in[p, c - 1, row].astype(F32)
            if k > 0:
                self.part[p, k - 1] = total.astype(BF16)
                self.z_copy(p, k).start()
            else:
                self.out(p)[...] = total

    def finish(self, p):
        Gather.wait_bytes(self.z_in.at[p], self.z_sems[1].at[p])
        for k in range(1, self.n_t):
            self.out(p)[...] += self.z_in[p, k - 1].astype(F32)
        Gather.wait_bytes(self.part.at[p], self.z_sems[0].at[p])
        Gather.wait_bytes(self.core_in.at[p], self.k_sems[0].at[p])
        Gather.wait_bytes(self.half.at[p], self.c_sems[0].at[p])


def greet(n_dp, n_t):
    dp, t = lax.axis_index("dp"), lax.axis_index("tensor")
    bar = pltpu.get_barrier_semaphore()
    for k in range(1, n_dp):
        pl.semaphore_signal(bar, inc=1, device_id={"dp": lax.rem(dp + k, n_dp)}, device_id_type=MESH)
    for k in range(1, n_t):
        pl.semaphore_signal(bar, inc=1, device_id={"tensor": lax.rem(t + k, n_t)}, device_id_type=MESH)


def greeted(n_dp, n_t):
    pl.semaphore_wait(pltpu.get_barrier_semaphore(), n_dp - 1 + n_t - 1)


class Exchange:
    def __init__(self, n_dp, src, dst, rows, send, recv, single):
        self.n_dp, self.src, self.dst, self.rows, self.send, self.recv = n_dp, src, dst, rows, send, recv
        self.dp, self.single = lax.axis_index("dp"), single

    def copy(self, k):
        to = lax.rem(self.dp + k, self.n_dp)
        recv = self.recv.at[k] if self.single else self.recv
        return remote(self.src.at[to, self.rows], self.dst.at[self.dp, self.rows], self.send, recv, {"dp": to})

    def start(self, k):
        self.copy(k).start()

    def start_all(self):
        for k in range(1, self.n_dp):
            self.start(k)

    def wait_from(self, k):
        self.copy(k).wait_recv()

    def wait_all(self):
        part = self.dst.at[pl.ds(0, self.n_dp - 1), self.rows]
        pltpu.make_async_copy(part, part, self.recv).wait()

    def wait_sent(self):
        part = self.src.at[pl.ds(0, self.n_dp - 1), self.rows]
        pltpu.make_async_copy(part, part, self.send).wait()


class Spread:
    def __init__(self, n_t, parts, send, recv):
        self.n_t, self.t, self.parts, self.send, self.recv = n_t, lax.axis_index("tensor"), parts, send, recv

    @staticmethod
    def scratch(n_t):
        return [DMA((2, n_t)), DMA((n_t,))]

    def hop(self, j, way):
        here = self.parts.at[j]
        return remote(here, here, self.send.at[way, j], self.recv.at[j], {"tensor": self.t + 1 - 2 * way})

    def step(self, s):
        for way, j, in_line, onward in (
            (0, self.t - s, self.t - s >= 0, self.t + 1 < self.n_t),
            (1, self.t + s, self.t + s < self.n_t, self.t > 0),
        ):
            if s > 0:

                @pl.when(in_line)
                def _():
                    self.hop(j, way).wait_recv()

            @pl.when(in_line & onward)
            def _():
                self.hop(j, way).start()

    def drain(self):
        for s in range(self.n_t):

            @pl.when((self.t - s >= 0) & (self.t + 1 < self.n_t))
            def _():
                self.hop(self.t - s, 0).wait_send()

            @pl.when((self.t + s < self.n_t) & (self.t > 0))
            def _():
                self.hop(self.t + s, 1).wait_send()


class Collect:
    def __init__(self, n_t, parts, came, send, recv):
        self.n_t, self.t, self.parts, self.came, self.send, self.recv = (
            n_t,
            lax.axis_index("tensor"),
            parts,
            came,
            send,
            recv,
        )

    @staticmethod
    def scratch(n_t):
        return [DMA((n_t,)), DMA((n_t + 1,))]

    def hop(self, j, way):
        slot = j if way == 0 else jnp.where(j == self.t - 1, self.n_t, j)
        to = self.t + 1 - 2 * way
        return remote(self.parts.at[j], self.came.at[slot], self.send.at[j], self.recv.at[slot], {"tensor": to})

    def wait_slot(self, slot):
        remote(self.parts.at[0], self.came.at[slot], self.send.at[0], self.recv.at[slot], {"tensor": self.t}).wait_recv()

    def begin(self, j):
        @pl.when((self.t == 0) & (j > 0))
        def _():
            self.hop(j, 0).start()

        @pl.when((self.t == self.n_t - 1) & (j < self.n_t - 1))
        def _():
            self.hop(j, 1).start()

    def step(self, e, far):
        if far:
            right, left = self.n_t - 1 - e + self.t, e - self.n_t + 1 + self.t
        else:
            right, left = e - self.t + 2, 2 * self.n_t - 4 - e - self.t
        for way, j, mine in (
            (0, right, (self.t >= 1) & (right <= self.n_t - 1) & (right > self.t)),
            (1, left, (self.t <= self.n_t - 2) & (left >= 0) & (left < self.t)),
        ):

            @pl.when(mine)
            def _():
                self.wait_slot(j)
                self.parts[j] = (self.parts[j].astype(F32) + self.came[j].astype(F32)).astype(BF16)
                self.hop(j, way).start()

    def finish(self, result):
        result[...] = self.parts[self.t].astype(F32)

        @pl.when(self.t > 0)
        def _():
            self.wait_slot(self.t)
            result[...] += self.came[self.t].astype(F32)

        @pl.when(self.t < self.n_t - 1)
        def _():
            self.wait_slot(self.n_t)
            result[...] += self.came[self.n_t].astype(F32)

        for j in range(self.n_t):

            @pl.when(self.t < j)
            def _():
                self.hop(j, 0).wait_send()

            @pl.when(self.t > j)
            def _():
                self.hop(j, 1).wait_send()


def centre(values):
    centred = values - jnp.mean(values, axis=1, keepdims=True)
    inverse = lax.rsqrt(jnp.mean(centred * centred, axis=1, keepdims=True) + 1e-06)
    return centred * inverse, inverse


def norm_back(grad, unit, inverse, gain):
    scaled = grad * gain
    back = inverse * (
        scaled
        - jnp.mean(scaled, axis=1, keepdims=True)
        - unit * jnp.mean(scaled * unit, axis=1, keepdims=True)
    )
    return back, jnp.sum(grad * unit, axis=0, keepdims=True), jnp.sum(grad, axis=0, keepdims=True)


def norm_picks(experts):
    row, lane = (lax.broadcasted_iota(jnp.int32, (8, LANES), axis) for axis in (0, 1))
    return (row + experts == lane).astype(F32).astype(BF16)


def norm_rows(small, experts):
    return nt(norm_picks(experts), small)


def small_grads(experts, grad_router, rows):
    line = lax.broadcasted_iota(jnp.int32, (8, rows[0].shape[1]), 0)
    stack = sum(jnp.where(line == at, row, 0.0) for at, row in enumerate(rows))
    return grad_router + tn(stack.astype(BF16), norm_picks(experts))


def image_bias(rows, padded):
    line = lax.broadcasted_iota(jnp.int32, (padded, padded), 0)
    column = lax.broadcasted_iota(jnp.int32, (padded, padded), 1)
    image_line, image_column = jnp.zeros_like(line), jnp.zeros_like(column)
    for at in range(SEQ, rows + 1, SEQ):
        image_line += (line >= at).astype(jnp.int32)
        image_column += (column >= at).astype(jnp.int32)
    return jnp.where((image_line == image_column) & (column < rows), 0.0, -1e30)


def half_masks():
    lane = lax.broadcasted_iota(jnp.int32, (1, LANES), 1)
    low = (lane < HEAD_DIM).astype(F32)
    return low.astype(BF16), (1.0 - low).astype(BF16)


def soft_scores(query, key, bias):
    scores = nt(query, key) * HEAD_DIM ** (-0.5) + bias
    power = jnp.exp(scores - jnp.max(scores, axis=1, keepdims=True))
    return power * (1.0 / jnp.sum(power, axis=1, keepdims=True))


def router_probs(logits, experts):
    lane = lax.broadcasted_iota(jnp.int32, logits.shape, 1)
    inside = lane < experts
    kept = jnp.where(inside, logits, -1e30)
    power = jnp.where(inside, jnp.exp(kept - jnp.max(kept, axis=1, keepdims=True)), 0.0)
    return power * (1.0 / jnp.sum(power, axis=1, keepdims=True))


def pick_gate(probs, choice):
    lane = lax.broadcasted_iota(jnp.int32, probs.shape, 1)
    return jnp.sum(jnp.where(lane == choice, probs, 0.0), axis=1, keepdims=True)


class Weights:
    def __init__(self, shard, width, gathered=None, whole=None):
        self.shard, self.width, self.gathered, self.whole = shard, width, gathered, whole

    def __call__(self, at):
        if self.whole is not None:
            return self.whole[at]
        part = self.gathered[:, :, at * self.shard : (at + 1) * self.shard, :]
        return part.reshape(self.width, self.width)

    def small(self):
        if self.whole is not None:
            return self.whole[SMALL, :, :LANES]
        part = self.gathered[:, :, SMALL * self.shard : (SMALL + 1) * self.shard, :LANES]
        return part.reshape(self.width, LANES)


def gelu_parts(hidden):
    bell = jnp.exp(-0.5 * hidden * hidden)
    near = 1.0 / (1.0 + 0.23164189 * jnp.abs(hidden))
    tail = near * (
        0.127414796 + near * (-0.142248368 + near * (0.7107068705 + near * (-0.7265760135 + near * 0.5307027145)))
    )
    tail = tail * bell
    share = jnp.where(hidden < 0.0, tail, 1.0 - tail)
    return hidden * share, share + hidden * bell * 0.3989422804014327


def forward_kernel(cfg, *refs):
    n_dp, n_t, rows, padded, width, experts, rooms, shard, inside = cfg
    refs = list(refs)

    def take(count):
        got = refs[:count]
        del refs[:count]
        return got

    x_ref, cot_ref, cols_ref, slots_ref, block_ref = take(5)
    gathered, recv_d, recv_s, res_ref, moe_ref, q_ref, k_ref, v_ref, mix_ref, norm_ref, probs_ref = take(11)
    full, cot_full, bias, send_d, send_s, d_send, d_recv, s_send, s_recv = take(9)
    dp = lax.axis_index("dp")
    meet(n_dp, n_t, inside)
    if inside:
        gather = Gather(n_dp, n_t, 0, block_ref.shape[0], block_ref, gathered, *refs)
        gather.start()
        weights = Weights(shard, width, gathered=gathered)
    else:
        gathered[...] = jnp.zeros_like(gathered)
        weights = Weights(shard, width, whole=block_ref)

    full[rows - rows % 8 :, :] = jnp.zeros((padded - rows + rows % 8, width), F32)
    full[:rows, :] = x_ref[...].astype(F32)
    cot_full[rows - rows % 8 :, :] = jnp.zeros((padded - rows + rows % 8, width), F32)
    cot_full[:rows, :] = cot_ref[...].astype(F32)
    bias[...] = image_bias(rows, padded)
    unit, _ = centre(full[...])
    norm_ref[...] = unit.astype(BF16)
    if inside:
        gather.pass_to_chips()
        gather.pass_to_core()
        gather.arrive()
        gather.drain()

    norms = norm_rows(weights.small(), experts)
    unit, _ = centre(full[...])
    normed = (unit * norms[0:1] + norms[1:2]).astype(BF16)
    norm_ref[...] = normed
    q_ref[...] = nn(normed, weights(0)).astype(BF16)
    k_ref[...] = nn(normed, weights(1)).astype(BF16)
    v_ref[...] = nn(normed, weights(2)).astype(BF16)
    low, high = half_masks()

    def heads(j, carry):
        at = pl.ds(pl.multiple_of(j * LANES, LANES), LANES)
        query, key, value = q_ref[:, at], k_ref[:, at], v_ref[:, at]
        first = nn(soft_scores(query * low, key, bias[...]).astype(BF16), value)
        second = nn(soft_scores(query * high, key, bias[...]).astype(BF16), value)
        mix_ref[:, at] = (first * low.astype(F32) + second * high.astype(F32)).astype(BF16)
        return carry

    lax.fori_loop(0, width // LANES, heads, 0)
    residual = full[...] + nn(mix_ref[...], weights(OUT))
    res_ref[...] = residual
    unit, _ = centre(residual)
    moe = (unit * norms[2:3] + norms[3:4]).astype(BF16)
    moe_ref[...] = moe
    probs = router_probs(nn(moe, weights.small()), experts)
    probs_ref[...] = probs
    cot = cot_full[...]
    full[...] = pick_gate(probs, cols_ref[:, 0:1]) * cot
    cot_full[...] = pick_gate(probs, cols_ref[:, 1:2]) * cot

    def selectors(p):
        slot = lax.broadcasted_iota(jnp.int32, (rooms, padded), 0) + p * rooms
        first = (slot == slots_ref[0:1, :]).astype(F32)
        second = (slot == slots_ref[1:2, :]).astype(F32)
        return first, second

    def d_copy(k):
        to = lax.rem(dp + k, n_dp)
        return remote(send_d.at[to], recv_d.at[dp], d_send.at[k], d_recv.at[k], {"dp": to})

    def s_copy(k):
        to = lax.rem(dp + k, n_dp)
        return remote(send_s.at[to], recv_s.at[dp], s_send.at[k], s_recv.at[k], {"dp": to})

    def dispatch(k, carry):
        to = lax.rem(dp + k, n_dp)
        first, second = selectors(to)
        send_d[to] = nn((first + second).astype(BF16), moe_ref[...]).astype(BF16)

        @pl.when(k > 0)
        def _():
            d_copy(k).start()

        return carry

    def dispatch_grad(k, carry):
        to = lax.rem(dp + k, n_dp)
        first, second = selectors(to)
        rows_grad = nn(first.astype(BF16), full[...].astype(BF16)) + nn(second.astype(BF16), cot_full[...].astype(BF16))
        send_s[to] = rows_grad.astype(BF16)

        @pl.when(k > 0)
        def _():
            s_copy(k).start()

        return carry

    lax.fori_loop(0, n_dp, dispatch, 0)
    lax.fori_loop(0, n_dp, dispatch_grad, 0)
    recv_d[dp] = send_d[dp]
    recv_s[dp] = send_s[dp]
    for k in range(1, n_dp):
        d_copy(k).wait()
    for k in range(1, n_dp):
        s_copy(k).wait()


def forward(cfg, cid, x, cot, cols, slots, block):
    n_dp, n_t, rows, padded, width, experts, rooms, shard, inside = cfg
    rows_block = ceil_to(5 * shard, 16)
    low = jax.ShapeDtypeStruct((padded, width), BF16)
    sent = jax.ShapeDtypeStruct((n_dp, rooms, width), BF16)
    gathered = (n_dp, n_t, rows_block, width) if inside else (1, 1, 16, LANES)
    outs = [jax.ShapeDtypeStruct(gathered, BF16), sent, sent, jax.ShapeDtypeStruct((padded, width), F32)]
    outs += [low] * 6 + [jax.ShapeDtypeStruct((padded, LANES), F32)]
    scratch = [
        VMEM((padded, width), F32),
        VMEM((padded, width), F32),
        VMEM((padded, padded), F32),
        VMEM((n_dp, rooms, width), BF16),
        VMEM((n_dp, rooms, width), BF16),
    ] + [DMA((n_dp,))] * 4
    if inside:
        scratch += Gather.scratch(n_dp, n_t)
    whole = pl.BlockSpec(memory_space=VMEM)
    return pl.pallas_call(
        partial(forward_kernel, cfg),
        out_shape=outs,
        in_specs=[whole] * 5,
        out_specs=[whole] * len(outs),
        scratch_shapes=scratch,
        compiler_params=pltpu.CompilerParams(
            collective_id=cid, has_side_effects=True, vmem_limit_bytes=56 * 2**20
        ),
        name="forward_" + str(rooms),
    )(x, cot, cols, slots, block)


def expert_kernel(chunks, d_ref, s_ref, w_in_ref, w_out_ref, ret_ref, back_ref, g_in_ref, g_out_ref, ret, back, g_in, g_out):
    step = pl.program_id(0)
    rows = d_ref.shape[0]
    chunk = rows // chunks

    @pl.when(step == 0)
    def _():
        ret[...] = jnp.zeros_like(ret)
        back[...] = jnp.zeros_like(back)

    g_in[...] = jnp.zeros_like(g_in)
    g_out[...] = jnp.zeros_like(g_out)
    w_in, w_out = w_in_ref[...], w_out_ref[...]

    def part(c, carry):
        at = pl.ds(pl.multiple_of(c * chunk, 16), chunk)
        took, slot_grad = d_ref[at, :], s_ref[at, :]
        active, slope = gelu_parts(nt(took, w_in))
        active = active.astype(BF16)
        grad_hidden = (nt(slot_grad, w_out) * slope).astype(BF16)
        ret[at, :] += nn(active, w_out)
        back[at, :] += nn(grad_hidden, w_in)
        g_out[...] += tn(active, slot_grad)
        g_in[...] += tn(grad_hidden, took)
        return carry

    lax.fori_loop(0, chunks, part, 0)
    g_in_ref[...] = g_in[...].astype(BF16)
    g_out_ref[...] = g_out[...].astype(BF16)

    @pl.when(step == pl.num_programs(0) - 1)
    def _():
        ret_ref[...] = ret[...].astype(BF16)
        back_ref[...] = back[...].astype(BF16)


def run_expert(took, slot_grad, w_in, w_out):
    rows, width = took.shape
    hidden = w_in.shape[0]
    block = 256
    chunks = next(c for c in range(max(1, rows // 400), rows + 1) if rows % c == 0 and (rows // c) % 16 == 0)
    whole = pl.BlockSpec((rows, width), lambda i: (0, 0))
    part = pl.BlockSpec((block, width), lambda i: (i, 0))
    low = jax.ShapeDtypeStruct((rows, width), BF16)
    grad = jax.ShapeDtypeStruct((hidden, width), BF16)
    return pl.pallas_call(
        partial(expert_kernel, chunks),
        grid=(hidden // block,),
        out_shape=[low, low, grad, grad],
        in_specs=[whole, whole, part, part],
        out_specs=[whole, whole, part, part],
        scratch_shapes=[
            VMEM((rows, width), F32),
            VMEM((rows, width), F32),
            VMEM((block, width), F32),
            VMEM((block, width), F32),
        ],
        compiler_params=pltpu.CompilerParams(vmem_limit_bytes=60 * 2**20),
        cost_estimate=pl.CostEstimate(
            flops=12 * rows * width * hidden, bytes_accessed=12 * rows * width + 8 * hidden * width, transcendentals=0
        ),
        name="expert_" + str(rows),
    )(took, slot_grad, w_in, w_out)


def backward_kernel(cfg, *refs):
    n_dp, n_t, rows, padded, width, experts, rooms, shard, inside = cfg
    refs = list(refs)

    def take(count):
        got = refs[:count]
        del refs[:count]
        return got

    ret_ref, back_ref, x_ref, cot_ref, cols_ref, weights_ref = take(6)
    res_ref, moe_ref, q_ref, k_ref, v_ref, mix_ref, norm_ref, probs_ref = take(8)
    out_ref, gx_ref, sum_ref = take(3)
    full, cot_full, bias, ret_in, back_in, grads, r_send, r_recv, b_send, b_recv = take(10)
    dq, dk, dv = take(3)
    dp = lax.axis_index("dp")
    meet(n_dp, n_t, inside)

    def r_copy(k):
        to = lax.rem(dp + k, n_dp)
        return remote(ret_ref.at[to], ret_in.at[dp], r_send.at[k], r_recv.at[k], {"dp": to})

    def b_copy(k):
        to = lax.rem(dp + k, n_dp)
        return remote(back_ref.at[to], back_in.at[dp], b_send.at[k], b_recv.at[k], {"dp": to})

    for k in range(1, n_dp):
        r_copy(k).start()
    for k in range(1, n_dp):
        b_copy(k).start()
    ret_in[dp] = ret_ref[dp]
    back_in[dp] = back_ref[dp]
    weights = Weights(shard, width, gathered=weights_ref) if inside else Weights(shard, width, whole=weights_ref)
    tail = rows - rows % 8
    full[tail:, :] = jnp.zeros((padded - tail, width), F32)
    full[:rows, :] = x_ref[...].astype(F32)
    cot_full[tail:, :] = jnp.zeros((padded - tail, width), F32)
    cot_full[:rows, :] = cot_ref[...].astype(F32)
    bias[...] = image_bias(rows, padded)
    norms = norm_rows(weights.small(), experts)
    slot_count = n_dp * rooms
    lane = lax.broadcasted_iota(jnp.int32, (padded, slot_count), 1)
    first = (lane == cols_ref[:, 2:3]).astype(F32)
    second = (lane == cols_ref[:, 3:4]).astype(F32)
    both = (first + second).astype(BF16)

    for k in range(1, n_dp):
        r_copy(k).wait()
    returned = ret_in[...].reshape(slot_count, width)
    first_rows = nn(first.astype(BF16), returned)
    second_rows = nn(second.astype(BF16), returned)
    probs = probs_ref[...]
    first_id, second_id = cols_ref[:, 0:1], cols_ref[:, 1:2]
    outcome = res_ref[...] + pick_gate(probs, first_id) * first_rows + pick_gate(probs, second_id) * second_rows
    out_ref[...] = outcome[:rows].astype(BF16)
    cot = cot_full[...]
    first_grad = jnp.sum(first_rows * cot, axis=1, keepdims=True)
    second_grad = jnp.sum(second_rows * cot, axis=1, keepdims=True)
    spot = lax.broadcasted_iota(jnp.int32, probs.shape, 1)
    grad_probs = jnp.where(spot == first_id, first_grad, 0.0) + jnp.where(spot == second_id, second_grad, 0.0)
    grad_logits = (probs * (grad_probs - jnp.sum(probs * grad_probs, axis=1, keepdims=True))).astype(BF16)
    grad_router = tn(moe_ref[...], grad_logits)

    for k in range(1, n_dp):
        b_copy(k).wait()
    grad_moe = nn(both, back_in[...].reshape(slot_count, width)) + nt(grad_logits, weights.small())
    unit, inverse = centre(res_ref[...])
    extra, gain_two, shift_two = norm_back(grad_moe, unit, inverse, norms[2:3])
    grad_residual = cot + extra
    cot_full[...] = grad_residual
    grad_attended = grad_residual.astype(BF16)
    n_all = n_dp * n_t

    def keep(at, value):
        if inside:
            grads[:, :, at * shard : (at + 1) * shard, :] = value.astype(BF16).reshape(n_dp, n_t, shard, width)
        else:
            sum_ref[at] = value

    keep(OUT, tn(mix_ref[...], grad_attended))
    mix_ref_grad = nt(grad_attended, weights(OUT)).astype(BF16)
    dq[...] = mix_ref_grad
    low, high = half_masks()
    low_f, high_f = low.astype(F32), high.astype(F32)
    scale = HEAD_DIM ** (-0.5)

    def heads(j, carry):
        at = pl.ds(pl.multiple_of(j * LANES, LANES), LANES)
        query, key, value, grad = q_ref[:, at], k_ref[:, at], v_ref[:, at], dq[:, at]
        for mask, mask_f in ((low, low_f), (high, high_f)):
            probs = soft_scores(query * mask, key, bias[...])
            grad_probs = nt(grad * mask, value)
            grad_scores = probs * (grad_probs - jnp.sum(probs * grad_probs, axis=1, keepdims=True))
            grad_scores = grad_scores.astype(BF16)
            part_v = tn(probs.astype(BF16), grad)
            part_q = nn(grad_scores, key) * scale
            part_k = tn(grad_scores, query) * scale
            if mask is low:
                sum_q, sum_k, sum_v = part_q * mask_f, part_k * mask_f, part_v * mask_f
            else:
                sum_q, sum_k, sum_v = sum_q + part_q * mask_f, sum_k + part_k * mask_f, sum_v + part_v * mask_f
        dq[:, at] = sum_q.astype(BF16)
        dk[:, at] = sum_k.astype(BF16)
        dv[:, at] = sum_v.astype(BF16)
        return carry

    lax.fori_loop(0, width // LANES, heads, 0)
    keep(0, tn(norm_ref[...], dq[...]))
    keep(1, tn(norm_ref[...], dk[...]))
    keep(2, tn(norm_ref[...], dv[...]))
    grad_normed = nt(dq[...], weights(0)) + nt(dk[...], weights(1)) + nt(dv[...], weights(2))
    unit, inverse = centre(full[...])
    extra, gain_one, shift_one = norm_back(grad_normed, unit, inverse, norms[0:1])
    gx_ref[...] = (cot_full[...] + extra)[:rows].astype(BF16)
    small = small_grads(experts, grad_router, (gain_one, shift_one, gain_two, shift_two))
    if inside:
        at = slice(SMALL * shard, (SMALL + 1) * shard)
        grads[:, :, at, :LANES] = small.astype(BF16).reshape(n_dp, n_t, shard, LANES)
        grads[:, :, at, LANES:] = jnp.zeros((n_dp, n_t, shard, width - LANES), BF16)
        Scatter(n_dp, n_t, grads, sum_ref, *refs).run()
    else:
        sum_ref[SMALL] = jnp.zeros((width, width), F32)
        sum_ref[SMALL, :, :LANES] = small


def backward(cfg, cid, *args):
    n_dp, n_t, rows, padded, width, experts, rooms, shard, inside = cfg
    rows_block = ceil_to(5 * shard, 16)
    total = (rows_block, width) if inside else (5, width, width)
    outs = [jax.ShapeDtypeStruct((rows, width), BF16)] * 2 + [jax.ShapeDtypeStruct(total, F32)]
    scratch = [
        VMEM((padded, width), F32),
        VMEM((padded, width), F32),
        VMEM((padded, padded), F32),
        VMEM((n_dp, rooms, width), BF16),
        VMEM((n_dp, rooms, width), BF16),
        VMEM((n_dp, n_t, rows_block, width) if inside else (1, 1, 16, LANES), BF16),
    ]
    scratch += [DMA((n_dp,))] * 4 + [VMEM((padded, width), BF16)] * 3
    if inside:
        scratch += Scatter.scratch(n_dp, n_t, (rows_block, width))
    whole = pl.BlockSpec(memory_space=VMEM)
    return pl.pallas_call(
        partial(backward_kernel, cfg),
        out_shape=outs,
        in_specs=[whole] * len(args),
        out_specs=[whole] * len(outs),
        scratch_shapes=scratch,
        compiler_params=pltpu.CompilerParams(
            collective_id=cid, has_side_effects=True, vmem_limit_bytes=56 * 2**20
        ),
        name="backward_" + str(rooms),
    )(*args)


def pack_block(refs, block, shard, width, experts):
    q_ref, k_ref, v_ref, o_ref, router_ref, *line_refs = refs
    for at, ref in ((0, q_ref), (1, k_ref), (2, v_ref), (OUT, o_ref)):
        block[at * shard : (at + 1) * shard, :] = ref[...].astype(BF16)
    here = slice(SMALL * shard, (SMALL + 1) * shard)
    block[here, :] = jnp.zeros((shard, width), BF16)
    row, column = (lax.broadcasted_iota(jnp.int32, (shard, shard), axis) for axis in (0, 1))
    lane = lax.broadcasted_iota(jnp.int32, (shard, LANES), 1)
    small = jnp.zeros((shard, LANES), F32)
    for at in range(experts + len(line_refs)):
        level = router_ref[at : at + 1, :] if at < experts else line_refs[at - experts][...]
        upright = jnp.sum(jnp.where(row == column, level, 0.0), axis=1, keepdims=True)
        small = jnp.where(lane == at, upright, small)
    block[here, :LANES] = small.astype(BF16)


def find_places(cfg, routes_ref, place, turned, over):
    n_dp, n_t, rows, padded, width, experts, rooms, shard, inside, hid = cfg
    t = lax.axis_index("tensor")
    tok_count = routes_ref.shape[1]
    capacity = (5 * tok_count + 2 * experts - 1) // (2 * experts)
    line = lax.broadcasted_iota(jnp.int32, (experts, tok_count), 0)
    lane = lax.broadcasted_iota(jnp.int32, (experts, tok_count), 1)

    def count(row, until):
        hot = (line == routes_ref[row : row + 1, :]) & (lane < until)
        return jnp.sum(hot.astype(F32), axis=1, keepdims=True)

    total = count(0, tok_count)
    before = (count(0, t * rows), count(1, t * rows))
    long = ceil_to(tok_count, LANES)
    wide = turned.shape[1]
    turned[...] = jnp.full(turned.shape, -1.0, F32)
    everyone = jnp.concatenate(
        [routes_ref[...], jnp.full((2, long - tok_count), experts, jnp.int32)], axis=1
    )
    everyone = jnp.concatenate([everyone, everyone, everyone, everyone], axis=0)
    mine = pltpu.roll(everyone, lax.rem(long - t * rows, long), 1)[:, :wide]
    spot = lax.broadcasted_iota(jnp.int32, (8, wide), 1)
    mine = jnp.where(spot < rows, mine, experts)
    line = lax.broadcasted_iota(jnp.int32, (experts, wide), 0)
    first, second = line == mine[0:1], line == mine[1:2]
    down, across = (lax.broadcasted_iota(jnp.int32, (wide, wide), axis) for axis in (0, 1))
    earlier = (down < across).astype(F32).astype(BF16)
    own = jnp.sum(first.astype(F32), axis=1, keepdims=True)
    first_rank = nn(first.astype(F32).astype(BF16), earlier)
    second_rank = nn(second.astype(F32).astype(BF16), earlier)

    def slot(choice, hot, rank, place):
        kept = hot & (place < capacity)
        here = jnp.sum(jnp.where(kept, rank + 1.0, 0.0), axis=0, keepdims=True) - 1.0
        good = (here >= 0.0) & (here < rooms)
        return jnp.where(good, choice.astype(F32) * rooms + here, -1.0), jnp.max(here, axis=1, keepdims=True)

    first_slot, first_most = slot(mine[0:1], first, first_rank, first_rank + before[0])
    second_slot, second_most = slot(mine[1:2], second, second_rank + own, second_rank + total + before[1])
    turned[0:1, :] = first_slot
    turned[1:2, :] = second_slot
    turned[2:3, :] = mine[0:1].astype(F32)
    turned[3:4, :] = mine[1:2].astype(F32)
    place[...] = turned[...].T
    most = jnp.maximum(first_most, second_most)
    over[...] = jnp.broadcast_to(jnp.where(most >= rooms, 1.0, 0.0), over.shape)


def step_kernel(cfg, *refs):
    n_dp, n_t, rows, padded, width, experts, rooms, shard, inside, hid = cfg
    refs = list(refs)

    def take(count):
        got = refs[:count]
        del refs[:count]
        return got

    x_ref, cot_ref, routes_ref, e_in_ref, e_out_ref = take(5)
    shared = take(9 if inside else 1)
    out_ref, gx_ref, sum_ref, in_ref, outer_ref = take(5)
    g_in_ref, g_out_ref = take(2)
    block, gathered, full, cot_full, bias, res, probs_s = take(7)
    place, turned, over, gate_m, gate_c, gate_s, gate_r, rise_s, rise_r = take(9)
    moe, q_s, k_s, v_s, mix, norm, dk, dv = take(8)
    send_d, send_s, recv_d, recv_s, ret_in, back_in, act, slope = take(8)
    wi, wo, gi, go, gi_in, go_in = take(6)
    d_send, d_recv, s_send, s_recv, r_send, r_recv, b_send, b_recv = take(8)
    f_send, f_recv, e_send, e_recv, own_sems = take(5)
    wi_spread, wo_spread = Spread(n_t, wi, *take(2)), Spread(n_t, wo, *take(2))
    gi_collect, go_collect = Collect(n_t, gi, gi_in, *take(2)), Collect(n_t, go, go_in, *take(2))
    dp, t = lax.axis_index("dp"), lax.axis_index("tensor")
    scale = HEAD_DIM ** (-0.5)
    slot_count = n_dp * rooms
    half, wide = min(256, hid), min(256, width)
    long = gate_m.shape[1]
    early = 2 if hid == width and n_t > 2 else 0
    table = [sorted(range(n_t), key=lambda j: (abs(j - at), j)) for at in range(n_t)]

    def order(p):
        found = jnp.int32(0)
        for at in range(n_t):
            for spot in range(n_t):
                found = found + jnp.where((t == at) & (p == spot), table[at][spot], 0)
        return found

    every = pl.ds(0, rooms)
    cut = max(rooms // 2 // 16 * 16, 16)
    d_copy = Exchange(n_dp, send_d, recv_d, every, d_send, d_recv, True)
    s_first = Exchange(n_dp, send_s, recv_s, pl.ds(0, cut), s_send.at[0], s_recv.at[0], False)
    s_second = Exchange(n_dp, send_s, recv_s, pl.ds(cut, rooms - cut), s_send.at[1], s_recv.at[1], False)
    r_first = Exchange(n_dp, send_d, ret_in, pl.ds(cut, rooms - cut), r_send.at[0], r_recv.at[0], False)
    r_second = Exchange(n_dp, send_d, ret_in, pl.ds(0, cut), r_send.at[1], r_recv.at[1], False)
    b_copy = Exchange(n_dp, send_s, back_in, every, b_send, b_recv, False)
    f_copy = Exchange(n_dp, gate_s, gate_r, pl.ds(0, 8), f_send, f_recv, False)
    e_copy = Exchange(n_dp, rise_s, rise_r, pl.ds(0, 8), e_send, e_recv, False)

    def column(at):
        return place[:padded, at : at + 1].astype(jnp.int32)

    greet(n_dp, n_t)
    load_in = pltpu.make_async_copy(e_in_ref, g_in_ref, own_sems.at[0])
    load_out = pltpu.make_async_copy(e_out_ref, g_out_ref, own_sems.at[1])
    load_in.start()
    load_out.start()
    if inside:
        pack_block(shared, block, shard, width, experts)
        size = len(Gather.scratch(n_dp, n_t))
        gather_a = Gather(n_dp, n_t, 0, OUT * shard, block, gathered, *take(size))
        gather_b = Gather(n_dp, n_t, OUT * shard, shard, block, gathered, *take(size))
        weights = Weights(shard, width, gathered=gathered)
    else:
        weights = Weights(shard, width, whole=shared[0])
    load_in.wait()
    wi[t] = g_in_ref[...].astype(BF16)
    greeted(n_dp, n_t)
    if inside:
        gather_a.start()
        gather_b.start()
    wi_spread.step(0)
    load_out.wait()
    wo[t] = g_out_ref[...].astype(BF16)
    tail = rows - rows % 8
    full[tail:, :] = jnp.zeros((padded - tail, width), F32)
    full[:rows, :] = x_ref[...].astype(F32)
    cot_full[tail:, :] = jnp.zeros((padded - tail, width), F32)
    cot_full[:rows, :] = cot_ref[...].astype(F32)
    bias[...] = image_bias(rows, padded)
    find_places(cfg, routes_ref, place, turned, over)

    def selectors(p):
        slot = lax.broadcasted_iota(jnp.int32, (rooms, padded), 0) + p * rooms
        first = (slot == turned[0:1, :padded].astype(jnp.int32)).astype(F32)
        second = (slot == turned[1:2, :padded].astype(jnp.int32)).astype(F32)
        return first, second

    dk[...] = cot_full[...].astype(BF16)

    def dispatch_grad(k, carry):
        to = lax.rem(dp + k, n_dp)
        first, second = selectors(to)
        got = nn((first + second).astype(BF16), dk[...]).astype(BF16)

        @pl.when(k > 0)
        def _():
            send_s[to] = got

        @pl.when(k == 0)
        def _():
            recv_s[to] = got

        return carry

    lax.fori_loop(0, n_dp, dispatch_grad, 0)
    if inside:
        gather_a.pass_to_chips()
        gather_b.pass_to_chips()
        gather_a.pass_to_core()
    if inside:
        gather_a.arrive()
    norms = norm_rows(weights.small(), experts)
    unit, _ = centre(full[...])
    norm[...] = (unit * norms[0:1] + norms[1:2]).astype(BF16)
    q_s[...] = nn(norm[...], weights(0)).astype(BF16)
    k_s[...] = nn(norm[...], weights(1)).astype(BF16)
    v_s[...] = nn(norm[...], weights(2)).astype(BF16)
    if inside:
        gather_b.pass_to_core()
    s_first.start_all()
    wi_spread.step(1)
    low, high = half_masks()
    low_f, high_f = low.astype(F32), high.astype(F32)

    def heads(j, carry):
        at = pl.ds(pl.multiple_of(j * LANES, LANES), LANES)
        query, key, value = q_s[:, at], k_s[:, at], v_s[:, at]
        first = nn(soft_scores(query * low, key, bias[...]).astype(BF16), value)
        second = nn(soft_scores(query * high, key, bias[...]).astype(BF16), value)
        mix[:, at] = (first * low_f + second * high_f).astype(BF16)
        return carry

    lax.fori_loop(0, width // LANES, heads, 0)
    if inside:
        gather_b.arrive()
    residual = full[...] + nn(mix[...], weights(OUT))
    res[...] = residual
    unit, _ = centre(residual)
    moe[...] = (unit * norms[2:3] + norms[3:4]).astype(BF16)
    probs_s[...] = router_probs(nn(moe[...], weights.small()), experts)

    spot = lax.broadcasted_iota(jnp.int32, (padded, LANES), 1)
    first_gate, second_gate = pick_gate(probs_s[...], column(2)), pick_gate(probs_s[...], column(3))
    place[:padded, :] = jnp.where(spot == 4, first_gate, jnp.where(spot == 5, second_gate, place[:padded, :]))
    turned[...] = place[...].T
    gate_line = lax.broadcasted_iota(jnp.int32, (8, padded), 0)

    def terms(gate):
        one = gate.astype(BF16).astype(F32)
        two = (gate - one).astype(BF16).astype(F32)
        three = gate - one - two
        stack = jnp.where(gate_line == 0, one, jnp.where(gate_line == 1, two, jnp.where(gate_line == 2, three, 0.0)))
        return stack.astype(BF16)

    first_terms, second_terms = terms(turned[4:5, :padded]), terms(turned[5:6, :padded])
    def dispatch(k, carry):
        to = lax.rem(dp + k, n_dp)
        first, second = selectors(to)
        got = nn((first + second).astype(BF16), moe[...]).astype(BF16)

        @pl.when(k > 0)
        def _():
            send_d[to] = got
            d_copy.start(k)

        @pl.when(k == 0)
        def _():
            recv_d[to] = got

        return carry

    lax.fori_loop(0, n_dp, dispatch, 0)

    if n_t > 2:
        wi_spread.step(2)

    def dispatch_gates(k, carry):
        to = lax.rem(dp + k, n_dp)
        first, second = selectors(to)
        gate = nt(first_terms, first.astype(BF16)) + nt(second_terms, second.astype(BF16))
        gate = jnp.sum(gate, axis=0, keepdims=True)

        @pl.when(k > 0)
        def _():
            gate_s[to, :, :rooms] = jnp.broadcast_to(gate, (8, rooms))
            f_copy.start(k)

        @pl.when(k == 0)
        def _():
            gate_r[to, :, :rooms] = jnp.broadcast_to(gate, (8, rooms))

        return carry

    lax.fori_loop(0, n_dp, dispatch_gates, 0)

    def hidden_units(j, g):
        active, steep = gelu_parts(nn(recv_d[g], wi[j]))
        act[j, g] = active.astype(BF16)
        slope[j, g] = steep.astype(BF16)

    def own_hidden(k, carry):
        @pl.when(k > 0)
        def _():
            d_copy.wait_from(k)

        @pl.when(k == n_dp // 2)
        def _():
            wo_spread.step(0)

        hidden_units(t, lax.rem(dp + n_dp - k, n_dp))
        return carry

    lax.fori_loop(0, n_dp, own_hidden, 0)
    s_second.start_all()

    def other_hidden(i, carry):
        q = i // n_dp
        p = jnp.where(q == 0, 1, jnp.where(q == 1, n_t - 1, q))
        hidden_units(order(p), lax.rem(i, n_dp))
        return carry

    lax.fori_loop(0, n_dp, other_hidden, 0)
    for s in range(3, n_t):
        wi_spread.step(s)
    if n_t > 2:
        lax.fori_loop(n_dp, 2 * n_dp, other_hidden, 0)
    gate_m[...] = jnp.zeros_like(gate_m)
    f_copy.wait_all()
    f_copy.wait_sent()
    for g in range(n_dp):
        gate_m[g : g + 1, :rooms] = gate_r[g, 0:1, :rooms]
    gate_c[...] = gate_m[...].T
    for half_copy in (s_first, s_second):
        half_copy.wait_all()
        half_copy.wait_sent()
    slot_grads = send_s
    room_lane = lax.broadcasted_iota(jnp.int32, (rooms, LANES), 1)

    def slot_grad(g, carry):
        gate = jnp.sum(jnp.where(room_lane == g, gate_c[:rooms, :], 0.0), axis=1, keepdims=True)
        slot_grads[g] = (gate * recv_s[g].astype(F32)).astype(BF16)
        return carry

    lax.fori_loop(0, n_dp, slot_grad, 0)

    def outer_grad(i, carry):
        j = order(n_t - 1 - i // (hid // half))
        at = pl.ds(pl.multiple_of(lax.rem(i, hid // half) * half, half), half)
        left = act[j, :, :, at].reshape(slot_count, half)
        go[j, at, :] = tn(left, slot_grads[...].reshape(slot_count, width)).astype(BF16)

        @pl.when(lax.rem(i, hid // half) == hid // half - 1)
        def _():
            go_collect.begin(j)

        return carry

    lax.fori_loop(0, hid // half, outer_grad, 0)
    wo_spread.step(1)
    if n_t > 3:
        lax.fori_loop(2 * n_dp, (n_t - 1) * n_dp, other_hidden, 0)
    lax.fori_loop(hid // half, n_t * (hid // half), outer_grad, 0)

    def hidden_grads(p):
        j = order(p)

        def one(i, inner):
            slope[j, i] = (nt(slot_grads[i], wo[j]) * slope[j, i].astype(F32)).astype(BF16)
            return inner

        lax.fori_loop(0, n_dp, one, 0)

    def inner_grads(p):
        j = order(p)

        def one(i, inner):
            at = pl.ds(pl.multiple_of(i * wide, wide), wide)
            left = recv_d[:, :, at].reshape(slot_count, wide)
            gi[j, at, :] = tn(left, slope[j].reshape(slot_count, hid)).astype(BF16)
            return inner

        lax.fori_loop(0, width // wide, one, 0)

    def split(total):
        main = total.astype(BF16)
        return main, (total - main.astype(F32)).astype(BF16)

    middle = (t > 0) & (t < n_t - 1)

    def hidden_step(p, carry):
        @pl.when(p == 1)
        def _():
            if n_t > 2:
                go_collect.step(1, True)

        @pl.when((p == 1) & middle)
        def _():
            if n_t > 2:
                wo_spread.step(2)

        @pl.when((p == 2) & jnp.logical_not(middle))
        def _():
            if n_t > 2:
                wo_spread.step(2)

        @pl.when(p == 3)
        def _():
            for e in range(2, n_t - 1):
                go_collect.step(e, True)
            for s in range(3, n_t):
                wo_spread.step(s)

        hidden_grads(p)

        @pl.when(p < n_t - 1)
        def _():
            inner_grads(p)

        if early:

            @pl.when(p == early)
            def _():
                near_a, near_b = order(0), order(1)

                def some_back(g, inner):
                    total = nn(act[near_a, g], wo[near_a]) + nn(act[near_b, g], wo[near_b])
                    act[near_a, g], act[near_b, g] = split(total)
                    return inner

                lax.fori_loop(0, n_dp, some_back, 0)

        return carry

    lax.fori_loop(0, n_t, hidden_step, 0)
    d_copy.wait_sent()

    def give_back_grad(i, carry):
        k = lax.rem(i + 1, n_dp)
        to = lax.rem(dp + k, n_dp)
        total = nt(slope[0, to], wi[0])
        for j in range(1, n_t):
            total = total + nt(slope[j, to], wi[j])
        total = total.astype(BF16)

        @pl.when(k > 0)
        def _():
            send_s[to] = total
            b_copy.start(k)

        @pl.when(k == 0)
        def _():
            back_in[to] = total

        return carry

    lax.fori_loop(0, n_dp, give_back_grad, 0)
    inner_grads(n_t - 1)

    def send_inner(p, carry):
        gi_collect.begin(order(n_t - 1 - p))
        return carry

    lax.fori_loop(0, n_t, send_inner, 0)
    gate_c[...] = jnp.zeros_like(gate_c)

    def give_back(i, carry):
        k = lax.rem(i + 1, n_dp)
        to = lax.rem(dp + k, n_dp)
        if early:
            near_a, near_b = order(0), order(1)
            total = act[near_a, to].astype(F32) + act[near_b, to].astype(F32)
        else:
            total = jnp.zeros((rooms, width), F32)
        for p in range(early, n_t):
            j = order(p)
            total = total + nn(act[j, to], wo[j])
        rise = jnp.sum(total * recv_s[to].astype(F32), axis=1, keepdims=True)
        gate_c[:rooms, :] = jnp.where(room_lane == to, rise, gate_c[:rooms, :])

        @pl.when(k > 0)
        def _():
            send_d[to] = total.astype(BF16)

        @pl.when(k == 0)
        def _():
            ret_in[to] = total.astype(BF16)

        return carry

    lax.fori_loop(0, n_dp, give_back, 0)
    gate_m[...] = gate_c[...].T
    for g in range(n_dp):
        row = jnp.broadcast_to(gate_m[g : g + 1, :], (8, long))

        @pl.when(dp == g)
        def _():
            rise_r[g] = row

        @pl.when(dp != g)
        def _():
            rise_s[g] = row

    e_copy.start_all()
    lane = lax.broadcasted_iota(jnp.int32, (padded, slot_count), 1)
    both = ((lane == column(0)).astype(F32) + (lane == column(1)).astype(F32)).astype(BF16)
    unit, inverse = centre(res[...])
    go_collect.finish(g_out_ref)
    store_out = pltpu.make_async_copy(g_out_ref, outer_ref, own_sems.at[1])
    store_out.start()
    b_copy.wait_sent()
    r_first.start_all()
    b_copy.wait_all()
    e_copy.wait_all()
    e_copy.wait_sent()
    room = lax.broadcasted_iota(jnp.int32, (padded, long), 1)

    slots_of = (column(0), column(1))

    found = [jnp.zeros((padded, long), F32)] * 2
    for e in range(n_dp):
        row = jnp.where(room[0:1] < rooms, rise_r[e, 0:1, :], 0.0)
        for at, slot in enumerate(slots_of):
            here = jnp.where(slot < (e + 1) * rooms, slot - e * rooms, -1)
            found[at] = jnp.where(room == here, row, found[at])
    first_grad, second_grad = (jnp.sum(one, axis=1, keepdims=True) for one in found)
    probs = probs_s[...]
    spot = lax.broadcasted_iota(jnp.int32, probs.shape, 1)
    grad_probs = jnp.where(spot == column(2), first_grad, 0.0) + jnp.where(spot == column(3), second_grad, 0.0)
    grad_logits = (probs * (grad_probs - jnp.sum(probs * grad_probs, axis=1, keepdims=True))).astype(BF16)
    grad_router = tn(moe[...], grad_logits)
    if n_t > 2:
        gi_collect.step(1, True)
    grad_moe = nn(both, back_in[...].reshape(slot_count, width)) + nt(grad_logits, weights.small())
    extra, gain_two, shift_two = norm_back(grad_moe, unit, inverse, norms[2:3])
    grad_residual = cot_full[...] + extra
    cot_full[...] = grad_residual
    grad_attended = grad_residual.astype(BF16)

    pairs = width // LANES
    if inside:
        size = len(Reduce.scratch(n_dp, n_t, 1, (shard, LANES)))
        out_sum = Reduce(n_dp, n_t, lambda p: sum_ref.at[pl.ds(OUT * shard, shard)], *take(size))
        pair_sum = Reduce(
            n_dp, n_t, lambda p: sum_ref.at[pl.ds(0, 3 * shard), pl.ds(pl.multiple_of(p * LANES, LANES), LANES)], *take(size)
        )
        small_sum = Reduce(n_dp, n_t, lambda p: sum_ref.at[pl.ds(SMALL * shard, shard), pl.ds(0, LANES)], *take(size))
        sum_ref[SMALL * shard : (SMALL + 1) * shard, LANES:] = jnp.zeros((shard, width - LANES), F32)
        out_sum.put(0, 0, tn(mix[...], grad_attended))
        out_sum.to_core(0)
    else:
        sum_ref[OUT] = tn(mix[...], grad_attended)
    dq = mix
    dq[...] = nt(grad_attended, weights(OUT)).astype(BF16)

    def heads_back(j, carry):
        at = pl.ds(pl.multiple_of(j * LANES, LANES), LANES)
        query, key, value, grad = q_s[:, at], k_s[:, at], v_s[:, at], dq[:, at]
        for mask, mask_f in ((low, low_f), (high, high_f)):
            probs = soft_scores(query * mask, key, bias[...])
            grad_probs = nt(grad * mask, value)
            grad_scores = probs * (grad_probs - jnp.sum(probs * grad_probs, axis=1, keepdims=True))
            grad_scores = grad_scores.astype(BF16)
            part_v = tn(probs.astype(BF16), grad)
            part_q = nn(grad_scores, key) * scale
            part_k = tn(grad_scores, query) * scale
            if mask is low:
                sum_q, sum_k, sum_v = part_q * mask_f, part_k * mask_f, part_v * mask_f
            else:
                sum_q, sum_k, sum_v = sum_q + part_q * mask_f, sum_k + part_k * mask_f, sum_v + part_v * mask_f
        dq[:, at] = sum_q.astype(BF16)
        dk[:, at] = sum_k.astype(BF16)
        dv[:, at] = sum_v.astype(BF16)
        if inside:
            for spot, ref in enumerate((dq, dk, dv)):
                pair_sum.put(j, spot * shard, tn(norm[...], ref[:, at]))
            pair_sum.to_core(j)

            @pl.when(j == 0)
            def _():
                out_sum.to_chips(0)

            @pl.when(j > 0)
            def _():
                pair_sum.to_chips(j - 1)

        return carry

    lax.fori_loop(0, pairs, heads_back, 0)
    for e in range(2, n_t - 1):
        gi_collect.step(e, True)
    if inside:
        pair_sum.to_chips(pairs - 1)
    else:
        for spot, ref in enumerate((dq, dk, dv)):
            sum_ref[spot] = tn(norm[...], ref[...])
    grad_normed = nt(dq[...], weights(0)) + nt(dk[...], weights(1)) + nt(dv[...], weights(2))
    full[tail:, :] = jnp.zeros((padded - tail, width), F32)
    full[:rows, :] = x_ref[...].astype(F32)
    unit, inverse = centre(full[...])
    extra, gain_one, shift_one = norm_back(grad_normed, unit, inverse, norms[0:1])
    gx_ref[...] = (cot_full[...] + extra)[:rows].astype(BF16)
    small = small_grads(experts, grad_router, (gain_one, shift_one, gain_two, shift_two))
    lane = lax.broadcasted_iota(jnp.int32, small.shape, 1)
    small = jnp.where(lane == experts + 4, over[0:1, :], small)
    def combine():
        for half_copy in (r_first, r_second):
            half_copy.wait_all()
            half_copy.wait_sent()
        returned = ret_in[...].reshape(slot_count, width)
        lane = lax.broadcasted_iota(jnp.int32, (padded, slot_count), 1)
        first, second = ((lane == column(at)).astype(F32).astype(BF16) for at in (0, 1))
        first_rows, second_rows = nn(first, returned), nn(second, returned)
        first_gate, second_gate = place[:padded, 4:5], place[:padded, 5:6]
        outcome = res[...] + first_gate * first_rows + second_gate * second_rows
        out_ref[...] = outcome[:rows].astype(BF16)

    if inside:
        small_sum.put(0, 0, small)
        small_sum.to_core(0)
        small_sum.to_chips(0)
        out_sum.to_line(0)

        def line(p, carry):
            pair_sum.to_line(p)
            return carry

        lax.fori_loop(0, pairs, line, 0)
        small_sum.to_line(0)
        r_second.start_all()
        combine()
        out_sum.finish(0)

        def last(p, carry):
            pair_sum.finish(p)
            return carry

        lax.fori_loop(0, pairs, last, 0)
        small_sum.finish(0)
        gather_a.drain()
        gather_b.drain()
    else:
        sum_ref[SMALL] = jnp.zeros((width, width), F32)
        sum_ref[SMALL, :, :LANES] = small
        r_second.start_all()
        combine()
    gi_collect.finish(g_in_ref)
    store_in = pltpu.make_async_copy(g_in_ref, in_ref, own_sems.at[0])
    store_in.start()
    wi_spread.drain()
    wo_spread.drain()
    store_out.wait()
    store_in.wait()


def run_step(cfg, cid, x, cot, routes, e_in, e_out, shared):
    n_dp, n_t, rows, padded, width, experts, rooms, shard, inside, hid = cfg
    rows_block = ceil_to(5 * shard, 16)
    total = (rows_block, width) if inside else (5, width, width)
    outs = [
        jax.ShapeDtypeStruct((rows, width), BF16),
        jax.ShapeDtypeStruct((rows, width), BF16),
        jax.ShapeDtypeStruct(total, F32),
        jax.ShapeDtypeStruct((width, hid), F32),
        jax.ShapeDtypeStruct((hid, width), F32),
    ]
    spread = (n_dp, n_t, rows_block, width) if inside else (1, 1, 16, LANES)
    wide, long = ceil_to(padded, LANES), ceil_to(rooms, LANES)
    rows_f, rows_b = VMEM((padded, width), F32), VMEM((padded, width), BF16)
    slots_b, units_b = VMEM((n_dp, rooms, width), BF16), VMEM((n_t, n_dp, rooms, hid), BF16)
    in_b, out_b = (VMEM((n_t,) + shape, BF16) for shape in ((width, hid), (hid, width)))
    in_more, out_more = (VMEM((n_t + 1,) + shape, BF16) for shape in ((width, hid), (hid, width)))
    scratch = [VMEM((width, hid), F32), VMEM((hid, width), F32)]
    scratch += [VMEM((rows_block, width), BF16), VMEM(spread, BF16)]
    scratch += [rows_f, rows_f, VMEM((padded, padded), F32), rows_f, VMEM((padded, LANES), F32)]
    scratch += [VMEM((wide, LANES), F32), VMEM((LANES, wide), F32), VMEM((8, LANES), F32)]
    scratch += [VMEM((LANES, long), F32), VMEM((long, LANES), F32)] + [VMEM((n_dp, 8, long), F32)] * 4
    scratch += [rows_b] * 8 + [slots_b] * 6 + [units_b] * 2
    scratch += [in_b, out_b, in_b, out_b, in_more, out_more]
    scratch += [DMA, DMA((n_dp,))] + [DMA((2,))] * 4 + [DMA] * 6 + [DMA((2,))] + Spread.scratch(n_t) * 2 + Collect.scratch(n_t) * 2
    if inside:
        scratch += Gather.scratch(n_dp, n_t) * 2 + Reduce.scratch(n_dp, n_t, 1, (shard, width))
        scratch += Reduce.scratch(n_dp, n_t, width // LANES, (3 * shard, LANES))
        scratch += Reduce.scratch(n_dp, n_t, 1, (shard, LANES))
    whole, anywhere = pl.BlockSpec(memory_space=VMEM), pl.BlockSpec(memory_space=pl.ANY)
    return pl.pallas_call(
        partial(step_kernel, cfg),
        out_shape=outs,
        in_specs=[whole] * 3 + [anywhere] * 2 + [whole] * len(shared),
        out_specs=[whole] * 3 + [anywhere] * 2,
        scratch_shapes=scratch,
        compiler_params=pltpu.CompilerParams(
            collective_id=cid, has_side_effects=True, vmem_limit_bytes=60 * 2**20
        ),
        name="step_" + str(rooms),
    )(x, cot, routes, e_in, e_out, *shared)


def lay_kernel(shard, experts, out_ref, gx_ref, sum_ref, in_ref, outer_ref, *outs):
    outs[0][...] = out_ref[...]
    outs[1][...] = gx_ref[...]
    for at, spot in ((0, 4), (1, 5), (2, 6), (OUT, 7)):
        outs[spot][...] = sum_ref[at * shard : (at + 1) * shard, :]
    small = sum_ref[SMALL * shard : (SMALL + 1) * shard, :LANES]
    row, column = (lax.broadcasted_iota(jnp.int32, (shard, shard), axis) for axis in (0, 1))
    for at, spot in enumerate((2, 3, 8, 9)):
        upright = small[:, experts + at : experts + at + 1]
        outs[spot][...] = jnp.sum(jnp.where(row == column, upright, 0.0), axis=0, keepdims=True)
    for at in range(experts):
        outs[10][at : at + 1, :] = jnp.sum(jnp.where(row == column, small[:, at : at + 1], 0.0), axis=0, keepdims=True)
    outs[11][...] = in_ref[...]
    outs[12][...] = outer_ref[...]


def lay_out(shard, experts, *args):
    rows, width = args[0].shape
    line = jax.ShapeDtypeStruct((1, shard), F32)
    square = jax.ShapeDtypeStruct((shard, width), F32)
    outs = [jax.ShapeDtypeStruct((rows, width), BF16)] * 2 + [line] * 2 + [square] * 4 + [line] * 2
    outs += [jax.ShapeDtypeStruct((experts, shard), F32)]
    outs += [jax.ShapeDtypeStruct(arg.shape, F32) for arg in args[3:]]

    def full(shape):
        return pl.BlockSpec(shape, lambda i: (0,) * len(shape))

    return pl.pallas_call(
        partial(lay_kernel, shard, experts),
        grid=(1,),
        out_shape=outs,
        in_specs=[full(arg.shape) for arg in args],
        out_specs=[full(out.shape) for out in outs],
        compiler_params=pltpu.CompilerParams(vmem_limit_bytes=32 * 2**20),
        name="outputs",
    )(*args)


def route_pairs(routes, t, row_count, experts, capacity):
    tok_count = routes.shape[0]
    ids = jnp.arange(experts, dtype=jnp.int32)[None, :]
    start = t * row_count
    rows = lax.dynamic_slice_in_dim(routes, start, row_count, 0)
    before = (jnp.arange(tok_count, dtype=jnp.int32) < start)[:, None]
    all_first = routes[:, 0:1] == ids
    all_second = routes[:, 1:2] == ids
    base_first = jnp.sum((all_first & before).astype(jnp.int32), axis=0)
    total_first = jnp.sum(all_first.astype(jnp.int32), axis=0)
    base_second = jnp.sum((all_second & before).astype(jnp.int32), axis=0)
    hot_first = rows[:, 0:1] == ids
    hot_second = rows[:, 1:2] == ids
    at = jnp.arange(row_count, dtype=jnp.int32)
    lower = (at[:, None] > at[None, :]).astype(BF16)
    both = jnp.concatenate([hot_first, hot_second], axis=1).astype(BF16)
    earlier = nn(lower, both).astype(jnp.int32)
    own_first = jnp.sum(hot_first.astype(jnp.int32), axis=0)
    rank_first = earlier[:, :experts]
    rank_second = earlier[:, experts:] + own_first
    place_first = rank_first + base_first
    place_second = earlier[:, experts:] + total_first + base_second
    first = jnp.sum(jnp.where(hot_first & (place_first < capacity), rank_first + 1, 0), axis=1) - 1
    second = jnp.sum(jnp.where(hot_second & (place_second < capacity), rank_second + 1, 0), axis=1) - 1
    return rows, first, second


def per_device(
    n_dp,
    n_t,
    inputs,
    cotangent,
    routes,
    gain_attn,
    shift_attn,
    query_w,
    key_w,
    value_w,
    out_w,
    gain_moe,
    shift_moe,
    router_w,
    expert_in,
    expert_out,
):
    t = lax.axis_index("tensor")
    shard, width = query_w.shape
    experts = router_w.shape[1]
    tok_count = routes.shape[0]
    rows = inputs.shape[0]
    hid = expert_in.shape[2]
    padded = ceil_to(rows, 16)
    capacity = (5 * tok_count + 2 * experts - 1) // (2 * experts)
    inside = shard % 16 == 0
    every = ("dp", "tensor")
    lines = (gain_attn, shift_attn, gain_moe, shift_moe)

    def stack():
        small = jnp.concatenate([router_w] + [line[:, None] for line in lines], axis=1)
        small = jnp.pad(small, ((0, 0), (0, width - small.shape[1])))
        return jnp.stack([query_w, key_w, value_w, small, out_w]).astype(BF16)

    if inside:
        shared = [query_w, key_w, value_w, out_w, router_w.T] + [line[None, :] for line in lines]
    else:
        shared = [lax.all_gather(stack(), every, axis=1, tiled=True)]

    def finish(results):
        summed = results[2]
        if not inside:
            summed = lax.psum_scatter(summed, every, scatter_dimension=1, tiled=True).reshape(5 * shard, width)
        outs = lay_out(shard, experts, results[0], results[1], summed, *results[3:])
        return tuple(outs)

    def slow(_):
        rooms = ceil_to(rows, 16)
        cfg = (n_dp, n_t, rows, padded, width, experts, rooms, shard, inside)
        route_rows, first_rank, second_rank = route_pairs(routes, t, rows, experts, capacity)

        def slot(choice, rank):
            return jnp.where(rank >= 0, choice * rooms + rank, -1)

        slots = jnp.stack([slot(route_rows[:, 0], first_rank), slot(route_rows[:, 1], second_rank)])
        slots = jnp.pad(slots, ((0, 0), (0, padded - rows)), constant_values=-1)
        cols = jnp.concatenate([jnp.pad(route_rows, ((0, padded - rows), (0, 0))), slots.T], axis=1)
        block = stack().reshape(5 * shard, width) if inside else shared[0]
        kept = forward(cfg, 1, inputs, cotangent, cols, slots, block)

        def turn(k):
            return [(i, (i + k) % n_t) for i in range(n_t)]

        both = jnp.stack([expert_in[0].T, expert_out[0]]).astype(BF16)
        parts = [both] + [lax.ppermute(both, "tensor", turn(k)) for k in range(1, n_t)]
        w_in, w_out = (jnp.concatenate([part[i] for part in parts], axis=0) for i in range(2))
        returned, back, grad_inner, grad_outer = run_expert(
            kept[1].reshape(n_dp * rooms, width), kept[2].reshape(n_dp * rooms, width), w_in, w_out
        )
        both = jnp.stack([grad_inner.reshape(n_t, hid, width), grad_outer.reshape(n_t, hid, width)], axis=1)
        total = both[0].astype(F32)
        for k in range(1, n_t):
            total = total + lax.ppermute(both[k], "tensor", turn(-k)).astype(F32)
        results = backward(
            cfg,
            2,
            returned.reshape(n_dp, rooms, width),
            back.reshape(n_dp, rooms, width),
            inputs,
            cotangent,
            cols,
            kept[0] if inside else block,
            *kept[3:],
        )
        return finish((*results, total[0].T, total[1]))

    rooms = min(ceil_to((7 * rows + 2 * experts - 1) // (2 * experts), 16), ceil_to(rows, 16))
    cfg = (n_dp, n_t, rows, padded, width, experts, rooms, shard, inside, hid)
    fast = run_step(cfg, 0, inputs, cotangent, routes.T, expert_in[0], expert_out[0], shared)
    if inside:
        crowded = fast[2][SMALL * shard, experts + 4] > 0.5
    else:
        crowded = lax.psum(fast[2][SMALL, 0, experts + 4], every) > 0.5
    outs = lax.cond(crowded, slow, finish, tuple(fast))
    lined = [out.reshape(shard) if at in (2, 3, 8, 9) else out for at, out in enumerate(outs)]
    lined[10], lined[11], lined[12] = lined[10].T, lined[11][None], lined[12][None]
    return tuple(lined)


def solution(mesh):
    every = ("dp", "tensor")
    rows, line = P(every, None), P(every)
    w_in, w_out = P("dp", None, "tensor"), P("dp", "tensor", None)
    return jax.shard_map(
        partial(per_device, mesh.shape["dp"], mesh.shape["tensor"]),
        mesh=mesh,
        in_specs=(rows, rows, P("dp", None), line, line, rows, rows, rows, rows, line, line, rows, w_in, w_out),
        out_specs=(rows, rows, line, line, rows, rows, rows, rows, line, line, rows, w_in, w_out),
        check_vma=False,
    )
```

```python
from functools import partial

import jax
import jax.numpy as jnp
from jax import lax
from jax.experimental import pallas as pl
from jax.experimental.pallas import tpu as pltpu
from jax.sharding import PartitionSpec as P

SEQ = 197
HEAD_DIM = 64
LANES = 128
MESH = pl.DeviceIdType.MESH
F32 = jnp.float32
BF16 = jnp.bfloat16
VMEM = pltpu.VMEM
DMA = pltpu.SemaphoreType.DMA
SMALL, OUT = 3, 4


def ceil_to(value, unit):
    return (value + unit - 1) // unit * unit


def nn(left, right):
    return lax.dot_general(left, right, (((1,), (0,)), ((), ())), preferred_element_type=F32)


def nt(left, right):
    return lax.dot_general(left, right, (((1,), (1,)), ((), ())), preferred_element_type=F32)


def tn(left, right):
    return lax.dot_general(left, right, (((0,), (0,)), ((), ())), preferred_element_type=F32)


def remote(src, dst, send, recv, device):
    return pltpu.make_async_remote_copy(
        src_ref=src, dst_ref=dst, send_sem=send, recv_sem=recv, device_id=device, device_id_type=MESH
    )


def meet(n_dp, n_t, z_too):
    dp = lax.axis_index("dp")
    t = lax.axis_index("tensor")
    bar = pltpu.get_barrier_semaphore()
    for k in range(1, n_dp):
        pl.semaphore_signal(bar, inc=1, device_id={"dp": lax.rem(dp + k, n_dp)}, device_id_type=MESH)
    if z_too:
        for k in range(1, n_t):
            pl.semaphore_signal(bar, inc=1, device_id={"tensor": lax.rem(t + k, n_t)}, device_id_type=MESH)
    pl.semaphore_wait(bar, n_dp - 1 + (n_t - 1 if z_too else 0))


class Gather:
    def __init__(self, n_dp, n_t, first, count, lanes, block, out, own_sem, z_send, z_recv, c_send, c_recv, k_send, k_recv):
        self.n_t, self.n_chip = n_t, n_dp // 2
        self.rows, self.lanes = pl.ds(first, count), pl.ds(0, lanes)
        self.block, self.out, self.own_sem = block.at[self.rows, self.lanes], out, own_sem
        self.z_sems, self.c_sems, self.k_sems = (z_send, z_recv), (c_send, c_recv), (k_send, k_recv)
        self.dp, self.t = lax.axis_index("dp"), lax.axis_index("tensor")
        self.chip, self.core = self.dp // 2, lax.rem(self.dp, 2)
        self.other = self.chip * 2 + 1 - self.core

    @staticmethod
    def scratch(n_dp, n_t):
        n_chip = n_dp // 2
        return [DMA, DMA, DMA((n_t,)), DMA, DMA((n_chip, n_t)), DMA, DMA]

    def place(self, dp, t):
        return self.out.at[dp, t, self.rows, self.lanes]

    def z_copy(self, k):
        send, recv = self.z_sems
        to = lax.rem(self.t + k, self.n_t)
        return remote(self.block, self.place(self.dp, self.t), send, recv.at[k], {"tensor": to})

    def chip_copy(self, k, j):
        send, recv = self.c_sems
        here = self.place(self.dp, lax.rem(self.t + self.n_t - j, self.n_t))
        to = lax.rem(self.chip + k, self.n_chip) * 2 + self.core
        return remote(self.block if j == 0 else here, here, send, recv.at[k, j], {"dp": to})

    def core_copy(self, k, j):
        send, recv = self.k_sems
        src = lax.rem(self.chip + self.n_chip - k, self.n_chip) * 2 + self.core
        here = self.place(src, lax.rem(self.t + self.n_t - j, self.n_t))
        own = k == 0 and j == 0
        return remote(self.block if own else here, here, send, recv, {"dp": self.other})

    def own_copy(self):
        return pltpu.make_async_copy(self.block, self.place(self.dp, self.t), self.own_sem)

    def start(self):
        for k in range(1, self.n_t):
            self.z_copy(k).start()
        self.own_copy().start()
        for k in range(1, self.n_chip):
            self.chip_copy(k, 0).start()
        self.core_copy(0, 0).start()

    def pass_to_chips(self):
        for j in range(1, self.n_t):
            self.z_copy(j).wait_recv()
            for k in range(1, self.n_chip):
                self.chip_copy(k, j).start()
            self.core_copy(0, j).start()

    def pass_to_core(self):
        for j in range(self.n_t):
            for k in range(1, self.n_chip):
                self.chip_copy(k, j).wait_recv()
                self.core_copy(k, j).start()

    def arrive(self):
        self.own_copy().wait()
        self.wait_bytes(self.out.at[pl.ds(0, self.n_chip), :, self.rows, self.lanes], self.k_sems[1])

    @staticmethod
    def wait_bytes(part, sem):
        pltpu.make_async_copy(part, part, sem).wait()

    def drain(self):
        self.wait_bytes(self.out.at[0, pl.ds(0, self.n_t - 1), self.rows, self.lanes], self.z_sems[0])
        self.wait_bytes(self.out.at[pl.ds(0, self.n_chip - 1), :, self.rows, self.lanes], self.c_sems[0])
        self.wait_bytes(self.out.at[pl.ds(0, self.n_chip), :, self.rows, self.lanes], self.k_sems[0])


class Scatter:
    def __init__(
        self, n_dp, n_t, grads, out, core_in, half, chip_in, part, z_in, k_send, k_recv, c_send, c_recv, z_send, z_recv
    ):
        self.n_t, self.n_chip = n_t, n_dp // 2
        self.grads, self.out = grads, out
        self.core_in, self.half, self.chip_in, self.part, self.z_in = core_in, half, chip_in, part, z_in
        self.k_sems, self.c_sems, self.z_sems = (k_send, k_recv), (c_send, c_recv), (z_send, z_recv)
        self.dp, self.t = lax.axis_index("dp"), lax.axis_index("tensor")
        self.chip, self.core = self.dp // 2, lax.rem(self.dp, 2)
        self.other = self.chip * 2 + 1 - self.core

    @staticmethod
    def scratch(n_dp, n_t, block):
        n_chip = n_dp // 2
        buffers = [VMEM((n_chip, n_t) + block, BF16)] + [VMEM((n_chip - 1, n_t) + block, BF16)] * 2
        buffers += [VMEM((n_t - 1,) + block, BF16)] * 2
        return buffers + [DMA((n_chip,))] * 4 + [DMA((n_t,))] * 2

    def core_copy(self, k):
        to = lax.rem(self.chip + k, self.n_chip)
        src = self.grads.at[to * 2 + 1 - self.core]
        return remote(src, self.core_in.at[k], self.k_sems[0].at[k], self.k_sems[1].at[k], {"dp": self.other})

    def chip_copy(self, k):
        to = lax.rem(self.chip + k, self.n_chip) * 2 + self.core
        return remote(self.half.at[k - 1], self.chip_in.at[k - 1], self.c_sems[0].at[k], self.c_sems[1].at[k], {"dp": to})

    def z_copy(self, k):
        to = lax.rem(self.t + k, self.n_t)
        return remote(self.part.at[k - 1], self.z_in.at[k - 1], self.z_sems[0].at[k], self.z_sems[1].at[k], {"tensor": to})

    def run(self, between=None, after=None):
        n_chip, n_t = self.n_chip, self.n_t
        order = list(range(1, n_chip)) + [0]
        for k in order:
            self.core_copy(k).start()
        for k in order:
            self.core_copy(k).wait_recv()
            if k > 0:
                to = lax.rem(self.chip + k, n_chip) * 2 + self.core
                self.half[k - 1] = (self.grads[to].astype(F32) + self.core_in[k].astype(F32)).astype(BF16)
                self.chip_copy(k).start()
        if between is not None:
            between()
        for k in range(1, n_chip):
            self.chip_copy(k).wait_recv()
        for k in list(range(1, n_t)) + [0]:
            row = lax.rem(self.t + k, n_t)
            total = self.grads[self.dp, row].astype(F32) + self.core_in[0, row].astype(F32)
            for c in range(1, n_chip):
                total = total + self.chip_in[c - 1, row].astype(F32)
            if k > 0:
                self.part[k - 1] = total.astype(BF16)
                self.z_copy(k).start()
            else:
                self.out[...] = total
        if after is not None:
            after()
        for k in range(1, n_t):
            self.z_copy(k).wait_recv()
            self.out[...] += self.z_in[k - 1].astype(F32)
        for k in range(n_chip):
            self.core_copy(k).wait_send()
        for k in range(1, n_chip):
            self.chip_copy(k).wait_send()
        for k in range(1, n_t):
            self.z_copy(k).wait_send()


class Reduce:
    def __init__(self, n_dp, n_t, out, grads, core_in, half, chip_in, part, z_in, *sems):
        self.n_t, self.n_chip, self.out = n_t, n_dp // 2, out
        self.grads, self.core_in, self.half = grads, core_in, half
        self.chip_in, self.part, self.z_in = chip_in, part, z_in
        self.k_sems, self.c_sems, self.z_sems = sems[0:3], sems[3:5], sems[5:7]
        self.dp, self.t = lax.axis_index("dp"), lax.axis_index("tensor")
        self.chip, self.core = self.dp // 2, lax.rem(self.dp, 2)
        self.other = self.chip * 2 + 1 - self.core

    @staticmethod
    def scratch(n_dp, n_t, parts, block):
        n_chip = n_dp // 2
        sizes = [(n_dp, n_t), (n_chip, n_t), (n_chip - 1, n_t), (n_chip - 1, n_t), (n_t - 1,), (n_t - 1,)]
        return [VMEM((parts,) + size + block, BF16) for size in sizes] + [DMA((parts,))] * 7

    def put(self, p, first, value):
        n_dp, n_t = self.n_chip * 2, self.n_t
        count, lanes = value.shape[0] // (n_dp * n_t), value.shape[1]
        self.grads[p, :, :, first : first + count, :] = value.astype(BF16).reshape(n_dp, n_t, count, lanes)

    def core_copy(self, p, k):
        src = self.grads.at[p, lax.rem(self.chip + k, self.n_chip) * 2 + 1 - self.core]
        send, far, near = self.k_sems
        recv = near if isinstance(k, int) and k == 0 else far
        return remote(src, self.core_in.at[p, k], send.at[p], recv.at[p], {"dp": self.other})

    def chip_copy(self, p, k):
        to = lax.rem(self.chip + k, self.n_chip) * 2 + self.core
        send, recv = self.c_sems
        return remote(self.half.at[p, k - 1], self.chip_in.at[p, k - 1], send.at[p], recv.at[p], {"dp": to})

    def z_copy(self, p, k):
        to = lax.rem(self.t + k, self.n_t)
        send, recv = self.z_sems
        return remote(self.part.at[p, k - 1], self.z_in.at[p, k - 1], send.at[p], recv.at[p], {"tensor": to})

    def to_core(self, p):
        for k in list(range(1, self.n_chip)) + [0]:
            self.core_copy(p, k).start()

    def to_chips(self, p):
        Gather.wait_bytes(self.core_in.at[p, pl.ds(1, self.n_chip - 1)], self.k_sems[1].at[p])
        for k in range(1, self.n_chip):
            to = lax.rem(self.chip + k, self.n_chip) * 2 + self.core
            self.half[p, k - 1] = (self.grads[p, to].astype(F32) + self.core_in[p, k].astype(F32)).astype(BF16)
            self.chip_copy(p, k).start()

    def to_line(self, p):
        self.core_copy(p, 0).wait_recv()
        Gather.wait_bytes(self.chip_in.at[p], self.c_sems[1].at[p])
        for k in list(range(1, self.n_t)) + [0]:
            row = lax.rem(self.t + k, self.n_t)
            total = self.grads[p, self.dp, row].astype(F32) + self.core_in[p, 0, row].astype(F32)
            for c in range(1, self.n_chip):
                total = total + self.chip_in[p, c - 1, row].astype(F32)
            if k > 0:
                self.part[p, k - 1] = total.astype(BF16)
                self.z_copy(p, k).start()
            else:
                self.out(p)[...] = total

    def finish(self, p):
        Gather.wait_bytes(self.z_in.at[p], self.z_sems[1].at[p])
        for k in range(1, self.n_t):
            self.out(p)[...] += self.z_in[p, k - 1].astype(F32)
        Gather.wait_bytes(self.part.at[p], self.z_sems[0].at[p])
        Gather.wait_bytes(self.core_in.at[p], self.k_sems[0].at[p])
        Gather.wait_bytes(self.half.at[p], self.c_sems[0].at[p])


def greet(n_dp, n_t):
    dp, t = lax.axis_index("dp"), lax.axis_index("tensor")
    bar = pltpu.get_barrier_semaphore()
    for k in range(1, n_dp):
        pl.semaphore_signal(bar, inc=1, device_id={"dp": lax.rem(dp + k, n_dp)}, device_id_type=MESH)
    for k in range(1, n_t):
        pl.semaphore_signal(bar, inc=1, device_id={"tensor": lax.rem(t + k, n_t)}, device_id_type=MESH)


def greeted(n_dp, n_t):
    pl.semaphore_wait(pltpu.get_barrier_semaphore(), n_dp - 1 + n_t - 1)


class Exchange:
    def __init__(self, n_dp, src, dst, rows, send, recv, single):
        self.n_dp, self.src, self.dst, self.rows, self.send, self.recv = n_dp, src, dst, rows, send, recv
        self.dp, self.single = lax.axis_index("dp"), single

    def copy(self, k):
        to = lax.rem(self.dp + k, self.n_dp)
        recv = self.recv.at[k] if self.single else self.recv
        return remote(self.src.at[to, self.rows], self.dst.at[self.dp, self.rows], self.send, recv, {"dp": to})

    def start(self, k):
        self.copy(k).start()

    def start_all(self):
        for k in range(1, self.n_dp):
            self.start(k)

    def wait_from(self, k):
        self.copy(k).wait_recv()

    def wait_all(self):
        part = self.dst.at[pl.ds(0, self.n_dp - 1), self.rows]
        pltpu.make_async_copy(part, part, self.recv).wait()

    def wait_sent(self):
        part = self.src.at[pl.ds(0, self.n_dp - 1), self.rows]
        pltpu.make_async_copy(part, part, self.send).wait()


class Spread:
    def __init__(self, n_t, parts, send, recv):
        self.n_t, self.t, self.parts, self.send, self.recv = n_t, lax.axis_index("tensor"), parts, send, recv

    @staticmethod
    def scratch(n_t):
        return [DMA((2, n_t)), DMA((n_t,))]

    def hop(self, j, way):
        here = self.parts.at[j]
        return remote(here, here, self.send.at[way, j], self.recv.at[j], {"tensor": self.t + 1 - 2 * way})

    def step(self, s):
        for way, j, in_line, onward in (
            (0, self.t - s, self.t - s >= 0, self.t + 1 < self.n_t),
            (1, self.t + s, self.t + s < self.n_t, self.t > 0),
        ):
            if s > 0:

                @pl.when(in_line)
                def _():
                    self.hop(j, way).wait_recv()

            @pl.when(in_line & onward)
            def _():
                self.hop(j, way).start()

    def drain(self):
        for s in range(self.n_t):

            @pl.when((self.t - s >= 0) & (self.t + 1 < self.n_t))
            def _():
                self.hop(self.t - s, 0).wait_send()

            @pl.when((self.t + s < self.n_t) & (self.t > 0))
            def _():
                self.hop(self.t + s, 1).wait_send()


class Collect:
    def __init__(self, n_t, parts, came, send, recv):
        self.n_t, self.t, self.parts, self.came, self.send, self.recv = (
            n_t,
            lax.axis_index("tensor"),
            parts,
            came,
            send,
            recv,
        )

    @staticmethod
    def scratch(n_t):
        return [DMA((n_t,)), DMA((n_t + 1,))]

    def hop(self, j, way):
        slot = j if way == 0 else jnp.where(j == self.t - 1, self.n_t, j)
        to = self.t + 1 - 2 * way
        return remote(self.parts.at[j], self.came.at[slot], self.send.at[j], self.recv.at[slot], {"tensor": to})

    def wait_slot(self, slot):
        remote(self.parts.at[0], self.came.at[slot], self.send.at[0], self.recv.at[slot], {"tensor": self.t}).wait_recv()

    def begin(self, j):
        @pl.when((self.t == 0) & (j > 0))
        def _():
            self.hop(j, 0).start()

        @pl.when((self.t == self.n_t - 1) & (j < self.n_t - 1))
        def _():
            self.hop(j, 1).start()

    def step(self, e, far):
        if far:
            right, left = self.n_t - 1 - e + self.t, e - self.n_t + 1 + self.t
        else:
            right, left = e - self.t + 2, 2 * self.n_t - 4 - e - self.t
        for way, j, mine in (
            (0, right, (self.t >= 1) & (right <= self.n_t - 1) & (right > self.t)),
            (1, left, (self.t <= self.n_t - 2) & (left >= 0) & (left < self.t)),
        ):

            @pl.when(mine)
            def _():
                self.wait_slot(j)
                self.parts[j] = (self.parts[j].astype(F32) + self.came[j].astype(F32)).astype(BF16)
                self.hop(j, way).start()

    def finish(self, result):
        result[...] = self.parts[self.t].astype(F32)

        @pl.when(self.t > 0)
        def _():
            self.wait_slot(self.t)
            result[...] += self.came[self.t].astype(F32)

        @pl.when(self.t < self.n_t - 1)
        def _():
            self.wait_slot(self.n_t)
            result[...] += self.came[self.n_t].astype(F32)

        for j in range(self.n_t):

            @pl.when(self.t < j)
            def _():
                self.hop(j, 0).wait_send()

            @pl.when(self.t > j)
            def _():
                self.hop(j, 1).wait_send()


def centre(values):
    centred = values - jnp.mean(values, axis=1, keepdims=True)
    inverse = lax.rsqrt(jnp.mean(centred * centred, axis=1, keepdims=True) + 1e-06)
    return centred * inverse, inverse


def norm_back(grad, unit, inverse, gain):
    scaled = grad * gain
    back = inverse * (
        scaled
        - jnp.mean(scaled, axis=1, keepdims=True)
        - unit * jnp.mean(scaled * unit, axis=1, keepdims=True)
    )
    return back, jnp.sum(grad * unit, axis=0, keepdims=True), jnp.sum(grad, axis=0, keepdims=True)


def norm_picks(experts):
    row, lane = (lax.broadcasted_iota(jnp.int32, (8, LANES), axis) for axis in (0, 1))
    return (row + experts == lane).astype(F32).astype(BF16)


def norm_rows(small, experts):
    return nt(norm_picks(experts), small)


def small_grads(experts, grad_router, rows):
    line = lax.broadcasted_iota(jnp.int32, (8, rows[0].shape[1]), 0)
    stack = sum(jnp.where(line == at, row, 0.0) for at, row in enumerate(rows))
    return grad_router + tn(stack.astype(BF16), norm_picks(experts))


def image_bias(rows, padded):
    line = lax.broadcasted_iota(jnp.int32, (padded, padded), 0)
    column = lax.broadcasted_iota(jnp.int32, (padded, padded), 1)
    image_line, image_column = jnp.zeros_like(line), jnp.zeros_like(column)
    for at in range(SEQ, rows + 1, SEQ):
        image_line += (line >= at).astype(jnp.int32)
        image_column += (column >= at).astype(jnp.int32)
    return jnp.where((image_line == image_column) & (column < rows), 0.0, -1e30)


def half_masks():
    lane = lax.broadcasted_iota(jnp.int32, (1, LANES), 1)
    low = (lane < HEAD_DIM).astype(F32)
    return low.astype(BF16), (1.0 - low).astype(BF16)


def soft_scores(query, key, bias):
    scores = nt(query, key) * HEAD_DIM ** (-0.5) + bias
    power = jnp.exp(scores - jnp.max(scores, axis=1, keepdims=True))
    return power * (1.0 / jnp.sum(power, axis=1, keepdims=True))


def router_probs(logits, experts):
    lane = lax.broadcasted_iota(jnp.int32, logits.shape, 1)
    inside = lane < experts
    kept = jnp.where(inside, logits, -1e30)
    power = jnp.where(inside, jnp.exp(kept - jnp.max(kept, axis=1, keepdims=True)), 0.0)
    return power * (1.0 / jnp.sum(power, axis=1, keepdims=True))


def pick_gate(probs, choice):
    lane = lax.broadcasted_iota(jnp.int32, probs.shape, 1)
    return jnp.sum(jnp.where(lane == choice, probs, 0.0), axis=1, keepdims=True)


class Weights:
    def __init__(self, shard, width, gathered=None, whole=None):
        self.shard, self.width, self.gathered, self.whole = shard, width, gathered, whole

    def __call__(self, at):
        if self.whole is not None:
            return self.whole[at]
        part = self.gathered[:, :, at * self.shard : (at + 1) * self.shard, :]
        return part.reshape(self.width, self.width)

    def small(self):
        if self.whole is not None:
            return self.whole[SMALL, :, :LANES]
        part = self.gathered[:, :, SMALL * self.shard : (SMALL + 1) * self.shard, :LANES]
        return part.reshape(self.width, LANES)


def gelu_parts(hidden):
    bell = jnp.exp(-0.5 * hidden * hidden)
    near = 1.0 / (1.0 + 0.23164189 * jnp.abs(hidden))
    tail = near * (
        0.127414796 + near * (-0.142248368 + near * (0.7107068705 + near * (-0.7265760135 + near * 0.5307027145)))
    )
    tail = tail * bell
    share = jnp.where(hidden < 0.0, tail, 1.0 - tail)
    return hidden * share, share + hidden * bell * 0.3989422804014327


def forward_kernel(cfg, *refs):
    n_dp, n_t, rows, padded, width, experts, rooms, shard, inside = cfg
    refs = list(refs)

    def take(count):
        got = refs[:count]
        del refs[:count]
        return got

    x_ref, cot_ref, cols_ref, slots_ref, block_ref = take(5)
    gathered, recv_d, recv_s, res_ref, moe_ref, q_ref, k_ref, v_ref, mix_ref, norm_ref, probs_ref = take(11)
    full, cot_full, bias, send_d, send_s, d_send, d_recv, s_send, s_recv = take(9)
    dp = lax.axis_index("dp")
    meet(n_dp, n_t, inside)
    if inside:
        gather = Gather(n_dp, n_t, 0, block_ref.shape[0], width, block_ref, gathered, *refs)
        gather.start()
        weights = Weights(shard, width, gathered=gathered)
    else:
        gathered[...] = jnp.zeros_like(gathered)
        weights = Weights(shard, width, whole=block_ref)

    full[rows - rows % 8 :, :] = jnp.zeros((padded - rows + rows % 8, width), F32)
    full[:rows, :] = x_ref[...].astype(F32)
    cot_full[rows - rows % 8 :, :] = jnp.zeros((padded - rows + rows % 8, width), F32)
    cot_full[:rows, :] = cot_ref[...].astype(F32)
    bias[...] = image_bias(rows, padded)
    unit, _ = centre(full[...])
    norm_ref[...] = unit.astype(BF16)
    if inside:
        gather.pass_to_chips()
        gather.pass_to_core()
        gather.arrive()
        gather.drain()

    norms = norm_rows(weights.small(), experts)
    unit, _ = centre(full[...])
    normed = (unit * norms[0:1] + norms[1:2]).astype(BF16)
    norm_ref[...] = normed
    q_ref[...] = nn(normed, weights(0)).astype(BF16)
    k_ref[...] = nn(normed, weights(1)).astype(BF16)
    v_ref[...] = nn(normed, weights(2)).astype(BF16)
    low, high = half_masks()

    def heads(j, carry):
        at = pl.ds(pl.multiple_of(j * LANES, LANES), LANES)
        query, key, value = q_ref[:, at], k_ref[:, at], v_ref[:, at]
        first = nn(soft_scores(query * low, key, bias[...]).astype(BF16), value)
        second = nn(soft_scores(query * high, key, bias[...]).astype(BF16), value)
        mix_ref[:, at] = (first * low.astype(F32) + second * high.astype(F32)).astype(BF16)
        return carry

    lax.fori_loop(0, width // LANES, heads, 0)
    residual = full[...] + nn(mix_ref[...], weights(OUT))
    res_ref[...] = residual
    unit, _ = centre(residual)
    moe = (unit * norms[2:3] + norms[3:4]).astype(BF16)
    moe_ref[...] = moe
    probs = router_probs(nn(moe, weights.small()), experts)
    probs_ref[...] = probs
    cot = cot_full[...]
    full[...] = pick_gate(probs, cols_ref[:, 0:1]) * cot
    cot_full[...] = pick_gate(probs, cols_ref[:, 1:2]) * cot

    def selectors(p):
        slot = lax.broadcasted_iota(jnp.int32, (rooms, padded), 0) + p * rooms
        first = (slot == slots_ref[0:1, :]).astype(F32)
        second = (slot == slots_ref[1:2, :]).astype(F32)
        return first, second

    def d_copy(k):
        to = lax.rem(dp + k, n_dp)
        return remote(send_d.at[to], recv_d.at[dp], d_send.at[k], d_recv.at[k], {"dp": to})

    def s_copy(k):
        to = lax.rem(dp + k, n_dp)
        return remote(send_s.at[to], recv_s.at[dp], s_send.at[k], s_recv.at[k], {"dp": to})

    def dispatch(k, carry):
        to = lax.rem(dp + k, n_dp)
        first, second = selectors(to)
        send_d[to] = nn((first + second).astype(BF16), moe_ref[...]).astype(BF16)

        @pl.when(k > 0)
        def _():
            d_copy(k).start()

        return carry

    def dispatch_grad(k, carry):
        to = lax.rem(dp + k, n_dp)
        first, second = selectors(to)
        rows_grad = nn(first.astype(BF16), full[...].astype(BF16)) + nn(second.astype(BF16), cot_full[...].astype(BF16))
        send_s[to] = rows_grad.astype(BF16)

        @pl.when(k > 0)
        def _():
            s_copy(k).start()

        return carry

    lax.fori_loop(0, n_dp, dispatch, 0)
    lax.fori_loop(0, n_dp, dispatch_grad, 0)
    recv_d[dp] = send_d[dp]
    recv_s[dp] = send_s[dp]
    for k in range(1, n_dp):
        d_copy(k).wait()
    for k in range(1, n_dp):
        s_copy(k).wait()


def forward(cfg, cid, x, cot, cols, slots, block):
    n_dp, n_t, rows, padded, width, experts, rooms, shard, inside = cfg
    rows_block = ceil_to(5 * shard, 16)
    low = jax.ShapeDtypeStruct((padded, width), BF16)
    sent = jax.ShapeDtypeStruct((n_dp, rooms, width), BF16)
    gathered = (n_dp, n_t, rows_block, width) if inside else (1, 1, 16, LANES)
    outs = [jax.ShapeDtypeStruct(gathered, BF16), sent, sent, jax.ShapeDtypeStruct((padded, width), F32)]
    outs += [low] * 6 + [jax.ShapeDtypeStruct((padded, LANES), F32)]
    scratch = [
        VMEM((padded, width), F32),
        VMEM((padded, width), F32),
        VMEM((padded, padded), F32),
        VMEM((n_dp, rooms, width), BF16),
        VMEM((n_dp, rooms, width), BF16),
    ] + [DMA((n_dp,))] * 4
    if inside:
        scratch += Gather.scratch(n_dp, n_t)
    whole = pl.BlockSpec(memory_space=VMEM)
    return pl.pallas_call(
        partial(forward_kernel, cfg),
        out_shape=outs,
        in_specs=[whole] * 5,
        out_specs=[whole] * len(outs),
        scratch_shapes=scratch,
        compiler_params=pltpu.CompilerParams(
            collective_id=cid, has_side_effects=True, vmem_limit_bytes=56 * 2**20
        ),
        name="forward_" + str(rooms),
    )(x, cot, cols, slots, block)


def expert_kernel(chunks, d_ref, s_ref, w_in_ref, w_out_ref, ret_ref, back_ref, g_in_ref, g_out_ref, ret, back, g_in, g_out):
    step = pl.program_id(0)
    rows = d_ref.shape[0]
    chunk = rows // chunks

    @pl.when(step == 0)
    def _():
        ret[...] = jnp.zeros_like(ret)
        back[...] = jnp.zeros_like(back)

    g_in[...] = jnp.zeros_like(g_in)
    g_out[...] = jnp.zeros_like(g_out)
    w_in, w_out = w_in_ref[...], w_out_ref[...]

    def part(c, carry):
        at = pl.ds(pl.multiple_of(c * chunk, 16), chunk)
        took, slot_grad = d_ref[at, :], s_ref[at, :]
        active, slope = gelu_parts(nt(took, w_in))
        active = active.astype(BF16)
        grad_hidden = (nt(slot_grad, w_out) * slope).astype(BF16)
        ret[at, :] += nn(active, w_out)
        back[at, :] += nn(grad_hidden, w_in)
        g_out[...] += tn(active, slot_grad)
        g_in[...] += tn(grad_hidden, took)
        return carry

    lax.fori_loop(0, chunks, part, 0)
    g_in_ref[...] = g_in[...].astype(BF16)
    g_out_ref[...] = g_out[...].astype(BF16)

    @pl.when(step == pl.num_programs(0) - 1)
    def _():
        ret_ref[...] = ret[...].astype(BF16)
        back_ref[...] = back[...].astype(BF16)


def run_expert(took, slot_grad, w_in, w_out):
    rows, width = took.shape
    hidden = w_in.shape[0]
    block = 256
    chunks = next(c for c in range(max(1, rows // 400), rows + 1) if rows % c == 0 and (rows // c) % 16 == 0)
    whole = pl.BlockSpec((rows, width), lambda i: (0, 0))
    part = pl.BlockSpec((block, width), lambda i: (i, 0))
    low = jax.ShapeDtypeStruct((rows, width), BF16)
    grad = jax.ShapeDtypeStruct((hidden, width), BF16)
    return pl.pallas_call(
        partial(expert_kernel, chunks),
        grid=(hidden // block,),
        out_shape=[low, low, grad, grad],
        in_specs=[whole, whole, part, part],
        out_specs=[whole, whole, part, part],
        scratch_shapes=[
            VMEM((rows, width), F32),
            VMEM((rows, width), F32),
            VMEM((block, width), F32),
            VMEM((block, width), F32),
        ],
        compiler_params=pltpu.CompilerParams(vmem_limit_bytes=60 * 2**20),
        cost_estimate=pl.CostEstimate(
            flops=12 * rows * width * hidden, bytes_accessed=12 * rows * width + 8 * hidden * width, transcendentals=0
        ),
        name="expert_" + str(rows),
    )(took, slot_grad, w_in, w_out)


def backward_kernel(cfg, *refs):
    n_dp, n_t, rows, padded, width, experts, rooms, shard, inside = cfg
    refs = list(refs)

    def take(count):
        got = refs[:count]
        del refs[:count]
        return got

    ret_ref, back_ref, x_ref, cot_ref, cols_ref, weights_ref = take(6)
    res_ref, moe_ref, q_ref, k_ref, v_ref, mix_ref, norm_ref, probs_ref = take(8)
    out_ref, gx_ref, sum_ref = take(3)
    full, cot_full, bias, ret_in, back_in, grads, r_send, r_recv, b_send, b_recv = take(10)
    dq, dk, dv = take(3)
    dp = lax.axis_index("dp")
    meet(n_dp, n_t, inside)

    def r_copy(k):
        to = lax.rem(dp + k, n_dp)
        return remote(ret_ref.at[to], ret_in.at[dp], r_send.at[k], r_recv.at[k], {"dp": to})

    def b_copy(k):
        to = lax.rem(dp + k, n_dp)
        return remote(back_ref.at[to], back_in.at[dp], b_send.at[k], b_recv.at[k], {"dp": to})

    for k in range(1, n_dp):
        r_copy(k).start()
    for k in range(1, n_dp):
        b_copy(k).start()
    ret_in[dp] = ret_ref[dp]
    back_in[dp] = back_ref[dp]
    weights = Weights(shard, width, gathered=weights_ref) if inside else Weights(shard, width, whole=weights_ref)
    tail = rows - rows % 8
    full[tail:, :] = jnp.zeros((padded - tail, width), F32)
    full[:rows, :] = x_ref[...].astype(F32)
    cot_full[tail:, :] = jnp.zeros((padded - tail, width), F32)
    cot_full[:rows, :] = cot_ref[...].astype(F32)
    bias[...] = image_bias(rows, padded)
    norms = norm_rows(weights.small(), experts)
    slot_count = n_dp * rooms
    lane = lax.broadcasted_iota(jnp.int32, (padded, slot_count), 1)
    first = (lane == cols_ref[:, 2:3]).astype(F32)
    second = (lane == cols_ref[:, 3:4]).astype(F32)
    both = (first + second).astype(BF16)

    for k in range(1, n_dp):
        r_copy(k).wait()
    returned = ret_in[...].reshape(slot_count, width)
    first_rows = nn(first.astype(BF16), returned)
    second_rows = nn(second.astype(BF16), returned)
    probs = probs_ref[...]
    first_id, second_id = cols_ref[:, 0:1], cols_ref[:, 1:2]
    outcome = res_ref[...] + pick_gate(probs, first_id) * first_rows + pick_gate(probs, second_id) * second_rows
    out_ref[...] = outcome[:rows].astype(BF16)
    cot = cot_full[...]
    first_grad = jnp.sum(first_rows * cot, axis=1, keepdims=True)
    second_grad = jnp.sum(second_rows * cot, axis=1, keepdims=True)
    spot = lax.broadcasted_iota(jnp.int32, probs.shape, 1)
    grad_probs = jnp.where(spot == first_id, first_grad, 0.0) + jnp.where(spot == second_id, second_grad, 0.0)
    grad_logits = (probs * (grad_probs - jnp.sum(probs * grad_probs, axis=1, keepdims=True))).astype(BF16)
    grad_router = tn(moe_ref[...], grad_logits)

    for k in range(1, n_dp):
        b_copy(k).wait()
    grad_moe = nn(both, back_in[...].reshape(slot_count, width)) + nt(grad_logits, weights.small())
    unit, inverse = centre(res_ref[...])
    extra, gain_two, shift_two = norm_back(grad_moe, unit, inverse, norms[2:3])
    grad_residual = cot + extra
    cot_full[...] = grad_residual
    grad_attended = grad_residual.astype(BF16)
    n_all = n_dp * n_t

    def keep(at, value):
        if inside:
            grads[:, :, at * shard : (at + 1) * shard, :] = value.astype(BF16).reshape(n_dp, n_t, shard, width)
        else:
            sum_ref[at] = value

    keep(OUT, tn(mix_ref[...], grad_attended))
    mix_ref_grad = nt(grad_attended, weights(OUT)).astype(BF16)
    dq[...] = mix_ref_grad
    low, high = half_masks()
    low_f, high_f = low.astype(F32), high.astype(F32)
    scale = HEAD_DIM ** (-0.5)

    def heads(j, carry):
        at = pl.ds(pl.multiple_of(j * LANES, LANES), LANES)
        query, key, value, grad = q_ref[:, at], k_ref[:, at], v_ref[:, at], dq[:, at]
        for mask, mask_f in ((low, low_f), (high, high_f)):
            probs = soft_scores(query * mask, key, bias[...])
            grad_probs = nt(grad * mask, value)
            grad_scores = probs * (grad_probs - jnp.sum(probs * grad_probs, axis=1, keepdims=True))
            grad_scores = grad_scores.astype(BF16)
            part_v = tn(probs.astype(BF16), grad)
            part_q = nn(grad_scores, key) * scale
            part_k = tn(grad_scores, query) * scale
            if mask is low:
                sum_q, sum_k, sum_v = part_q * mask_f, part_k * mask_f, part_v * mask_f
            else:
                sum_q, sum_k, sum_v = sum_q + part_q * mask_f, sum_k + part_k * mask_f, sum_v + part_v * mask_f
        dq[:, at] = sum_q.astype(BF16)
        dk[:, at] = sum_k.astype(BF16)
        dv[:, at] = sum_v.astype(BF16)
        return carry

    lax.fori_loop(0, width // LANES, heads, 0)
    keep(0, tn(norm_ref[...], dq[...]))
    keep(1, tn(norm_ref[...], dk[...]))
    keep(2, tn(norm_ref[...], dv[...]))
    grad_normed = nt(dq[...], weights(0)) + nt(dk[...], weights(1)) + nt(dv[...], weights(2))
    unit, inverse = centre(full[...])
    extra, gain_one, shift_one = norm_back(grad_normed, unit, inverse, norms[0:1])
    gx_ref[...] = (cot_full[...] + extra)[:rows].astype(BF16)
    small = small_grads(experts, grad_router, (gain_one, shift_one, gain_two, shift_two))
    if inside:
        at = slice(SMALL * shard, (SMALL + 1) * shard)
        grads[:, :, at, :LANES] = small.astype(BF16).reshape(n_dp, n_t, shard, LANES)
        grads[:, :, at, LANES:] = jnp.zeros((n_dp, n_t, shard, width - LANES), BF16)
        Scatter(n_dp, n_t, grads, sum_ref, *refs).run()
    else:
        sum_ref[SMALL] = jnp.zeros((width, width), F32)
        sum_ref[SMALL, :, :LANES] = small


def backward(cfg, cid, *args):
    n_dp, n_t, rows, padded, width, experts, rooms, shard, inside = cfg
    rows_block = ceil_to(5 * shard, 16)
    total = (rows_block, width) if inside else (5, width, width)
    outs = [jax.ShapeDtypeStruct((rows, width), BF16)] * 2 + [jax.ShapeDtypeStruct(total, F32)]
    scratch = [
        VMEM((padded, width), F32),
        VMEM((padded, width), F32),
        VMEM((padded, padded), F32),
        VMEM((n_dp, rooms, width), BF16),
        VMEM((n_dp, rooms, width), BF16),
        VMEM((n_dp, n_t, rows_block, width) if inside else (1, 1, 16, LANES), BF16),
    ]
    scratch += [DMA((n_dp,))] * 4 + [VMEM((padded, width), BF16)] * 3
    if inside:
        scratch += Scatter.scratch(n_dp, n_t, (rows_block, width))
    whole = pl.BlockSpec(memory_space=VMEM)
    return pl.pallas_call(
        partial(backward_kernel, cfg),
        out_shape=outs,
        in_specs=[whole] * len(args),
        out_specs=[whole] * len(outs),
        scratch_shapes=scratch,
        compiler_params=pltpu.CompilerParams(
            collective_id=cid, has_side_effects=True, vmem_limit_bytes=56 * 2**20
        ),
        name="backward_" + str(rooms),
    )(*args)


def image_blocks(rows):
    blocks = []
    for first in range(0, rows, SEQ):
        start = first // 16 * 16
        blocks.append((start, ceil_to(first - start + SEQ, 16), first - start))
    return blocks


def inside_image(size, first, axis):
    shape = (size, 1) if axis == 0 else (1, size)
    spot = lax.broadcasted_iota(jnp.int32, shape, axis)
    return (spot >= first) & (spot < first + SEQ)


def image_probs(query, key, size, first):
    scores = nt(query, key) * HEAD_DIM ** (-0.5) + jnp.where(inside_image(size, first, 1), 0.0, -1e30)
    power = jnp.exp(scores - jnp.max(scores, axis=1, keepdims=True))
    total = jnp.sum(power, axis=1, keepdims=True)
    return power * jnp.where(inside_image(size, first, 0), 1.0 / total, 0.0)


def join_images(parts, blocks):
    whole = parts[0]
    for (start, _, _), part in zip(blocks[1:], parts[1:]):
        shared = whole.shape[0] - start
        pieces = [whole[:start]]
        if shared > 0:
            pieces.append(whole[start:] + part[:shared])
        whole = jnp.concatenate(pieces + [part[shared:]], axis=0)
    return whole


def pack_block(refs, block, shard, width, experts):
    q_ref, k_ref, v_ref, o_ref, router_ref, *line_refs = refs
    for at, ref in ((0, q_ref), (1, k_ref), (2, v_ref), (OUT, o_ref)):
        block[at * shard : (at + 1) * shard, :] = ref[...].astype(BF16)
    here = slice(SMALL * shard, (SMALL + 1) * shard)
    block[here, :] = jnp.zeros((shard, width), BF16)
    row, column = (lax.broadcasted_iota(jnp.int32, (shard, shard), axis) for axis in (0, 1))
    lane = lax.broadcasted_iota(jnp.int32, (shard, LANES), 1)
    small = jnp.zeros((shard, LANES), F32)
    for at in range(experts + len(line_refs)):
        level = router_ref[at : at + 1, :] if at < experts else line_refs[at - experts][...]
        upright = jnp.sum(jnp.where(row == column, level, 0.0), axis=1, keepdims=True)
        small = jnp.where(lane == at, upright, small)
    block[here, :LANES] = small.astype(BF16)


def find_places(cfg, routes_ref, place, turned, over):
    n_dp, n_t, rows, padded, width, experts, rooms, shard, inside, hid = cfg
    t = lax.axis_index("tensor")
    tok_count = routes_ref.shape[1]
    capacity = (5 * tok_count + 2 * experts - 1) // (2 * experts)
    line = lax.broadcasted_iota(jnp.int32, (experts, tok_count), 0)
    lane = lax.broadcasted_iota(jnp.int32, (experts, tok_count), 1)

    def count(row, until):
        hot = (line == routes_ref[row : row + 1, :]) & (lane < until)
        return jnp.sum(hot.astype(F32), axis=1, keepdims=True)

    total = count(0, tok_count)
    before = (count(0, t * rows), count(1, t * rows))
    long = ceil_to(tok_count, LANES)
    wide = turned.shape[1]
    turned[...] = jnp.full(turned.shape, -1.0, F32)
    everyone = jnp.concatenate(
        [routes_ref[...], jnp.full((2, long - tok_count), experts, jnp.int32)], axis=1
    )
    everyone = jnp.concatenate([everyone, everyone, everyone, everyone], axis=0)
    mine = pltpu.roll(everyone, lax.rem(long - t * rows, long), 1)[:, :wide]
    spot = lax.broadcasted_iota(jnp.int32, (8, wide), 1)
    mine = jnp.where(spot < rows, mine, experts)
    line = lax.broadcasted_iota(jnp.int32, (experts, wide), 0)
    first, second = line == mine[0:1], line == mine[1:2]
    down, across = (lax.broadcasted_iota(jnp.int32, (wide, wide), axis) for axis in (0, 1))
    earlier = (down < across).astype(F32).astype(BF16)
    own = jnp.sum(first.astype(F32), axis=1, keepdims=True)
    first_rank = nn(first.astype(F32).astype(BF16), earlier)
    second_rank = nn(second.astype(F32).astype(BF16), earlier)

    def slot(choice, hot, rank, place):
        kept = hot & (place < capacity)
        here = jnp.sum(jnp.where(kept, rank + 1.0, 0.0), axis=0, keepdims=True) - 1.0
        good = (here >= 0.0) & (here < rooms)
        return jnp.where(good, choice.astype(F32) * rooms + here, -1.0), jnp.max(here, axis=1, keepdims=True)

    first_slot, first_most = slot(mine[0:1], first, first_rank, first_rank + before[0])
    second_slot, second_most = slot(mine[1:2], second, second_rank + own, second_rank + total + before[1])
    turned[0:1, :] = first_slot
    turned[1:2, :] = second_slot
    turned[2:3, :] = mine[0:1].astype(F32)
    turned[3:4, :] = mine[1:2].astype(F32)
    place[...] = turned[...].T
    most = jnp.maximum(first_most, second_most)
    over[...] = jnp.broadcast_to(jnp.where(most >= rooms, 1.0, 0.0), over.shape)


def step_kernel(cfg, *refs):
    n_dp, n_t, rows, padded, width, experts, rooms, shard, inside, hid = cfg
    refs = list(refs)

    def take(count):
        got = refs[:count]
        del refs[:count]
        return got

    x_ref, cot_ref, routes_ref, e_in_ref, e_out_ref = take(5)
    shared = take(9 if inside else 1)
    out_ref, gx_ref, sum_ref, in_ref, outer_ref = take(5)
    g_in_ref, g_out_ref = take(2)
    block, gathered, full, cot_full, bias, res, probs_s = take(7)
    place, turned, over, gate_m, gate_c, gate_s, gate_r, rise_s, rise_r = take(9)
    moe, q_s, k_s, v_s, mix, norm, dk, dv = take(8)
    send_d, send_s, recv_d, recv_s, ret_in, back_in, act, slope = take(8)
    wi, wo, gi, go, gi_in, go_in = take(6)
    d_send, d_recv, s_send, s_recv, r_send, r_recv, b_send, b_recv = take(8)
    f_send, f_recv, e_send, e_recv, own_sems = take(5)
    wi_spread, wo_spread = Spread(n_t, wi, *take(2)), Spread(n_t, wo, *take(2))
    gi_collect, go_collect = Collect(n_t, gi, gi_in, *take(2)), Collect(n_t, go, go_in, *take(2))
    dp, t = lax.axis_index("dp"), lax.axis_index("tensor")
    scale = HEAD_DIM ** (-0.5)
    slot_count = n_dp * rooms
    half, wide = min(256, hid), min(256, width)
    long = gate_m.shape[1]
    early = 2 if hid == width and n_t > 2 else 0
    table = [sorted(range(n_t), key=lambda j: (abs(j - at), j)) for at in range(n_t)]

    def order(p):
        found = jnp.int32(0)
        for at in range(n_t):
            for spot in range(n_t):
                found = found + jnp.where((t == at) & (p == spot), table[at][spot], 0)
        return found

    every = pl.ds(0, rooms)
    cut = max(rooms // 2 // 16 * 16, 16)
    d_copy = Exchange(n_dp, send_d, recv_d, every, d_send, d_recv, True)
    s_first = Exchange(n_dp, send_s, recv_s, pl.ds(0, cut), s_send.at[0], s_recv.at[0], False)
    s_second = Exchange(n_dp, send_s, recv_s, pl.ds(cut, rooms - cut), s_send.at[1], s_recv.at[1], False)
    late = max(rooms // 5 * 2 // 16 * 16, 16)
    r_first = Exchange(n_dp, send_d, ret_in, pl.ds(late, rooms - late), r_send.at[0], r_recv.at[0], False)
    r_second = Exchange(n_dp, send_d, ret_in, pl.ds(0, late), r_send.at[1], r_recv.at[1], False)
    b_copy = Exchange(n_dp, send_s, back_in, every, b_send, b_recv, False)
    f_copy = Exchange(n_dp, gate_s, gate_r, pl.ds(0, 8), f_send, f_recv, False)
    e_copy = Exchange(n_dp, rise_s, rise_r, pl.ds(0, 8), e_send, e_recv, False)

    def column(at):
        return place[:padded, at : at + 1].astype(jnp.int32)

    greet(n_dp, n_t)
    load_in = pltpu.make_async_copy(e_in_ref, g_in_ref, own_sems.at[0])
    load_out = pltpu.make_async_copy(e_out_ref, g_out_ref, own_sems.at[1])
    load_in.start()
    load_out.start()
    if inside:
        pack_block(shared, block, shard, width, experts)
        size = len(Gather.scratch(n_dp, n_t))
        gather_a = Gather(n_dp, n_t, 0, SMALL * shard, width, block, gathered, *take(size))
        gather_s = Gather(n_dp, n_t, SMALL * shard, shard, LANES, block, gathered, *take(size))
        gather_b = Gather(n_dp, n_t, OUT * shard, shard, width, block, gathered, *take(size))
        weights = Weights(shard, width, gathered=gathered)
    else:
        weights = Weights(shard, width, whole=shared[0])
    load_in.wait()
    wi[t] = g_in_ref[...].astype(BF16)
    greeted(n_dp, n_t)
    if inside:
        gather_a.start()
        gather_s.start()
        gather_b.start()
    wi_spread.step(0)
    load_out.wait()
    wo[t] = g_out_ref[...].astype(BF16)
    tail = rows - rows % 8
    full[tail:, :] = jnp.zeros((padded - tail, width), F32)
    full[:rows, :] = x_ref[...].astype(F32)
    cot_full[tail:, :] = jnp.zeros((padded - tail, width), F32)
    cot_full[:rows, :] = cot_ref[...].astype(F32)
    bias[...] = image_bias(rows, padded)
    find_places(cfg, routes_ref, place, turned, over)

    def selectors(p):
        slot = lax.broadcasted_iota(jnp.int32, (rooms, padded), 0) + p * rooms
        first = (slot == turned[0:1, :padded].astype(jnp.int32)).astype(F32)
        second = (slot == turned[1:2, :padded].astype(jnp.int32)).astype(F32)
        return first, second

    dk[...] = cot_full[...].astype(BF16)

    def dispatch_grad(k, carry):
        to = lax.rem(dp + k, n_dp)
        first, second = selectors(to)
        got = nn((first + second).astype(BF16), dk[...]).astype(BF16)

        @pl.when(k > 0)
        def _():
            send_s[to] = got

        @pl.when(k == 0)
        def _():
            recv_s[to] = got

        return carry

    lax.fori_loop(0, n_dp, dispatch_grad, 0)
    if inside:
        gather_a.pass_to_chips()
        gather_s.pass_to_chips()
        gather_b.pass_to_chips()
        gather_a.pass_to_core()
        gather_s.pass_to_core()
    if inside:
        gather_a.arrive()
        gather_s.arrive()
    norms = norm_rows(weights.small(), experts)
    unit, _ = centre(full[...])
    norm[...] = (unit * norms[0:1] + norms[1:2]).astype(BF16)
    q_s[...] = nn(norm[...], weights(0)).astype(BF16)
    k_s[...] = nn(norm[...], weights(1)).astype(BF16)
    v_s[...] = nn(norm[...], weights(2)).astype(BF16)
    if inside:
        gather_b.pass_to_core()
    s_first.start_all()
    wi_spread.step(1)
    middle = (t > 0) & (t < n_t - 1)

    @pl.when(jnp.logical_not(middle))
    def _():
        wo_spread.step(0)

    low, high = half_masks()
    low_f, high_f = low.astype(F32), high.astype(F32)
    blocks = image_blocks(rows)

    def heads(j, carry):
        at = pl.ds(pl.multiple_of(j * LANES, LANES), LANES)
        parts = []
        for start, size, first in blocks:
            here = pl.ds(start, size)
            query, key, value = q_s[here, at], k_s[here, at], v_s[here, at]
            one = nn(image_probs(query * low, key, size, first).astype(BF16), value)
            two = nn(image_probs(query * high, key, size, first).astype(BF16), value)
            parts.append(one * low_f + two * high_f)
        mix[:, at] = join_images(parts, blocks).astype(BF16)
        return carry

    lax.fori_loop(0, width // LANES, heads, 0)
    if inside:
        gather_b.arrive()
    residual = full[...] + nn(mix[...], weights(OUT))
    res[...] = residual
    unit, _ = centre(residual)
    moe[...] = (unit * norms[2:3] + norms[3:4]).astype(BF16)
    probs_s[...] = router_probs(nn(moe[...], weights.small()), experts)

    spot = lax.broadcasted_iota(jnp.int32, (padded, LANES), 1)
    first_gate, second_gate = pick_gate(probs_s[...], column(2)), pick_gate(probs_s[...], column(3))
    place[:padded, :] = jnp.where(spot == 4, first_gate, jnp.where(spot == 5, second_gate, place[:padded, :]))
    turned[...] = place[...].T
    gate_line = lax.broadcasted_iota(jnp.int32, (8, padded), 0)

    def terms(gate):
        one = gate.astype(BF16).astype(F32)
        two = (gate - one).astype(BF16).astype(F32)
        three = gate - one - two
        stack = jnp.where(gate_line == 0, one, jnp.where(gate_line == 1, two, jnp.where(gate_line == 2, three, 0.0)))
        return stack.astype(BF16)

    first_terms, second_terms = terms(turned[4:5, :padded]), terms(turned[5:6, :padded])
    def dispatch(k, carry):
        to = lax.rem(dp + k, n_dp)
        first, second = selectors(to)
        got = nn((first + second).astype(BF16), moe[...]).astype(BF16)

        @pl.when(k > 0)
        def _():
            send_d[to] = got
            d_copy.start(k)

        @pl.when(k == 0)
        def _():
            recv_d[to] = got

        return carry

    lax.fori_loop(0, n_dp, dispatch, 0)

    if n_t > 2:
        wi_spread.step(2)

    @pl.when(middle)
    def _():
        wo_spread.step(0)

    def dispatch_gates(k, carry):
        to = lax.rem(dp + k, n_dp)
        first, second = selectors(to)
        gate = nt(first_terms, first.astype(BF16)) + nt(second_terms, second.astype(BF16))
        gate = jnp.sum(gate, axis=0, keepdims=True)

        @pl.when(k > 0)
        def _():
            gate_s[to, :, :rooms] = jnp.broadcast_to(gate, (8, rooms))
            f_copy.start(k)

        @pl.when(k == 0)
        def _():
            gate_r[to, :, :rooms] = jnp.broadcast_to(gate, (8, rooms))

        return carry

    lax.fori_loop(0, n_dp, dispatch_gates, 0)

    def hidden_units(j, g):
        active, steep = gelu_parts(nn(recv_d[g], wi[j]))
        act[j, g] = active.astype(BF16)
        slope[j, g] = steep.astype(BF16)

    def own_hidden(k, carry):
        @pl.when(k > 0)
        def _():
            d_copy.wait_from(k)

        hidden_units(t, lax.rem(dp + n_dp - k, n_dp))
        return carry

    lax.fori_loop(0, n_dp, own_hidden, 0)
    s_second.start_all()

    @pl.when(middle)
    def _():
        wo_spread.step(1)


    def other_hidden(i, carry):
        q = i // n_dp
        p = jnp.where(q == 0, 1, jnp.where(q == 1, n_t - 1, q))
        hidden_units(order(p), lax.rem(i, n_dp))
        return carry

    lax.fori_loop(0, n_dp, other_hidden, 0, unroll=2)
    for s in range(3, n_t):
        wi_spread.step(s)
    if n_t > 2:
        lax.fori_loop(n_dp, 2 * n_dp, other_hidden, 0, unroll=2)
    gate_m[...] = jnp.zeros_like(gate_m)
    f_copy.wait_all()
    f_copy.wait_sent()
    for g in range(n_dp):
        gate_m[g : g + 1, :rooms] = gate_r[g, 0:1, :rooms]
    gate_c[...] = gate_m[...].T
    for half_copy in (s_first, s_second):
        half_copy.wait_all()
        half_copy.wait_sent()
    slot_grads = send_s
    room_lane = lax.broadcasted_iota(jnp.int32, (rooms, LANES), 1)

    def slot_grad(g, carry):
        gate = jnp.sum(jnp.where(room_lane == g, gate_c[:rooms, :], 0.0), axis=1, keepdims=True)
        slot_grads[g] = (gate * recv_s[g].astype(F32)).astype(BF16)
        return carry

    lax.fori_loop(0, n_dp, slot_grad, 0)

    def outer_grad(i, carry):
        j = order(n_t - 1 - i // (hid // half))
        at = pl.ds(pl.multiple_of(lax.rem(i, hid // half) * half, half), half)
        left = act[j, :, :, at].reshape(slot_count, half)
        go[j, at, :] = tn(left, slot_grads[...].reshape(slot_count, width)).astype(BF16)

        @pl.when(lax.rem(i, hid // half) == hid // half - 1)
        def _():
            go_collect.begin(j)

        return carry

    lax.fori_loop(0, hid // half, outer_grad, 0)
    if n_t > 3:
        lax.fori_loop(2 * n_dp, (n_t - 1) * n_dp, other_hidden, 0, unroll=2)
    @pl.when(jnp.logical_not(middle))
    def _():
        wo_spread.step(1)

    @pl.when(middle)
    def _():
        if n_t > 2:
            wo_spread.step(2)

    lax.fori_loop(hid // half, n_t * (hid // half), outer_grad, 0)

    def hidden_grads(p):
        j = order(p)

        def one(i, inner):
            slope[j, i] = (nt(slot_grads[i], wo[j]) * slope[j, i].astype(F32)).astype(BF16)
            return inner

        lax.fori_loop(0, n_dp, one, 0, unroll=2)

    def inner_grads(p):
        j = order(p)

        def one(i, inner):
            at = pl.ds(pl.multiple_of(i * wide, wide), wide)
            left = recv_d[:, :, at].reshape(slot_count, wide)
            gi[j, at, :] = tn(left, slope[j].reshape(slot_count, hid)).astype(BF16)
            return inner

        lax.fori_loop(0, width // wide, one, 0)

    def split(total):
        main = total.astype(BF16)
        return main, (total - main.astype(F32)).astype(BF16)

    def some_back(g, inner):
        near_a, near_b = order(0), order(1)
        total = nn(act[near_a, g], wo[near_a]) + nn(act[near_b, g], wo[near_b])
        act[near_a, g], act[near_b, g] = split(total)
        return inner

    def hidden_step(p, carry):
        @pl.when(p == 1)
        def _():
            if n_t > 2:
                go_collect.step(1, True)

        @pl.when((p == 2) & jnp.logical_not(middle))
        def _():
            if n_t > 2:
                wo_spread.step(2)

        @pl.when(p == 3)
        def _():
            for s in range(3, n_t):
                wo_spread.step(s)

        hidden_grads(p)

        @pl.when((p < n_t - 1) & jnp.logical_not(middle))
        def _():
            inner_grads(p)

        if early:

            @pl.when((p == early) & jnp.logical_not(middle))
            def _():
                lax.fori_loop(0, n_dp, some_back, 0)

        return carry

    lax.fori_loop(0, n_t, hidden_step, 0)
    d_copy.wait_sent()

    def give_back_grad(i, carry):
        k = lax.rem(i + 1, n_dp)
        to = lax.rem(dp + k, n_dp)
        total = nt(slope[0, to], wi[0])
        for j in range(1, n_t):
            total = total + nt(slope[j, to], wi[j])
        total = total.astype(BF16)

        @pl.when(k > 0)
        def _():
            send_s[to] = total
            b_copy.start(k)

        @pl.when(k == 0)
        def _():
            back_in[to] = total

        return carry

    lax.fori_loop(0, n_dp, give_back_grad, 0)

    for e in range(2, n_t - 1):
        go_collect.step(e, True)

    @pl.when(middle)
    def _():
        def one(p, inner):
            inner_grads(p)
            return inner

        lax.fori_loop(0, n_t - 1, one, 0)
        if early:
            lax.fori_loop(0, n_dp, some_back, 0)

    inner_grads(n_t - 1)

    def send_inner(p, carry):
        gi_collect.begin(order(n_t - 1 - p))
        return carry

    lax.fori_loop(0, n_t, send_inner, 0)
    gate_c[...] = jnp.zeros_like(gate_c)

    def give_back(i, carry):
        k = lax.rem(i + 1, n_dp)
        to = lax.rem(dp + k, n_dp)
        if early:
            near_a, near_b = order(0), order(1)
            total = act[near_a, to].astype(F32) + act[near_b, to].astype(F32)
        else:
            total = jnp.zeros((rooms, width), F32)
        for p in range(early, n_t):
            j = order(p)
            total = total + nn(act[j, to], wo[j])
        rise = jnp.sum(total * recv_s[to].astype(F32), axis=1, keepdims=True)
        gate_c[:rooms, :] = jnp.where(room_lane == to, rise, gate_c[:rooms, :])

        @pl.when(k > 0)
        def _():
            send_d[to] = total.astype(BF16)

        @pl.when(k == 0)
        def _():
            ret_in[to] = total.astype(BF16)

        return carry

    lax.fori_loop(0, n_dp, give_back, 0)
    gate_m[...] = gate_c[...].T
    for g in range(n_dp):
        row = jnp.broadcast_to(gate_m[g : g + 1, :], (8, long))

        @pl.when(dp == g)
        def _():
            rise_r[g] = row

        @pl.when(dp != g)
        def _():
            rise_s[g] = row

    e_copy.start_all()
    lane = lax.broadcasted_iota(jnp.int32, (padded, slot_count), 1)
    both = ((lane == column(0)).astype(F32) + (lane == column(1)).astype(F32)).astype(BF16)
    unit, inverse = centre(res[...])
    go_collect.finish(g_out_ref)
    store_out = pltpu.make_async_copy(g_out_ref, outer_ref, own_sems.at[1])
    store_out.start()
    b_copy.wait_sent()
    r_first.start_all()
    b_copy.wait_all()
    e_copy.wait_all()
    e_copy.wait_sent()
    room = lax.broadcasted_iota(jnp.int32, (padded, long), 1)

    slots_of = (column(0), column(1))

    found = [jnp.zeros((padded, long), F32)] * 2
    for e in range(n_dp):
        row = jnp.where(room[0:1] < rooms, rise_r[e, 0:1, :], 0.0)
        for at, slot in enumerate(slots_of):
            here = jnp.where(slot < (e + 1) * rooms, slot - e * rooms, -1)
            found[at] = jnp.where(room == here, row, found[at])
    first_grad, second_grad = (jnp.sum(one, axis=1, keepdims=True) for one in found)
    probs = probs_s[...]
    spot = lax.broadcasted_iota(jnp.int32, probs.shape, 1)
    grad_probs = jnp.where(spot == column(2), first_grad, 0.0) + jnp.where(spot == column(3), second_grad, 0.0)
    grad_logits = (probs * (grad_probs - jnp.sum(probs * grad_probs, axis=1, keepdims=True))).astype(BF16)
    grad_router = tn(moe[...], grad_logits)
    if n_t > 2:
        gi_collect.step(1, True)
    grad_moe = nn(both, back_in[...].reshape(slot_count, width)) + nt(grad_logits, weights.small())
    extra, gain_two, shift_two = norm_back(grad_moe, unit, inverse, norms[2:3])
    grad_residual = cot_full[...] + extra
    cot_full[...] = grad_residual
    grad_attended = grad_residual.astype(BF16)

    pairs = width // LANES
    if inside:
        size = len(Reduce.scratch(n_dp, n_t, 1, (shard, LANES)))
        out_sum = Reduce(n_dp, n_t, lambda p: sum_ref.at[pl.ds(OUT * shard, shard)], *take(size))
        pair_sum = Reduce(
            n_dp, n_t, lambda p: sum_ref.at[pl.ds(0, 3 * shard), pl.ds(pl.multiple_of(p * LANES, LANES), LANES)], *take(size)
        )
        small_sum = Reduce(n_dp, n_t, lambda p: sum_ref.at[pl.ds(SMALL * shard, shard), pl.ds(0, LANES)], *take(size))
        sum_ref[SMALL * shard : (SMALL + 1) * shard, LANES:] = jnp.zeros((shard, width - LANES), F32)
        out_sum.put(0, 0, tn(mix[...], grad_attended))
        out_sum.to_core(0)
    else:
        sum_ref[OUT] = tn(mix[...], grad_attended)
    dq = mix
    dq[...] = nt(grad_attended, weights(OUT)).astype(BF16)

    def heads_back(j, carry):
        at = pl.ds(pl.multiple_of(j * LANES, LANES), LANES)
        query, key, value, grad = q_s[:, at], k_s[:, at], v_s[:, at], dq[:, at]
        for mask, mask_f in ((low, low_f), (high, high_f)):
            probs = soft_scores(query * mask, key, bias[...])
            grad_probs = nt(grad * mask, value)
            grad_scores = probs * (grad_probs - jnp.sum(probs * grad_probs, axis=1, keepdims=True))
            grad_scores = grad_scores.astype(BF16)
            part_v = tn(probs.astype(BF16), grad)
            part_q = nn(grad_scores, key) * scale
            part_k = tn(grad_scores, query) * scale
            if mask is low:
                sum_q, sum_k, sum_v = part_q * mask_f, part_k * mask_f, part_v * mask_f
            else:
                sum_q, sum_k, sum_v = sum_q + part_q * mask_f, sum_k + part_k * mask_f, sum_v + part_v * mask_f
        dq[:, at] = sum_q.astype(BF16)
        dk[:, at] = sum_k.astype(BF16)
        dv[:, at] = sum_v.astype(BF16)
        if inside:
            for spot, ref in enumerate((dq, dk, dv)):
                pair_sum.put(j, spot * shard, tn(norm[...], ref[:, at]))
            pair_sum.to_core(j)

            @pl.when(j == 0)
            def _():
                out_sum.to_chips(0)

            @pl.when(j > 0)
            def _():
                pair_sum.to_chips(j - 1)

        return carry

    lax.fori_loop(0, pairs, heads_back, 0)
    for e in range(2, n_t - 1):
        gi_collect.step(e, True)
    if inside:
        pair_sum.to_chips(pairs - 1)
    else:
        for spot, ref in enumerate((dq, dk, dv)):
            sum_ref[spot] = tn(norm[...], ref[...])
    grad_normed = nt(dq[...], weights(0)) + nt(dk[...], weights(1)) + nt(dv[...], weights(2))
    full[tail:, :] = jnp.zeros((padded - tail, width), F32)
    full[:rows, :] = x_ref[...].astype(F32)
    unit, inverse = centre(full[...])
    extra, gain_one, shift_one = norm_back(grad_normed, unit, inverse, norms[0:1])
    gx_ref[...] = (cot_full[...] + extra)[:rows].astype(BF16)
    small = small_grads(experts, grad_router, (gain_one, shift_one, gain_two, shift_two))
    lane = lax.broadcasted_iota(jnp.int32, small.shape, 1)
    small = jnp.where(lane == experts + 4, over[0:1, :], small)
    def combine():
        for half_copy in (r_first, r_second):
            half_copy.wait_all()
            half_copy.wait_sent()
        returned = ret_in[...].reshape(slot_count, width)
        lane = lax.broadcasted_iota(jnp.int32, (padded, slot_count), 1)
        first, second = ((lane == column(at)).astype(F32).astype(BF16) for at in (0, 1))
        first_rows, second_rows = nn(first, returned), nn(second, returned)
        first_gate, second_gate = place[:padded, 4:5], place[:padded, 5:6]
        outcome = res[...] + first_gate * first_rows + second_gate * second_rows
        out_ref[...] = outcome[:rows].astype(BF16)

    if inside:
        small_sum.put(0, 0, small)
        small_sum.to_core(0)
        small_sum.to_chips(0)
        out_sum.to_line(0)

        def line(p, carry):
            pair_sum.to_line(p)
            return carry

        lax.fori_loop(0, pairs, line, 0)
        small_sum.to_line(0)
        r_second.start_all()
        combine()
        out_sum.finish(0)

        def last(p, carry):
            pair_sum.finish(p)
            return carry

        lax.fori_loop(0, pairs, last, 0)
        small_sum.finish(0)
        gather_a.drain()
        gather_s.drain()
        gather_b.drain()
    else:
        sum_ref[SMALL] = jnp.zeros((width, width), F32)
        sum_ref[SMALL, :, :LANES] = small
        r_second.start_all()
        combine()
    gi_collect.finish(g_in_ref)
    store_in = pltpu.make_async_copy(g_in_ref, in_ref, own_sems.at[0])
    store_in.start()
    wi_spread.drain()
    wo_spread.drain()
    store_out.wait()
    store_in.wait()


def run_step(cfg, cid, x, cot, routes, e_in, e_out, shared):
    n_dp, n_t, rows, padded, width, experts, rooms, shard, inside, hid = cfg
    rows_block = ceil_to(5 * shard, 16)
    total = (rows_block, width) if inside else (5, width, width)
    outs = [
        jax.ShapeDtypeStruct((rows, width), BF16),
        jax.ShapeDtypeStruct((rows, width), BF16),
        jax.ShapeDtypeStruct(total, F32),
        jax.ShapeDtypeStruct((width, hid), F32),
        jax.ShapeDtypeStruct((hid, width), F32),
    ]
    spread = (n_dp, n_t, rows_block, width) if inside else (1, 1, 16, LANES)
    wide, long = ceil_to(padded, LANES), ceil_to(rooms, LANES)
    rows_f, rows_b = VMEM((padded, width), F32), VMEM((padded, width), BF16)
    slots_b, units_b = VMEM((n_dp, rooms, width), BF16), VMEM((n_t, n_dp, rooms, hid), BF16)
    in_b, out_b = (VMEM((n_t,) + shape, BF16) for shape in ((width, hid), (hid, width)))
    in_more, out_more = (VMEM((n_t + 1,) + shape, BF16) for shape in ((width, hid), (hid, width)))
    scratch = [VMEM((width, hid), F32), VMEM((hid, width), F32)]
    scratch += [VMEM((rows_block, width), BF16), VMEM(spread, BF16)]
    scratch += [rows_f, rows_f, VMEM((padded, padded), F32), rows_f, VMEM((padded, LANES), F32)]
    scratch += [VMEM((wide, LANES), F32), VMEM((LANES, wide), F32), VMEM((8, LANES), F32)]
    scratch += [VMEM((LANES, long), F32), VMEM((long, LANES), F32)] + [VMEM((n_dp, 8, long), F32)] * 4
    scratch += [rows_b] * 8 + [slots_b] * 6 + [units_b] * 2
    scratch += [in_b, out_b, in_b, out_b, in_more, out_more]
    scratch += [DMA, DMA((n_dp,))] + [DMA((2,))] * 4 + [DMA] * 6 + [DMA((2,))] + Spread.scratch(n_t) * 2 + Collect.scratch(n_t) * 2
    if inside:
        scratch += Gather.scratch(n_dp, n_t) * 3 + Reduce.scratch(n_dp, n_t, 1, (shard, width))
        scratch += Reduce.scratch(n_dp, n_t, width // LANES, (3 * shard, LANES))
        scratch += Reduce.scratch(n_dp, n_t, 1, (shard, LANES))
    whole, anywhere = pl.BlockSpec(memory_space=VMEM), pl.BlockSpec(memory_space=pl.ANY)
    return pl.pallas_call(
        partial(step_kernel, cfg),
        out_shape=outs,
        in_specs=[whole] * 3 + [anywhere] * 2 + [whole] * len(shared),
        out_specs=[whole] * 3 + [anywhere] * 2,
        scratch_shapes=scratch,
        compiler_params=pltpu.CompilerParams(
            collective_id=cid, has_side_effects=True, vmem_limit_bytes=60 * 2**20
        ),
        name="step_" + str(rooms),
    )(x, cot, routes, e_in, e_out, *shared)


def lay_kernel(shard, experts, out_ref, gx_ref, sum_ref, in_ref, outer_ref, *outs):
    outs[0][...] = out_ref[...]
    outs[1][...] = gx_ref[...]
    for at, spot in ((0, 4), (1, 5), (2, 6), (OUT, 7)):
        outs[spot][...] = sum_ref[at * shard : (at + 1) * shard, :]
    small = sum_ref[SMALL * shard : (SMALL + 1) * shard, :LANES]
    row, column = (lax.broadcasted_iota(jnp.int32, (shard, shard), axis) for axis in (0, 1))
    for at, spot in enumerate((2, 3, 8, 9)):
        upright = small[:, experts + at : experts + at + 1]
        outs[spot][...] = jnp.sum(jnp.where(row == column, upright, 0.0), axis=0, keepdims=True)
    for at in range(experts):
        outs[10][at : at + 1, :] = jnp.sum(jnp.where(row == column, small[:, at : at + 1], 0.0), axis=0, keepdims=True)
    outs[11][...] = in_ref[...]
    outs[12][...] = outer_ref[...]


def lay_out(shard, experts, *args):
    rows, width = args[0].shape
    line = jax.ShapeDtypeStruct((1, shard), F32)
    square = jax.ShapeDtypeStruct((shard, width), F32)
    outs = [jax.ShapeDtypeStruct((rows, width), BF16)] * 2 + [line] * 2 + [square] * 4 + [line] * 2
    outs += [jax.ShapeDtypeStruct((experts, shard), F32)]
    outs += [jax.ShapeDtypeStruct(arg.shape, F32) for arg in args[3:]]

    def full(shape):
        return pl.BlockSpec(shape, lambda i: (0,) * len(shape))

    return pl.pallas_call(
        partial(lay_kernel, shard, experts),
        grid=(1,),
        out_shape=outs,
        in_specs=[full(arg.shape) for arg in args],
        out_specs=[full(out.shape) for out in outs],
        compiler_params=pltpu.CompilerParams(vmem_limit_bytes=32 * 2**20),
        name="outputs",
    )(*args)


def route_pairs(routes, t, row_count, experts, capacity):
    tok_count = routes.shape[0]
    ids = jnp.arange(experts, dtype=jnp.int32)[None, :]
    start = t * row_count
    rows = lax.dynamic_slice_in_dim(routes, start, row_count, 0)
    before = (jnp.arange(tok_count, dtype=jnp.int32) < start)[:, None]
    all_first = routes[:, 0:1] == ids
    all_second = routes[:, 1:2] == ids
    base_first = jnp.sum((all_first & before).astype(jnp.int32), axis=0)
    total_first = jnp.sum(all_first.astype(jnp.int32), axis=0)
    base_second = jnp.sum((all_second & before).astype(jnp.int32), axis=0)
    hot_first = rows[:, 0:1] == ids
    hot_second = rows[:, 1:2] == ids
    at = jnp.arange(row_count, dtype=jnp.int32)
    lower = (at[:, None] > at[None, :]).astype(BF16)
    both = jnp.concatenate([hot_first, hot_second], axis=1).astype(BF16)
    earlier = nn(lower, both).astype(jnp.int32)
    own_first = jnp.sum(hot_first.astype(jnp.int32), axis=0)
    rank_first = earlier[:, :experts]
    rank_second = earlier[:, experts:] + own_first
    place_first = rank_first + base_first
    place_second = earlier[:, experts:] + total_first + base_second
    first = jnp.sum(jnp.where(hot_first & (place_first < capacity), rank_first + 1, 0), axis=1) - 1
    second = jnp.sum(jnp.where(hot_second & (place_second < capacity), rank_second + 1, 0), axis=1) - 1
    return rows, first, second


def per_device(
    n_dp,
    n_t,
    inputs,
    cotangent,
    routes,
    gain_attn,
    shift_attn,
    query_w,
    key_w,
    value_w,
    out_w,
    gain_moe,
    shift_moe,
    router_w,
    expert_in,
    expert_out,
):
    t = lax.axis_index("tensor")
    shard, width = query_w.shape
    experts = router_w.shape[1]
    tok_count = routes.shape[0]
    rows = inputs.shape[0]
    hid = expert_in.shape[2]
    padded = ceil_to(rows, 16)
    capacity = (5 * tok_count + 2 * experts - 1) // (2 * experts)
    inside = shard % 16 == 0
    every = ("dp", "tensor")
    lines = (gain_attn, shift_attn, gain_moe, shift_moe)

    def stack():
        small = jnp.concatenate([router_w] + [line[:, None] for line in lines], axis=1)
        small = jnp.pad(small, ((0, 0), (0, width - small.shape[1])))
        return jnp.stack([query_w, key_w, value_w, small, out_w]).astype(BF16)

    if inside:
        shared = [query_w, key_w, value_w, out_w, router_w.T] + [line[None, :] for line in lines]
    else:
        shared = [lax.all_gather(stack(), every, axis=1, tiled=True)]

    def finish(results):
        summed = results[2]
        if not inside:
            summed = lax.psum_scatter(summed, every, scatter_dimension=1, tiled=True).reshape(5 * shard, width)
        outs = lay_out(shard, experts, results[0], results[1], summed, *results[3:])
        return tuple(outs)

    def slow(_):
        rooms = ceil_to(rows, 16)
        cfg = (n_dp, n_t, rows, padded, width, experts, rooms, shard, inside)
        route_rows, first_rank, second_rank = route_pairs(routes, t, rows, experts, capacity)

        def slot(choice, rank):
            return jnp.where(rank >= 0, choice * rooms + rank, -1)

        slots = jnp.stack([slot(route_rows[:, 0], first_rank), slot(route_rows[:, 1], second_rank)])
        slots = jnp.pad(slots, ((0, 0), (0, padded - rows)), constant_values=-1)
        cols = jnp.concatenate([jnp.pad(route_rows, ((0, padded - rows), (0, 0))), slots.T], axis=1)
        block = stack().reshape(5 * shard, width) if inside else shared[0]
        kept = forward(cfg, 1, inputs, cotangent, cols, slots, block)

        def turn(k):
            return [(i, (i + k) % n_t) for i in range(n_t)]

        both = jnp.stack([expert_in[0].T, expert_out[0]]).astype(BF16)
        parts = [both] + [lax.ppermute(both, "tensor", turn(k)) for k in range(1, n_t)]
        w_in, w_out = (jnp.concatenate([part[i] for part in parts], axis=0) for i in range(2))
        returned, back, grad_inner, grad_outer = run_expert(
            kept[1].reshape(n_dp * rooms, width), kept[2].reshape(n_dp * rooms, width), w_in, w_out
        )
        both = jnp.stack([grad_inner.reshape(n_t, hid, width), grad_outer.reshape(n_t, hid, width)], axis=1)
        total = both[0].astype(F32)
        for k in range(1, n_t):
            total = total + lax.ppermute(both[k], "tensor", turn(-k)).astype(F32)
        results = backward(
            cfg,
            2,
            returned.reshape(n_dp, rooms, width),
            back.reshape(n_dp, rooms, width),
            inputs,
            cotangent,
            cols,
            kept[0] if inside else block,
            *kept[3:],
        )
        return finish((*results, total[0].T, total[1]))

    rooms = min(ceil_to((7 * rows + 2 * experts - 1) // (2 * experts), 16), ceil_to(rows, 16))
    cfg = (n_dp, n_t, rows, padded, width, experts, rooms, shard, inside, hid)
    fast = run_step(cfg, 0, inputs, cotangent, routes.T, expert_in[0], expert_out[0], shared)
    if inside:
        crowded = fast[2][SMALL * shard, experts + 4] > 0.5
    else:
        crowded = lax.psum(fast[2][SMALL, 0, experts + 4], every) > 0.5
    outs = lax.cond(crowded, slow, finish, tuple(fast))
    lined = [out.reshape(shard) if at in (2, 3, 8, 9) else out for at, out in enumerate(outs)]
    lined[10], lined[11], lined[12] = lined[10].T, lined[11][None], lined[12][None]
    return tuple(lined)


def solution(mesh):
    every = ("dp", "tensor")
    rows, line = P(every, None), P(every)
    w_in, w_out = P("dp", None, "tensor"), P("dp", "tensor", None)
    return jax.shard_map(
        partial(per_device, mesh.shape["dp"], mesh.shape["tensor"]),
        mesh=mesh,
        in_specs=(rows, rows, P("dp", None), line, line, rows, rows, rows, rows, line, line, rows, w_in, w_out),
        out_specs=(rows, rows, line, line, rows, rows, rows, rows, line, line, rows, w_in, w_out),
        check_vma=False,
    )
```

```python
from functools import partial

import jax
import jax.numpy as jnp
from jax import lax
from jax.experimental import pallas as pl
from jax.experimental.pallas import tpu as pltpu
from jax.sharding import PartitionSpec as P

SEQ = 197
HEAD_DIM = 64
LANES = 128
MESH = pl.DeviceIdType.MESH
F32 = jnp.float32
BF16 = jnp.bfloat16
VMEM = pltpu.VMEM
DMA = pltpu.SemaphoreType.DMA
SMALL, OUT = 3, 4


def ceil_to(value, unit):
    return (value + unit - 1) // unit * unit


def nn(left, right):
    return lax.dot_general(left, right, (((1,), (0,)), ((), ())), preferred_element_type=F32)


def nt(left, right):
    return lax.dot_general(left, right, (((1,), (1,)), ((), ())), preferred_element_type=F32)


def tn(left, right):
    return lax.dot_general(left, right, (((0,), (0,)), ((), ())), preferred_element_type=F32)


def remote(src, dst, send, recv, device):
    return pltpu.make_async_remote_copy(
        src_ref=src, dst_ref=dst, send_sem=send, recv_sem=recv, device_id=device, device_id_type=MESH
    )


def meet(n_dp, n_t, z_too):
    dp = lax.axis_index("dp")
    t = lax.axis_index("tensor")
    bar = pltpu.get_barrier_semaphore()
    for k in range(1, n_dp):
        pl.semaphore_signal(bar, inc=1, device_id={"dp": lax.rem(dp + k, n_dp)}, device_id_type=MESH)
    if z_too:
        for k in range(1, n_t):
            pl.semaphore_signal(bar, inc=1, device_id={"tensor": lax.rem(t + k, n_t)}, device_id_type=MESH)
    pl.semaphore_wait(bar, n_dp - 1 + (n_t - 1 if z_too else 0))


class Gather:
    def __init__(self, n_dp, n_t, first, count, lanes, block, out, own_sem, z_send, z_recv, c_send, c_recv, k_send, k_recv):
        self.n_t, self.n_chip = n_t, n_dp // 2
        self.rows, self.lanes = pl.ds(first, count), pl.ds(0, lanes)
        self.block, self.out, self.own_sem = block.at[self.rows, self.lanes], out, own_sem
        self.z_sems, self.c_sems, self.k_sems = (z_send, z_recv), (c_send, c_recv), (k_send, k_recv)
        self.dp, self.t = lax.axis_index("dp"), lax.axis_index("tensor")
        self.chip, self.core = self.dp // 2, lax.rem(self.dp, 2)
        self.other = self.chip * 2 + 1 - self.core

    @staticmethod
    def scratch(n_dp, n_t):
        n_chip = n_dp // 2
        return [DMA, DMA, DMA((n_t,)), DMA, DMA((n_chip, n_t)), DMA, DMA]

    def place(self, dp, t):
        return self.out.at[dp, t, self.rows, self.lanes]

    def z_copy(self, k):
        send, recv = self.z_sems
        to = lax.rem(self.t + k, self.n_t)
        return remote(self.block, self.place(self.dp, self.t), send, recv.at[k], {"tensor": to})

    def chip_copy(self, k, j):
        send, recv = self.c_sems
        here = self.place(self.dp, lax.rem(self.t + self.n_t - j, self.n_t))
        to = lax.rem(self.chip + k, self.n_chip) * 2 + self.core
        return remote(self.block if j == 0 else here, here, send, recv.at[k, j], {"dp": to})

    def core_copy(self, k, j):
        send, recv = self.k_sems
        src = lax.rem(self.chip + self.n_chip - k, self.n_chip) * 2 + self.core
        here = self.place(src, lax.rem(self.t + self.n_t - j, self.n_t))
        own = k == 0 and j == 0
        return remote(self.block if own else here, here, send, recv, {"dp": self.other})

    def own_copy(self):
        return pltpu.make_async_copy(self.block, self.place(self.dp, self.t), self.own_sem)

    def start(self):
        for k in range(1, self.n_t):
            self.z_copy(k).start()
        self.own_copy().start()
        for k in range(1, self.n_chip):
            self.chip_copy(k, 0).start()
        self.core_copy(0, 0).start()

    def pass_to_chips(self):
        for j in range(1, self.n_t):
            self.z_copy(j).wait_recv()
            for k in range(1, self.n_chip):
                self.chip_copy(k, j).start()
            self.core_copy(0, j).start()

    def pass_to_core(self):
        for j in range(self.n_t):
            for k in range(1, self.n_chip):
                self.chip_copy(k, j).wait_recv()
                self.core_copy(k, j).start()

    def arrive(self):
        self.own_copy().wait()
        self.wait_bytes(self.out.at[pl.ds(0, self.n_chip), :, self.rows, self.lanes], self.k_sems[1])

    @staticmethod
    def wait_bytes(part, sem):
        pltpu.make_async_copy(part, part, sem).wait()

    def drain(self):
        self.wait_bytes(self.out.at[0, pl.ds(0, self.n_t - 1), self.rows, self.lanes], self.z_sems[0])
        self.wait_bytes(self.out.at[pl.ds(0, self.n_chip - 1), :, self.rows, self.lanes], self.c_sems[0])
        self.wait_bytes(self.out.at[pl.ds(0, self.n_chip), :, self.rows, self.lanes], self.k_sems[0])


class Scatter:
    def __init__(
        self, n_dp, n_t, grads, out, core_in, half, chip_in, part, z_in, k_send, k_recv, c_send, c_recv, z_send, z_recv
    ):
        self.n_t, self.n_chip = n_t, n_dp // 2
        self.grads, self.out = grads, out
        self.core_in, self.half, self.chip_in, self.part, self.z_in = core_in, half, chip_in, part, z_in
        self.k_sems, self.c_sems, self.z_sems = (k_send, k_recv), (c_send, c_recv), (z_send, z_recv)
        self.dp, self.t = lax.axis_index("dp"), lax.axis_index("tensor")
        self.chip, self.core = self.dp // 2, lax.rem(self.dp, 2)
        self.other = self.chip * 2 + 1 - self.core

    @staticmethod
    def scratch(n_dp, n_t, block):
        n_chip = n_dp // 2
        buffers = [VMEM((n_chip, n_t) + block, BF16)] + [VMEM((n_chip - 1, n_t) + block, BF16)] * 2
        buffers += [VMEM((n_t - 1,) + block, BF16)] * 2
        return buffers + [DMA((n_chip,))] * 4 + [DMA((n_t,))] * 2

    def core_copy(self, k):
        to = lax.rem(self.chip + k, self.n_chip)
        src = self.grads.at[to * 2 + 1 - self.core]
        return remote(src, self.core_in.at[k], self.k_sems[0].at[k], self.k_sems[1].at[k], {"dp": self.other})

    def chip_copy(self, k):
        to = lax.rem(self.chip + k, self.n_chip) * 2 + self.core
        return remote(self.half.at[k - 1], self.chip_in.at[k - 1], self.c_sems[0].at[k], self.c_sems[1].at[k], {"dp": to})

    def z_copy(self, k):
        to = lax.rem(self.t + k, self.n_t)
        return remote(self.part.at[k - 1], self.z_in.at[k - 1], self.z_sems[0].at[k], self.z_sems[1].at[k], {"tensor": to})

    def run(self, between=None, after=None):
        n_chip, n_t = self.n_chip, self.n_t
        order = list(range(1, n_chip)) + [0]
        for k in order:
            self.core_copy(k).start()
        for k in order:
            self.core_copy(k).wait_recv()
            if k > 0:
                to = lax.rem(self.chip + k, n_chip) * 2 + self.core
                self.half[k - 1] = (self.grads[to].astype(F32) + self.core_in[k].astype(F32)).astype(BF16)
                self.chip_copy(k).start()
        if between is not None:
            between()
        for k in range(1, n_chip):
            self.chip_copy(k).wait_recv()
        for k in list(range(1, n_t)) + [0]:
            row = lax.rem(self.t + k, n_t)
            total = self.grads[self.dp, row].astype(F32) + self.core_in[0, row].astype(F32)
            for c in range(1, n_chip):
                total = total + self.chip_in[c - 1, row].astype(F32)
            if k > 0:
                self.part[k - 1] = total.astype(BF16)
                self.z_copy(k).start()
            else:
                self.out[...] = total
        if after is not None:
            after()
        for k in range(1, n_t):
            self.z_copy(k).wait_recv()
            self.out[...] += self.z_in[k - 1].astype(F32)
        for k in range(n_chip):
            self.core_copy(k).wait_send()
        for k in range(1, n_chip):
            self.chip_copy(k).wait_send()
        for k in range(1, n_t):
            self.z_copy(k).wait_send()


class Reduce:
    def __init__(self, n_dp, n_t, out, grads, core_in, half, chip_in, part, z_in, *sems):
        self.n_t, self.n_chip, self.out = n_t, n_dp // 2, out
        self.grads, self.core_in, self.half = grads, core_in, half
        self.chip_in, self.part, self.z_in = chip_in, part, z_in
        self.k_sems, self.c_sems, self.z_sems = sems[0:3], sems[3:5], sems[5:7]
        self.dp, self.t = lax.axis_index("dp"), lax.axis_index("tensor")
        self.chip, self.core = self.dp // 2, lax.rem(self.dp, 2)
        self.other = self.chip * 2 + 1 - self.core

    @staticmethod
    def scratch(n_dp, n_t, parts, block):
        n_chip = n_dp // 2
        sizes = [(n_dp, n_t), (n_chip, n_t), (n_chip - 1, n_t), (n_chip - 1, n_t), (n_t - 1,), (n_t - 1,)]
        return [VMEM((parts,) + size + block, BF16) for size in sizes] + [DMA((parts,))] * 7

    def put(self, p, first, value):
        n_dp, n_t = self.n_chip * 2, self.n_t
        count, lanes = value.shape[0] // (n_dp * n_t), value.shape[1]
        self.grads[p, :, :, first : first + count, :] = value.astype(BF16).reshape(n_dp, n_t, count, lanes)

    def core_copy(self, p, k):
        src = self.grads.at[p, lax.rem(self.chip + k, self.n_chip) * 2 + 1 - self.core]
        send, far, near = self.k_sems
        recv = near if isinstance(k, int) and k == 0 else far
        return remote(src, self.core_in.at[p, k], send.at[p], recv.at[p], {"dp": self.other})

    def chip_copy(self, p, k):
        to = lax.rem(self.chip + k, self.n_chip) * 2 + self.core
        send, recv = self.c_sems
        return remote(self.half.at[p, k - 1], self.chip_in.at[p, k - 1], send.at[p], recv.at[p], {"dp": to})

    def z_copy(self, p, k):
        to = lax.rem(self.t + k, self.n_t)
        send, recv = self.z_sems
        return remote(self.part.at[p, k - 1], self.z_in.at[p, k - 1], send.at[p], recv.at[p], {"tensor": to})

    def to_core(self, p):
        for k in list(range(1, self.n_chip)) + [0]:
            self.core_copy(p, k).start()

    def to_chips(self, p):
        Gather.wait_bytes(self.core_in.at[p, pl.ds(1, self.n_chip - 1)], self.k_sems[1].at[p])
        for k in range(1, self.n_chip):
            to = lax.rem(self.chip + k, self.n_chip) * 2 + self.core
            self.half[p, k - 1] = (self.grads[p, to].astype(F32) + self.core_in[p, k].astype(F32)).astype(BF16)
            self.chip_copy(p, k).start()

    def to_line(self, p):
        self.core_copy(p, 0).wait_recv()
        Gather.wait_bytes(self.chip_in.at[p], self.c_sems[1].at[p])
        for k in list(range(1, self.n_t)) + [0]:
            row = lax.rem(self.t + k, self.n_t)
            total = self.grads[p, self.dp, row].astype(F32) + self.core_in[p, 0, row].astype(F32)
            for c in range(1, self.n_chip):
                total = total + self.chip_in[p, c - 1, row].astype(F32)
            if k > 0:
                self.part[p, k - 1] = total.astype(BF16)
                self.z_copy(p, k).start()
            else:
                self.out(p)[...] = total

    def finish(self, p):
        Gather.wait_bytes(self.z_in.at[p], self.z_sems[1].at[p])
        for k in range(1, self.n_t):
            self.out(p)[...] += self.z_in[p, k - 1].astype(F32)
        Gather.wait_bytes(self.part.at[p], self.z_sems[0].at[p])
        Gather.wait_bytes(self.core_in.at[p], self.k_sems[0].at[p])
        Gather.wait_bytes(self.half.at[p], self.c_sems[0].at[p])


def greet(n_dp, n_t):
    dp, t = lax.axis_index("dp"), lax.axis_index("tensor")
    bar = pltpu.get_barrier_semaphore()
    for k in range(1, n_dp):
        pl.semaphore_signal(bar, inc=1, device_id={"dp": lax.rem(dp + k, n_dp)}, device_id_type=MESH)
    for k in range(1, n_t):
        pl.semaphore_signal(bar, inc=1, device_id={"tensor": lax.rem(t + k, n_t)}, device_id_type=MESH)


def greeted(n_dp, n_t):
    pl.semaphore_wait(pltpu.get_barrier_semaphore(), n_dp - 1 + n_t - 1)


class Exchange:
    def __init__(self, n_dp, src, dst, rows, send, recv, single):
        self.n_dp, self.src, self.dst, self.rows, self.send, self.recv = n_dp, src, dst, rows, send, recv
        self.dp, self.single = lax.axis_index("dp"), single

    def copy(self, k):
        to = lax.rem(self.dp + k, self.n_dp)
        recv = self.recv.at[k] if self.single else self.recv
        return remote(self.src.at[to, self.rows], self.dst.at[self.dp, self.rows], self.send, recv, {"dp": to})

    def start(self, k):
        self.copy(k).start()

    def start_all(self):
        for k in range(1, self.n_dp):
            self.start(k)

    def wait_from(self, k):
        self.copy(k).wait_recv()

    def wait_all(self):
        part = self.dst.at[pl.ds(0, self.n_dp - 1), self.rows]
        pltpu.make_async_copy(part, part, self.recv).wait()

    def wait_sent(self):
        part = self.src.at[pl.ds(0, self.n_dp - 1), self.rows]
        pltpu.make_async_copy(part, part, self.send).wait()


class Spread:
    def __init__(self, n_t, parts, send, recv):
        self.n_t, self.t, self.parts, self.send, self.recv = n_t, lax.axis_index("tensor"), parts, send, recv

    @staticmethod
    def scratch(n_t):
        return [DMA((2, n_t)), DMA((n_t,))]

    def hop(self, j, way):
        here = self.parts.at[j]
        return remote(here, here, self.send.at[way, j], self.recv.at[j], {"tensor": self.t + 1 - 2 * way})

    def step(self, s):
        for way, j, in_line, onward in (
            (0, self.t - s, self.t - s >= 0, self.t + 1 < self.n_t),
            (1, self.t + s, self.t + s < self.n_t, self.t > 0),
        ):
            if s > 0:

                @pl.when(in_line)
                def _():
                    self.hop(j, way).wait_recv()

            @pl.when(in_line & onward)
            def _():
                self.hop(j, way).start()

    def drain(self):
        for s in range(self.n_t):

            @pl.when((self.t - s >= 0) & (self.t + 1 < self.n_t))
            def _():
                self.hop(self.t - s, 0).wait_send()

            @pl.when((self.t + s < self.n_t) & (self.t > 0))
            def _():
                self.hop(self.t + s, 1).wait_send()


class Collect:
    def __init__(self, n_t, parts, came, send, recv):
        self.n_t, self.t, self.parts, self.came, self.send, self.recv = (
            n_t,
            lax.axis_index("tensor"),
            parts,
            came,
            send,
            recv,
        )

    @staticmethod
    def scratch(n_t):
        return [DMA((n_t,)), DMA((n_t + 1,))]

    def hop(self, j, way):
        slot = j if way == 0 else jnp.where(j == self.t - 1, self.n_t, j)
        to = self.t + 1 - 2 * way
        return remote(self.parts.at[j], self.came.at[slot], self.send.at[j], self.recv.at[slot], {"tensor": to})

    def wait_slot(self, slot):
        remote(self.parts.at[0], self.came.at[slot], self.send.at[0], self.recv.at[slot], {"tensor": self.t}).wait_recv()

    def begin(self, j):
        @pl.when((self.t == 0) & (j > 0))
        def _():
            self.hop(j, 0).start()

        @pl.when((self.t == self.n_t - 1) & (j < self.n_t - 1))
        def _():
            self.hop(j, 1).start()

    def step(self, e, far):
        if far:
            right, left = self.n_t - 1 - e + self.t, e - self.n_t + 1 + self.t
        else:
            right, left = e - self.t + 2, 2 * self.n_t - 4 - e - self.t
        for way, j, mine in (
            (0, right, (self.t >= 1) & (right <= self.n_t - 1) & (right > self.t)),
            (1, left, (self.t <= self.n_t - 2) & (left >= 0) & (left < self.t)),
        ):

            @pl.when(mine)
            def _():
                self.wait_slot(j)
                self.parts[j] = (self.parts[j].astype(F32) + self.came[j].astype(F32)).astype(BF16)
                self.hop(j, way).start()

    def finish(self, result):
        result[...] = self.parts[self.t].astype(F32)

        @pl.when(self.t > 0)
        def _():
            self.wait_slot(self.t)
            result[...] += self.came[self.t].astype(F32)

        @pl.when(self.t < self.n_t - 1)
        def _():
            self.wait_slot(self.n_t)
            result[...] += self.came[self.n_t].astype(F32)

        for j in range(self.n_t):

            @pl.when(self.t < j)
            def _():
                self.hop(j, 0).wait_send()

            @pl.when(self.t > j)
            def _():
                self.hop(j, 1).wait_send()


def centre(values):
    centred = values - jnp.mean(values, axis=1, keepdims=True)
    inverse = lax.rsqrt(jnp.mean(centred * centred, axis=1, keepdims=True) + 1e-06)
    return centred * inverse, inverse


def norm_back(grad, unit, inverse, gain):
    scaled = grad * gain
    back = inverse * (
        scaled
        - jnp.mean(scaled, axis=1, keepdims=True)
        - unit * jnp.mean(scaled * unit, axis=1, keepdims=True)
    )
    return back, jnp.sum(grad * unit, axis=0, keepdims=True), jnp.sum(grad, axis=0, keepdims=True)


def norm_picks(experts):
    row, lane = (lax.broadcasted_iota(jnp.int32, (8, LANES), axis) for axis in (0, 1))
    return (row + experts == lane).astype(F32).astype(BF16)


def norm_rows(small, experts):
    return nt(norm_picks(experts), small)


def small_grads(experts, grad_router, rows):
    line = lax.broadcasted_iota(jnp.int32, (8, rows[0].shape[1]), 0)
    stack = sum(jnp.where(line == at, row, 0.0) for at, row in enumerate(rows))
    return grad_router + tn(stack.astype(BF16), norm_picks(experts))


def image_bias(rows, padded):
    line = lax.broadcasted_iota(jnp.int32, (padded, padded), 0)
    column = lax.broadcasted_iota(jnp.int32, (padded, padded), 1)
    image_line, image_column = jnp.zeros_like(line), jnp.zeros_like(column)
    for at in range(SEQ, rows + 1, SEQ):
        image_line += (line >= at).astype(jnp.int32)
        image_column += (column >= at).astype(jnp.int32)
    return jnp.where((image_line == image_column) & (column < rows), 0.0, -1e30)


def half_masks():
    lane = lax.broadcasted_iota(jnp.int32, (1, LANES), 1)
    low = (lane < HEAD_DIM).astype(F32)
    return low.astype(BF16), (1.0 - low).astype(BF16)


def soft_scores(query, key, bias):
    scores = nt(query, key) * HEAD_DIM ** (-0.5) + bias
    power = jnp.exp(scores - jnp.max(scores, axis=1, keepdims=True))
    return power * (1.0 / jnp.sum(power, axis=1, keepdims=True))


def router_probs(logits, experts):
    lane = lax.broadcasted_iota(jnp.int32, logits.shape, 1)
    inside = lane < experts
    kept = jnp.where(inside, logits, -1e30)
    power = jnp.where(inside, jnp.exp(kept - jnp.max(kept, axis=1, keepdims=True)), 0.0)
    return power * (1.0 / jnp.sum(power, axis=1, keepdims=True))


def pick_gate(probs, choice):
    lane = lax.broadcasted_iota(jnp.int32, probs.shape, 1)
    return jnp.sum(jnp.where(lane == choice, probs, 0.0), axis=1, keepdims=True)


class Weights:
    def __init__(self, shard, width, gathered=None, whole=None):
        self.shard, self.width, self.gathered, self.whole = shard, width, gathered, whole

    def __call__(self, at):
        if self.whole is not None:
            return self.whole[at]
        part = self.gathered[:, :, at * self.shard : (at + 1) * self.shard, :]
        return part.reshape(self.width, self.width)

    def small(self):
        if self.whole is not None:
            return self.whole[SMALL, :, :LANES]
        part = self.gathered[:, :, SMALL * self.shard : (SMALL + 1) * self.shard, :LANES]
        return part.reshape(self.width, LANES)


def gelu_parts(hidden):
    bell = jnp.exp(-0.5 * hidden * hidden)
    near = 1.0 / (1.0 + 0.23164189 * jnp.abs(hidden))
    tail = near * (
        0.127414796 + near * (-0.142248368 + near * (0.7107068705 + near * (-0.7265760135 + near * 0.5307027145)))
    )
    tail = tail * bell
    share = jnp.where(hidden < 0.0, tail, 1.0 - tail)
    return hidden * share, share + hidden * bell * 0.3989422804014327


def forward_kernel(cfg, *refs):
    n_dp, n_t, rows, padded, width, experts, rooms, shard, inside = cfg
    refs = list(refs)

    def take(count):
        got = refs[:count]
        del refs[:count]
        return got

    x_ref, cot_ref, cols_ref, slots_ref, block_ref = take(5)
    gathered, recv_d, recv_s, res_ref, moe_ref, q_ref, k_ref, v_ref, mix_ref, norm_ref, probs_ref = take(11)
    full, cot_full, bias, send_d, send_s, d_send, d_recv, s_send, s_recv = take(9)
    dp = lax.axis_index("dp")
    meet(n_dp, n_t, inside)
    if inside:
        gather = Gather(n_dp, n_t, 0, block_ref.shape[0], width, block_ref, gathered, *refs)
        gather.start()
        weights = Weights(shard, width, gathered=gathered)
    else:
        gathered[...] = jnp.zeros_like(gathered)
        weights = Weights(shard, width, whole=block_ref)

    full[rows - rows % 8 :, :] = jnp.zeros((padded - rows + rows % 8, width), F32)
    full[:rows, :] = x_ref[...].astype(F32)
    cot_full[rows - rows % 8 :, :] = jnp.zeros((padded - rows + rows % 8, width), F32)
    cot_full[:rows, :] = cot_ref[...].astype(F32)
    bias[...] = image_bias(rows, padded)
    unit, _ = centre(full[...])
    norm_ref[...] = unit.astype(BF16)
    if inside:
        gather.pass_to_chips()
        gather.pass_to_core()
        gather.arrive()
        gather.drain()

    norms = norm_rows(weights.small(), experts)
    unit, _ = centre(full[...])
    normed = (unit * norms[0:1] + norms[1:2]).astype(BF16)
    norm_ref[...] = normed
    q_ref[...] = nn(normed, weights(0)).astype(BF16)
    k_ref[...] = nn(normed, weights(1)).astype(BF16)
    v_ref[...] = nn(normed, weights(2)).astype(BF16)
    low, high = half_masks()

    def heads(j, carry):
        at = pl.ds(pl.multiple_of(j * LANES, LANES), LANES)
        query, key, value = q_ref[:, at], k_ref[:, at], v_ref[:, at]
        first = nn(soft_scores(query * low, key, bias[...]).astype(BF16), value)
        second = nn(soft_scores(query * high, key, bias[...]).astype(BF16), value)
        mix_ref[:, at] = (first * low.astype(F32) + second * high.astype(F32)).astype(BF16)
        return carry

    lax.fori_loop(0, width // LANES, heads, 0)
    residual = full[...] + nn(mix_ref[...], weights(OUT))
    res_ref[...] = residual
    unit, _ = centre(residual)
    moe = (unit * norms[2:3] + norms[3:4]).astype(BF16)
    moe_ref[...] = moe
    probs = router_probs(nn(moe, weights.small()), experts)
    probs_ref[...] = probs
    cot = cot_full[...]
    full[...] = pick_gate(probs, cols_ref[:, 0:1]) * cot
    cot_full[...] = pick_gate(probs, cols_ref[:, 1:2]) * cot

    def selectors(p):
        slot = lax.broadcasted_iota(jnp.int32, (rooms, padded), 0) + p * rooms
        first = (slot == slots_ref[0:1, :]).astype(F32)
        second = (slot == slots_ref[1:2, :]).astype(F32)
        return first, second

    def d_copy(k):
        to = lax.rem(dp + k, n_dp)
        return remote(send_d.at[to], recv_d.at[dp], d_send.at[k], d_recv.at[k], {"dp": to})

    def s_copy(k):
        to = lax.rem(dp + k, n_dp)
        return remote(send_s.at[to], recv_s.at[dp], s_send.at[k], s_recv.at[k], {"dp": to})

    def dispatch(k, carry):
        to = lax.rem(dp + k, n_dp)
        first, second = selectors(to)
        send_d[to] = nn((first + second).astype(BF16), moe_ref[...]).astype(BF16)

        @pl.when(k > 0)
        def _():
            d_copy(k).start()

        return carry

    def dispatch_grad(k, carry):
        to = lax.rem(dp + k, n_dp)
        first, second = selectors(to)
        rows_grad = nn(first.astype(BF16), full[...].astype(BF16)) + nn(second.astype(BF16), cot_full[...].astype(BF16))
        send_s[to] = rows_grad.astype(BF16)

        @pl.when(k > 0)
        def _():
            s_copy(k).start()

        return carry

    lax.fori_loop(0, n_dp, dispatch, 0)
    lax.fori_loop(0, n_dp, dispatch_grad, 0)
    recv_d[dp] = send_d[dp]
    recv_s[dp] = send_s[dp]
    for k in range(1, n_dp):
        d_copy(k).wait()
    for k in range(1, n_dp):
        s_copy(k).wait()


def forward(cfg, cid, x, cot, cols, slots, block):
    n_dp, n_t, rows, padded, width, experts, rooms, shard, inside = cfg
    rows_block = ceil_to(5 * shard, 16)
    low = jax.ShapeDtypeStruct((padded, width), BF16)
    sent = jax.ShapeDtypeStruct((n_dp, rooms, width), BF16)
    gathered = (n_dp, n_t, rows_block, width) if inside else (1, 1, 16, LANES)
    outs = [jax.ShapeDtypeStruct(gathered, BF16), sent, sent, jax.ShapeDtypeStruct((padded, width), F32)]
    outs += [low] * 6 + [jax.ShapeDtypeStruct((padded, LANES), F32)]
    scratch = [
        VMEM((padded, width), F32),
        VMEM((padded, width), F32),
        VMEM((padded, padded), F32),
        VMEM((n_dp, rooms, width), BF16),
        VMEM((n_dp, rooms, width), BF16),
    ] + [DMA((n_dp,))] * 4
    if inside:
        scratch += Gather.scratch(n_dp, n_t)
    whole = pl.BlockSpec(memory_space=VMEM)
    return pl.pallas_call(
        partial(forward_kernel, cfg),
        out_shape=outs,
        in_specs=[whole] * 5,
        out_specs=[whole] * len(outs),
        scratch_shapes=scratch,
        compiler_params=pltpu.CompilerParams(
            collective_id=cid, has_side_effects=True, vmem_limit_bytes=56 * 2**20
        ),
        name="forward_" + str(rooms),
    )(x, cot, cols, slots, block)


def expert_kernel(chunks, d_ref, s_ref, w_in_ref, w_out_ref, ret_ref, back_ref, g_in_ref, g_out_ref, ret, back, g_in, g_out):
    step = pl.program_id(0)
    rows = d_ref.shape[0]
    chunk = rows // chunks

    @pl.when(step == 0)
    def _():
        ret[...] = jnp.zeros_like(ret)
        back[...] = jnp.zeros_like(back)

    g_in[...] = jnp.zeros_like(g_in)
    g_out[...] = jnp.zeros_like(g_out)
    w_in, w_out = w_in_ref[...], w_out_ref[...]

    def part(c, carry):
        at = pl.ds(pl.multiple_of(c * chunk, 16), chunk)
        took, slot_grad = d_ref[at, :], s_ref[at, :]
        active, slope = gelu_parts(nt(took, w_in))
        active = active.astype(BF16)
        grad_hidden = (nt(slot_grad, w_out) * slope).astype(BF16)
        ret[at, :] += nn(active, w_out)
        back[at, :] += nn(grad_hidden, w_in)
        g_out[...] += tn(active, slot_grad)
        g_in[...] += tn(grad_hidden, took)
        return carry

    lax.fori_loop(0, chunks, part, 0)
    g_in_ref[...] = g_in[...].astype(BF16)
    g_out_ref[...] = g_out[...].astype(BF16)

    @pl.when(step == pl.num_programs(0) - 1)
    def _():
        ret_ref[...] = ret[...].astype(BF16)
        back_ref[...] = back[...].astype(BF16)


def run_expert(took, slot_grad, w_in, w_out):
    rows, width = took.shape
    hidden = w_in.shape[0]
    block = 256
    chunks = next(c for c in range(max(1, rows // 400), rows + 1) if rows % c == 0 and (rows // c) % 16 == 0)
    whole = pl.BlockSpec((rows, width), lambda i: (0, 0))
    part = pl.BlockSpec((block, width), lambda i: (i, 0))
    low = jax.ShapeDtypeStruct((rows, width), BF16)
    grad = jax.ShapeDtypeStruct((hidden, width), BF16)
    return pl.pallas_call(
        partial(expert_kernel, chunks),
        grid=(hidden // block,),
        out_shape=[low, low, grad, grad],
        in_specs=[whole, whole, part, part],
        out_specs=[whole, whole, part, part],
        scratch_shapes=[
            VMEM((rows, width), F32),
            VMEM((rows, width), F32),
            VMEM((block, width), F32),
            VMEM((block, width), F32),
        ],
        compiler_params=pltpu.CompilerParams(vmem_limit_bytes=60 * 2**20),
        cost_estimate=pl.CostEstimate(
            flops=12 * rows * width * hidden, bytes_accessed=12 * rows * width + 8 * hidden * width, transcendentals=0
        ),
        name="expert_" + str(rows),
    )(took, slot_grad, w_in, w_out)


def backward_kernel(cfg, *refs):
    n_dp, n_t, rows, padded, width, experts, rooms, shard, inside = cfg
    refs = list(refs)

    def take(count):
        got = refs[:count]
        del refs[:count]
        return got

    ret_ref, back_ref, x_ref, cot_ref, cols_ref, weights_ref = take(6)
    res_ref, moe_ref, q_ref, k_ref, v_ref, mix_ref, norm_ref, probs_ref = take(8)
    out_ref, gx_ref, sum_ref = take(3)
    full, cot_full, bias, ret_in, back_in, grads, r_send, r_recv, b_send, b_recv = take(10)
    dq, dk, dv = take(3)
    dp = lax.axis_index("dp")
    meet(n_dp, n_t, inside)

    def r_copy(k):
        to = lax.rem(dp + k, n_dp)
        return remote(ret_ref.at[to], ret_in.at[dp], r_send.at[k], r_recv.at[k], {"dp": to})

    def b_copy(k):
        to = lax.rem(dp + k, n_dp)
        return remote(back_ref.at[to], back_in.at[dp], b_send.at[k], b_recv.at[k], {"dp": to})

    for k in range(1, n_dp):
        r_copy(k).start()
    for k in range(1, n_dp):
        b_copy(k).start()
    ret_in[dp] = ret_ref[dp]
    back_in[dp] = back_ref[dp]
    weights = Weights(shard, width, gathered=weights_ref) if inside else Weights(shard, width, whole=weights_ref)
    tail = rows - rows % 8
    full[tail:, :] = jnp.zeros((padded - tail, width), F32)
    full[:rows, :] = x_ref[...].astype(F32)
    cot_full[tail:, :] = jnp.zeros((padded - tail, width), F32)
    cot_full[:rows, :] = cot_ref[...].astype(F32)
    bias[...] = image_bias(rows, padded)
    norms = norm_rows(weights.small(), experts)
    slot_count = n_dp * rooms
    lane = lax.broadcasted_iota(jnp.int32, (padded, slot_count), 1)
    first = (lane == cols_ref[:, 2:3]).astype(F32)
    second = (lane == cols_ref[:, 3:4]).astype(F32)
    both = (first + second).astype(BF16)

    for k in range(1, n_dp):
        r_copy(k).wait()
    returned = ret_in[...].reshape(slot_count, width)
    first_rows = nn(first.astype(BF16), returned)
    second_rows = nn(second.astype(BF16), returned)
    probs = probs_ref[...]
    first_id, second_id = cols_ref[:, 0:1], cols_ref[:, 1:2]
    outcome = res_ref[...] + pick_gate(probs, first_id) * first_rows + pick_gate(probs, second_id) * second_rows
    out_ref[...] = outcome[:rows].astype(BF16)
    cot = cot_full[...]
    first_grad = jnp.sum(first_rows * cot, axis=1, keepdims=True)
    second_grad = jnp.sum(second_rows * cot, axis=1, keepdims=True)
    spot = lax.broadcasted_iota(jnp.int32, probs.shape, 1)
    grad_probs = jnp.where(spot == first_id, first_grad, 0.0) + jnp.where(spot == second_id, second_grad, 0.0)
    grad_logits = (probs * (grad_probs - jnp.sum(probs * grad_probs, axis=1, keepdims=True))).astype(BF16)
    grad_router = tn(moe_ref[...], grad_logits)

    for k in range(1, n_dp):
        b_copy(k).wait()
    grad_moe = nn(both, back_in[...].reshape(slot_count, width)) + nt(grad_logits, weights.small())
    unit, inverse = centre(res_ref[...])
    extra, gain_two, shift_two = norm_back(grad_moe, unit, inverse, norms[2:3])
    grad_residual = cot + extra
    cot_full[...] = grad_residual
    grad_attended = grad_residual.astype(BF16)
    n_all = n_dp * n_t

    def keep(at, value):
        if inside:
            grads[:, :, at * shard : (at + 1) * shard, :] = value.astype(BF16).reshape(n_dp, n_t, shard, width)
        else:
            sum_ref[at] = value

    keep(OUT, tn(mix_ref[...], grad_attended))
    mix_ref_grad = nt(grad_attended, weights(OUT)).astype(BF16)
    dq[...] = mix_ref_grad
    low, high = half_masks()
    low_f, high_f = low.astype(F32), high.astype(F32)
    scale = HEAD_DIM ** (-0.5)

    def heads(j, carry):
        at = pl.ds(pl.multiple_of(j * LANES, LANES), LANES)
        query, key, value, grad = q_ref[:, at], k_ref[:, at], v_ref[:, at], dq[:, at]
        for mask, mask_f in ((low, low_f), (high, high_f)):
            probs = soft_scores(query * mask, key, bias[...])
            grad_probs = nt(grad * mask, value)
            grad_scores = probs * (grad_probs - jnp.sum(probs * grad_probs, axis=1, keepdims=True))
            grad_scores = grad_scores.astype(BF16)
            part_v = tn(probs.astype(BF16), grad)
            part_q = nn(grad_scores, key) * scale
            part_k = tn(grad_scores, query) * scale
            if mask is low:
                sum_q, sum_k, sum_v = part_q * mask_f, part_k * mask_f, part_v * mask_f
            else:
                sum_q, sum_k, sum_v = sum_q + part_q * mask_f, sum_k + part_k * mask_f, sum_v + part_v * mask_f
        dq[:, at] = sum_q.astype(BF16)
        dk[:, at] = sum_k.astype(BF16)
        dv[:, at] = sum_v.astype(BF16)
        return carry

    lax.fori_loop(0, width // LANES, heads, 0)
    keep(0, tn(norm_ref[...], dq[...]))
    keep(1, tn(norm_ref[...], dk[...]))
    keep(2, tn(norm_ref[...], dv[...]))
    grad_normed = nt(dq[...], weights(0)) + nt(dk[...], weights(1)) + nt(dv[...], weights(2))
    unit, inverse = centre(full[...])
    extra, gain_one, shift_one = norm_back(grad_normed, unit, inverse, norms[0:1])
    gx_ref[...] = (cot_full[...] + extra)[:rows].astype(BF16)
    small = small_grads(experts, grad_router, (gain_one, shift_one, gain_two, shift_two))
    if inside:
        at = slice(SMALL * shard, (SMALL + 1) * shard)
        grads[:, :, at, :LANES] = small.astype(BF16).reshape(n_dp, n_t, shard, LANES)
        grads[:, :, at, LANES:] = jnp.zeros((n_dp, n_t, shard, width - LANES), BF16)
        Scatter(n_dp, n_t, grads, sum_ref, *refs).run()
    else:
        sum_ref[SMALL] = jnp.zeros((width, width), F32)
        sum_ref[SMALL, :, :LANES] = small


def backward(cfg, cid, *args):
    n_dp, n_t, rows, padded, width, experts, rooms, shard, inside = cfg
    rows_block = ceil_to(5 * shard, 16)
    total = (rows_block, width) if inside else (5, width, width)
    outs = [jax.ShapeDtypeStruct((rows, width), BF16)] * 2 + [jax.ShapeDtypeStruct(total, F32)]
    scratch = [
        VMEM((padded, width), F32),
        VMEM((padded, width), F32),
        VMEM((padded, padded), F32),
        VMEM((n_dp, rooms, width), BF16),
        VMEM((n_dp, rooms, width), BF16),
        VMEM((n_dp, n_t, rows_block, width) if inside else (1, 1, 16, LANES), BF16),
    ]
    scratch += [DMA((n_dp,))] * 4 + [VMEM((padded, width), BF16)] * 3
    if inside:
        scratch += Scatter.scratch(n_dp, n_t, (rows_block, width))
    whole = pl.BlockSpec(memory_space=VMEM)
    return pl.pallas_call(
        partial(backward_kernel, cfg),
        out_shape=outs,
        in_specs=[whole] * len(args),
        out_specs=[whole] * len(outs),
        scratch_shapes=scratch,
        compiler_params=pltpu.CompilerParams(
            collective_id=cid, has_side_effects=True, vmem_limit_bytes=56 * 2**20
        ),
        name="backward_" + str(rooms),
    )(*args)


def image_blocks(rows):
    blocks = []
    for first in range(0, rows, SEQ):
        start = first // 16 * 16
        blocks.append((start, ceil_to(first - start + SEQ, 16), first - start))
    return blocks


def inside_image(size, first, axis):
    shape = (size, 1) if axis == 0 else (1, size)
    spot = lax.broadcasted_iota(jnp.int32, shape, axis)
    return (spot >= first) & (spot < first + SEQ)


def image_probs(query, key, size, first):
    scores = nt(query, key) * HEAD_DIM ** (-0.5) + jnp.where(inside_image(size, first, 1), 0.0, -1e30)
    power = jnp.exp(scores - jnp.max(scores, axis=1, keepdims=True))
    total = jnp.sum(power, axis=1, keepdims=True)
    return power * jnp.where(inside_image(size, first, 0), 1.0 / total, 0.0)


def join_images(parts, blocks):
    whole = parts[0]
    for (start, _, _), part in zip(blocks[1:], parts[1:]):
        shared = whole.shape[0] - start
        pieces = [whole[:start]]
        if shared > 0:
            pieces.append(whole[start:] + part[:shared])
        whole = jnp.concatenate(pieces + [part[shared:]], axis=0)
    return whole


def pack_block(refs, block, shard, width, experts):
    q_ref, k_ref, v_ref, o_ref, router_ref, *line_refs = refs
    for at, ref in ((0, q_ref), (1, k_ref), (2, v_ref), (OUT, o_ref)):
        block[at * shard : (at + 1) * shard, :] = ref[...].astype(BF16)
    here = slice(SMALL * shard, (SMALL + 1) * shard)
    block[here, :] = jnp.zeros((shard, width), BF16)
    row, column = (lax.broadcasted_iota(jnp.int32, (shard, shard), axis) for axis in (0, 1))
    lane = lax.broadcasted_iota(jnp.int32, (shard, LANES), 1)
    small = jnp.zeros((shard, LANES), F32)
    for at in range(experts + len(line_refs)):
        level = router_ref[at : at + 1, :] if at < experts else line_refs[at - experts][...]
        upright = jnp.sum(jnp.where(row == column, level, 0.0), axis=1, keepdims=True)
        small = jnp.where(lane == at, upright, small)
    block[here, :LANES] = small.astype(BF16)


def find_places(cfg, routes_ref, place, turned, over):
    n_dp, n_t, rows, padded, width, experts, rooms, shard, inside, hid = cfg
    t = lax.axis_index("tensor")
    tok_count = routes_ref.shape[1]
    capacity = (5 * tok_count + 2 * experts - 1) // (2 * experts)
    line = lax.broadcasted_iota(jnp.int32, (experts, tok_count), 0)
    lane = lax.broadcasted_iota(jnp.int32, (experts, tok_count), 1)

    def count(row, until):
        hot = (line == routes_ref[row : row + 1, :]) & (lane < until)
        return jnp.sum(hot.astype(F32), axis=1, keepdims=True)

    total = count(0, tok_count)
    before = (count(0, t * rows), count(1, t * rows))
    long = ceil_to(tok_count, LANES)
    wide = turned.shape[1]
    turned[...] = jnp.full(turned.shape, -1.0, F32)
    everyone = jnp.concatenate(
        [routes_ref[...], jnp.full((2, long - tok_count), experts, jnp.int32)], axis=1
    )
    everyone = jnp.concatenate([everyone, everyone, everyone, everyone], axis=0)
    mine = pltpu.roll(everyone, lax.rem(long - t * rows, long), 1)[:, :wide]
    spot = lax.broadcasted_iota(jnp.int32, (8, wide), 1)
    mine = jnp.where(spot < rows, mine, experts)
    line = lax.broadcasted_iota(jnp.int32, (experts, wide), 0)
    first, second = line == mine[0:1], line == mine[1:2]
    down, across = (lax.broadcasted_iota(jnp.int32, (wide, wide), axis) for axis in (0, 1))
    earlier = (down < across).astype(F32).astype(BF16)
    own = jnp.sum(first.astype(F32), axis=1, keepdims=True)
    first_rank = nn(first.astype(F32).astype(BF16), earlier)
    second_rank = nn(second.astype(F32).astype(BF16), earlier)

    def slot(choice, hot, rank, place):
        kept = hot & (place < capacity)
        here = jnp.sum(jnp.where(kept, rank + 1.0, 0.0), axis=0, keepdims=True) - 1.0
        good = (here >= 0.0) & (here < rooms)
        return jnp.where(good, choice.astype(F32) * rooms + here, -1.0), jnp.max(here, axis=1, keepdims=True)

    first_slot, first_most = slot(mine[0:1], first, first_rank, first_rank + before[0])
    second_slot, second_most = slot(mine[1:2], second, second_rank + own, second_rank + total + before[1])
    turned[0:1, :] = first_slot
    turned[1:2, :] = second_slot
    turned[2:3, :] = mine[0:1].astype(F32)
    turned[3:4, :] = mine[1:2].astype(F32)
    place[...] = turned[...].T
    most = jnp.maximum(first_most, second_most)
    over[...] = jnp.broadcast_to(jnp.where(most >= rooms, 1.0, 0.0), over.shape)


def step_kernel(cfg, *refs):
    n_dp, n_t, rows, padded, width, experts, rooms, shard, inside, hid = cfg
    refs = list(refs)

    def take(count):
        got = refs[:count]
        del refs[:count]
        return got

    x_ref, cot_ref, routes_ref, e_in_ref, e_out_ref = take(5)
    shared = take(9 if inside else 1)
    out_ref, gx_ref, sum_ref, g_in_ref, g_out_ref = take(5)
    block, gathered, full, cot_full, bias, res, probs_s = take(7)
    place, turned, over, gate_m, gate_c, gate_s, gate_r, rise_s, rise_r = take(9)
    moe, q_s, k_s, v_s, mix, norm, dk, dv = take(8)
    send_d, send_s, recv_d, recv_s, ret_in, back_in, act, slope = take(8)
    wi, wo, gi, go, gi_in, go_in = take(6)
    d_send, d_recv, s_send, s_recv, r_send, r_recv, b_send, b_recv = take(8)
    f_send, f_recv, e_send, e_recv, own_sems = take(5)
    wi_spread, wo_spread = Spread(n_t, wi, *take(2)), Spread(n_t, wo, *take(2))
    gi_collect, go_collect = Collect(n_t, gi, gi_in, *take(2)), Collect(n_t, go, go_in, *take(2))
    dp, t = lax.axis_index("dp"), lax.axis_index("tensor")
    scale = HEAD_DIM ** (-0.5)
    slot_count = n_dp * rooms
    half, wide = min(256, hid), min(256, width)
    long = gate_m.shape[1]
    early = 2 if hid == width and n_t > 2 else 0
    table = [sorted(range(n_t), key=lambda j: (abs(j - at), j)) for at in range(n_t)]

    def order(p):
        found = jnp.int32(0)
        for at in range(n_t):
            for spot in range(n_t):
                found = found + jnp.where((t == at) & (p == spot), table[at][spot], 0)
        return found

    every = pl.ds(0, rooms)
    cut = max(rooms // 2 // 16 * 16, 16)
    d_copy = Exchange(n_dp, send_d, recv_d, every, d_send, d_recv, True)
    s_first = Exchange(n_dp, send_s, recv_s, pl.ds(0, cut), s_send.at[0], s_recv.at[0], False)
    s_second = Exchange(n_dp, send_s, recv_s, pl.ds(cut, rooms - cut), s_send.at[1], s_recv.at[1], False)
    late = max(rooms * 2 // 5 // 16 * 16, 16)
    r_first = Exchange(n_dp, send_d, ret_in, pl.ds(late, rooms - late), r_send.at[0], r_recv.at[0], False)
    r_second = Exchange(n_dp, send_d, ret_in, pl.ds(0, late), r_send.at[1], r_recv.at[1], False)
    b_copy = Exchange(n_dp, send_s, back_in, every, b_send, b_recv, False)
    f_copy = Exchange(n_dp, gate_s, gate_r, pl.ds(0, 8), f_send, f_recv, False)
    e_copy = Exchange(n_dp, rise_s, rise_r, pl.ds(0, 8), e_send, e_recv, False)

    def column(at):
        return place[:padded, at : at + 1].astype(jnp.int32)

    greet(n_dp, n_t)
    load_in = pltpu.make_async_copy(e_in_ref, g_in_ref, own_sems.at[0])
    load_out = pltpu.make_async_copy(e_out_ref, g_out_ref, own_sems.at[1])
    load_in.start()
    load_out.start()
    if inside:
        pack_block(shared, block, shard, width, experts)
        size = len(Gather.scratch(n_dp, n_t))
        gather_a = Gather(n_dp, n_t, 0, SMALL * shard, width, block, gathered, *take(size))
        gather_s = Gather(n_dp, n_t, SMALL * shard, shard, LANES, block, gathered, *take(size))
        gather_b = Gather(n_dp, n_t, OUT * shard, shard, width, block, gathered, *take(size))
        weights = Weights(shard, width, gathered=gathered)
    else:
        weights = Weights(shard, width, whole=shared[0])
    load_in.wait()
    wi[t] = g_in_ref[...].astype(BF16)
    greeted(n_dp, n_t)
    if inside:
        gather_a.start()
        gather_s.start()
        gather_b.start()
    wi_spread.step(0)
    load_out.wait()
    wo[t] = g_out_ref[...].astype(BF16)
    tail = rows - rows % 8
    full[tail:, :] = jnp.zeros((padded - tail, width), F32)
    full[:rows, :] = x_ref[...].astype(F32)
    cot_full[tail:, :] = jnp.zeros((padded - tail, width), F32)
    cot_full[:rows, :] = cot_ref[...].astype(F32)
    bias[...] = image_bias(rows, padded)
    find_places(cfg, routes_ref, place, turned, over)

    def selectors(p):
        slot = lax.broadcasted_iota(jnp.int32, (rooms, padded), 0) + p * rooms
        first = (slot == turned[0:1, :padded].astype(jnp.int32)).astype(F32)
        second = (slot == turned[1:2, :padded].astype(jnp.int32)).astype(F32)
        return first, second

    dk[...] = cot_full[...].astype(BF16)

    def dispatch_grad(k, carry):
        to = lax.rem(dp + k, n_dp)
        first, second = selectors(to)
        got = nn((first + second).astype(BF16), dk[...]).astype(BF16)

        @pl.when(k > 0)
        def _():
            send_s[to] = got

        @pl.when(k == 0)
        def _():
            recv_s[to] = got

        return carry

    lax.fori_loop(0, n_dp, dispatch_grad, 0)
    if inside:
        gather_a.pass_to_chips()
        gather_s.pass_to_chips()
        gather_b.pass_to_chips()
        gather_a.pass_to_core()
        gather_s.pass_to_core()
    if inside:
        gather_a.arrive()
        gather_s.arrive()
    norms = norm_rows(weights.small(), experts)
    unit, _ = centre(full[...])
    norm[...] = (unit * norms[0:1] + norms[1:2]).astype(BF16)
    q_s[...] = nn(norm[...], weights(0)).astype(BF16)
    k_s[...] = nn(norm[...], weights(1)).astype(BF16)
    v_s[...] = nn(norm[...], weights(2)).astype(BF16)
    if inside:
        gather_b.pass_to_core()
    s_first.start_all()
    middle = (t > 0) & (t < n_t - 1)

    @pl.when(jnp.logical_not(middle))
    def _():
        wo_spread.step(0)

    low, high = half_masks()
    low_f, high_f = low.astype(F32), high.astype(F32)
    blocks = image_blocks(rows)

    def heads(j, carry):
        at = pl.ds(pl.multiple_of(j * LANES, LANES), LANES)
        parts = []
        for start, size, first in blocks:
            here = pl.ds(start, size)
            query, key, value = q_s[here, at], k_s[here, at], v_s[here, at]
            one = nn(image_probs(query * low, key, size, first).astype(BF16), value)
            two = nn(image_probs(query * high, key, size, first).astype(BF16), value)
            parts.append(one * low_f + two * high_f)
        mix[:, at] = join_images(parts, blocks).astype(BF16)
        return carry

    lax.fori_loop(0, width // LANES // 2, heads, 0)
    @pl.when(middle)
    def _():
        wi_spread.step(1)

    lax.fori_loop(width // LANES // 2, width // LANES, heads, 0)
    if inside:
        gather_b.arrive()
    residual = full[...] + nn(mix[...], weights(OUT))
    res[...] = residual
    unit, _ = centre(residual)
    moe[...] = (unit * norms[2:3] + norms[3:4]).astype(BF16)
    probs_s[...] = router_probs(nn(moe[...], weights.small()), experts)

    spot = lax.broadcasted_iota(jnp.int32, (padded, LANES), 1)
    first_gate, second_gate = pick_gate(probs_s[...], column(2)), pick_gate(probs_s[...], column(3))
    place[:padded, :] = jnp.where(spot == 4, first_gate, jnp.where(spot == 5, second_gate, place[:padded, :]))
    turned[...] = place[...].T
    gate_line = lax.broadcasted_iota(jnp.int32, (8, padded), 0)

    def terms(gate):
        one = gate.astype(BF16).astype(F32)
        two = (gate - one).astype(BF16).astype(F32)
        three = gate - one - two
        stack = jnp.where(gate_line == 0, one, jnp.where(gate_line == 1, two, jnp.where(gate_line == 2, three, 0.0)))
        return stack.astype(BF16)

    first_terms, second_terms = terms(turned[4:5, :padded]), terms(turned[5:6, :padded])
    def dispatch(k, carry):
        to = lax.rem(dp + k, n_dp)
        first, second = selectors(to)
        got = nn((first + second).astype(BF16), moe[...]).astype(BF16)

        @pl.when(k > 0)
        def _():
            send_d[to] = got
            d_copy.start(k)

        @pl.when(k == 0)
        def _():
            recv_d[to] = got

        return carry

    lax.fori_loop(0, n_dp, dispatch, 0)

    @pl.when(middle)
    def _():
        if n_t > 2:
            wi_spread.step(2)
        wo_spread.step(0)

    def dispatch_gates(k, carry):
        to = lax.rem(dp + k, n_dp)
        first, second = selectors(to)
        gate = nt(first_terms, first.astype(BF16)) + nt(second_terms, second.astype(BF16))
        gate = jnp.sum(gate, axis=0, keepdims=True)

        @pl.when(k > 0)
        def _():
            gate_s[to, :, :rooms] = jnp.broadcast_to(gate, (8, rooms))
            f_copy.start(k)

        @pl.when(k == 0)
        def _():
            gate_r[to, :, :rooms] = jnp.broadcast_to(gate, (8, rooms))

        return carry

    lax.fori_loop(0, n_dp, dispatch_gates, 0)

    def hidden_units(j, g):
        active, steep = gelu_parts(nn(recv_d[g], wi[j]))
        act[j, g] = active.astype(BF16)
        slope[j, g] = steep.astype(BF16)

    n_chip, chip = n_dp // 2, dp // 2

    def chip_rows(ref, c, *lead):
        value = ref[(*lead, pl.ds(2 * c, 2))]
        return value.reshape(2 * rooms, value.shape[-1])

    def chip_store(ref, c, value, *lead):
        ref[(*lead, pl.ds(2 * c, 2))] = value.reshape(2, rooms, value.shape[-1])

    def own_hidden(k, carry):
        @pl.when(k > 0)
        def _():
            d_copy.wait_from(k)

        hidden_units(t, lax.rem(dp + n_dp - k, n_dp))
        return carry

    lax.fori_loop(0, n_dp, own_hidden, 0)
    s_second.start_all()

    @pl.when(middle)
    def _():
        wo_spread.step(1)


    @pl.when(jnp.logical_not(middle))
    def _():
        wi_spread.step(1)
        if n_t > 2:
            wi_spread.step(2)

    def other_hidden(i, carry):
        q = i // n_dp
        p = jnp.where(q == 0, 1, jnp.where(q == 1, n_t - 1, q))
        hidden_units(order(p), lax.rem(i, n_dp))
        return carry

    lax.fori_loop(0, n_dp, other_hidden, 0, unroll=2)
    for s in range(3, n_t):
        wi_spread.step(s)
    if n_t > 2:
        lax.fori_loop(n_dp, 2 * n_dp, other_hidden, 0, unroll=2)
    gate_m[...] = jnp.zeros_like(gate_m)
    f_copy.wait_all()
    f_copy.wait_sent()
    for g in range(n_dp):
        gate_m[g : g + 1, :rooms] = gate_r[g, 0:1, :rooms]
    gate_c[...] = gate_m[...].T
    for half_copy in (s_first, s_second):
        half_copy.wait_all()
        half_copy.wait_sent()
    slot_grads = send_s
    room_lane = lax.broadcasted_iota(jnp.int32, (rooms, LANES), 1)

    def slot_grad(g, carry):
        gate = jnp.sum(jnp.where(room_lane == g, gate_c[:rooms, :], 0.0), axis=1, keepdims=True)
        slot_grads[g] = (gate * recv_s[g].astype(F32)).astype(BF16)
        return carry

    lax.fori_loop(0, n_dp, slot_grad, 0)

    def outer_grad(i, carry):
        j = order(n_t - 1 - i // (hid // half))
        at = pl.ds(pl.multiple_of(lax.rem(i, hid // half) * half, half), half)
        left = act[j, :, :, at].reshape(slot_count, half)
        go[j, at, :] = tn(left, slot_grads[...].reshape(slot_count, width)).astype(BF16)

        @pl.when(lax.rem(i, hid // half) == hid // half - 1)
        def _():
            go_collect.begin(j)

        return carry

    lax.fori_loop(0, hid // half, outer_grad, 0)
    if n_t > 3:
        lax.fori_loop(2 * n_dp, (n_t - 1) * n_dp, other_hidden, 0, unroll=2)
    @pl.when(jnp.logical_not(middle))
    def _():
        wo_spread.step(1)

    @pl.when(middle)
    def _():
        if n_t > 2:
            wo_spread.step(2)

    lax.fori_loop(hid // half, n_t * (hid // half), outer_grad, 0)

    def hidden_grads(p):
        j = order(p)

        def one(i, inner):
            grad = nt(chip_rows(slot_grads, i), wo[j]) * chip_rows(slope, i, j).astype(F32)
            chip_store(slope, i, grad.astype(BF16), j)
            return inner

        lax.fori_loop(0, n_chip, one, 0, unroll=2)

    def inner_grads(p):
        j = order(p)

        def one(i, inner):
            at = pl.ds(pl.multiple_of(i * wide, wide), wide)
            left = recv_d[:, :, at].reshape(slot_count, wide)
            gi[j, at, :] = tn(left, slope[j].reshape(slot_count, hid)).astype(BF16)
            return inner

        lax.fori_loop(0, width // wide, one, 0)

    def split(total):
        main = total.astype(BF16)
        return main, (total - main.astype(F32)).astype(BF16)

    def some_back(g, inner):
        near_a, near_b = order(0), order(1)
        total = nn(chip_rows(act, g, near_a), wo[near_a]) + nn(chip_rows(act, g, near_b), wo[near_b])
        for j, part in zip((near_a, near_b), split(total)):
            chip_store(act, g, part, j)
        return inner

    def hidden_step(p, carry):
        @pl.when(p == 1)
        def _():
            if n_t > 2:
                go_collect.step(1, True)

        @pl.when((p == 2) & jnp.logical_not(middle))
        def _():
            if n_t > 2:
                wo_spread.step(2)

        @pl.when(p == 3)
        def _():
            for s in range(3, n_t):
                wo_spread.step(s)

        hidden_grads(p)

        @pl.when((p < n_t - 1) & jnp.logical_not(middle))
        def _():
            inner_grads(p)

        if early:

            @pl.when((p == early) & jnp.logical_not(middle))
            def _():
                lax.fori_loop(0, n_chip, some_back, 0)

        return carry

    lax.fori_loop(0, n_t, hidden_step, 0)
    d_copy.wait_sent()

    def hand_out(c, value, buffer, own, copies):
        for q in range(2):
            to = 2 * c + q
            k = lax.rem(to - dp + n_dp, n_dp)
            part = value[q * rooms : (q + 1) * rooms]

            @pl.when(k > 0)
            def _():
                buffer[to] = part
                if copies is not None:
                    copies.start(k)

            @pl.when(k == 0)
            def _():
                own[to] = part

    def give_back_grad(i, carry):
        c = lax.rem(chip + 1 + i, n_chip)
        total = nt(chip_rows(slope, c, 0), wi[0])
        for j in range(1, n_t):
            total = total + nt(chip_rows(slope, c, j), wi[j])
        hand_out(c, total.astype(BF16), send_s, back_in, b_copy)
        return carry

    lax.fori_loop(0, n_chip, give_back_grad, 0)
    for e in range(2, n_t - 1):
        go_collect.step(e, True)

    gate_c[...] = jnp.zeros_like(gate_c)

    def give_back(c, total):
        rise = jnp.sum(total * chip_rows(recv_s, c).astype(F32), axis=1, keepdims=True)
        for q in range(2):
            found = rise[q * rooms : (q + 1) * rooms]
            gate_c[:rooms, :] = jnp.where(room_lane == 2 * c + q, found, gate_c[:rooms, :])
        hand_out(c, total.astype(BF16), send_d, ret_in, None)

    def give_back_whole(c, carry):
        total = nn(chip_rows(act, c, 0), wo[0])
        for j in range(1, n_t):
            total = total + nn(chip_rows(act, c, j), wo[j])
        give_back(c, total)
        return carry

    def give_back_rest(c, carry):
        near_a, near_b = order(0), order(1)
        total = chip_rows(act, c, near_a).astype(F32) + chip_rows(act, c, near_b).astype(F32)
        for p in range(early, n_t):
            j = order(p)
            total = total + nn(chip_rows(act, c, j), wo[j])
        give_back(c, total)
        return carry

    def last_inner():
        inner_grads(n_t - 1)

        def send_inner(p, carry):
            gi_collect.begin(order(n_t - 1 - p))
            return carry

        lax.fori_loop(0, n_t, send_inner, 0)

    if early:

        @pl.when(jnp.logical_not(middle))
        def _():
            last_inner()
            lax.fori_loop(0, n_chip, give_back_rest, 0)

        @pl.when(middle)
        def _():
            lax.fori_loop(0, n_chip, give_back_whole, 0)

    else:

        @pl.when(jnp.logical_not(middle))
        def _():
            last_inner()

        lax.fori_loop(0, n_chip, give_back_whole, 0)

    gate_m[...] = gate_c[...].T
    for g in range(n_dp):
        row = jnp.broadcast_to(gate_m[g : g + 1, :], (8, long))

        @pl.when(dp == g)
        def _():
            rise_r[g] = row

        @pl.when(dp != g)
        def _():
            rise_s[g] = row

    e_copy.start_all()

    @pl.when(middle)
    def _():
        def one(p, inner):
            inner_grads(p)
            return inner

        lax.fori_loop(0, n_t, one, 0)

    lane = lax.broadcasted_iota(jnp.int32, (padded, slot_count), 1)
    both = ((lane == column(0)).astype(F32) + (lane == column(1)).astype(F32)).astype(BF16)
    unit, inverse = centre(res[...])
    b_copy.wait_sent()
    r_first.start_all()
    b_copy.wait_all()
    e_copy.wait_all()
    e_copy.wait_sent()
    room = lax.broadcasted_iota(jnp.int32, (padded, long), 1)

    slots_of = (column(0), column(1))

    found = [jnp.zeros((padded, long), F32)] * 2
    for e in range(n_dp):
        row = jnp.where(room[0:1] < rooms, rise_r[e, 0:1, :], 0.0)
        for at, slot in enumerate(slots_of):
            here = jnp.where(slot < (e + 1) * rooms, slot - e * rooms, -1)
            found[at] = jnp.where(room == here, row, found[at])
    first_grad, second_grad = (jnp.sum(one, axis=1, keepdims=True) for one in found)
    probs = probs_s[...]
    spot = lax.broadcasted_iota(jnp.int32, probs.shape, 1)
    grad_probs = jnp.where(spot == column(2), first_grad, 0.0) + jnp.where(spot == column(3), second_grad, 0.0)
    grad_logits = (probs * (grad_probs - jnp.sum(probs * grad_probs, axis=1, keepdims=True))).astype(BF16)
    grad_router = tn(moe[...], grad_logits)
    grad_moe = nn(both, back_in[...].reshape(slot_count, width)) + nt(grad_logits, weights.small())
    extra, gain_two, shift_two = norm_back(grad_moe, unit, inverse, norms[2:3])
    grad_residual = cot_full[...] + extra
    cot_full[...] = grad_residual
    grad_attended = grad_residual.astype(BF16)

    pairs = width // LANES
    if inside:
        size = len(Reduce.scratch(n_dp, n_t, 1, (shard, LANES)))
        out_sum = Reduce(n_dp, n_t, lambda p: sum_ref.at[pl.ds(OUT * shard, shard)], *take(size))
        pair_sum = Reduce(
            n_dp, n_t, lambda p: sum_ref.at[pl.ds(0, 3 * shard), pl.ds(pl.multiple_of(p * LANES, LANES), LANES)], *take(size)
        )
        small_sum = Reduce(n_dp, n_t, lambda p: sum_ref.at[pl.ds(SMALL * shard, shard), pl.ds(0, LANES)], *take(size))
        sum_ref[SMALL * shard : (SMALL + 1) * shard, LANES:] = jnp.zeros((shard, width - LANES), F32)
        out_sum.put(0, 0, tn(mix[...], grad_attended))
        out_sum.to_core(0)
    else:
        sum_ref[OUT] = tn(mix[...], grad_attended)
    dq = mix
    dq[...] = nt(grad_attended, weights(OUT)).astype(BF16)

    def heads_back(j, carry):
        at = pl.ds(pl.multiple_of(j * LANES, LANES), LANES)
        query, key, value, grad = q_s[:, at], k_s[:, at], v_s[:, at], dq[:, at]
        for mask, mask_f in ((low, low_f), (high, high_f)):
            probs = soft_scores(query * mask, key, bias[...])
            grad_probs = nt(grad * mask, value)
            grad_scores = probs * (grad_probs - jnp.sum(probs * grad_probs, axis=1, keepdims=True))
            grad_scores = grad_scores.astype(BF16)
            part_v = tn(probs.astype(BF16), grad)
            part_q = nn(grad_scores, key) * scale
            part_k = tn(grad_scores, query) * scale
            if mask is low:
                sum_q, sum_k, sum_v = part_q * mask_f, part_k * mask_f, part_v * mask_f
            else:
                sum_q, sum_k, sum_v = sum_q + part_q * mask_f, sum_k + part_k * mask_f, sum_v + part_v * mask_f
        dq[:, at] = sum_q.astype(BF16)
        dk[:, at] = sum_k.astype(BF16)
        dv[:, at] = sum_v.astype(BF16)
        @pl.when(j == pairs // 2)
        def _():
            if n_t > 2:
                gi_collect.step(1, True)

        if inside:
            for spot, ref in enumerate((dq, dk, dv)):
                pair_sum.put(j, spot * shard, tn(norm[...], ref[:, at]))
            pair_sum.to_core(j)

            @pl.when(j == 0)
            def _():
                out_sum.to_chips(0)

            @pl.when(j > 0)
            def _():
                pair_sum.to_chips(j - 1)

        return carry

    lax.fori_loop(0, pairs, heads_back, 0)
    if inside:
        pair_sum.to_chips(pairs - 1)
    else:
        for spot, ref in enumerate((dq, dk, dv)):
            sum_ref[spot] = tn(norm[...], ref[...])
    grad_normed = nt(dq[...], weights(0)) + nt(dk[...], weights(1)) + nt(dv[...], weights(2))
    full[tail:, :] = jnp.zeros((padded - tail, width), F32)
    full[:rows, :] = x_ref[...].astype(F32)
    unit, inverse = centre(full[...])
    extra, gain_one, shift_one = norm_back(grad_normed, unit, inverse, norms[0:1])
    gx_ref[...] = (cot_full[...] + extra)[:rows].astype(BF16)
    small = small_grads(experts, grad_router, (gain_one, shift_one, gain_two, shift_two))
    lane = lax.broadcasted_iota(jnp.int32, small.shape, 1)
    small = jnp.where(lane == experts + 4, over[0:1, :], small)
    def combine():
        for half_copy in (r_first, r_second):
            half_copy.wait_all()
            half_copy.wait_sent()
        returned = ret_in[...].reshape(slot_count, width)
        lane = lax.broadcasted_iota(jnp.int32, (padded, slot_count), 1)
        first, second = ((lane == column(at)).astype(F32).astype(BF16) for at in (0, 1))
        first_rows, second_rows = nn(first, returned), nn(second, returned)
        first_gate, second_gate = place[:padded, 4:5], place[:padded, 5:6]
        outcome = res[...] + first_gate * first_rows + second_gate * second_rows
        out_ref[...] = outcome[:rows].astype(BF16)

    if inside:
        small_sum.put(0, 0, small)
        small_sum.to_core(0)
        small_sum.to_chips(0)
        r_second.start_all()
        out_sum.to_line(0)

        def line(p, carry):
            pair_sum.to_line(p)
            return carry

        lax.fori_loop(0, pairs, line, 0)
        small_sum.to_line(0)
        for e in range(2, n_t - 1):
            gi_collect.step(e, True)
        go_collect.finish(g_out_ref)
        combine()
        out_sum.finish(0)

        def last(p, carry):
            pair_sum.finish(p)
            return carry

        lax.fori_loop(0, pairs, last, 0)
        small_sum.finish(0)
        gather_a.drain()
        gather_s.drain()
        gather_b.drain()
    else:
        sum_ref[SMALL] = jnp.zeros((width, width), F32)
        sum_ref[SMALL, :, :LANES] = small
        r_second.start_all()
        for e in range(2, n_t - 1):
            gi_collect.step(e, True)
        go_collect.finish(g_out_ref)
        combine()
    gi_collect.finish(g_in_ref)
    wi_spread.drain()
    wo_spread.drain()


def run_step(cfg, cid, x, cot, routes, e_in, e_out, shared):
    n_dp, n_t, rows, padded, width, experts, rooms, shard, inside, hid = cfg
    rows_block = ceil_to(5 * shard, 16)
    total = (rows_block, width) if inside else (5, width, width)
    outs = [
        jax.ShapeDtypeStruct((rows, width), BF16),
        jax.ShapeDtypeStruct((rows, width), BF16),
        jax.ShapeDtypeStruct(total, F32),
        jax.ShapeDtypeStruct((width, hid), F32),
        jax.ShapeDtypeStruct((hid, width), F32),
    ]
    spread = (n_dp, n_t, rows_block, width) if inside else (1, 1, 16, LANES)
    wide, long = ceil_to(padded, LANES), ceil_to(rooms, LANES)
    rows_f, rows_b = VMEM((padded, width), F32), VMEM((padded, width), BF16)
    slots_b, units_b = VMEM((n_dp, rooms, width), BF16), VMEM((n_t, n_dp, rooms, hid), BF16)
    in_b, out_b = (VMEM((n_t,) + shape, BF16) for shape in ((width, hid), (hid, width)))
    in_more, out_more = (VMEM((n_t + 1,) + shape, BF16) for shape in ((width, hid), (hid, width)))
    scratch = [VMEM((rows_block, width), BF16), VMEM(spread, BF16)]
    scratch += [rows_f, rows_f, VMEM((padded, padded), F32), rows_f, VMEM((padded, LANES), F32)]
    scratch += [VMEM((wide, LANES), F32), VMEM((LANES, wide), F32), VMEM((8, LANES), F32)]
    scratch += [VMEM((LANES, long), F32), VMEM((long, LANES), F32)] + [VMEM((n_dp, 8, long), F32)] * 4
    scratch += [rows_b] * 8 + [slots_b] * 6 + [units_b] * 2
    scratch += [in_b, out_b, in_b, out_b, in_more, out_more]
    scratch += [DMA, DMA((n_dp,))] + [DMA((2,))] * 4 + [DMA] * 6 + [DMA((2,))] + Spread.scratch(n_t) * 2 + Collect.scratch(n_t) * 2
    if inside:
        scratch += Gather.scratch(n_dp, n_t) * 3 + Reduce.scratch(n_dp, n_t, 1, (shard, width))
        scratch += Reduce.scratch(n_dp, n_t, width // LANES, (3 * shard, LANES))
        scratch += Reduce.scratch(n_dp, n_t, 1, (shard, LANES))
    whole, anywhere = pl.BlockSpec(memory_space=VMEM), pl.BlockSpec(memory_space=pl.ANY)
    return pl.pallas_call(
        partial(step_kernel, cfg),
        out_shape=outs,
        in_specs=[whole] * 3 + [anywhere] * 2 + [whole] * len(shared),
        out_specs=[whole] * len(outs),
        scratch_shapes=scratch,
        compiler_params=pltpu.CompilerParams(
            collective_id=cid, has_side_effects=True, vmem_limit_bytes=57 * 2**20
        ),
        name="step_" + str(rooms),
    )(x, cot, routes, e_in, e_out, *shared)


def lay_kernel(shard, experts, out_ref, gx_ref, sum_ref, in_ref, outer_ref, *outs):
    outs[0][...] = out_ref[...]
    outs[1][...] = gx_ref[...]
    for at, spot in ((0, 4), (1, 5), (2, 6), (OUT, 7)):
        outs[spot][...] = sum_ref[at * shard : (at + 1) * shard, :]
    small = sum_ref[SMALL * shard : (SMALL + 1) * shard, :LANES]
    row, column = (lax.broadcasted_iota(jnp.int32, (shard, shard), axis) for axis in (0, 1))
    for at, spot in enumerate((2, 3, 8, 9)):
        upright = small[:, experts + at : experts + at + 1]
        outs[spot][...] = jnp.sum(jnp.where(row == column, upright, 0.0), axis=0, keepdims=True)
    for at in range(experts):
        outs[10][at : at + 1, :] = jnp.sum(jnp.where(row == column, small[:, at : at + 1], 0.0), axis=0, keepdims=True)
    outs[11][...] = in_ref[...]
    outs[12][...] = outer_ref[...]


def lay_out(shard, experts, *args):
    rows, width = args[0].shape
    line = jax.ShapeDtypeStruct((1, shard), F32)
    square = jax.ShapeDtypeStruct((shard, width), F32)
    outs = [jax.ShapeDtypeStruct((rows, width), BF16)] * 2 + [line] * 2 + [square] * 4 + [line] * 2
    outs += [jax.ShapeDtypeStruct((experts, shard), F32)]
    outs += [jax.ShapeDtypeStruct(arg.shape, F32) for arg in args[3:]]

    def full(shape):
        return pl.BlockSpec(shape, lambda i: (0,) * len(shape))

    return pl.pallas_call(
        partial(lay_kernel, shard, experts),
        grid=(1,),
        out_shape=outs,
        in_specs=[full(arg.shape) for arg in args],
        out_specs=[full(out.shape) for out in outs],
        compiler_params=pltpu.CompilerParams(vmem_limit_bytes=32 * 2**20),
        name="outputs",
    )(*args)


def route_pairs(routes, t, row_count, experts, capacity):
    tok_count = routes.shape[0]
    ids = jnp.arange(experts, dtype=jnp.int32)[None, :]
    start = t * row_count
    rows = lax.dynamic_slice_in_dim(routes, start, row_count, 0)
    before = (jnp.arange(tok_count, dtype=jnp.int32) < start)[:, None]
    all_first = routes[:, 0:1] == ids
    all_second = routes[:, 1:2] == ids
    base_first = jnp.sum((all_first & before).astype(jnp.int32), axis=0)
    total_first = jnp.sum(all_first.astype(jnp.int32), axis=0)
    base_second = jnp.sum((all_second & before).astype(jnp.int32), axis=0)
    hot_first = rows[:, 0:1] == ids
    hot_second = rows[:, 1:2] == ids
    at = jnp.arange(row_count, dtype=jnp.int32)
    lower = (at[:, None] > at[None, :]).astype(BF16)
    both = jnp.concatenate([hot_first, hot_second], axis=1).astype(BF16)
    earlier = nn(lower, both).astype(jnp.int32)
    own_first = jnp.sum(hot_first.astype(jnp.int32), axis=0)
    rank_first = earlier[:, :experts]
    rank_second = earlier[:, experts:] + own_first
    place_first = rank_first + base_first
    place_second = earlier[:, experts:] + total_first + base_second
    first = jnp.sum(jnp.where(hot_first & (place_first < capacity), rank_first + 1, 0), axis=1) - 1
    second = jnp.sum(jnp.where(hot_second & (place_second < capacity), rank_second + 1, 0), axis=1) - 1
    return rows, first, second


def per_device(
    n_dp,
    n_t,
    inputs,
    cotangent,
    routes,
    gain_attn,
    shift_attn,
    query_w,
    key_w,
    value_w,
    out_w,
    gain_moe,
    shift_moe,
    router_w,
    expert_in,
    expert_out,
):
    t = lax.axis_index("tensor")
    shard, width = query_w.shape
    experts = router_w.shape[1]
    tok_count = routes.shape[0]
    rows = inputs.shape[0]
    hid = expert_in.shape[2]
    padded = ceil_to(rows, 16)
    capacity = (5 * tok_count + 2 * experts - 1) // (2 * experts)
    inside = shard % 16 == 0
    every = ("dp", "tensor")
    lines = (gain_attn, shift_attn, gain_moe, shift_moe)

    def stack():
        small = jnp.concatenate([router_w] + [line[:, None] for line in lines], axis=1)
        small = jnp.pad(small, ((0, 0), (0, width - small.shape[1])))
        return jnp.stack([query_w, key_w, value_w, small, out_w]).astype(BF16)

    if inside:
        shared = [query_w, key_w, value_w, out_w, router_w.T] + [line[None, :] for line in lines]
    else:
        shared = [lax.all_gather(stack(), every, axis=1, tiled=True)]

    def finish(results):
        summed = results[2]
        if not inside:
            summed = lax.psum_scatter(summed, every, scatter_dimension=1, tiled=True).reshape(5 * shard, width)
        outs = lay_out(shard, experts, results[0], results[1], summed, *results[3:])
        return tuple(outs)

    def slow(_):
        rooms = ceil_to(rows, 16)
        cfg = (n_dp, n_t, rows, padded, width, experts, rooms, shard, inside)
        route_rows, first_rank, second_rank = route_pairs(routes, t, rows, experts, capacity)

        def slot(choice, rank):
            return jnp.where(rank >= 0, choice * rooms + rank, -1)

        slots = jnp.stack([slot(route_rows[:, 0], first_rank), slot(route_rows[:, 1], second_rank)])
        slots = jnp.pad(slots, ((0, 0), (0, padded - rows)), constant_values=-1)
        cols = jnp.concatenate([jnp.pad(route_rows, ((0, padded - rows), (0, 0))), slots.T], axis=1)
        block = stack().reshape(5 * shard, width) if inside else shared[0]
        kept = forward(cfg, 1, inputs, cotangent, cols, slots, block)

        def turn(k):
            return [(i, (i + k) % n_t) for i in range(n_t)]

        both = jnp.stack([expert_in[0].T, expert_out[0]]).astype(BF16)
        parts = [both] + [lax.ppermute(both, "tensor", turn(k)) for k in range(1, n_t)]
        w_in, w_out = (jnp.concatenate([part[i] for part in parts], axis=0) for i in range(2))
        returned, back, grad_inner, grad_outer = run_expert(
            kept[1].reshape(n_dp * rooms, width), kept[2].reshape(n_dp * rooms, width), w_in, w_out
        )
        both = jnp.stack([grad_inner.reshape(n_t, hid, width), grad_outer.reshape(n_t, hid, width)], axis=1)
        total = both[0].astype(F32)
        for k in range(1, n_t):
            total = total + lax.ppermute(both[k], "tensor", turn(-k)).astype(F32)
        results = backward(
            cfg,
            2,
            returned.reshape(n_dp, rooms, width),
            back.reshape(n_dp, rooms, width),
            inputs,
            cotangent,
            cols,
            kept[0] if inside else block,
            *kept[3:],
        )
        return finish((*results, total[0].T, total[1]))

    rooms = min(ceil_to((7 * rows + 2 * experts - 1) // (2 * experts), 16), ceil_to(rows, 16))
    cfg = (n_dp, n_t, rows, padded, width, experts, rooms, shard, inside, hid)
    fast = run_step(cfg, 0, inputs, cotangent, routes.T, expert_in[0], expert_out[0], shared)
    if inside:
        crowded = fast[2][SMALL * shard, experts + 4] > 0.5
    else:
        crowded = lax.psum(fast[2][SMALL, 0, experts + 4], every) > 0.5
    outs = lax.cond(crowded, slow, finish, tuple(fast))
    lined = [out.reshape(shard) if at in (2, 3, 8, 9) else out for at, out in enumerate(outs)]
    lined[10], lined[11], lined[12] = lined[10].T, lined[11][None], lined[12][None]
    return tuple(lined)


def solution(mesh):
    every = ("dp", "tensor")
    rows, line = P(every, None), P(every)
    w_in, w_out = P("dp", None, "tensor"), P("dp", "tensor", None)
    return jax.shard_map(
        partial(per_device, mesh.shape["dp"], mesh.shape["tensor"]),
        mesh=mesh,
        in_specs=(rows, rows, P("dp", None), line, line, rows, rows, rows, rows, line, line, rows, w_in, w_out),
        out_specs=(rows, rows, line, line, rows, rows, rows, rows, line, line, rows, w_in, w_out),
        check_vma=False,
    )
```

```python
from functools import partial

import jax
import jax.numpy as jnp
from jax import lax
from jax.experimental import pallas as pl
from jax.experimental.pallas import tpu as pltpu
from jax.sharding import PartitionSpec as P

SEQ = 197
HEAD_DIM = 64
LANES = 128
MESH = pl.DeviceIdType.MESH
F32 = jnp.float32
BF16 = jnp.bfloat16
VMEM = pltpu.VMEM
DMA = pltpu.SemaphoreType.DMA
SMALL, OUT = 3, 4


def ceil_to(value, unit):
    return (value + unit - 1) // unit * unit


def nn(left, right):
    return lax.dot_general(left, right, (((1,), (0,)), ((), ())), preferred_element_type=F32)


def nt(left, right):
    return lax.dot_general(left, right, (((1,), (1,)), ((), ())), preferred_element_type=F32)


def tn(left, right):
    return lax.dot_general(left, right, (((0,), (0,)), ((), ())), preferred_element_type=F32)


def remote(src, dst, send, recv, device):
    return pltpu.make_async_remote_copy(
        src_ref=src, dst_ref=dst, send_sem=send, recv_sem=recv, device_id=device, device_id_type=MESH
    )


def meet(n_dp, n_t, z_too):
    dp = lax.axis_index("dp")
    t = lax.axis_index("tensor")
    bar = pltpu.get_barrier_semaphore()
    for k in range(1, n_dp):
        pl.semaphore_signal(bar, inc=1, device_id={"dp": lax.rem(dp + k, n_dp)}, device_id_type=MESH)
    if z_too:
        for k in range(1, n_t):
            pl.semaphore_signal(bar, inc=1, device_id={"tensor": lax.rem(t + k, n_t)}, device_id_type=MESH)
    pl.semaphore_wait(bar, n_dp - 1 + (n_t - 1 if z_too else 0))


class Gather:
    def __init__(self, n_dp, n_t, first, count, lanes, block, out, own_sem, z_send, z_recv, c_send, c_recv, k_send, k_recv):
        self.n_t, self.n_chip = n_t, n_dp // 2
        self.rows, self.lanes = pl.ds(first, count), pl.ds(0, lanes)
        self.block, self.out, self.own_sem = block.at[self.rows, self.lanes], out, own_sem
        self.z_sems, self.c_sems, self.k_sems = (z_send, z_recv), (c_send, c_recv), (k_send, k_recv)
        self.dp, self.t = lax.axis_index("dp"), lax.axis_index("tensor")
        self.chip, self.core = self.dp // 2, lax.rem(self.dp, 2)
        self.other = self.chip * 2 + 1 - self.core

    @staticmethod
    def scratch(n_dp, n_t):
        n_chip = n_dp // 2
        return [DMA, DMA, DMA((n_t,)), DMA, DMA((n_chip, n_t)), DMA, DMA]

    def place(self, dp, t):
        return self.out.at[dp, t, self.rows, self.lanes]

    def z_copy(self, k):
        send, recv = self.z_sems
        to = lax.rem(self.t + k, self.n_t)
        return remote(self.block, self.place(self.dp, self.t), send, recv.at[k], {"tensor": to})

    def chip_copy(self, k, j):
        send, recv = self.c_sems
        here = self.place(self.dp, lax.rem(self.t + self.n_t - j, self.n_t))
        to = lax.rem(self.chip + k, self.n_chip) * 2 + self.core
        return remote(self.block if j == 0 else here, here, send, recv.at[k, j], {"dp": to})

    def core_copy(self, k, j):
        send, recv = self.k_sems
        src = lax.rem(self.chip + self.n_chip - k, self.n_chip) * 2 + self.core
        here = self.place(src, lax.rem(self.t + self.n_t - j, self.n_t))
        own = k == 0 and j == 0
        return remote(self.block if own else here, here, send, recv, {"dp": self.other})

    def own_copy(self):
        return pltpu.make_async_copy(self.block, self.place(self.dp, self.t), self.own_sem)

    def start(self):
        for k in range(1, self.n_t):
            self.z_copy(k).start()
        self.own_copy().start()
        for k in range(1, self.n_chip):
            self.chip_copy(k, 0).start()
        self.core_copy(0, 0).start()

    def pass_to_chips(self):
        for j in range(1, self.n_t):
            self.z_copy(j).wait_recv()
            for k in range(1, self.n_chip):
                self.chip_copy(k, j).start()
            self.core_copy(0, j).start()

    def pass_to_core(self):
        for j in range(self.n_t):
            for k in range(1, self.n_chip):
                self.chip_copy(k, j).wait_recv()
                self.core_copy(k, j).start()

    def arrive(self):
        self.own_copy().wait()
        self.wait_bytes(self.out.at[pl.ds(0, self.n_chip), :, self.rows, self.lanes], self.k_sems[1])

    @staticmethod
    def wait_bytes(part, sem):
        pltpu.make_async_copy(part, part, sem).wait()

    def drain(self):
        self.wait_bytes(self.out.at[0, pl.ds(0, self.n_t - 1), self.rows, self.lanes], self.z_sems[0])
        self.wait_bytes(self.out.at[pl.ds(0, self.n_chip - 1), :, self.rows, self.lanes], self.c_sems[0])
        self.wait_bytes(self.out.at[pl.ds(0, self.n_chip), :, self.rows, self.lanes], self.k_sems[0])


class Scatter:
    def __init__(
        self, n_dp, n_t, grads, out, core_in, half, chip_in, part, z_in, k_send, k_recv, c_send, c_recv, z_send, z_recv
    ):
        self.n_t, self.n_chip = n_t, n_dp // 2
        self.grads, self.out = grads, out
        self.core_in, self.half, self.chip_in, self.part, self.z_in = core_in, half, chip_in, part, z_in
        self.k_sems, self.c_sems, self.z_sems = (k_send, k_recv), (c_send, c_recv), (z_send, z_recv)
        self.dp, self.t = lax.axis_index("dp"), lax.axis_index("tensor")
        self.chip, self.core = self.dp // 2, lax.rem(self.dp, 2)
        self.other = self.chip * 2 + 1 - self.core

    @staticmethod
    def scratch(n_dp, n_t, block):
        n_chip = n_dp // 2
        buffers = [VMEM((n_chip, n_t) + block, BF16)] + [VMEM((n_chip - 1, n_t) + block, BF16)] * 2
        buffers += [VMEM((n_t - 1,) + block, BF16)] * 2
        return buffers + [DMA((n_chip,))] * 4 + [DMA((n_t,))] * 2

    def core_copy(self, k):
        to = lax.rem(self.chip + k, self.n_chip)
        src = self.grads.at[to * 2 + 1 - self.core]
        return remote(src, self.core_in.at[k], self.k_sems[0].at[k], self.k_sems[1].at[k], {"dp": self.other})

    def chip_copy(self, k):
        to = lax.rem(self.chip + k, self.n_chip) * 2 + self.core
        return remote(self.half.at[k - 1], self.chip_in.at[k - 1], self.c_sems[0].at[k], self.c_sems[1].at[k], {"dp": to})

    def z_copy(self, k):
        to = lax.rem(self.t + k, self.n_t)
        return remote(self.part.at[k - 1], self.z_in.at[k - 1], self.z_sems[0].at[k], self.z_sems[1].at[k], {"tensor": to})

    def run(self, between=None, after=None):
        n_chip, n_t = self.n_chip, self.n_t
        order = list(range(1, n_chip)) + [0]
        for k in order:
            self.core_copy(k).start()
        for k in order:
            self.core_copy(k).wait_recv()
            if k > 0:
                to = lax.rem(self.chip + k, n_chip) * 2 + self.core
                self.half[k - 1] = (self.grads[to].astype(F32) + self.core_in[k].astype(F32)).astype(BF16)
                self.chip_copy(k).start()
        if between is not None:
            between()
        for k in range(1, n_chip):
            self.chip_copy(k).wait_recv()
        for k in list(range(1, n_t)) + [0]:
            row = lax.rem(self.t + k, n_t)
            total = self.grads[self.dp, row].astype(F32) + self.core_in[0, row].astype(F32)
            for c in range(1, n_chip):
                total = total + self.chip_in[c - 1, row].astype(F32)
            if k > 0:
                self.part[k - 1] = total.astype(BF16)
                self.z_copy(k).start()
            else:
                self.out[...] = total
        if after is not None:
            after()
        for k in range(1, n_t):
            self.z_copy(k).wait_recv()
            self.out[...] += self.z_in[k - 1].astype(F32)
        for k in range(n_chip):
            self.core_copy(k).wait_send()
        for k in range(1, n_chip):
            self.chip_copy(k).wait_send()
        for k in range(1, n_t):
            self.z_copy(k).wait_send()


class Reduce:
    def __init__(self, n_dp, n_t, out, grads, core_in, half, chip_in, part, z_in, *sems):
        self.n_t, self.n_chip, self.out = n_t, n_dp // 2, out
        self.grads, self.core_in, self.half = grads, core_in, half
        self.chip_in, self.part, self.z_in = chip_in, part, z_in
        self.k_sems, self.c_sems, self.z_sems = sems[0:3], sems[3:5], sems[5:7]
        self.dp, self.t = lax.axis_index("dp"), lax.axis_index("tensor")
        self.chip, self.core = self.dp // 2, lax.rem(self.dp, 2)
        self.other = self.chip * 2 + 1 - self.core

    @staticmethod
    def scratch(n_dp, n_t, parts, block):
        n_chip = n_dp // 2
        sizes = [(n_dp, n_t), (n_chip, n_t), (n_chip - 1, n_t), (n_chip - 1, n_t), (n_t - 1,), (n_t - 1,)]
        return [VMEM((parts,) + size + block, BF16) for size in sizes] + [DMA((parts,))] * 7

    def put(self, p, first, value):
        n_dp, n_t = self.n_chip * 2, self.n_t
        count, lanes = value.shape[0] // (n_dp * n_t), value.shape[1]
        self.grads[p, :, :, first : first + count, :] = value.astype(BF16).reshape(n_dp, n_t, count, lanes)

    def core_copy(self, p, k):
        src = self.grads.at[p, lax.rem(self.chip + k, self.n_chip) * 2 + 1 - self.core]
        send, far, near = self.k_sems
        recv = near if isinstance(k, int) and k == 0 else far
        return remote(src, self.core_in.at[p, k], send.at[p], recv.at[p], {"dp": self.other})

    def chip_copy(self, p, k):
        to = lax.rem(self.chip + k, self.n_chip) * 2 + self.core
        send, recv = self.c_sems
        return remote(self.half.at[p, k - 1], self.chip_in.at[p, k - 1], send.at[p], recv.at[p], {"dp": to})

    def z_copy(self, p, k):
        to = lax.rem(self.t + k, self.n_t)
        send, recv = self.z_sems
        return remote(self.part.at[p, k - 1], self.z_in.at[p, k - 1], send.at[p], recv.at[p], {"tensor": to})

    def to_core(self, p):
        for k in list(range(1, self.n_chip)) + [0]:
            self.core_copy(p, k).start()

    def to_chips(self, p):
        Gather.wait_bytes(self.core_in.at[p, pl.ds(1, self.n_chip - 1)], self.k_sems[1].at[p])
        for k in range(1, self.n_chip):
            to = lax.rem(self.chip + k, self.n_chip) * 2 + self.core
            self.half[p, k - 1] = (self.grads[p, to].astype(F32) + self.core_in[p, k].astype(F32)).astype(BF16)
            self.chip_copy(p, k).start()

    def to_line(self, p):
        self.core_copy(p, 0).wait_recv()
        Gather.wait_bytes(self.chip_in.at[p], self.c_sems[1].at[p])
        for k in list(range(1, self.n_t)) + [0]:
            row = lax.rem(self.t + k, self.n_t)
            total = self.grads[p, self.dp, row].astype(F32) + self.core_in[p, 0, row].astype(F32)
            for c in range(1, self.n_chip):
                total = total + self.chip_in[p, c - 1, row].astype(F32)
            if k > 0:
                self.part[p, k - 1] = total.astype(BF16)
                self.z_copy(p, k).start()
            else:
                self.out(p)[...] = total

    def finish(self, p):
        Gather.wait_bytes(self.z_in.at[p], self.z_sems[1].at[p])
        for k in range(1, self.n_t):
            self.out(p)[...] += self.z_in[p, k - 1].astype(F32)
        Gather.wait_bytes(self.part.at[p], self.z_sems[0].at[p])
        Gather.wait_bytes(self.core_in.at[p], self.k_sems[0].at[p])
        Gather.wait_bytes(self.half.at[p], self.c_sems[0].at[p])


def greet(n_dp, n_t):
    dp, t = lax.axis_index("dp"), lax.axis_index("tensor")
    bar = pltpu.get_barrier_semaphore()
    for k in range(1, n_dp):
        pl.semaphore_signal(bar, inc=1, device_id={"dp": lax.rem(dp + k, n_dp)}, device_id_type=MESH)
    for k in range(1, n_t):
        pl.semaphore_signal(bar, inc=1, device_id={"tensor": lax.rem(t + k, n_t)}, device_id_type=MESH)


def greeted(n_dp, n_t):
    pl.semaphore_wait(pltpu.get_barrier_semaphore(), n_dp - 1 + n_t - 1)


class Exchange:
    def __init__(self, n_dp, src, dst, rows, send, recv, single):
        self.n_dp, self.src, self.dst, self.rows, self.send, self.recv = n_dp, src, dst, rows, send, recv
        self.dp, self.single = lax.axis_index("dp"), single

    def copy(self, k):
        to = lax.rem(self.dp + k, self.n_dp)
        recv = self.recv.at[k] if self.single else self.recv
        return remote(self.src.at[to, self.rows], self.dst.at[self.dp, self.rows], self.send, recv, {"dp": to})

    def start(self, k):
        self.copy(k).start()

    def start_all(self):
        for k in range(1, self.n_dp):
            self.start(k)

    def wait_from(self, k):
        self.copy(k).wait_recv()

    def wait_all(self):
        part = self.dst.at[pl.ds(0, self.n_dp - 1), self.rows]
        pltpu.make_async_copy(part, part, self.recv).wait()

    def wait_sent(self):
        part = self.src.at[pl.ds(0, self.n_dp - 1), self.rows]
        pltpu.make_async_copy(part, part, self.send).wait()


class Spread:
    def __init__(self, n_t, parts, send, recv):
        self.n_t, self.t, self.parts, self.send, self.recv = n_t, lax.axis_index("tensor"), parts, send, recv

    @staticmethod
    def scratch(n_t):
        return [DMA((2, n_t)), DMA((n_t,))]

    def hop(self, j, way):
        here = self.parts.at[j]
        return remote(here, here, self.send.at[way, j], self.recv.at[j], {"tensor": self.t + 1 - 2 * way})

    def step(self, s):
        for way, j, in_line, onward in (
            (0, self.t - s, self.t - s >= 0, self.t + 1 < self.n_t),
            (1, self.t + s, self.t + s < self.n_t, self.t > 0),
        ):
            if s > 0:

                @pl.when(in_line)
                def _():
                    self.hop(j, way).wait_recv()

            @pl.when(in_line & onward)
            def _():
                self.hop(j, way).start()

    def drain(self):
        for s in range(self.n_t):

            @pl.when((self.t - s >= 0) & (self.t + 1 < self.n_t))
            def _():
                self.hop(self.t - s, 0).wait_send()

            @pl.when((self.t + s < self.n_t) & (self.t > 0))
            def _():
                self.hop(self.t + s, 1).wait_send()


class Collect:
    def __init__(self, n_t, parts, came, send, recv):
        self.n_t, self.t, self.parts, self.came, self.send, self.recv = (
            n_t,
            lax.axis_index("tensor"),
            parts,
            came,
            send,
            recv,
        )

    @staticmethod
    def scratch(n_t):
        return [DMA((n_t,)), DMA((n_t + 1,))]

    def hop(self, j, way):
        slot = j if way == 0 else jnp.where(j == self.t - 1, self.n_t, j)
        to = self.t + 1 - 2 * way
        return remote(self.parts.at[j], self.came.at[slot], self.send.at[j], self.recv.at[slot], {"tensor": to})

    def wait_slot(self, slot):
        remote(self.parts.at[0], self.came.at[slot], self.send.at[0], self.recv.at[slot], {"tensor": self.t}).wait_recv()

    def begin(self, j):
        @pl.when((self.t == 0) & (j > 0))
        def _():
            self.hop(j, 0).start()

        @pl.when((self.t == self.n_t - 1) & (j < self.n_t - 1))
        def _():
            self.hop(j, 1).start()

    def step(self, e, far):
        if far:
            right, left = self.n_t - 1 - e + self.t, e - self.n_t + 1 + self.t
        else:
            right, left = e - self.t + 2, 2 * self.n_t - 4 - e - self.t
        for way, j, mine in (
            (0, right, (self.t >= 1) & (right <= self.n_t - 1) & (right > self.t)),
            (1, left, (self.t <= self.n_t - 2) & (left >= 0) & (left < self.t)),
        ):

            @pl.when(mine)
            def _():
                self.wait_slot(j)
                self.parts[j] = (self.parts[j].astype(F32) + self.came[j].astype(F32)).astype(BF16)
                self.hop(j, way).start()

    def finish(self, result):
        result[...] = self.parts[self.t].astype(F32)

        @pl.when(self.t > 0)
        def _():
            self.wait_slot(self.t)
            result[...] += self.came[self.t].astype(F32)

        @pl.when(self.t < self.n_t - 1)
        def _():
            self.wait_slot(self.n_t)
            result[...] += self.came[self.n_t].astype(F32)

        for j in range(self.n_t):

            @pl.when(self.t < j)
            def _():
                self.hop(j, 0).wait_send()

            @pl.when(self.t > j)
            def _():
                self.hop(j, 1).wait_send()


def centre(values):
    centred = values - jnp.mean(values, axis=1, keepdims=True)
    inverse = lax.rsqrt(jnp.mean(centred * centred, axis=1, keepdims=True) + 1e-06)
    return centred * inverse, inverse


def norm_back(grad, unit, inverse, gain):
    scaled = grad * gain
    back = inverse * (
        scaled
        - jnp.mean(scaled, axis=1, keepdims=True)
        - unit * jnp.mean(scaled * unit, axis=1, keepdims=True)
    )
    return back, jnp.sum(grad * unit, axis=0, keepdims=True), jnp.sum(grad, axis=0, keepdims=True)


def norm_picks(experts):
    row, lane = (lax.broadcasted_iota(jnp.int32, (8, LANES), axis) for axis in (0, 1))
    return (row + experts == lane).astype(F32).astype(BF16)


def norm_rows(small, experts):
    return nt(norm_picks(experts), small)


def small_grads(experts, grad_router, rows):
    line = lax.broadcasted_iota(jnp.int32, (8, rows[0].shape[1]), 0)
    stack = sum(jnp.where(line == at, row, 0.0) for at, row in enumerate(rows))
    return grad_router + tn(stack.astype(BF16), norm_picks(experts))


def image_bias(rows, padded):
    line = lax.broadcasted_iota(jnp.int32, (padded, padded), 0)
    column = lax.broadcasted_iota(jnp.int32, (padded, padded), 1)
    image_line, image_column = jnp.zeros_like(line), jnp.zeros_like(column)
    for at in range(SEQ, rows + 1, SEQ):
        image_line += (line >= at).astype(jnp.int32)
        image_column += (column >= at).astype(jnp.int32)
    return jnp.where((image_line == image_column) & (column < rows), 0.0, -1e30)


def half_masks():
    lane = lax.broadcasted_iota(jnp.int32, (1, LANES), 1)
    low = (lane < HEAD_DIM).astype(F32)
    return low.astype(BF16), (1.0 - low).astype(BF16)


def soft_scores(query, key, bias):
    scores = nt(query, key) * HEAD_DIM ** (-0.5) + bias
    power = jnp.exp(scores - jnp.max(scores, axis=1, keepdims=True))
    return power * (1.0 / jnp.sum(power, axis=1, keepdims=True))


def router_probs(logits, experts):
    lane = lax.broadcasted_iota(jnp.int32, logits.shape, 1)
    inside = lane < experts
    kept = jnp.where(inside, logits, -1e30)
    power = jnp.where(inside, jnp.exp(kept - jnp.max(kept, axis=1, keepdims=True)), 0.0)
    return power * (1.0 / jnp.sum(power, axis=1, keepdims=True))


def pick_gate(probs, choice):
    lane = lax.broadcasted_iota(jnp.int32, probs.shape, 1)
    return jnp.sum(jnp.where(lane == choice, probs, 0.0), axis=1, keepdims=True)


class Weights:
    def __init__(self, shard, width, gathered=None, whole=None):
        self.shard, self.width, self.gathered, self.whole = shard, width, gathered, whole

    def __call__(self, at):
        if self.whole is not None:
            return self.whole[at]
        part = self.gathered[:, :, at * self.shard : (at + 1) * self.shard, :]
        return part.reshape(self.width, self.width)

    def small(self):
        if self.whole is not None:
            return self.whole[SMALL, :, :LANES]
        part = self.gathered[:, :, SMALL * self.shard : (SMALL + 1) * self.shard, :LANES]
        return part.reshape(self.width, LANES)


def gelu_parts(hidden):
    bell = jnp.exp(-0.5 * hidden * hidden)
    near = 1.0 / (1.0 + 0.23164189 * jnp.abs(hidden))
    tail = near * (
        0.127414796 + near * (-0.142248368 + near * (0.7107068705 + near * (-0.7265760135 + near * 0.5307027145)))
    )
    tail = tail * bell
    share = jnp.where(hidden < 0.0, tail, 1.0 - tail)
    return hidden * share, share + hidden * bell * 0.3989422804014327


def forward_kernel(cfg, *refs):
    n_dp, n_t, rows, padded, width, experts, rooms, shard, inside = cfg
    refs = list(refs)

    def take(count):
        got = refs[:count]
        del refs[:count]
        return got

    x_ref, cot_ref, cols_ref, slots_ref, block_ref = take(5)
    gathered, recv_d, recv_s, res_ref, moe_ref, q_ref, k_ref, v_ref, mix_ref, norm_ref, probs_ref = take(11)
    full, cot_full, bias, send_d, send_s, d_send, d_recv, s_send, s_recv = take(9)
    dp = lax.axis_index("dp")
    meet(n_dp, n_t, inside)
    if inside:
        gather = Gather(n_dp, n_t, 0, block_ref.shape[0], width, block_ref, gathered, *refs)
        gather.start()
        weights = Weights(shard, width, gathered=gathered)
    else:
        gathered[...] = jnp.zeros_like(gathered)
        weights = Weights(shard, width, whole=block_ref)

    full[rows - rows % 8 :, :] = jnp.zeros((padded - rows + rows % 8, width), F32)
    full[:rows, :] = x_ref[...].astype(F32)
    cot_full[rows - rows % 8 :, :] = jnp.zeros((padded - rows + rows % 8, width), F32)
    cot_full[:rows, :] = cot_ref[...].astype(F32)
    bias[...] = image_bias(rows, padded)
    unit, _ = centre(full[...])
    norm_ref[...] = unit.astype(BF16)
    if inside:
        gather.pass_to_chips()
        gather.pass_to_core()
        gather.arrive()
        gather.drain()

    norms = norm_rows(weights.small(), experts)
    unit, _ = centre(full[...])
    normed = (unit * norms[0:1] + norms[1:2]).astype(BF16)
    norm_ref[...] = normed
    q_ref[...] = nn(normed, weights(0)).astype(BF16)
    k_ref[...] = nn(normed, weights(1)).astype(BF16)
    v_ref[...] = nn(normed, weights(2)).astype(BF16)
    low, high = half_masks()

    def heads(j, carry):
        at = pl.ds(pl.multiple_of(j * LANES, LANES), LANES)
        query, key, value = q_ref[:, at], k_ref[:, at], v_ref[:, at]
        first = nn(soft_scores(query * low, key, bias[...]).astype(BF16), value)
        second = nn(soft_scores(query * high, key, bias[...]).astype(BF16), value)
        mix_ref[:, at] = (first * low.astype(F32) + second * high.astype(F32)).astype(BF16)
        return carry

    lax.fori_loop(0, width // LANES, heads, 0)
    residual = full[...] + nn(mix_ref[...], weights(OUT))
    res_ref[...] = residual
    unit, _ = centre(residual)
    moe = (unit * norms[2:3] + norms[3:4]).astype(BF16)
    moe_ref[...] = moe
    probs = router_probs(nn(moe, weights.small()), experts)
    probs_ref[...] = probs
    cot = cot_full[...]
    full[...] = pick_gate(probs, cols_ref[:, 0:1]) * cot
    cot_full[...] = pick_gate(probs, cols_ref[:, 1:2]) * cot

    def selectors(p):
        slot = lax.broadcasted_iota(jnp.int32, (rooms, padded), 0) + p * rooms
        first = (slot == slots_ref[0:1, :]).astype(F32)
        second = (slot == slots_ref[1:2, :]).astype(F32)
        return first, second

    def d_copy(k):
        to = lax.rem(dp + k, n_dp)
        return remote(send_d.at[to], recv_d.at[dp], d_send.at[k], d_recv.at[k], {"dp": to})

    def s_copy(k):
        to = lax.rem(dp + k, n_dp)
        return remote(send_s.at[to], recv_s.at[dp], s_send.at[k], s_recv.at[k], {"dp": to})

    def dispatch(k, carry):
        to = lax.rem(dp + k, n_dp)
        first, second = selectors(to)
        send_d[to] = nn((first + second).astype(BF16), moe_ref[...]).astype(BF16)

        @pl.when(k > 0)
        def _():
            d_copy(k).start()

        return carry

    def dispatch_grad(k, carry):
        to = lax.rem(dp + k, n_dp)
        first, second = selectors(to)
        rows_grad = nn(first.astype(BF16), full[...].astype(BF16)) + nn(second.astype(BF16), cot_full[...].astype(BF16))
        send_s[to] = rows_grad.astype(BF16)

        @pl.when(k > 0)
        def _():
            s_copy(k).start()

        return carry

    lax.fori_loop(0, n_dp, dispatch, 0)
    lax.fori_loop(0, n_dp, dispatch_grad, 0)
    recv_d[dp] = send_d[dp]
    recv_s[dp] = send_s[dp]
    for k in range(1, n_dp):
        d_copy(k).wait()
    for k in range(1, n_dp):
        s_copy(k).wait()


def forward(cfg, cid, x, cot, cols, slots, block):
    n_dp, n_t, rows, padded, width, experts, rooms, shard, inside = cfg
    rows_block = ceil_to(5 * shard, 16)
    low = jax.ShapeDtypeStruct((padded, width), BF16)
    sent = jax.ShapeDtypeStruct((n_dp, rooms, width), BF16)
    gathered = (n_dp, n_t, rows_block, width) if inside else (1, 1, 16, LANES)
    outs = [jax.ShapeDtypeStruct(gathered, BF16), sent, sent, jax.ShapeDtypeStruct((padded, width), F32)]
    outs += [low] * 6 + [jax.ShapeDtypeStruct((padded, LANES), F32)]
    scratch = [
        VMEM((padded, width), F32),
        VMEM((padded, width), F32),
        VMEM((padded, padded), F32),
        VMEM((n_dp, rooms, width), BF16),
        VMEM((n_dp, rooms, width), BF16),
    ] + [DMA((n_dp,))] * 4
    if inside:
        scratch += Gather.scratch(n_dp, n_t)
    whole = pl.BlockSpec(memory_space=VMEM)
    return pl.pallas_call(
        partial(forward_kernel, cfg),
        out_shape=outs,
        in_specs=[whole] * 5,
        out_specs=[whole] * len(outs),
        scratch_shapes=scratch,
        compiler_params=pltpu.CompilerParams(
            collective_id=cid, has_side_effects=True, vmem_limit_bytes=56 * 2**20
        ),
        name="forward_" + str(rooms),
    )(x, cot, cols, slots, block)


def expert_kernel(chunks, d_ref, s_ref, w_in_ref, w_out_ref, ret_ref, back_ref, g_in_ref, g_out_ref, ret, back, g_in, g_out):
    step = pl.program_id(0)
    rows = d_ref.shape[0]
    chunk = rows // chunks

    @pl.when(step == 0)
    def _():
        ret[...] = jnp.zeros_like(ret)
        back[...] = jnp.zeros_like(back)

    g_in[...] = jnp.zeros_like(g_in)
    g_out[...] = jnp.zeros_like(g_out)
    w_in, w_out = w_in_ref[...], w_out_ref[...]

    def part(c, carry):
        at = pl.ds(pl.multiple_of(c * chunk, 16), chunk)
        took, slot_grad = d_ref[at, :], s_ref[at, :]
        active, slope = gelu_parts(nt(took, w_in))
        active = active.astype(BF16)
        grad_hidden = (nt(slot_grad, w_out) * slope).astype(BF16)
        ret[at, :] += nn(active, w_out)
        back[at, :] += nn(grad_hidden, w_in)
        g_out[...] += tn(active, slot_grad)
        g_in[...] += tn(grad_hidden, took)
        return carry

    lax.fori_loop(0, chunks, part, 0)
    g_in_ref[...] = g_in[...].astype(BF16)
    g_out_ref[...] = g_out[...].astype(BF16)

    @pl.when(step == pl.num_programs(0) - 1)
    def _():
        ret_ref[...] = ret[...].astype(BF16)
        back_ref[...] = back[...].astype(BF16)


def run_expert(took, slot_grad, w_in, w_out):
    rows, width = took.shape
    hidden = w_in.shape[0]
    block = 256
    chunks = next(c for c in range(max(1, rows // 400), rows + 1) if rows % c == 0 and (rows // c) % 16 == 0)
    whole = pl.BlockSpec((rows, width), lambda i: (0, 0))
    part = pl.BlockSpec((block, width), lambda i: (i, 0))
    low = jax.ShapeDtypeStruct((rows, width), BF16)
    grad = jax.ShapeDtypeStruct((hidden, width), BF16)
    return pl.pallas_call(
        partial(expert_kernel, chunks),
        grid=(hidden // block,),
        out_shape=[low, low, grad, grad],
        in_specs=[whole, whole, part, part],
        out_specs=[whole, whole, part, part],
        scratch_shapes=[
            VMEM((rows, width), F32),
            VMEM((rows, width), F32),
            VMEM((block, width), F32),
            VMEM((block, width), F32),
        ],
        compiler_params=pltpu.CompilerParams(vmem_limit_bytes=60 * 2**20),
        cost_estimate=pl.CostEstimate(
            flops=12 * rows * width * hidden, bytes_accessed=12 * rows * width + 8 * hidden * width, transcendentals=0
        ),
        name="expert_" + str(rows),
    )(took, slot_grad, w_in, w_out)


def backward_kernel(cfg, *refs):
    n_dp, n_t, rows, padded, width, experts, rooms, shard, inside = cfg
    refs = list(refs)

    def take(count):
        got = refs[:count]
        del refs[:count]
        return got

    ret_ref, back_ref, x_ref, cot_ref, cols_ref, weights_ref = take(6)
    res_ref, moe_ref, q_ref, k_ref, v_ref, mix_ref, norm_ref, probs_ref = take(8)
    out_ref, gx_ref, sum_ref = take(3)
    full, cot_full, bias, ret_in, back_in, grads, r_send, r_recv, b_send, b_recv = take(10)
    dq, dk, dv = take(3)
    dp = lax.axis_index("dp")
    meet(n_dp, n_t, inside)

    def r_copy(k):
        to = lax.rem(dp + k, n_dp)
        return remote(ret_ref.at[to], ret_in.at[dp], r_send.at[k], r_recv.at[k], {"dp": to})

    def b_copy(k):
        to = lax.rem(dp + k, n_dp)
        return remote(back_ref.at[to], back_in.at[dp], b_send.at[k], b_recv.at[k], {"dp": to})

    for k in range(1, n_dp):
        r_copy(k).start()
    for k in range(1, n_dp):
        b_copy(k).start()
    ret_in[dp] = ret_ref[dp]
    back_in[dp] = back_ref[dp]
    weights = Weights(shard, width, gathered=weights_ref) if inside else Weights(shard, width, whole=weights_ref)
    tail = rows - rows % 8
    full[tail:, :] = jnp.zeros((padded - tail, width), F32)
    full[:rows, :] = x_ref[...].astype(F32)
    cot_full[tail:, :] = jnp.zeros((padded - tail, width), F32)
    cot_full[:rows, :] = cot_ref[...].astype(F32)
    bias[...] = image_bias(rows, padded)
    norms = norm_rows(weights.small(), experts)

    def selectors(e):
        lane = lax.broadcasted_iota(jnp.int32, (padded, rooms), 1) + e * rooms
        return (lane == cols_ref[:, 2:3]).astype(F32), (lane == cols_ref[:, 3:4]).astype(F32)

    for k in range(1, n_dp):
        r_copy(k).wait()

    def pick(e, carry):
        return tuple(rows + nn(one.astype(BF16), ret_in[e]) for rows, one in zip(carry, selectors(e)))

    zero = jnp.zeros((padded, width), F32)
    first_rows, second_rows = lax.fori_loop(0, n_dp, pick, (zero, zero))
    probs = probs_ref[...]
    first_id, second_id = cols_ref[:, 0:1], cols_ref[:, 1:2]
    outcome = res_ref[...] + pick_gate(probs, first_id) * first_rows + pick_gate(probs, second_id) * second_rows
    out_ref[...] = outcome[:rows].astype(BF16)
    cot = cot_full[...]
    first_grad = jnp.sum(first_rows * cot, axis=1, keepdims=True)
    second_grad = jnp.sum(second_rows * cot, axis=1, keepdims=True)
    spot = lax.broadcasted_iota(jnp.int32, probs.shape, 1)
    grad_probs = jnp.where(spot == first_id, first_grad, 0.0) + jnp.where(spot == second_id, second_grad, 0.0)
    grad_logits = (probs * (grad_probs - jnp.sum(probs * grad_probs, axis=1, keepdims=True))).astype(BF16)
    grad_router = tn(moe_ref[...], grad_logits)

    for k in range(1, n_dp):
        b_copy(k).wait()

    def pick_both(e, rows):
        first, second = selectors(e)
        return rows + nn((first + second).astype(BF16), back_in[e])

    grad_moe = lax.fori_loop(0, n_dp, pick_both, nt(grad_logits, weights.small()))
    unit, inverse = centre(res_ref[...])
    extra, gain_two, shift_two = norm_back(grad_moe, unit, inverse, norms[2:3])
    grad_residual = cot + extra
    cot_full[...] = grad_residual
    grad_attended = grad_residual.astype(BF16)
    n_all = n_dp * n_t

    def keep(at, value):
        if inside:
            grads[:, :, at * shard : (at + 1) * shard, :] = value.astype(BF16).reshape(n_dp, n_t, shard, width)
        else:
            sum_ref[at] = value

    keep(OUT, tn(mix_ref[...], grad_attended))
    mix_ref_grad = nt(grad_attended, weights(OUT)).astype(BF16)
    dq[...] = mix_ref_grad
    low, high = half_masks()
    low_f, high_f = low.astype(F32), high.astype(F32)
    scale = HEAD_DIM ** (-0.5)

    def heads(j, carry):
        at = pl.ds(pl.multiple_of(j * LANES, LANES), LANES)
        query, key, value, grad = q_ref[:, at], k_ref[:, at], v_ref[:, at], dq[:, at]
        for mask, mask_f in ((low, low_f), (high, high_f)):
            probs = soft_scores(query * mask, key, bias[...])
            grad_probs = nt(grad * mask, value)
            grad_scores = probs * (grad_probs - jnp.sum(probs * grad_probs, axis=1, keepdims=True))
            grad_scores = grad_scores.astype(BF16)
            part_v = tn(probs.astype(BF16), grad)
            part_q = nn(grad_scores, key) * scale
            part_k = tn(grad_scores, query) * scale
            if mask is low:
                sum_q, sum_k, sum_v = part_q * mask_f, part_k * mask_f, part_v * mask_f
            else:
                sum_q, sum_k, sum_v = sum_q + part_q * mask_f, sum_k + part_k * mask_f, sum_v + part_v * mask_f
        dq[:, at] = sum_q.astype(BF16)
        dk[:, at] = sum_k.astype(BF16)
        dv[:, at] = sum_v.astype(BF16)
        return carry

    lax.fori_loop(0, width // LANES, heads, 0)
    keep(0, tn(norm_ref[...], dq[...]))
    keep(1, tn(norm_ref[...], dk[...]))
    keep(2, tn(norm_ref[...], dv[...]))
    grad_normed = nt(dq[...], weights(0)) + nt(dk[...], weights(1)) + nt(dv[...], weights(2))
    unit, inverse = centre(full[...])
    extra, gain_one, shift_one = norm_back(grad_normed, unit, inverse, norms[0:1])
    gx_ref[...] = (cot_full[...] + extra)[:rows].astype(BF16)
    small = small_grads(experts, grad_router, (gain_one, shift_one, gain_two, shift_two))
    if inside:
        at = slice(SMALL * shard, (SMALL + 1) * shard)
        grads[:, :, at, :LANES] = small.astype(BF16).reshape(n_dp, n_t, shard, LANES)
        grads[:, :, at, LANES:] = jnp.zeros((n_dp, n_t, shard, width - LANES), BF16)
        Scatter(n_dp, n_t, grads, sum_ref, *refs).run()
    else:
        sum_ref[SMALL] = jnp.zeros((width, width), F32)
        sum_ref[SMALL, :, :LANES] = small


def backward(cfg, cid, *args):
    n_dp, n_t, rows, padded, width, experts, rooms, shard, inside = cfg
    rows_block = ceil_to(5 * shard, 16)
    total = (rows_block, width) if inside else (5, width, width)
    outs = [jax.ShapeDtypeStruct((rows, width), BF16)] * 2 + [jax.ShapeDtypeStruct(total, F32)]
    scratch = [
        VMEM((padded, width), F32),
        VMEM((padded, width), F32),
        VMEM((padded, padded), F32),
        VMEM((n_dp, rooms, width), BF16),
        VMEM((n_dp, rooms, width), BF16),
        VMEM((n_dp, n_t, rows_block, width) if inside else (1, 1, 16, LANES), BF16),
    ]
    scratch += [DMA((n_dp,))] * 4 + [VMEM((padded, width), BF16)] * 3
    if inside:
        scratch += Scatter.scratch(n_dp, n_t, (rows_block, width))
    whole = pl.BlockSpec(memory_space=VMEM)
    return pl.pallas_call(
        partial(backward_kernel, cfg),
        out_shape=outs,
        in_specs=[whole] * len(args),
        out_specs=[whole] * len(outs),
        scratch_shapes=scratch,
        compiler_params=pltpu.CompilerParams(
            collective_id=cid, has_side_effects=True, vmem_limit_bytes=56 * 2**20
        ),
        name="backward_" + str(rooms),
    )(*args)


def image_blocks(rows):
    blocks = []
    for first in range(0, rows, SEQ):
        start = first // 16 * 16
        blocks.append((start, ceil_to(first - start + SEQ, 16), first - start))
    return blocks


def inside_image(size, first, axis):
    shape = (size, 1) if axis == 0 else (1, size)
    spot = lax.broadcasted_iota(jnp.int32, shape, axis)
    return (spot >= first) & (spot < first + SEQ)


def image_probs(query, key, size, first):
    scores = nt(query, key) * HEAD_DIM ** (-0.5) + jnp.where(inside_image(size, first, 1), 0.0, -1e30)
    power = jnp.exp(scores - jnp.max(scores, axis=1, keepdims=True))
    total = jnp.sum(power, axis=1, keepdims=True)
    return power * jnp.where(inside_image(size, first, 0), 1.0 / total, 0.0)


def join_images(parts, blocks):
    whole = parts[0]
    for (start, _, _), part in zip(blocks[1:], parts[1:]):
        shared = whole.shape[0] - start
        pieces = [whole[:start]]
        if shared > 0:
            pieces.append(whole[start:] + part[:shared])
        whole = jnp.concatenate(pieces + [part[shared:]], axis=0)
    return whole


def pack_block(refs, block, shard, width, experts):
    q_ref, k_ref, v_ref, o_ref, router_ref, *line_refs = refs
    for at, ref in ((0, q_ref), (1, k_ref), (2, v_ref), (OUT, o_ref)):
        block[at * shard : (at + 1) * shard, :] = ref[...].astype(BF16)
    here = slice(SMALL * shard, (SMALL + 1) * shard)
    block[here, :] = jnp.zeros((shard, width), BF16)
    row, column = (lax.broadcasted_iota(jnp.int32, (shard, shard), axis) for axis in (0, 1))
    lane = lax.broadcasted_iota(jnp.int32, (shard, LANES), 1)
    small = jnp.zeros((shard, LANES), F32)
    for at in range(experts + len(line_refs)):
        level = router_ref[at : at + 1, :] if at < experts else line_refs[at - experts][...]
        upright = jnp.sum(jnp.where(row == column, level, 0.0), axis=1, keepdims=True)
        small = jnp.where(lane == at, upright, small)
    block[here, :LANES] = small.astype(BF16)


def find_places(cfg, routes_ref, place, turned, over):
    n_dp, n_t, rows, padded, width, experts, rooms, shard, inside, hid = cfg
    t = lax.axis_index("tensor")
    tok_count = routes_ref.shape[1]
    capacity = (5 * tok_count + 2 * experts - 1) // (2 * experts)
    line = lax.broadcasted_iota(jnp.int32, (experts, tok_count), 0)
    lane = lax.broadcasted_iota(jnp.int32, (experts, tok_count), 1)

    def count(row, until):
        hot = (line == routes_ref[row : row + 1, :]) & (lane < until)
        return jnp.sum(hot.astype(F32), axis=1, keepdims=True)

    total = count(0, tok_count)
    before = (count(0, t * rows), count(1, t * rows))
    long = ceil_to(tok_count, LANES)
    wide = turned.shape[1]
    turned[...] = jnp.full(turned.shape, -1.0, F32)
    everyone = jnp.concatenate(
        [routes_ref[...], jnp.full((2, long - tok_count), experts, jnp.int32)], axis=1
    )
    everyone = jnp.concatenate([everyone, everyone, everyone, everyone], axis=0)
    mine = pltpu.roll(everyone, lax.rem(long - t * rows, long), 1)[:, :wide]
    spot = lax.broadcasted_iota(jnp.int32, (8, wide), 1)
    mine = jnp.where(spot < rows, mine, experts)
    line = lax.broadcasted_iota(jnp.int32, (experts, wide), 0)
    first, second = line == mine[0:1], line == mine[1:2]
    down, across = (lax.broadcasted_iota(jnp.int32, (wide, wide), axis) for axis in (0, 1))
    earlier = (down < across).astype(F32).astype(BF16)
    own = jnp.sum(first.astype(F32), axis=1, keepdims=True)
    first_rank = nn(first.astype(F32).astype(BF16), earlier)
    second_rank = nn(second.astype(F32).astype(BF16), earlier)

    def slot(choice, hot, rank, place):
        kept = hot & (place < capacity)
        here = jnp.sum(jnp.where(kept, rank + 1.0, 0.0), axis=0, keepdims=True) - 1.0
        good = (here >= 0.0) & (here < rooms)
        return jnp.where(good, choice.astype(F32) * rooms + here, -1.0), jnp.max(here, axis=1, keepdims=True)

    first_slot, first_most = slot(mine[0:1], first, first_rank, first_rank + before[0])
    second_slot, second_most = slot(mine[1:2], second, second_rank + own, second_rank + total + before[1])
    turned[0:1, :] = first_slot
    turned[1:2, :] = second_slot
    turned[2:3, :] = mine[0:1].astype(F32)
    turned[3:4, :] = mine[1:2].astype(F32)
    place[...] = turned[...].T
    most = jnp.maximum(first_most, second_most)
    over[...] = jnp.broadcast_to(jnp.where(most >= rooms, 1.0, 0.0), over.shape)


def step_kernel(cfg, *refs):
    n_dp, n_t, rows, padded, width, experts, rooms, shard, inside, hid = cfg
    refs = list(refs)

    def take(count):
        got = refs[:count]
        del refs[:count]
        return got

    x_ref, cot_ref, routes_ref, e_in_ref, e_out_ref = take(5)
    shared = take(9 if inside else 1)
    out_ref, gx_ref, sum_ref, g_in_ref, g_out_ref = take(5)
    block, gathered, full, cot_full, bias, res, probs_s = take(7)
    place, turned, over, gate_m, gate_c, gate_s, gate_r, rise_s, rise_r = take(9)
    moe, q_s, k_s, v_s, mix, norm, dk, dv = take(8)
    send_d, send_s, recv_d, recv_s, ret_in, back_in, act, slope = take(8)
    wi, wo, gi, go, gi_in, go_in = take(6)
    d_send, d_recv, s_send, s_recv, r_send, r_recv, b_send, b_recv = take(8)
    f_send, f_recv, e_send, e_recv, own_sems = take(5)
    wi_spread, wo_spread = Spread(n_t, wi, *take(2)), Spread(n_t, wo, *take(2))
    gi_collect, go_collect = Collect(n_t, gi, gi_in, *take(2)), Collect(n_t, go, go_in, *take(2))
    dp, t = lax.axis_index("dp"), lax.axis_index("tensor")
    scale = HEAD_DIM ** (-0.5)
    slot_count = n_dp * rooms
    half, wide = min(256, hid), min(256, width)
    long = gate_m.shape[1]
    early = 2 if hid == width and n_t > 2 else 0
    table = [sorted(range(n_t), key=lambda j: (abs(j - at), j)) for at in range(n_t)]

    def order(p):
        found = jnp.int32(0)
        for at in range(n_t):
            for spot in range(n_t):
                found = found + jnp.where((t == at) & (p == spot), table[at][spot], 0)
        return found

    every = pl.ds(0, rooms)
    cut = max(rooms // 2 // 16 * 16, 16)
    d_copy = Exchange(n_dp, send_d, recv_d, every, d_send, d_recv, True)
    s_first = Exchange(n_dp, send_s, recv_s, pl.ds(0, cut), s_send.at[0], s_recv.at[0], False)
    s_second = Exchange(n_dp, send_s, recv_s, pl.ds(cut, rooms - cut), s_send.at[1], s_recv.at[1], False)
    late = max(rooms * 2 // 5 // 16 * 16, 16)
    r_first = Exchange(n_dp, send_d, ret_in, pl.ds(late, rooms - late), r_send.at[0], r_recv.at[0], False)
    r_second = Exchange(n_dp, send_d, ret_in, pl.ds(0, late), r_send.at[1], r_recv.at[1], False)
    b_copy = Exchange(n_dp, send_s, back_in, every, b_send, b_recv, False)
    f_copy = Exchange(n_dp, gate_s, gate_r, pl.ds(0, 8), f_send, f_recv, False)
    e_copy = Exchange(n_dp, rise_s, rise_r, pl.ds(0, 8), e_send, e_recv, False)

    def column(at):
        return place[:padded, at : at + 1].astype(jnp.int32)

    greet(n_dp, n_t)
    load_in = pltpu.make_async_copy(e_in_ref, g_in_ref, own_sems.at[0])
    load_out = pltpu.make_async_copy(e_out_ref, g_out_ref, own_sems.at[1])
    load_in.start()
    load_out.start()
    if inside:
        pack_block(shared, block, shard, width, experts)
        size = len(Gather.scratch(n_dp, n_t))
        gather_a = Gather(n_dp, n_t, 0, SMALL * shard, width, block, gathered, *take(size))
        gather_s = Gather(n_dp, n_t, SMALL * shard, shard, LANES, block, gathered, *take(size))
        gather_b = Gather(n_dp, n_t, OUT * shard, shard, width, block, gathered, *take(size))
        weights = Weights(shard, width, gathered=gathered)
    else:
        weights = Weights(shard, width, whole=shared[0])
    load_in.wait()
    wi[t] = g_in_ref[...].astype(BF16)
    greeted(n_dp, n_t)
    if inside:
        gather_a.start()
        gather_s.start()
        gather_b.start()
    wi_spread.step(0)
    load_out.wait()
    wo[t] = g_out_ref[...].astype(BF16)
    tail = rows - rows % 8
    full[tail:, :] = jnp.zeros((padded - tail, width), F32)
    full[:rows, :] = x_ref[...].astype(F32)
    cot_full[tail:, :] = jnp.zeros((padded - tail, width), F32)
    cot_full[:rows, :] = cot_ref[...].astype(F32)
    bias[...] = image_bias(rows, padded)
    find_places(cfg, routes_ref, place, turned, over)

    def selectors(p):
        slot = lax.broadcasted_iota(jnp.int32, (rooms, padded), 0) + p * rooms
        first = (slot == turned[0:1, :padded].astype(jnp.int32)).astype(F32)
        second = (slot == turned[1:2, :padded].astype(jnp.int32)).astype(F32)
        return first, second

    dk[...] = cot_full[...].astype(BF16)

    def dispatch_grad(k, carry):
        to = lax.rem(dp + k, n_dp)
        first, second = selectors(to)
        got = nn((first + second).astype(BF16), dk[...]).astype(BF16)

        @pl.when(k > 0)
        def _():
            send_s[to] = got

        @pl.when(k == 0)
        def _():
            recv_s[to] = got

        return carry

    lax.fori_loop(0, n_dp, dispatch_grad, 0)
    if inside:
        gather_a.pass_to_chips()
        gather_s.pass_to_chips()
        gather_b.pass_to_chips()
        gather_a.pass_to_core()
        gather_s.pass_to_core()
    if inside:
        gather_a.arrive()
        gather_s.arrive()
    norms = norm_rows(weights.small(), experts)
    unit, _ = centre(full[...])
    norm[...] = (unit * norms[0:1] + norms[1:2]).astype(BF16)
    q_s[...] = nn(norm[...], weights(0)).astype(BF16)
    k_s[...] = nn(norm[...], weights(1)).astype(BF16)
    v_s[...] = nn(norm[...], weights(2)).astype(BF16)
    if inside:
        gather_b.pass_to_core()
    s_first.start_all()
    middle = (t > 0) & (t < n_t - 1)

    @pl.when(jnp.logical_not(middle))
    def _():
        wo_spread.step(0)

    low, high = half_masks()
    low_f, high_f = low.astype(F32), high.astype(F32)
    blocks = image_blocks(rows)

    def heads(j, carry):
        at = pl.ds(pl.multiple_of(j * LANES, LANES), LANES)
        parts = []
        for start, size, first in blocks:
            here = pl.ds(start, size)
            query, key, value = q_s[here, at], k_s[here, at], v_s[here, at]
            one = nn(image_probs(query * low, key, size, first).astype(BF16), value)
            two = nn(image_probs(query * high, key, size, first).astype(BF16), value)
            parts.append(one * low_f + two * high_f)
        mix[:, at] = join_images(parts, blocks).astype(BF16)
        return carry

    lax.fori_loop(0, width // LANES // 2, heads, 0)
    @pl.when(middle)
    def _():
        wi_spread.step(1)

    lax.fori_loop(width // LANES // 2, width // LANES, heads, 0)
    if inside:
        gather_b.arrive()
    residual = full[...] + nn(mix[...], weights(OUT))
    res[...] = residual
    unit, _ = centre(residual)
    moe[...] = (unit * norms[2:3] + norms[3:4]).astype(BF16)
    probs_s[...] = router_probs(nn(moe[...], weights.small()), experts)

    spot = lax.broadcasted_iota(jnp.int32, (padded, LANES), 1)
    first_gate, second_gate = pick_gate(probs_s[...], column(2)), pick_gate(probs_s[...], column(3))
    place[:padded, :] = jnp.where(spot == 4, first_gate, jnp.where(spot == 5, second_gate, place[:padded, :]))
    turned[...] = place[...].T
    gate_line = lax.broadcasted_iota(jnp.int32, (8, padded), 0)

    def terms(gate):
        one = gate.astype(BF16).astype(F32)
        two = (gate - one).astype(BF16).astype(F32)
        three = gate - one - two
        stack = jnp.where(gate_line == 0, one, jnp.where(gate_line == 1, two, jnp.where(gate_line == 2, three, 0.0)))
        return stack.astype(BF16)

    first_terms, second_terms = terms(turned[4:5, :padded]), terms(turned[5:6, :padded])
    def dispatch(k, carry):
        to = lax.rem(dp + k, n_dp)
        first, second = selectors(to)
        got = nn((first + second).astype(BF16), moe[...]).astype(BF16)

        @pl.when(k > 0)
        def _():
            send_d[to] = got
            d_copy.start(k)

        @pl.when(k == 0)
        def _():
            recv_d[to] = got

        return carry

    lax.fori_loop(0, n_dp, dispatch, 0)

    @pl.when(middle)
    def _():
        if n_t > 2:
            wi_spread.step(2)
        wo_spread.step(0)

    def dispatch_gates(k, carry):
        to = lax.rem(dp + k, n_dp)
        first, second = selectors(to)
        gate = nt(first_terms, first.astype(BF16)) + nt(second_terms, second.astype(BF16))
        gate = jnp.sum(gate, axis=0, keepdims=True)

        @pl.when(k > 0)
        def _():
            gate_s[to, :, :rooms] = jnp.broadcast_to(gate, (8, rooms))
            f_copy.start(k)

        @pl.when(k == 0)
        def _():
            gate_r[to, :, :rooms] = jnp.broadcast_to(gate, (8, rooms))

        return carry

    lax.fori_loop(0, n_dp, dispatch_gates, 0)

    def hidden_units(j, g):
        active, steep = gelu_parts(nn(recv_d[g], wi[j]))
        act[j, g] = active.astype(BF16)
        slope[j, g] = steep.astype(BF16)

    n_chip, chip = n_dp // 2, dp // 2

    def chip_rows(ref, c, *lead):
        value = ref[(*lead, pl.ds(2 * c, 2))]
        return value.reshape(2 * rooms, value.shape[-1])

    def chip_store(ref, c, value, *lead):
        ref[(*lead, pl.ds(2 * c, 2))] = value.reshape(2, rooms, value.shape[-1])

    def own_hidden(k, carry):
        @pl.when(k > 0)
        def _():
            d_copy.wait_from(k)

        hidden_units(t, lax.rem(dp + n_dp - k, n_dp))
        return carry

    lax.fori_loop(0, n_dp, own_hidden, 0)
    s_second.start_all()

    @pl.when(middle)
    def _():
        wo_spread.step(1)


    @pl.when(jnp.logical_not(middle))
    def _():
        wi_spread.step(1)
        if n_t > 2:
            wi_spread.step(2)

    slot_grads = send_s
    room_lane = lax.broadcasted_iota(jnp.int32, (rooms, LANES), 1)

    def slot_grad(g, carry):
        gate = jnp.sum(jnp.where(room_lane == g, gate_c[:rooms, :], 0.0), axis=1, keepdims=True)
        slot_grads[g] = (gate * recv_s[g].astype(F32)).astype(BF16)
        return carry

    def outer_grad(i, carry):
        j = order(n_t - 1 - i // (hid // half))
        at = pl.ds(pl.multiple_of(lax.rem(i, hid // half) * half, half), half)
        left = act[j, :, :, at].reshape(slot_count, half)
        go[j, at, :] = tn(left, slot_grads[...].reshape(slot_count, width)).astype(BF16)

        @pl.when(lax.rem(i, hid // half) == hid // half - 1)
        def _():
            go_collect.begin(j)

        return carry

    def cotangent_arrives():
        gate_m[...] = jnp.zeros_like(gate_m)
        f_copy.wait_all()
        f_copy.wait_sent()
        for g in range(n_dp):
            gate_m[g : g + 1, :rooms] = gate_r[g, 0:1, :rooms]
        gate_c[...] = gate_m[...].T
        for half_copy in (s_first, s_second):
            half_copy.wait_all()
            half_copy.wait_sent()
    def other_hidden(q, carry):
        p = jnp.where(q == 0, 1, jnp.where(q == 1, n_t - 1, q))

        @pl.when(q == 1)
        def _():
            for s in range(3, n_t):
                wi_spread.step(s)

        def one(g, inner):
            hidden_units(order(p), g)
            return inner

        lax.fori_loop(0, n_dp, one, 0, unroll=2)

        @pl.when(q == min(1, n_t - 2))
        def _():
            cotangent_arrives()
            lax.fori_loop(0, n_dp, slot_grad, 0)
            lax.fori_loop(0, hid // half, outer_grad, 0)

        return carry

    lax.fori_loop(0, n_t - 1, other_hidden, 0)
    @pl.when(jnp.logical_not(middle))
    def _():
        wo_spread.step(1)

    @pl.when(middle)
    def _():
        if n_t > 2:
            wo_spread.step(2)

    lax.fori_loop(hid // half, n_t * (hid // half), outer_grad, 0)

    def hidden_grads(p):
        j = order(p)

        def one(i, inner):
            grad = nt(chip_rows(slot_grads, i), wo[j]) * chip_rows(slope, i, j).astype(F32)
            chip_store(slope, i, grad.astype(BF16), j)
            return inner

        lax.fori_loop(0, n_chip, one, 0, unroll=2)

    def inner_grads(p):
        j = order(p)

        def one(i, inner):
            at = pl.ds(pl.multiple_of(i * wide, wide), wide)
            left = recv_d[:, :, at].reshape(slot_count, wide)
            gi[j, at, :] = tn(left, slope[j].reshape(slot_count, hid)).astype(BF16)
            return inner

        lax.fori_loop(0, width // wide, one, 0)

    def split(total):
        main = total.astype(BF16)
        return main, (total - main.astype(F32)).astype(BF16)

    def some_back(g, inner):
        near_a, near_b = order(0), order(1)
        total = nn(chip_rows(act, g, near_a), wo[near_a]) + nn(chip_rows(act, g, near_b), wo[near_b])
        for j, part in zip((near_a, near_b), split(total)):
            chip_store(act, g, part, j)
        return inner

    def hidden_step(p, carry):
        @pl.when(p == 1)
        def _():
            if n_t > 2:
                go_collect.step(1, True)

        @pl.when((p == 2) & jnp.logical_not(middle))
        def _():
            if n_t > 2:
                wo_spread.step(2)

        @pl.when(p == 3)
        def _():
            for s in range(3, n_t):
                wo_spread.step(s)

        hidden_grads(p)

        @pl.when((p < n_t - 1) & jnp.logical_not(middle))
        def _():
            inner_grads(p)

        if early:

            @pl.when((p == early) & jnp.logical_not(middle))
            def _():
                lax.fori_loop(0, n_chip, some_back, 0)

        return carry

    lax.fori_loop(0, n_t, hidden_step, 0)
    d_copy.wait_sent()

    def hand_out(c, value, buffer, own, copies):
        for q in range(2):
            to = 2 * c + q
            k = lax.rem(to - dp + n_dp, n_dp)
            part = value[q * rooms : (q + 1) * rooms]

            @pl.when(k > 0)
            def _():
                buffer[to] = part
                if copies is not None:
                    copies.start(k)

            @pl.when(k == 0)
            def _():
                own[to] = part

    def give_back_grad(i, carry):
        c = lax.rem(chip + 1 + i, n_chip)
        total = nt(chip_rows(slope, c, 0), wi[0])
        for j in range(1, n_t):
            total = total + nt(chip_rows(slope, c, j), wi[j])
        hand_out(c, total.astype(BF16), send_s, back_in, b_copy)
        return carry

    lax.fori_loop(0, n_chip, give_back_grad, 0)
    for e in range(2, n_t - 1):
        go_collect.step(e, True)

    gate_c[...] = jnp.zeros_like(gate_c)

    def give_back(c, total):
        rise = jnp.sum(total * chip_rows(recv_s, c).astype(F32), axis=1, keepdims=True)
        for q in range(2):
            found = rise[q * rooms : (q + 1) * rooms]
            gate_c[:rooms, :] = jnp.where(room_lane == 2 * c + q, found, gate_c[:rooms, :])
        hand_out(c, total.astype(BF16), send_d, ret_in, None)

    def give_back_whole(c, carry):
        total = nn(chip_rows(act, c, 0), wo[0])
        for j in range(1, n_t):
            total = total + nn(chip_rows(act, c, j), wo[j])
        give_back(c, total)
        return carry

    def give_back_rest(c, carry):
        near_a, near_b = order(0), order(1)
        total = chip_rows(act, c, near_a).astype(F32) + chip_rows(act, c, near_b).astype(F32)
        for p in range(early, n_t):
            j = order(p)
            total = total + nn(chip_rows(act, c, j), wo[j])
        give_back(c, total)
        return carry

    def last_inner():
        inner_grads(n_t - 1)

        def send_inner(p, carry):
            gi_collect.begin(order(n_t - 1 - p))
            return carry

        lax.fori_loop(0, n_t, send_inner, 0)

    if early:

        @pl.when(jnp.logical_not(middle))
        def _():
            last_inner()
            lax.fori_loop(0, n_chip, give_back_rest, 0)

        @pl.when(middle)
        def _():
            lax.fori_loop(0, n_chip, give_back_whole, 0)

    else:

        @pl.when(jnp.logical_not(middle))
        def _():
            last_inner()

        lax.fori_loop(0, n_chip, give_back_whole, 0)

    gate_m[...] = gate_c[...].T
    for g in range(n_dp):
        row = jnp.broadcast_to(gate_m[g : g + 1, :], (8, long))

        @pl.when(dp == g)
        def _():
            rise_r[g] = row

        @pl.when(dp != g)
        def _():
            rise_s[g] = row

    e_copy.start_all()

    @pl.when(middle)
    def _():
        def one(p, inner):
            inner_grads(p)
            return inner

        lax.fori_loop(0, n_t, one, 0)

    lane = lax.broadcasted_iota(jnp.int32, (padded, slot_count), 1)
    both = ((lane == column(0)).astype(F32) + (lane == column(1)).astype(F32)).astype(BF16)
    unit, inverse = centre(res[...])
    b_copy.wait_sent()
    r_first.start_all()
    b_copy.wait_all()
    e_copy.wait_all()
    e_copy.wait_sent()
    room = lax.broadcasted_iota(jnp.int32, (padded, long), 1)

    slots_of = (column(0), column(1))

    found = [jnp.zeros((padded, long), F32)] * 2
    for e in range(n_dp):
        row = jnp.where(room[0:1] < rooms, rise_r[e, 0:1, :], 0.0)
        for at, slot in enumerate(slots_of):
            here = jnp.where(slot < (e + 1) * rooms, slot - e * rooms, -1)
            found[at] = jnp.where(room == here, row, found[at])
    first_grad, second_grad = (jnp.sum(one, axis=1, keepdims=True) for one in found)
    probs = probs_s[...]
    spot = lax.broadcasted_iota(jnp.int32, probs.shape, 1)
    grad_probs = jnp.where(spot == column(2), first_grad, 0.0) + jnp.where(spot == column(3), second_grad, 0.0)
    grad_logits = (probs * (grad_probs - jnp.sum(probs * grad_probs, axis=1, keepdims=True))).astype(BF16)
    grad_router = tn(moe[...], grad_logits)
    grad_moe = nn(both, back_in[...].reshape(slot_count, width)) + nt(grad_logits, weights.small())
    extra, gain_two, shift_two = norm_back(grad_moe, unit, inverse, norms[2:3])
    grad_residual = cot_full[...] + extra
    cot_full[...] = grad_residual
    grad_attended = grad_residual.astype(BF16)

    pairs = width // LANES
    if inside:
        size = len(Reduce.scratch(n_dp, n_t, 1, (shard, LANES)))
        out_sum = Reduce(n_dp, n_t, lambda p: sum_ref.at[pl.ds(OUT * shard, shard)], *take(size))
        pair_sum = Reduce(
            n_dp, n_t, lambda p: sum_ref.at[pl.ds(0, 3 * shard), pl.ds(pl.multiple_of(p * LANES, LANES), LANES)], *take(size)
        )
        small_sum = Reduce(n_dp, n_t, lambda p: sum_ref.at[pl.ds(SMALL * shard, shard), pl.ds(0, LANES)], *take(size))
        sum_ref[SMALL * shard : (SMALL + 1) * shard, LANES:] = jnp.zeros((shard, width - LANES), F32)
        out_sum.put(0, 0, tn(mix[...], grad_attended))
        out_sum.to_core(0)
    else:
        sum_ref[OUT] = tn(mix[...], grad_attended)
    dq = mix
    dq[...] = nt(grad_attended, weights(OUT)).astype(BF16)

    def heads_back(j, carry):
        at = pl.ds(pl.multiple_of(j * LANES, LANES), LANES)
        query, key, value, grad = q_s[:, at], k_s[:, at], v_s[:, at], dq[:, at]
        for mask, mask_f in ((low, low_f), (high, high_f)):
            probs = soft_scores(query * mask, key, bias[...])
            grad_probs = nt(grad * mask, value)
            grad_scores = probs * (grad_probs - jnp.sum(probs * grad_probs, axis=1, keepdims=True))
            grad_scores = grad_scores.astype(BF16)
            part_v = tn(probs.astype(BF16), grad)
            part_q = nn(grad_scores, key) * scale
            part_k = tn(grad_scores, query) * scale
            if mask is low:
                sum_q, sum_k, sum_v = part_q * mask_f, part_k * mask_f, part_v * mask_f
            else:
                sum_q, sum_k, sum_v = sum_q + part_q * mask_f, sum_k + part_k * mask_f, sum_v + part_v * mask_f
        dq[:, at] = sum_q.astype(BF16)
        dk[:, at] = sum_k.astype(BF16)
        dv[:, at] = sum_v.astype(BF16)
        @pl.when(j == pairs // 2)
        def _():
            if n_t > 2:
                gi_collect.step(1, True)

        if inside:
            for spot, ref in enumerate((dq, dk, dv)):
                pair_sum.put(j, spot * shard, tn(norm[...], ref[:, at]))
            pair_sum.to_core(j)

            @pl.when(j == 0)
            def _():
                out_sum.to_chips(0)

            @pl.when(j > 0)
            def _():
                pair_sum.to_chips(j - 1)

        return carry

    lax.fori_loop(0, pairs, heads_back, 0)
    if inside:
        pair_sum.to_chips(pairs - 1)
    else:
        for spot, ref in enumerate((dq, dk, dv)):
            sum_ref[spot] = tn(norm[...], ref[...])
    grad_normed = nt(dq[...], weights(0)) + nt(dk[...], weights(1)) + nt(dv[...], weights(2))
    full[tail:, :] = jnp.zeros((padded - tail, width), F32)
    full[:rows, :] = x_ref[...].astype(F32)
    unit, inverse = centre(full[...])
    extra, gain_one, shift_one = norm_back(grad_normed, unit, inverse, norms[0:1])
    gx_ref[...] = (cot_full[...] + extra)[:rows].astype(BF16)
    small = small_grads(experts, grad_router, (gain_one, shift_one, gain_two, shift_two))
    lane = lax.broadcasted_iota(jnp.int32, small.shape, 1)
    small = jnp.where(lane == experts + 4, over[0:1, :], small)
    def combine():
        for half_copy in (r_first, r_second):
            half_copy.wait_all()
            half_copy.wait_sent()
        returned = ret_in[...].reshape(slot_count, width)
        lane = lax.broadcasted_iota(jnp.int32, (padded, slot_count), 1)
        first, second = ((lane == column(at)).astype(F32).astype(BF16) for at in (0, 1))
        first_rows, second_rows = nn(first, returned), nn(second, returned)
        first_gate, second_gate = place[:padded, 4:5], place[:padded, 5:6]
        outcome = res[...] + first_gate * first_rows + second_gate * second_rows
        out_ref[...] = outcome[:rows].astype(BF16)

    if inside:
        small_sum.put(0, 0, small)
        small_sum.to_core(0)
        small_sum.to_chips(0)
        r_second.start_all()
        out_sum.to_line(0)

        def line(p, carry):
            pair_sum.to_line(p)
            return carry

        lax.fori_loop(0, pairs, line, 0)
        small_sum.to_line(0)
        for e in range(2, n_t - 1):
            gi_collect.step(e, True)
        go_collect.finish(g_out_ref)
        combine()
        out_sum.finish(0)

        def last(p, carry):
            pair_sum.finish(p)
            return carry

        lax.fori_loop(0, pairs, last, 0)
        small_sum.finish(0)
        gather_a.drain()
        gather_s.drain()
        gather_b.drain()
    else:
        sum_ref[SMALL] = jnp.zeros((width, width), F32)
        sum_ref[SMALL, :, :LANES] = small
        r_second.start_all()
        for e in range(2, n_t - 1):
            gi_collect.step(e, True)
        go_collect.finish(g_out_ref)
        combine()
    gi_collect.finish(g_in_ref)
    wi_spread.drain()
    wo_spread.drain()


def run_step(cfg, cid, x, cot, routes, e_in, e_out, shared):
    n_dp, n_t, rows, padded, width, experts, rooms, shard, inside, hid = cfg
    rows_block = ceil_to(5 * shard, 16)
    total = (rows_block, width) if inside else (5, width, width)
    outs = [
        jax.ShapeDtypeStruct((rows, width), BF16),
        jax.ShapeDtypeStruct((rows, width), BF16),
        jax.ShapeDtypeStruct(total, F32),
        jax.ShapeDtypeStruct((width, hid), F32),
        jax.ShapeDtypeStruct((hid, width), F32),
    ]
    spread = (n_dp, n_t, rows_block, width) if inside else (1, 1, 16, LANES)
    wide, long = ceil_to(padded, LANES), ceil_to(rooms, LANES)
    rows_f, rows_b = VMEM((padded, width), F32), VMEM((padded, width), BF16)
    slots_b, units_b = VMEM((n_dp, rooms, width), BF16), VMEM((n_t, n_dp, rooms, hid), BF16)
    in_b, out_b = (VMEM((n_t,) + shape, BF16) for shape in ((width, hid), (hid, width)))
    in_more, out_more = (VMEM((n_t + 1,) + shape, BF16) for shape in ((width, hid), (hid, width)))
    scratch = [VMEM((rows_block, width), BF16), VMEM(spread, BF16)]
    scratch += [rows_f, rows_f, VMEM((padded, padded), F32), rows_f, VMEM((padded, LANES), F32)]
    scratch += [VMEM((wide, LANES), F32), VMEM((LANES, wide), F32), VMEM((8, LANES), F32)]
    scratch += [VMEM((LANES, long), F32), VMEM((long, LANES), F32)] + [VMEM((n_dp, 8, long), F32)] * 4
    scratch += [rows_b] * 8 + [slots_b] * 6 + [units_b] * 2
    scratch += [in_b, out_b, in_b, out_b, in_more, out_more]
    scratch += [DMA, DMA((n_dp,))] + [DMA((2,))] * 4 + [DMA] * 6 + [DMA((2,))] + Spread.scratch(n_t) * 2 + Collect.scratch(n_t) * 2
    if inside:
        scratch += Gather.scratch(n_dp, n_t) * 3 + Reduce.scratch(n_dp, n_t, 1, (shard, width))
        scratch += Reduce.scratch(n_dp, n_t, width // LANES, (3 * shard, LANES))
        scratch += Reduce.scratch(n_dp, n_t, 1, (shard, LANES))
    whole, anywhere = pl.BlockSpec(memory_space=VMEM), pl.BlockSpec(memory_space=pl.ANY)
    return pl.pallas_call(
        partial(step_kernel, cfg),
        out_shape=outs,
        in_specs=[whole] * 3 + [anywhere] * 2 + [whole] * len(shared),
        out_specs=[whole] * len(outs),
        scratch_shapes=scratch,
        compiler_params=pltpu.CompilerParams(
            collective_id=cid, has_side_effects=True, vmem_limit_bytes=57 * 2**20
        ),
        name="step_" + str(rooms),
    )(x, cot, routes, e_in, e_out, *shared)


def lay_kernel(shard, experts, out_ref, gx_ref, sum_ref, in_ref, outer_ref, *outs):
    outs[0][...] = out_ref[...]
    outs[1][...] = gx_ref[...]
    for at, spot in ((0, 4), (1, 5), (2, 6), (OUT, 7)):
        outs[spot][...] = sum_ref[at * shard : (at + 1) * shard, :]
    small = sum_ref[SMALL * shard : (SMALL + 1) * shard, :LANES]
    row, column = (lax.broadcasted_iota(jnp.int32, (shard, shard), axis) for axis in (0, 1))
    for at, spot in enumerate((2, 3, 8, 9)):
        upright = small[:, experts + at : experts + at + 1]
        outs[spot][...] = jnp.sum(jnp.where(row == column, upright, 0.0), axis=0, keepdims=True)
    for at in range(experts):
        outs[10][at : at + 1, :] = jnp.sum(jnp.where(row == column, small[:, at : at + 1], 0.0), axis=0, keepdims=True)
    outs[11][...] = in_ref[...]
    outs[12][...] = outer_ref[...]


def lay_out(shard, experts, *args):
    rows, width = args[0].shape
    line = jax.ShapeDtypeStruct((1, shard), F32)
    square = jax.ShapeDtypeStruct((shard, width), F32)
    outs = [jax.ShapeDtypeStruct((rows, width), BF16)] * 2 + [line] * 2 + [square] * 4 + [line] * 2
    outs += [jax.ShapeDtypeStruct((experts, shard), F32)]
    outs += [jax.ShapeDtypeStruct(arg.shape, F32) for arg in args[3:]]

    def full(shape):
        return pl.BlockSpec(shape, lambda i: (0,) * len(shape))

    return pl.pallas_call(
        partial(lay_kernel, shard, experts),
        grid=(1,),
        out_shape=outs,
        in_specs=[full(arg.shape) for arg in args],
        out_specs=[full(out.shape) for out in outs],
        compiler_params=pltpu.CompilerParams(vmem_limit_bytes=32 * 2**20),
        name="outputs",
    )(*args)


def route_pairs(routes, t, row_count, experts, capacity):
    tok_count = routes.shape[0]
    ids = jnp.arange(experts, dtype=jnp.int32)[None, :]
    start = t * row_count
    rows = lax.dynamic_slice_in_dim(routes, start, row_count, 0)
    before = (jnp.arange(tok_count, dtype=jnp.int32) < start)[:, None]
    all_first = routes[:, 0:1] == ids
    all_second = routes[:, 1:2] == ids
    base_first = jnp.sum((all_first & before).astype(jnp.int32), axis=0)
    total_first = jnp.sum(all_first.astype(jnp.int32), axis=0)
    base_second = jnp.sum((all_second & before).astype(jnp.int32), axis=0)
    hot_first = rows[:, 0:1] == ids
    hot_second = rows[:, 1:2] == ids
    at = jnp.arange(row_count, dtype=jnp.int32)
    lower = (at[:, None] > at[None, :]).astype(BF16)
    both = jnp.concatenate([hot_first, hot_second], axis=1).astype(BF16)
    earlier = nn(lower, both).astype(jnp.int32)
    own_first = jnp.sum(hot_first.astype(jnp.int32), axis=0)
    rank_first = earlier[:, :experts]
    rank_second = earlier[:, experts:] + own_first
    place_first = rank_first + base_first
    place_second = earlier[:, experts:] + total_first + base_second
    first = jnp.sum(jnp.where(hot_first & (place_first < capacity), rank_first + 1, 0), axis=1) - 1
    second = jnp.sum(jnp.where(hot_second & (place_second < capacity), rank_second + 1, 0), axis=1) - 1
    return rows, first, second


def per_device(
    n_dp,
    n_t,
    inputs,
    cotangent,
    routes,
    gain_attn,
    shift_attn,
    query_w,
    key_w,
    value_w,
    out_w,
    gain_moe,
    shift_moe,
    router_w,
    expert_in,
    expert_out,
):
    t = lax.axis_index("tensor")
    shard, width = query_w.shape
    experts = router_w.shape[1]
    tok_count = routes.shape[0]
    rows = inputs.shape[0]
    hid = expert_in.shape[2]
    padded = ceil_to(rows, 16)
    capacity = (5 * tok_count + 2 * experts - 1) // (2 * experts)
    inside = shard % 16 == 0
    every = ("dp", "tensor")
    lines = (gain_attn, shift_attn, gain_moe, shift_moe)

    def stack():
        small = jnp.concatenate([router_w] + [line[:, None] for line in lines], axis=1)
        small = jnp.pad(small, ((0, 0), (0, width - small.shape[1])))
        return jnp.stack([query_w, key_w, value_w, small, out_w]).astype(BF16)

    if inside:
        shared = [query_w, key_w, value_w, out_w, router_w.T] + [line[None, :] for line in lines]
    else:
        shared = [lax.all_gather(stack(), every, axis=1, tiled=True)]

    def finish(results):
        summed = results[2]
        if not inside:
            summed = lax.psum_scatter(summed, every, scatter_dimension=1, tiled=True).reshape(5 * shard, width)
        outs = lay_out(shard, experts, results[0], results[1], summed, *results[3:])
        return tuple(outs)

    def slow(_):
        rooms = ceil_to(rows, 16)
        cfg = (n_dp, n_t, rows, padded, width, experts, rooms, shard, inside)
        route_rows, first_rank, second_rank = route_pairs(routes, t, rows, experts, capacity)

        def slot(choice, rank):
            return jnp.where(rank >= 0, choice * rooms + rank, -1)

        slots = jnp.stack([slot(route_rows[:, 0], first_rank), slot(route_rows[:, 1], second_rank)])
        slots = jnp.pad(slots, ((0, 0), (0, padded - rows)), constant_values=-1)
        cols = jnp.concatenate([jnp.pad(route_rows, ((0, padded - rows), (0, 0))), slots.T], axis=1)
        block = stack().reshape(5 * shard, width) if inside else shared[0]
        kept = forward(cfg, 1, inputs, cotangent, cols, slots, block)

        def turn(k):
            return [(i, (i + k) % n_t) for i in range(n_t)]

        both = jnp.stack([expert_in[0].T, expert_out[0]]).astype(BF16)
        parts = [both] + [lax.ppermute(both, "tensor", turn(k)) for k in range(1, n_t)]
        w_in, w_out = (jnp.concatenate([part[i] for part in parts], axis=0) for i in range(2))
        returned, back, grad_inner, grad_outer = run_expert(
            kept[1].reshape(n_dp * rooms, width), kept[2].reshape(n_dp * rooms, width), w_in, w_out
        )
        both = jnp.stack([grad_inner.reshape(n_t, hid, width), grad_outer.reshape(n_t, hid, width)], axis=1)
        total = both[0].astype(F32)
        for k in range(1, n_t):
            total = total + lax.ppermute(both[k], "tensor", turn(-k)).astype(F32)
        results = backward(
            cfg,
            2,
            returned.reshape(n_dp, rooms, width),
            back.reshape(n_dp, rooms, width),
            inputs,
            cotangent,
            cols,
            kept[0] if inside else block,
            *kept[3:],
        )
        return finish((*results, total[0].T, total[1]))

    rooms = min(ceil_to((7 * rows + 2 * experts - 1) // (2 * experts), 16), ceil_to(rows, 16))
    cfg = (n_dp, n_t, rows, padded, width, experts, rooms, shard, inside, hid)
    fast = run_step(cfg, 0, inputs, cotangent, routes.T, expert_in[0], expert_out[0], shared)
    if inside:
        crowded = fast[2][SMALL * shard, experts + 4] > 0.5
    else:
        crowded = lax.psum(fast[2][SMALL, 0, experts + 4], every) > 0.5
    outs = lax.cond(crowded, slow, finish, tuple(fast))
    lined = [out.reshape(shard) if at in (2, 3, 8, 9) else out for at, out in enumerate(outs)]
    lined[10], lined[11], lined[12] = lined[10].T, lined[11][None], lined[12][None]
    return tuple(lined)


def solution(mesh):
    every = ("dp", "tensor")
    rows, line = P(every, None), P(every)
    w_in, w_out = P("dp", None, "tensor"), P("dp", "tensor", None)
    return jax.shard_map(
        partial(per_device, mesh.shape["dp"], mesh.shape["tensor"]),
        mesh=mesh,
        in_specs=(rows, rows, P("dp", None), line, line, rows, rows, rows, rows, line, line, rows, w_in, w_out),
        out_specs=(rows, rows, line, line, rows, rows, rows, rows, line, line, rows, w_in, w_out),
        check_vma=False,
    )
```

```python
from functools import partial

import jax
import jax.numpy as jnp
from jax import lax
from jax.experimental import pallas as pl
from jax.experimental.pallas import tpu as pltpu
from jax.sharding import PartitionSpec as P

SEQ = 197
HEAD_DIM = 64
LANES = 128
MESH = pl.DeviceIdType.MESH
F32 = jnp.float32
BF16 = jnp.bfloat16
VMEM = pltpu.VMEM
DMA = pltpu.SemaphoreType.DMA
SMALL, OUT = 3, 4


def ceil_to(value, unit):
    return (value + unit - 1) // unit * unit


def nn(left, right):
    return lax.dot_general(left, right, (((1,), (0,)), ((), ())), preferred_element_type=F32)


def nt(left, right):
    return lax.dot_general(left, right, (((1,), (1,)), ((), ())), preferred_element_type=F32)


def tn(left, right):
    return lax.dot_general(left, right, (((0,), (0,)), ((), ())), preferred_element_type=F32)


def remote(src, dst, send, recv, device):
    return pltpu.make_async_remote_copy(
        src_ref=src, dst_ref=dst, send_sem=send, recv_sem=recv, device_id=device, device_id_type=MESH
    )


def meet(n_dp, n_t, z_too):
    dp = lax.axis_index("dp")
    t = lax.axis_index("tensor")
    bar = pltpu.get_barrier_semaphore()
    for k in range(1, n_dp):
        pl.semaphore_signal(bar, inc=1, device_id={"dp": lax.rem(dp + k, n_dp)}, device_id_type=MESH)
    if z_too:
        for k in range(1, n_t):
            pl.semaphore_signal(bar, inc=1, device_id={"tensor": lax.rem(t + k, n_t)}, device_id_type=MESH)
    pl.semaphore_wait(bar, n_dp - 1 + (n_t - 1 if z_too else 0))


class Gather:
    def __init__(self, n_dp, n_t, first, count, lanes, block, out, own_sem, z_send, z_recv, c_send, c_recv, k_send, k_recv):
        self.n_t, self.n_chip = n_t, n_dp // 2
        self.rows, self.lanes = pl.ds(first, count), pl.ds(0, lanes)
        self.block, self.out, self.own_sem = block.at[self.rows, self.lanes], out, own_sem
        self.z_sems, self.c_sems, self.k_sems = (z_send, z_recv), (c_send, c_recv), (k_send, k_recv)
        self.dp, self.t = lax.axis_index("dp"), lax.axis_index("tensor")
        self.chip, self.core = self.dp // 2, lax.rem(self.dp, 2)
        self.other = self.chip * 2 + 1 - self.core

    @staticmethod
    def scratch(n_dp, n_t):
        n_chip = n_dp // 2
        return [DMA, DMA, DMA((n_t,)), DMA, DMA((n_chip, n_t)), DMA, DMA]

    def place(self, dp, t):
        return self.out.at[dp, t, self.rows, self.lanes]

    def z_copy(self, k):
        send, recv = self.z_sems
        to = lax.rem(self.t + k, self.n_t)
        return remote(self.block, self.place(self.dp, self.t), send, recv.at[k], {"tensor": to})

    def chip_copy(self, k, j):
        send, recv = self.c_sems
        here = self.place(self.dp, lax.rem(self.t + self.n_t - j, self.n_t))
        to = lax.rem(self.chip + k, self.n_chip) * 2 + self.core
        return remote(self.block if j == 0 else here, here, send, recv.at[k, j], {"dp": to})

    def core_copy(self, k, j):
        send, recv = self.k_sems
        src = lax.rem(self.chip + self.n_chip - k, self.n_chip) * 2 + self.core
        here = self.place(src, lax.rem(self.t + self.n_t - j, self.n_t))
        own = k == 0 and j == 0
        return remote(self.block if own else here, here, send, recv, {"dp": self.other})

    def own_copy(self):
        return pltpu.make_async_copy(self.block, self.place(self.dp, self.t), self.own_sem)

    def start(self):
        for k in range(1, self.n_t):
            self.z_copy(k).start()
        self.own_copy().start()
        for k in range(1, self.n_chip):
            self.chip_copy(k, 0).start()
        self.core_copy(0, 0).start()

    def pass_to_chips(self):
        for j in range(1, self.n_t):
            self.z_copy(j).wait_recv()
            for k in range(1, self.n_chip):
                self.chip_copy(k, j).start()
            self.core_copy(0, j).start()

    def pass_to_core(self):
        for j in range(self.n_t):
            for k in range(1, self.n_chip):
                self.chip_copy(k, j).wait_recv()
                self.core_copy(k, j).start()

    def arrive(self):
        self.own_copy().wait()
        self.wait_bytes(self.out.at[pl.ds(0, self.n_chip), :, self.rows, self.lanes], self.k_sems[1])

    @staticmethod
    def wait_bytes(part, sem):
        pltpu.make_async_copy(part, part, sem).wait()

    def drain(self):
        self.wait_bytes(self.out.at[0, pl.ds(0, self.n_t - 1), self.rows, self.lanes], self.z_sems[0])
        self.wait_bytes(self.out.at[pl.ds(0, self.n_chip - 1), :, self.rows, self.lanes], self.c_sems[0])
        self.wait_bytes(self.out.at[pl.ds(0, self.n_chip), :, self.rows, self.lanes], self.k_sems[0])


class Scatter:
    def __init__(
        self, n_dp, n_t, grads, out, core_in, half, chip_in, part, z_in, k_send, k_recv, c_send, c_recv, z_send, z_recv
    ):
        self.n_t, self.n_chip = n_t, n_dp // 2
        self.grads, self.out = grads, out
        self.core_in, self.half, self.chip_in, self.part, self.z_in = core_in, half, chip_in, part, z_in
        self.k_sems, self.c_sems, self.z_sems = (k_send, k_recv), (c_send, c_recv), (z_send, z_recv)
        self.dp, self.t = lax.axis_index("dp"), lax.axis_index("tensor")
        self.chip, self.core = self.dp // 2, lax.rem(self.dp, 2)
        self.other = self.chip * 2 + 1 - self.core

    @staticmethod
    def scratch(n_dp, n_t, block):
        n_chip = n_dp // 2
        buffers = [VMEM((n_chip, n_t) + block, BF16)] + [VMEM((n_chip - 1, n_t) + block, BF16)] * 2
        buffers += [VMEM((n_t - 1,) + block, BF16)] * 2
        return buffers + [DMA((n_chip,))] * 4 + [DMA((n_t,))] * 2

    def core_copy(self, k):
        to = lax.rem(self.chip + k, self.n_chip)
        src = self.grads.at[to * 2 + 1 - self.core]
        return remote(src, self.core_in.at[k], self.k_sems[0].at[k], self.k_sems[1].at[k], {"dp": self.other})

    def chip_copy(self, k):
        to = lax.rem(self.chip + k, self.n_chip) * 2 + self.core
        return remote(self.half.at[k - 1], self.chip_in.at[k - 1], self.c_sems[0].at[k], self.c_sems[1].at[k], {"dp": to})

    def z_copy(self, k):
        to = lax.rem(self.t + k, self.n_t)
        return remote(self.part.at[k - 1], self.z_in.at[k - 1], self.z_sems[0].at[k], self.z_sems[1].at[k], {"tensor": to})

    def run(self, between=None, after=None):
        n_chip, n_t = self.n_chip, self.n_t
        order = list(range(1, n_chip)) + [0]
        for k in order:
            self.core_copy(k).start()
        for k in order:
            self.core_copy(k).wait_recv()
            if k > 0:
                to = lax.rem(self.chip + k, n_chip) * 2 + self.core
                self.half[k - 1] = (self.grads[to].astype(F32) + self.core_in[k].astype(F32)).astype(BF16)
                self.chip_copy(k).start()
        if between is not None:
            between()
        for k in range(1, n_chip):
            self.chip_copy(k).wait_recv()
        for k in list(range(1, n_t)) + [0]:
            row = lax.rem(self.t + k, n_t)
            total = self.grads[self.dp, row].astype(F32) + self.core_in[0, row].astype(F32)
            for c in range(1, n_chip):
                total = total + self.chip_in[c - 1, row].astype(F32)
            if k > 0:
                self.part[k - 1] = total.astype(BF16)
                self.z_copy(k).start()
            else:
                self.out[...] = total
        if after is not None:
            after()
        for k in range(1, n_t):
            self.z_copy(k).wait_recv()
            self.out[...] += self.z_in[k - 1].astype(F32)
        for k in range(n_chip):
            self.core_copy(k).wait_send()
        for k in range(1, n_chip):
            self.chip_copy(k).wait_send()
        for k in range(1, n_t):
            self.z_copy(k).wait_send()


class Reduce:
    def __init__(self, n_dp, n_t, out, grads, core_in, half, chip_in, part, z_in, *sems):
        self.n_t, self.n_chip, self.out = n_t, n_dp // 2, out
        self.grads, self.core_in, self.half = grads, core_in, half
        self.chip_in, self.part, self.z_in = chip_in, part, z_in
        self.k_sems, self.c_sems, self.z_sems = sems[0:3], sems[3:5], sems[5:7]
        self.dp, self.t = lax.axis_index("dp"), lax.axis_index("tensor")
        self.chip, self.core = self.dp // 2, lax.rem(self.dp, 2)
        self.other = self.chip * 2 + 1 - self.core

    @staticmethod
    def scratch(n_dp, n_t, parts, block):
        n_chip = n_dp // 2
        sizes = [(n_dp, n_t), (n_chip, n_t), (n_chip - 1, n_t), (n_chip - 1, n_t), (n_t - 1,), (n_t - 1,)]
        return [VMEM((parts,) + size + block, BF16) for size in sizes] + [DMA((parts,))] * 7

    def put(self, p, first, value):
        n_dp, n_t = self.n_chip * 2, self.n_t
        count, lanes = value.shape[0] // (n_dp * n_t), value.shape[1]
        self.grads[p, :, :, first : first + count, :] = value.astype(BF16).reshape(n_dp, n_t, count, lanes)

    def core_copy(self, p, k):
        src = self.grads.at[p, lax.rem(self.chip + k, self.n_chip) * 2 + 1 - self.core]
        send, far, near = self.k_sems
        recv = near if isinstance(k, int) and k == 0 else far
        return remote(src, self.core_in.at[p, k], send.at[p], recv.at[p], {"dp": self.other})

    def chip_copy(self, p, k):
        to = lax.rem(self.chip + k, self.n_chip) * 2 + self.core
        send, recv = self.c_sems
        return remote(self.half.at[p, k - 1], self.chip_in.at[p, k - 1], send.at[p], recv.at[p], {"dp": to})

    def z_copy(self, p, k):
        to = lax.rem(self.t + k, self.n_t)
        send, recv = self.z_sems
        return remote(self.part.at[p, k - 1], self.z_in.at[p, k - 1], send.at[p], recv.at[p], {"tensor": to})

    def to_core(self, p):
        for k in list(range(1, self.n_chip)) + [0]:
            self.core_copy(p, k).start()

    def to_chips(self, p):
        Gather.wait_bytes(self.core_in.at[p, pl.ds(1, self.n_chip - 1)], self.k_sems[1].at[p])
        for k in range(1, self.n_chip):
            to = lax.rem(self.chip + k, self.n_chip) * 2 + self.core
            self.half[p, k - 1] = (self.grads[p, to].astype(F32) + self.core_in[p, k].astype(F32)).astype(BF16)
            self.chip_copy(p, k).start()

    def to_line(self, p):
        self.core_copy(p, 0).wait_recv()
        Gather.wait_bytes(self.chip_in.at[p], self.c_sems[1].at[p])
        for k in list(range(1, self.n_t)) + [0]:
            row = lax.rem(self.t + k, self.n_t)
            total = self.grads[p, self.dp, row].astype(F32) + self.core_in[p, 0, row].astype(F32)
            for c in range(1, self.n_chip):
                total = total + self.chip_in[p, c - 1, row].astype(F32)
            if k > 0:
                self.part[p, k - 1] = total.astype(BF16)
                self.z_copy(p, k).start()
            else:
                self.out(p)[...] = total

    def finish(self, p):
        Gather.wait_bytes(self.z_in.at[p], self.z_sems[1].at[p])
        for k in range(1, self.n_t):
            self.out(p)[...] += self.z_in[p, k - 1].astype(F32)
        Gather.wait_bytes(self.part.at[p], self.z_sems[0].at[p])
        Gather.wait_bytes(self.core_in.at[p], self.k_sems[0].at[p])
        Gather.wait_bytes(self.half.at[p], self.c_sems[0].at[p])


def greet(n_dp, n_t):
    dp, t = lax.axis_index("dp"), lax.axis_index("tensor")
    bar = pltpu.get_barrier_semaphore()
    for k in range(1, n_dp):
        pl.semaphore_signal(bar, inc=1, device_id={"dp": lax.rem(dp + k, n_dp)}, device_id_type=MESH)
    for k in range(1, n_t):
        pl.semaphore_signal(bar, inc=1, device_id={"tensor": lax.rem(t + k, n_t)}, device_id_type=MESH)


def greeted(n_dp, n_t):
    pl.semaphore_wait(pltpu.get_barrier_semaphore(), n_dp - 1 + n_t - 1)


class Exchange:
    def __init__(self, n_dp, src, dst, rows, send, recv, single):
        self.n_dp, self.src, self.dst, self.rows, self.send, self.recv = n_dp, src, dst, rows, send, recv
        self.dp, self.single = lax.axis_index("dp"), single

    def copy(self, k):
        to = lax.rem(self.dp + k, self.n_dp)
        recv = self.recv.at[k] if self.single else self.recv
        return remote(self.src.at[to, self.rows], self.dst.at[self.dp, self.rows], self.send, recv, {"dp": to})

    def start(self, k):
        self.copy(k).start()

    def start_all(self):
        for k in range(1, self.n_dp):
            self.start(k)

    def wait_from(self, k):
        self.copy(k).wait_recv()

    def wait_all(self):
        part = self.dst.at[pl.ds(0, self.n_dp - 1), self.rows]
        pltpu.make_async_copy(part, part, self.recv).wait()

    def wait_sent(self):
        part = self.src.at[pl.ds(0, self.n_dp - 1), self.rows]
        pltpu.make_async_copy(part, part, self.send).wait()


class Spread:
    def __init__(self, n_t, parts, send, recv):
        self.n_t, self.t, self.parts, self.send, self.recv = n_t, lax.axis_index("tensor"), parts, send, recv

    @staticmethod
    def scratch(n_t):
        return [DMA((2, n_t)), DMA((n_t,))]

    def hop(self, j, way):
        here = self.parts.at[j]
        return remote(here, here, self.send.at[way, j], self.recv.at[j], {"tensor": self.t + 1 - 2 * way})

    def step(self, s):
        for way, j, in_line, onward in (
            (0, self.t - s, self.t - s >= 0, self.t + 1 < self.n_t),
            (1, self.t + s, self.t + s < self.n_t, self.t > 0),
        ):
            if s > 0:

                @pl.when(in_line)
                def _():
                    self.hop(j, way).wait_recv()

            @pl.when(in_line & onward)
            def _():
                self.hop(j, way).start()

    def drain(self):
        for s in range(self.n_t):

            @pl.when((self.t - s >= 0) & (self.t + 1 < self.n_t))
            def _():
                self.hop(self.t - s, 0).wait_send()

            @pl.when((self.t + s < self.n_t) & (self.t > 0))
            def _():
                self.hop(self.t + s, 1).wait_send()


class Collect:
    def __init__(self, n_t, parts, came, send, recv):
        self.n_t, self.t, self.parts, self.came, self.send, self.recv = (
            n_t,
            lax.axis_index("tensor"),
            parts,
            came,
            send,
            recv,
        )

    @staticmethod
    def scratch(n_t):
        return [DMA((n_t,)), DMA((n_t + 1,))]

    def hop(self, j, way):
        slot = j if way == 0 else jnp.where(j == self.t - 1, self.n_t, j)
        to = self.t + 1 - 2 * way
        return remote(self.parts.at[j], self.came.at[slot], self.send.at[j], self.recv.at[slot], {"tensor": to})

    def wait_slot(self, slot):
        remote(self.parts.at[0], self.came.at[slot], self.send.at[0], self.recv.at[slot], {"tensor": self.t}).wait_recv()

    def begin(self, j):
        @pl.when((self.t == 0) & (j > 0))
        def _():
            self.hop(j, 0).start()

        @pl.when((self.t == self.n_t - 1) & (j < self.n_t - 1))
        def _():
            self.hop(j, 1).start()

    def step(self, e, far):
        if far:
            right, left = self.n_t - 1 - e + self.t, e - self.n_t + 1 + self.t
        else:
            right, left = e - self.t + 2, 2 * self.n_t - 4 - e - self.t
        for way, j, mine in (
            (0, right, (self.t >= 1) & (right <= self.n_t - 1) & (right > self.t)),
            (1, left, (self.t <= self.n_t - 2) & (left >= 0) & (left < self.t)),
        ):

            @pl.when(mine)
            def _():
                self.wait_slot(j)
                self.parts[j] = (self.parts[j].astype(F32) + self.came[j].astype(F32)).astype(BF16)
                self.hop(j, way).start()

    def finish(self, result):
        result[...] = self.parts[self.t].astype(F32)

        @pl.when(self.t > 0)
        def _():
            self.wait_slot(self.t)
            result[...] += self.came[self.t].astype(F32)

        @pl.when(self.t < self.n_t - 1)
        def _():
            self.wait_slot(self.n_t)
            result[...] += self.came[self.n_t].astype(F32)

        for j in range(self.n_t):

            @pl.when(self.t < j)
            def _():
                self.hop(j, 0).wait_send()

            @pl.when(self.t > j)
            def _():
                self.hop(j, 1).wait_send()


def centre(values):
    centred = values - jnp.mean(values, axis=1, keepdims=True)
    inverse = lax.rsqrt(jnp.mean(centred * centred, axis=1, keepdims=True) + 1e-06)
    return centred * inverse, inverse


def norm_back(grad, unit, inverse, gain):
    scaled = grad * gain
    back = inverse * (
        scaled
        - jnp.mean(scaled, axis=1, keepdims=True)
        - unit * jnp.mean(scaled * unit, axis=1, keepdims=True)
    )
    return back, jnp.sum(grad * unit, axis=0, keepdims=True), jnp.sum(grad, axis=0, keepdims=True)


def norm_picks(experts):
    row, lane = (lax.broadcasted_iota(jnp.int32, (8, LANES), axis) for axis in (0, 1))
    return (row + experts == lane).astype(F32).astype(BF16)


def norm_rows(small, experts):
    return nt(norm_picks(experts), small)


def small_grads(experts, grad_router, rows):
    line = lax.broadcasted_iota(jnp.int32, (8, rows[0].shape[1]), 0)
    stack = sum(jnp.where(line == at, row, 0.0) for at, row in enumerate(rows))
    return grad_router + tn(stack.astype(BF16), norm_picks(experts))


def image_bias(rows, padded):
    line = lax.broadcasted_iota(jnp.int32, (padded, padded), 0)
    column = lax.broadcasted_iota(jnp.int32, (padded, padded), 1)
    image_line, image_column = jnp.zeros_like(line), jnp.zeros_like(column)
    for at in range(SEQ, rows + 1, SEQ):
        image_line += (line >= at).astype(jnp.int32)
        image_column += (column >= at).astype(jnp.int32)
    return jnp.where((image_line == image_column) & (column < rows), 0.0, -1e30)


def half_masks():
    lane = lax.broadcasted_iota(jnp.int32, (1, LANES), 1)
    low = (lane < HEAD_DIM).astype(F32)
    return low.astype(BF16), (1.0 - low).astype(BF16)


def soft_scores(query, key, bias):
    scores = nt(query, key) * HEAD_DIM ** (-0.5) + bias
    power = jnp.exp(scores - jnp.max(scores, axis=1, keepdims=True))
    return power * (1.0 / jnp.sum(power, axis=1, keepdims=True))


def router_probs(logits, experts):
    lane = lax.broadcasted_iota(jnp.int32, logits.shape, 1)
    inside = lane < experts
    kept = jnp.where(inside, logits, -1e30)
    power = jnp.where(inside, jnp.exp(kept - jnp.max(kept, axis=1, keepdims=True)), 0.0)
    return power * (1.0 / jnp.sum(power, axis=1, keepdims=True))


def pick_gate(probs, choice):
    lane = lax.broadcasted_iota(jnp.int32, probs.shape, 1)
    return jnp.sum(jnp.where(lane == choice, probs, 0.0), axis=1, keepdims=True)


class Weights:
    def __init__(self, shard, width, gathered=None, whole=None):
        self.shard, self.width, self.gathered, self.whole = shard, width, gathered, whole

    def __call__(self, at):
        if self.whole is not None:
            return self.whole[at]
        part = self.gathered[:, :, at * self.shard : (at + 1) * self.shard, :]
        return part.reshape(self.width, self.width)

    def small(self):
        if self.whole is not None:
            return self.whole[SMALL, :, :LANES]
        part = self.gathered[:, :, SMALL * self.shard : (SMALL + 1) * self.shard, :LANES]
        return part.reshape(self.width, LANES)


def gelu_parts(hidden):
    bell = jnp.exp(-0.5 * hidden * hidden)
    near = 1.0 / (1.0 + 0.23164189 * jnp.abs(hidden))
    tail = near * (
        0.127414796 + near * (-0.142248368 + near * (0.7107068705 + near * (-0.7265760135 + near * 0.5307027145)))
    )
    tail = tail * bell
    share = jnp.where(hidden < 0.0, tail, 1.0 - tail)
    return hidden * share, share + hidden * bell * 0.3989422804014327


def forward_kernel(cfg, *refs):
    n_dp, n_t, rows, padded, width, experts, rooms, shard, inside = cfg
    refs = list(refs)

    def take(count):
        got = refs[:count]
        del refs[:count]
        return got

    x_ref, cot_ref, cols_ref, slots_ref, block_ref = take(5)
    gathered, recv_d, recv_s, res_ref, moe_ref, q_ref, k_ref, v_ref, mix_ref, norm_ref, probs_ref = take(11)
    full, cot_full, bias, send_d, send_s, d_send, d_recv, s_send, s_recv = take(9)
    dp = lax.axis_index("dp")
    meet(n_dp, n_t, inside)
    if inside:
        gather = Gather(n_dp, n_t, 0, block_ref.shape[0], width, block_ref, gathered, *refs)
        gather.start()
        weights = Weights(shard, width, gathered=gathered)
    else:
        gathered[...] = jnp.zeros_like(gathered)
        weights = Weights(shard, width, whole=block_ref)

    full[rows - rows % 8 :, :] = jnp.zeros((padded - rows + rows % 8, width), F32)
    full[:rows, :] = x_ref[...].astype(F32)
    cot_full[rows - rows % 8 :, :] = jnp.zeros((padded - rows + rows % 8, width), F32)
    cot_full[:rows, :] = cot_ref[...].astype(F32)
    bias[...] = image_bias(rows, padded)
    unit, _ = centre(full[...])
    norm_ref[...] = unit.astype(BF16)
    if inside:
        gather.pass_to_chips()
        gather.pass_to_core()
        gather.arrive()
        gather.drain()

    norms = norm_rows(weights.small(), experts)
    unit, _ = centre(full[...])
    normed = (unit * norms[0:1] + norms[1:2]).astype(BF16)
    norm_ref[...] = normed
    q_ref[...] = nn(normed, weights(0)).astype(BF16)
    k_ref[...] = nn(normed, weights(1)).astype(BF16)
    v_ref[...] = nn(normed, weights(2)).astype(BF16)
    low, high = half_masks()

    def heads(j, carry):
        at = pl.ds(pl.multiple_of(j * LANES, LANES), LANES)
        query, key, value = q_ref[:, at], k_ref[:, at], v_ref[:, at]
        first = nn(soft_scores(query * low, key, bias[...]).astype(BF16), value)
        second = nn(soft_scores(query * high, key, bias[...]).astype(BF16), value)
        mix_ref[:, at] = (first * low.astype(F32) + second * high.astype(F32)).astype(BF16)
        return carry

    lax.fori_loop(0, width // LANES, heads, 0)
    residual = full[...] + nn(mix_ref[...], weights(OUT))
    res_ref[...] = residual
    unit, _ = centre(residual)
    moe = (unit * norms[2:3] + norms[3:4]).astype(BF16)
    moe_ref[...] = moe
    probs = router_probs(nn(moe, weights.small()), experts)
    probs_ref[...] = probs
    cot = cot_full[...]
    full[...] = pick_gate(probs, cols_ref[:, 0:1]) * cot
    cot_full[...] = pick_gate(probs, cols_ref[:, 1:2]) * cot

    def selectors(p):
        slot = lax.broadcasted_iota(jnp.int32, (rooms, padded), 0) + p * rooms
        first = (slot == slots_ref[0:1, :]).astype(F32)
        second = (slot == slots_ref[1:2, :]).astype(F32)
        return first, second

    def d_copy(k):
        to = lax.rem(dp + k, n_dp)
        return remote(send_d.at[to], recv_d.at[dp], d_send.at[k], d_recv.at[k], {"dp": to})

    def s_copy(k):
        to = lax.rem(dp + k, n_dp)
        return remote(send_s.at[to], recv_s.at[dp], s_send.at[k], s_recv.at[k], {"dp": to})

    def dispatch(k, carry):
        to = lax.rem(dp + k, n_dp)
        first, second = selectors(to)
        send_d[to] = nn((first + second).astype(BF16), moe_ref[...]).astype(BF16)

        @pl.when(k > 0)
        def _():
            d_copy(k).start()

        return carry

    def dispatch_grad(k, carry):
        to = lax.rem(dp + k, n_dp)
        first, second = selectors(to)
        rows_grad = nn(first.astype(BF16), full[...].astype(BF16)) + nn(second.astype(BF16), cot_full[...].astype(BF16))
        send_s[to] = rows_grad.astype(BF16)

        @pl.when(k > 0)
        def _():
            s_copy(k).start()

        return carry

    lax.fori_loop(0, n_dp, dispatch, 0)
    lax.fori_loop(0, n_dp, dispatch_grad, 0)
    recv_d[dp] = send_d[dp]
    recv_s[dp] = send_s[dp]
    for k in range(1, n_dp):
        d_copy(k).wait()
    for k in range(1, n_dp):
        s_copy(k).wait()


def forward(cfg, cid, x, cot, cols, slots, block):
    n_dp, n_t, rows, padded, width, experts, rooms, shard, inside = cfg
    rows_block = ceil_to(5 * shard, 16)
    low = jax.ShapeDtypeStruct((padded, width), BF16)
    sent = jax.ShapeDtypeStruct((n_dp, rooms, width), BF16)
    gathered = (n_dp, n_t, rows_block, width) if inside else (1, 1, 16, LANES)
    outs = [jax.ShapeDtypeStruct(gathered, BF16), sent, sent, jax.ShapeDtypeStruct((padded, width), F32)]
    outs += [low] * 6 + [jax.ShapeDtypeStruct((padded, LANES), F32)]
    scratch = [
        VMEM((padded, width), F32),
        VMEM((padded, width), F32),
        VMEM((padded, padded), F32),
        VMEM((n_dp, rooms, width), BF16),
        VMEM((n_dp, rooms, width), BF16),
    ] + [DMA((n_dp,))] * 4
    if inside:
        scratch += Gather.scratch(n_dp, n_t)
    whole = pl.BlockSpec(memory_space=VMEM)
    return pl.pallas_call(
        partial(forward_kernel, cfg),
        out_shape=outs,
        in_specs=[whole] * 5,
        out_specs=[whole] * len(outs),
        scratch_shapes=scratch,
        compiler_params=pltpu.CompilerParams(
            collective_id=cid, has_side_effects=True, vmem_limit_bytes=56 * 2**20
        ),
        name="forward_" + str(rooms),
    )(x, cot, cols, slots, block)


def expert_kernel(chunks, d_ref, s_ref, w_in_ref, w_out_ref, ret_ref, back_ref, g_in_ref, g_out_ref, ret, back, g_in, g_out):
    step = pl.program_id(0)
    rows = d_ref.shape[0]
    chunk = rows // chunks

    @pl.when(step == 0)
    def _():
        ret[...] = jnp.zeros_like(ret)
        back[...] = jnp.zeros_like(back)

    g_in[...] = jnp.zeros_like(g_in)
    g_out[...] = jnp.zeros_like(g_out)
    w_in, w_out = w_in_ref[...], w_out_ref[...]

    def part(c, carry):
        at = pl.ds(pl.multiple_of(c * chunk, 16), chunk)
        took, slot_grad = d_ref[at, :], s_ref[at, :]
        active, slope = gelu_parts(nt(took, w_in))
        active = active.astype(BF16)
        grad_hidden = (nt(slot_grad, w_out) * slope).astype(BF16)
        ret[at, :] += nn(active, w_out)
        back[at, :] += nn(grad_hidden, w_in)
        g_out[...] += tn(active, slot_grad)
        g_in[...] += tn(grad_hidden, took)
        return carry

    lax.fori_loop(0, chunks, part, 0)
    g_in_ref[...] = g_in[...].astype(BF16)
    g_out_ref[...] = g_out[...].astype(BF16)

    @pl.when(step == pl.num_programs(0) - 1)
    def _():
        ret_ref[...] = ret[...].astype(BF16)
        back_ref[...] = back[...].astype(BF16)


def run_expert(took, slot_grad, w_in, w_out):
    rows, width = took.shape
    hidden = w_in.shape[0]
    block = 256
    chunks = next(c for c in range(max(1, rows // 400), rows + 1) if rows % c == 0 and (rows // c) % 16 == 0)
    whole = pl.BlockSpec((rows, width), lambda i: (0, 0))
    part = pl.BlockSpec((block, width), lambda i: (i, 0))
    low = jax.ShapeDtypeStruct((rows, width), BF16)
    grad = jax.ShapeDtypeStruct((hidden, width), BF16)
    return pl.pallas_call(
        partial(expert_kernel, chunks),
        grid=(hidden // block,),
        out_shape=[low, low, grad, grad],
        in_specs=[whole, whole, part, part],
        out_specs=[whole, whole, part, part],
        scratch_shapes=[
            VMEM((rows, width), F32),
            VMEM((rows, width), F32),
            VMEM((block, width), F32),
            VMEM((block, width), F32),
        ],
        compiler_params=pltpu.CompilerParams(vmem_limit_bytes=60 * 2**20),
        cost_estimate=pl.CostEstimate(
            flops=12 * rows * width * hidden, bytes_accessed=12 * rows * width + 8 * hidden * width, transcendentals=0
        ),
        name="expert_" + str(rows),
    )(took, slot_grad, w_in, w_out)


def backward_kernel(cfg, *refs):
    n_dp, n_t, rows, padded, width, experts, rooms, shard, inside = cfg
    refs = list(refs)

    def take(count):
        got = refs[:count]
        del refs[:count]
        return got

    ret_ref, back_ref, x_ref, cot_ref, cols_ref, weights_ref = take(6)
    res_ref, moe_ref, q_ref, k_ref, v_ref, mix_ref, norm_ref, probs_ref = take(8)
    out_ref, gx_ref, sum_ref = take(3)
    full, cot_full, bias, ret_in, back_in, grads, r_send, r_recv, b_send, b_recv = take(10)
    dq, dk, dv = take(3)
    dp = lax.axis_index("dp")
    meet(n_dp, n_t, inside)

    def r_copy(k):
        to = lax.rem(dp + k, n_dp)
        return remote(ret_ref.at[to], ret_in.at[dp], r_send.at[k], r_recv.at[k], {"dp": to})

    def b_copy(k):
        to = lax.rem(dp + k, n_dp)
        return remote(back_ref.at[to], back_in.at[dp], b_send.at[k], b_recv.at[k], {"dp": to})

    for k in range(1, n_dp):
        r_copy(k).start()
    for k in range(1, n_dp):
        b_copy(k).start()
    ret_in[dp] = ret_ref[dp]
    back_in[dp] = back_ref[dp]
    weights = Weights(shard, width, gathered=weights_ref) if inside else Weights(shard, width, whole=weights_ref)
    tail = rows - rows % 8
    full[tail:, :] = jnp.zeros((padded - tail, width), F32)
    full[:rows, :] = x_ref[...].astype(F32)
    cot_full[tail:, :] = jnp.zeros((padded - tail, width), F32)
    cot_full[:rows, :] = cot_ref[...].astype(F32)
    bias[...] = image_bias(rows, padded)
    norms = norm_rows(weights.small(), experts)

    def selectors(e):
        lane = lax.broadcasted_iota(jnp.int32, (padded, rooms), 1) + e * rooms
        return (lane == cols_ref[:, 2:3]).astype(F32), (lane == cols_ref[:, 3:4]).astype(F32)

    for k in range(1, n_dp):
        r_copy(k).wait()

    def pick(e, carry):
        return tuple(rows + nn(one.astype(BF16), ret_in[e]) for rows, one in zip(carry, selectors(e)))

    zero = jnp.zeros((padded, width), F32)
    first_rows, second_rows = lax.fori_loop(0, n_dp, pick, (zero, zero))
    probs = probs_ref[...]
    first_id, second_id = cols_ref[:, 0:1], cols_ref[:, 1:2]
    outcome = res_ref[...] + pick_gate(probs, first_id) * first_rows + pick_gate(probs, second_id) * second_rows
    out_ref[...] = outcome[:rows].astype(BF16)
    cot = cot_full[...]
    first_grad = jnp.sum(first_rows * cot, axis=1, keepdims=True)
    second_grad = jnp.sum(second_rows * cot, axis=1, keepdims=True)
    spot = lax.broadcasted_iota(jnp.int32, probs.shape, 1)
    grad_probs = jnp.where(spot == first_id, first_grad, 0.0) + jnp.where(spot == second_id, second_grad, 0.0)
    grad_logits = (probs * (grad_probs - jnp.sum(probs * grad_probs, axis=1, keepdims=True))).astype(BF16)
    grad_router = tn(moe_ref[...], grad_logits)

    for k in range(1, n_dp):
        b_copy(k).wait()

    def pick_both(e, rows):
        first, second = selectors(e)
        return rows + nn((first + second).astype(BF16), back_in[e])

    grad_moe = lax.fori_loop(0, n_dp, pick_both, nt(grad_logits, weights.small()))
    unit, inverse = centre(res_ref[...])
    extra, gain_two, shift_two = norm_back(grad_moe, unit, inverse, norms[2:3])
    grad_residual = cot + extra
    cot_full[...] = grad_residual
    grad_attended = grad_residual.astype(BF16)
    n_all = n_dp * n_t

    def keep(at, value):
        if inside:
            grads[:, :, at * shard : (at + 1) * shard, :] = value.astype(BF16).reshape(n_dp, n_t, shard, width)
        else:
            sum_ref[at] = value

    keep(OUT, tn(mix_ref[...], grad_attended))
    mix_ref_grad = nt(grad_attended, weights(OUT)).astype(BF16)
    dq[...] = mix_ref_grad
    low, high = half_masks()
    low_f, high_f = low.astype(F32), high.astype(F32)
    scale = HEAD_DIM ** (-0.5)

    def heads(j, carry):
        at = pl.ds(pl.multiple_of(j * LANES, LANES), LANES)
        query, key, value, grad = q_ref[:, at], k_ref[:, at], v_ref[:, at], dq[:, at]
        for mask, mask_f in ((low, low_f), (high, high_f)):
            probs = soft_scores(query * mask, key, bias[...])
            grad_probs = nt(grad * mask, value)
            grad_scores = probs * (grad_probs - jnp.sum(probs * grad_probs, axis=1, keepdims=True))
            grad_scores = grad_scores.astype(BF16)
            part_v = tn(probs.astype(BF16), grad)
            part_q = nn(grad_scores, key) * scale
            part_k = tn(grad_scores, query) * scale
            if mask is low:
                sum_q, sum_k, sum_v = part_q * mask_f, part_k * mask_f, part_v * mask_f
            else:
                sum_q, sum_k, sum_v = sum_q + part_q * mask_f, sum_k + part_k * mask_f, sum_v + part_v * mask_f
        dq[:, at] = sum_q.astype(BF16)
        dk[:, at] = sum_k.astype(BF16)
        dv[:, at] = sum_v.astype(BF16)
        return carry

    lax.fori_loop(0, width // LANES, heads, 0)
    keep(0, tn(norm_ref[...], dq[...]))
    keep(1, tn(norm_ref[...], dk[...]))
    keep(2, tn(norm_ref[...], dv[...]))
    grad_normed = nt(dq[...], weights(0)) + nt(dk[...], weights(1)) + nt(dv[...], weights(2))
    unit, inverse = centre(full[...])
    extra, gain_one, shift_one = norm_back(grad_normed, unit, inverse, norms[0:1])
    gx_ref[...] = (cot_full[...] + extra)[:rows].astype(BF16)
    small = small_grads(experts, grad_router, (gain_one, shift_one, gain_two, shift_two))
    if inside:
        at = slice(SMALL * shard, (SMALL + 1) * shard)
        grads[:, :, at, :LANES] = small.astype(BF16).reshape(n_dp, n_t, shard, LANES)
        grads[:, :, at, LANES:] = jnp.zeros((n_dp, n_t, shard, width - LANES), BF16)
        Scatter(n_dp, n_t, grads, sum_ref, *refs).run()
    else:
        sum_ref[SMALL] = jnp.zeros((width, width), F32)
        sum_ref[SMALL, :, :LANES] = small


def backward(cfg, cid, *args):
    n_dp, n_t, rows, padded, width, experts, rooms, shard, inside = cfg
    rows_block = ceil_to(5 * shard, 16)
    total = (rows_block, width) if inside else (5, width, width)
    outs = [jax.ShapeDtypeStruct((rows, width), BF16)] * 2 + [jax.ShapeDtypeStruct(total, F32)]
    scratch = [
        VMEM((padded, width), F32),
        VMEM((padded, width), F32),
        VMEM((padded, padded), F32),
        VMEM((n_dp, rooms, width), BF16),
        VMEM((n_dp, rooms, width), BF16),
        VMEM((n_dp, n_t, rows_block, width) if inside else (1, 1, 16, LANES), BF16),
    ]
    scratch += [DMA((n_dp,))] * 4 + [VMEM((padded, width), BF16)] * 3
    if inside:
        scratch += Scatter.scratch(n_dp, n_t, (rows_block, width))
    whole = pl.BlockSpec(memory_space=VMEM)
    return pl.pallas_call(
        partial(backward_kernel, cfg),
        out_shape=outs,
        in_specs=[whole] * len(args),
        out_specs=[whole] * len(outs),
        scratch_shapes=scratch,
        compiler_params=pltpu.CompilerParams(
            collective_id=cid, has_side_effects=True, vmem_limit_bytes=56 * 2**20
        ),
        name="backward_" + str(rooms),
    )(*args)


def image_blocks(rows):
    blocks = []
    for first in range(0, rows, SEQ):
        start = first // 16 * 16
        blocks.append((start, ceil_to(first - start + SEQ, 16), first - start))
    return blocks


def inside_image(size, first, axis):
    shape = (size, 1) if axis == 0 else (1, size)
    spot = lax.broadcasted_iota(jnp.int32, shape, axis)
    return (spot >= first) & (spot < first + SEQ)


def image_probs(query, key, size, first):
    scores = nt(query, key) * HEAD_DIM ** (-0.5) + jnp.where(inside_image(size, first, 1), 0.0, -1e30)
    power = jnp.exp(scores - jnp.max(scores, axis=1, keepdims=True))
    total = jnp.sum(power, axis=1, keepdims=True)
    return power * jnp.where(inside_image(size, first, 0), 1.0 / total, 0.0)


def join_images(parts, blocks):
    whole = parts[0]
    for (start, _, _), part in zip(blocks[1:], parts[1:]):
        shared = whole.shape[0] - start
        pieces = [whole[:start]]
        if shared > 0:
            pieces.append(whole[start:] + part[:shared])
        whole = jnp.concatenate(pieces + [part[shared:]], axis=0)
    return whole


def pack_block(refs, block, shard, width, experts):
    q_ref, k_ref, v_ref, o_ref, router_ref, *line_refs = refs
    for at, ref in ((0, q_ref), (1, k_ref), (2, v_ref), (OUT, o_ref)):
        block[at * shard : (at + 1) * shard, :] = ref[...].astype(BF16)
    here = slice(SMALL * shard, (SMALL + 1) * shard)
    block[here, :] = jnp.zeros((shard, width), BF16)
    row, column = (lax.broadcasted_iota(jnp.int32, (shard, shard), axis) for axis in (0, 1))
    lane = lax.broadcasted_iota(jnp.int32, (shard, LANES), 1)
    small = jnp.zeros((shard, LANES), F32)
    for at in range(experts + len(line_refs)):
        level = router_ref[at : at + 1, :] if at < experts else line_refs[at - experts][...]
        upright = jnp.sum(jnp.where(row == column, level, 0.0), axis=1, keepdims=True)
        small = jnp.where(lane == at, upright, small)
    block[here, :LANES] = small.astype(BF16)


def find_places(cfg, routes_ref, place, turned, over):
    n_dp, n_t, rows, padded, width, experts, rooms, shard, inside, hid = cfg
    t = lax.axis_index("tensor")
    tok_count = routes_ref.shape[1]
    capacity = (5 * tok_count + 2 * experts - 1) // (2 * experts)
    line = lax.broadcasted_iota(jnp.int32, (experts, tok_count), 0)
    lane = lax.broadcasted_iota(jnp.int32, (experts, tok_count), 1)

    def count(row, until):
        hot = (line == routes_ref[row : row + 1, :]) & (lane < until)
        return jnp.sum(hot.astype(F32), axis=1, keepdims=True)

    total = count(0, tok_count)
    before = (count(0, t * rows), count(1, t * rows))
    long = ceil_to(tok_count, LANES)
    wide = turned.shape[1]
    turned[...] = jnp.full(turned.shape, -1.0, F32)
    everyone = jnp.concatenate(
        [routes_ref[...], jnp.full((2, long - tok_count), experts, jnp.int32)], axis=1
    )
    everyone = jnp.concatenate([everyone, everyone, everyone, everyone], axis=0)
    mine = pltpu.roll(everyone, lax.rem(long - t * rows, long), 1)[:, :wide]
    spot = lax.broadcasted_iota(jnp.int32, (8, wide), 1)
    mine = jnp.where(spot < rows, mine, experts)
    line = lax.broadcasted_iota(jnp.int32, (experts, wide), 0)
    first, second = line == mine[0:1], line == mine[1:2]
    down, across = (lax.broadcasted_iota(jnp.int32, (wide, wide), axis) for axis in (0, 1))
    earlier = (down < across).astype(F32).astype(BF16)
    own = jnp.sum(first.astype(F32), axis=1, keepdims=True)
    first_rank = nn(first.astype(F32).astype(BF16), earlier)
    second_rank = nn(second.astype(F32).astype(BF16), earlier)

    def slot(choice, hot, rank, place):
        kept = hot & (place < capacity)
        here = jnp.sum(jnp.where(kept, rank + 1.0, 0.0), axis=0, keepdims=True) - 1.0
        good = (here >= 0.0) & (here < rooms)
        return jnp.where(good, choice.astype(F32) * rooms + here, -1.0), jnp.max(here, axis=1, keepdims=True)

    first_slot, first_most = slot(mine[0:1], first, first_rank, first_rank + before[0])
    second_slot, second_most = slot(mine[1:2], second, second_rank + own, second_rank + total + before[1])
    turned[0:1, :] = first_slot
    turned[1:2, :] = second_slot
    turned[2:3, :] = mine[0:1].astype(F32)
    turned[3:4, :] = mine[1:2].astype(F32)
    place[...] = turned[...].T
    most = jnp.maximum(first_most, second_most)
    over[...] = jnp.broadcast_to(jnp.where(most >= rooms, 1.0, 0.0), over.shape)


def step_kernel(cfg, *refs):
    n_dp, n_t, rows, padded, width, experts, rooms, shard, inside, hid = cfg
    refs = list(refs)

    def take(count):
        got = refs[:count]
        del refs[:count]
        return got

    here = take(3)
    e_in_ref, e_out_ref = take(2)
    here += take(9 if inside else 1)
    out_ref, gx_ref, sum_ref, g_in_ref, g_out_ref = take(5)
    held = take(len(here))
    x_ref, cot_ref, routes_ref, *shared = held
    here_sems = take(1)[0]
    block, gathered, full, cot_full, bias, res, probs_s = take(7)
    place, turned, over, gate_m, gate_c, gate_s, gate_r, rise_s, rise_r = take(9)
    moe, q_s, k_s, v_s, mix, norm, dk, dv = take(8)
    send_d, send_s, recv_d, recv_s, ret_in, back_in, act, slope = take(8)
    wi, wo, gi, go, gi_in, go_in = take(6)
    d_send, d_recv, s_send, s_recv, r_send, r_recv, b_send, b_recv = take(8)
    f_send, f_recv, e_send, e_recv, own_sems = take(5)
    wi_spread, wo_spread = Spread(n_t, wi, *take(2)), Spread(n_t, wo, *take(2))
    gi_collect, go_collect = Collect(n_t, gi, gi_in, *take(2)), Collect(n_t, go, go_in, *take(2))
    dp, t = lax.axis_index("dp"), lax.axis_index("tensor")
    scale = HEAD_DIM ** (-0.5)
    slot_count = n_dp * rooms
    half, wide = min(256, hid), min(256, width)
    long = gate_m.shape[1]
    early = 2 if hid == width and n_t > 2 else 0
    table = [sorted(range(n_t), key=lambda j: (abs(j - at), j)) for at in range(n_t)]

    def order(p):
        found = jnp.int32(0)
        for at in range(n_t):
            for spot in range(n_t):
                found = found + jnp.where((t == at) & (p == spot), table[at][spot], 0)
        return found

    every = pl.ds(0, rooms)
    cut = max(rooms // 2 // 16 * 16, 16)
    d_copy = Exchange(n_dp, send_d, recv_d, every, d_send, d_recv, True)
    s_first = Exchange(n_dp, send_s, recv_s, pl.ds(0, cut), s_send.at[0], s_recv.at[0], False)
    s_second = Exchange(n_dp, send_s, recv_s, pl.ds(cut, rooms - cut), s_send.at[1], s_recv.at[1], False)
    late = max(rooms * 2 // 5 // 16 * 16, 16)
    r_first = Exchange(n_dp, send_d, ret_in, pl.ds(late, rooms - late), r_send.at[0], r_recv.at[0], False)
    r_second = Exchange(n_dp, send_d, ret_in, pl.ds(0, late), r_send.at[1], r_recv.at[1], False)
    b_copy = Exchange(n_dp, send_s, back_in, every, b_send, b_recv, False)
    f_copy = Exchange(n_dp, gate_s, gate_r, pl.ds(0, 8), f_send, f_recv, False)
    e_copy = Exchange(n_dp, rise_s, rise_r, pl.ds(0, 8), e_send, e_recv, False)

    def column(at):
        return place[:padded, at : at + 1].astype(jnp.int32)

    greet(n_dp, n_t)
    load_in = pltpu.make_async_copy(e_in_ref, g_in_ref, own_sems.at[0])
    load_out = pltpu.make_async_copy(e_out_ref, g_out_ref, own_sems.at[1])
    loads = [pltpu.make_async_copy(src, dst, here_sems.at[at]) for at, (src, dst) in enumerate(zip(here, held))]
    for load in loads[3:]:
        load.start()
    load_in.start()
    for load in loads[:3]:
        load.start()
    load_out.start()
    for load in loads[3:]:
        load.wait()
    if inside:
        pack_block(shared, block, shard, width, experts)
        size = len(Gather.scratch(n_dp, n_t))
        gather_a = Gather(n_dp, n_t, 0, SMALL * shard, width, block, gathered, *take(size))
        gather_s = Gather(n_dp, n_t, SMALL * shard, shard, LANES, block, gathered, *take(size))
        gather_b = Gather(n_dp, n_t, OUT * shard, shard, width, block, gathered, *take(size))
        weights = Weights(shard, width, gathered=gathered)
    else:
        weights = Weights(shard, width, whole=shared[0])
    load_in.wait()
    wi[t] = g_in_ref[...].astype(BF16)
    greeted(n_dp, n_t)
    if inside:
        gather_a.start()
        gather_s.start()
        gather_b.start()
    wi_spread.step(0)
    for load in loads[:3]:
        load.wait()
    load_out.wait()
    wo[t] = g_out_ref[...].astype(BF16)
    tail = rows - rows % 8
    full[tail:, :] = jnp.zeros((padded - tail, width), F32)
    full[:rows, :] = x_ref[...].astype(F32)
    cot_full[tail:, :] = jnp.zeros((padded - tail, width), F32)
    cot_full[:rows, :] = cot_ref[...].astype(F32)
    bias[...] = image_bias(rows, padded)
    find_places(cfg, routes_ref, place, turned, over)

    def selectors(p):
        slot = lax.broadcasted_iota(jnp.int32, (rooms, padded), 0) + p * rooms
        first = (slot == turned[0:1, :padded].astype(jnp.int32)).astype(F32)
        second = (slot == turned[1:2, :padded].astype(jnp.int32)).astype(F32)
        return first, second

    dk[...] = cot_full[...].astype(BF16)

    def dispatch_grad(k, carry):
        to = lax.rem(dp + k, n_dp)
        first, second = selectors(to)
        got = nn((first + second).astype(BF16), dk[...]).astype(BF16)

        @pl.when(k > 0)
        def _():
            send_s[to] = got

        @pl.when(k == 0)
        def _():
            recv_s[to] = got

        return carry

    lax.fori_loop(0, n_dp, dispatch_grad, 0)
    if inside:
        gather_a.pass_to_chips()
        gather_s.pass_to_chips()
        gather_b.pass_to_chips()
        gather_a.pass_to_core()
        gather_s.pass_to_core()
    if inside:
        gather_a.arrive()
        gather_s.arrive()
    norms = norm_rows(weights.small(), experts)
    unit, _ = centre(full[...])
    norm[...] = (unit * norms[0:1] + norms[1:2]).astype(BF16)
    q_s[...] = nn(norm[...], weights(0)).astype(BF16)
    k_s[...] = nn(norm[...], weights(1)).astype(BF16)
    v_s[...] = nn(norm[...], weights(2)).astype(BF16)
    if inside:
        gather_b.pass_to_core()
    s_first.start_all()
    middle = (t > 0) & (t < n_t - 1)

    @pl.when(jnp.logical_not(middle))
    def _():
        wo_spread.step(0)

    low, high = half_masks()
    low_f, high_f = low.astype(F32), high.astype(F32)
    blocks = image_blocks(rows)

    def heads(j, carry):
        at = pl.ds(pl.multiple_of(j * LANES, LANES), LANES)
        parts = []
        for start, size, first in blocks:
            here = pl.ds(start, size)
            query, key, value = q_s[here, at], k_s[here, at], v_s[here, at]
            one = nn(image_probs(query * low, key, size, first).astype(BF16), value)
            two = nn(image_probs(query * high, key, size, first).astype(BF16), value)
            parts.append(one * low_f + two * high_f)
        mix[:, at] = join_images(parts, blocks).astype(BF16)
        return carry

    lax.fori_loop(0, width // LANES // 2, heads, 0)
    @pl.when(middle)
    def _():
        wi_spread.step(1)

    lax.fori_loop(width // LANES // 2, width // LANES, heads, 0)
    if inside:
        gather_b.arrive()
    residual = full[...] + nn(mix[...], weights(OUT))
    res[...] = residual
    unit, _ = centre(residual)
    moe[...] = (unit * norms[2:3] + norms[3:4]).astype(BF16)
    probs_s[...] = router_probs(nn(moe[...], weights.small()), experts)

    spot = lax.broadcasted_iota(jnp.int32, (padded, LANES), 1)
    first_gate, second_gate = pick_gate(probs_s[...], column(2)), pick_gate(probs_s[...], column(3))
    place[:padded, :] = jnp.where(spot == 4, first_gate, jnp.where(spot == 5, second_gate, place[:padded, :]))
    turned[...] = place[...].T
    gate_line = lax.broadcasted_iota(jnp.int32, (8, padded), 0)

    def terms(gate):
        one = gate.astype(BF16).astype(F32)
        two = (gate - one).astype(BF16).astype(F32)
        three = gate - one - two
        stack = jnp.where(gate_line == 0, one, jnp.where(gate_line == 1, two, jnp.where(gate_line == 2, three, 0.0)))
        return stack.astype(BF16)

    first_terms, second_terms = terms(turned[4:5, :padded]), terms(turned[5:6, :padded])
    def dispatch(k, carry):
        to = lax.rem(dp + k, n_dp)
        first, second = selectors(to)
        got = nn((first + second).astype(BF16), moe[...]).astype(BF16)

        @pl.when(k > 0)
        def _():
            send_d[to] = got
            d_copy.start(k)

        @pl.when(k == 0)
        def _():
            recv_d[to] = got

        return carry

    lax.fori_loop(0, n_dp, dispatch, 0)

    @pl.when(middle)
    def _():
        if n_t > 2:
            wi_spread.step(2)
        wo_spread.step(0)

    def dispatch_gates(k, carry):
        to = lax.rem(dp + k, n_dp)
        first, second = selectors(to)
        gate = nt(first_terms, first.astype(BF16)) + nt(second_terms, second.astype(BF16))
        gate = jnp.sum(gate, axis=0, keepdims=True)

        @pl.when(k > 0)
        def _():
            gate_s[to, :, :rooms] = jnp.broadcast_to(gate, (8, rooms))
            f_copy.start(k)

        @pl.when(k == 0)
        def _():
            gate_r[to, :, :rooms] = jnp.broadcast_to(gate, (8, rooms))

        return carry

    lax.fori_loop(0, n_dp, dispatch_gates, 0)

    def hidden_units(j, g):
        active, steep = gelu_parts(nn(recv_d[g], wi[j]))
        act[j, g] = active.astype(BF16)
        slope[j, g] = steep.astype(BF16)

    n_chip, chip = n_dp // 2, dp // 2

    def chip_rows(ref, c, *lead):
        value = ref[(*lead, pl.ds(2 * c, 2))]
        return value.reshape(2 * rooms, value.shape[-1])

    def chip_store(ref, c, value, *lead):
        ref[(*lead, pl.ds(2 * c, 2))] = value.reshape(2, rooms, value.shape[-1])

    def own_hidden(k, carry):
        @pl.when(k > 0)
        def _():
            d_copy.wait_from(k)

        hidden_units(t, lax.rem(dp + n_dp - k, n_dp))
        return carry

    lax.fori_loop(0, n_dp, own_hidden, 0)
    s_second.start_all()

    @pl.when(middle)
    def _():
        wo_spread.step(1)


    @pl.when(jnp.logical_not(middle))
    def _():
        wi_spread.step(1)
        if n_t > 2:
            wi_spread.step(2)

    slot_grads = send_s
    room_lane = lax.broadcasted_iota(jnp.int32, (rooms, LANES), 1)

    def slot_grad(g, carry):
        gate = jnp.sum(jnp.where(room_lane == g, gate_c[:rooms, :], 0.0), axis=1, keepdims=True)
        slot_grads[g] = (gate * recv_s[g].astype(F32)).astype(BF16)
        return carry

    def outer_grad(i, carry):
        j = order(n_t - 1 - i // (hid // half))
        at = pl.ds(pl.multiple_of(lax.rem(i, hid // half) * half, half), half)
        left = act[j, :, :, at].reshape(slot_count, half)
        go[j, at, :] = tn(left, slot_grads[...].reshape(slot_count, width)).astype(BF16)

        @pl.when(lax.rem(i, hid // half) == hid // half - 1)
        def _():
            go_collect.begin(j)

        return carry

    def cotangent_arrives():
        gate_m[...] = jnp.zeros_like(gate_m)
        f_copy.wait_all()
        f_copy.wait_sent()
        for g in range(n_dp):
            gate_m[g : g + 1, :rooms] = gate_r[g, 0:1, :rooms]
        gate_c[...] = gate_m[...].T
        for half_copy in (s_first, s_second):
            half_copy.wait_all()
            half_copy.wait_sent()
    def other_hidden(q, carry):
        p = jnp.where(q == 0, 1, jnp.where(q == 1, n_t - 1, q))

        @pl.when(q == 1)
        def _():
            for s in range(3, n_t):
                wi_spread.step(s)

        def one(g, inner):
            hidden_units(order(p), g)
            return inner

        lax.fori_loop(0, n_dp, one, 0, unroll=2)

        @pl.when(q == min(1, n_t - 2))
        def _():
            cotangent_arrives()
            lax.fori_loop(0, n_dp, slot_grad, 0)
            lax.fori_loop(0, hid // half, outer_grad, 0)

        return carry

    lax.fori_loop(0, n_t - 1, other_hidden, 0)
    @pl.when(jnp.logical_not(middle))
    def _():
        wo_spread.step(1)

    @pl.when(middle)
    def _():
        if n_t > 2:
            wo_spread.step(2)

    lax.fori_loop(hid // half, n_t * (hid // half), outer_grad, 0)

    def hidden_grads(p):
        j = order(p)

        def one(i, inner):
            grad = nt(chip_rows(slot_grads, i), wo[j]) * chip_rows(slope, i, j).astype(F32)
            chip_store(slope, i, grad.astype(BF16), j)
            return inner

        lax.fori_loop(0, n_chip, one, 0, unroll=2)

    def inner_grads(p):
        j = order(p)

        def one(i, inner):
            at = pl.ds(pl.multiple_of(i * wide, wide), wide)
            left = recv_d[:, :, at].reshape(slot_count, wide)
            gi[j, at, :] = tn(left, slope[j].reshape(slot_count, hid)).astype(BF16)
            return inner

        lax.fori_loop(0, width // wide, one, 0)

    def split(total):
        main = total.astype(BF16)
        return main, (total - main.astype(F32)).astype(BF16)

    def some_back(g, inner):
        near_a, near_b = order(0), order(1)
        total = nn(chip_rows(act, g, near_a), wo[near_a]) + nn(chip_rows(act, g, near_b), wo[near_b])
        for j, part in zip((near_a, near_b), split(total)):
            chip_store(act, g, part, j)
        return inner

    def hidden_step(p, carry):
        @pl.when(p == 1)
        def _():
            if n_t > 2:
                go_collect.step(1, True)

        @pl.when((p == 2) & jnp.logical_not(middle))
        def _():
            if n_t > 2:
                wo_spread.step(2)

        @pl.when(p == 3)
        def _():
            for s in range(3, n_t):
                wo_spread.step(s)

        hidden_grads(p)

        @pl.when((p < n_t - 1) & jnp.logical_not(middle))
        def _():
            inner_grads(p)

        if early:

            @pl.when((p == early) & jnp.logical_not(middle))
            def _():
                lax.fori_loop(0, n_chip, some_back, 0)

        return carry

    lax.fori_loop(0, n_t, hidden_step, 0)
    d_copy.wait_sent()

    def hand_out(c, value, buffer, own, copies):
        for q in range(2):
            to = 2 * c + q
            k = lax.rem(to - dp + n_dp, n_dp)
            part = value[q * rooms : (q + 1) * rooms]

            @pl.when(k > 0)
            def _():
                buffer[to] = part
                if copies is not None:
                    copies.start(k)

            @pl.when(k == 0)
            def _():
                own[to] = part

    def give_back_grad(i, carry):
        c = lax.rem(chip + 1 + i, n_chip)
        total = nt(chip_rows(slope, c, 0), wi[0])
        for j in range(1, n_t):
            total = total + nt(chip_rows(slope, c, j), wi[j])
        hand_out(c, total.astype(BF16), send_s, back_in, b_copy)
        return carry

    lax.fori_loop(0, n_chip, give_back_grad, 0)
    for e in range(2, n_t - 1):
        go_collect.step(e, True)

    gate_c[...] = jnp.zeros_like(gate_c)

    def give_back(c, total):
        rise = jnp.sum(total * chip_rows(recv_s, c).astype(F32), axis=1, keepdims=True)
        for q in range(2):
            found = rise[q * rooms : (q + 1) * rooms]
            gate_c[:rooms, :] = jnp.where(room_lane == 2 * c + q, found, gate_c[:rooms, :])
        hand_out(c, total.astype(BF16), send_d, ret_in, None)

    def give_back_whole(c, carry):
        total = nn(chip_rows(act, c, 0), wo[0])
        for j in range(1, n_t):
            total = total + nn(chip_rows(act, c, j), wo[j])
        give_back(c, total)
        return carry

    def give_back_rest(c, carry):
        near_a, near_b = order(0), order(1)
        total = chip_rows(act, c, near_a).astype(F32) + chip_rows(act, c, near_b).astype(F32)
        for p in range(early, n_t):
            j = order(p)
            total = total + nn(chip_rows(act, c, j), wo[j])
        give_back(c, total)
        return carry

    def last_inner():
        inner_grads(n_t - 1)

        def send_inner(p, carry):
            gi_collect.begin(order(n_t - 1 - p))
            return carry

        lax.fori_loop(0, n_t, send_inner, 0)

    if early:

        @pl.when(jnp.logical_not(middle))
        def _():
            last_inner()
            lax.fori_loop(0, n_chip, give_back_rest, 0)

        @pl.when(middle)
        def _():
            lax.fori_loop(0, n_chip, give_back_whole, 0)

    else:

        @pl.when(jnp.logical_not(middle))
        def _():
            last_inner()

        lax.fori_loop(0, n_chip, give_back_whole, 0)

    gate_m[...] = gate_c[...].T
    for g in range(n_dp):
        row = jnp.broadcast_to(gate_m[g : g + 1, :], (8, long))

        @pl.when(dp == g)
        def _():
            rise_r[g] = row

        @pl.when(dp != g)
        def _():
            rise_s[g] = row

    e_copy.start_all()

    @pl.when(middle)
    def _():
        def one(p, inner):
            inner_grads(p)
            return inner

        lax.fori_loop(0, n_t, one, 0)

    lane = lax.broadcasted_iota(jnp.int32, (padded, slot_count), 1)
    both = ((lane == column(0)).astype(F32) + (lane == column(1)).astype(F32)).astype(BF16)
    unit, inverse = centre(res[...])
    b_copy.wait_sent()
    r_first.start_all()
    b_copy.wait_all()
    e_copy.wait_all()
    e_copy.wait_sent()
    room = lax.broadcasted_iota(jnp.int32, (padded, long), 1)

    slots_of = (column(0), column(1))

    found = [jnp.zeros((padded, long), F32)] * 2
    for e in range(n_dp):
        row = jnp.where(room[0:1] < rooms, rise_r[e, 0:1, :], 0.0)
        for at, slot in enumerate(slots_of):
            here = jnp.where(slot < (e + 1) * rooms, slot - e * rooms, -1)
            found[at] = jnp.where(room == here, row, found[at])
    first_grad, second_grad = (jnp.sum(one, axis=1, keepdims=True) for one in found)
    probs = probs_s[...]
    spot = lax.broadcasted_iota(jnp.int32, probs.shape, 1)
    grad_probs = jnp.where(spot == column(2), first_grad, 0.0) + jnp.where(spot == column(3), second_grad, 0.0)
    grad_logits = (probs * (grad_probs - jnp.sum(probs * grad_probs, axis=1, keepdims=True))).astype(BF16)
    grad_router = tn(moe[...], grad_logits)
    grad_moe = nn(both, back_in[...].reshape(slot_count, width)) + nt(grad_logits, weights.small())
    extra, gain_two, shift_two = norm_back(grad_moe, unit, inverse, norms[2:3])
    grad_residual = cot_full[...] + extra
    cot_full[...] = grad_residual
    grad_attended = grad_residual.astype(BF16)

    pairs = width // LANES
    if inside:
        size = len(Reduce.scratch(n_dp, n_t, 1, (shard, LANES)))
        out_sum = Reduce(n_dp, n_t, lambda p: sum_ref.at[pl.ds(OUT * shard, shard)], *take(size))
        pair_sum = Reduce(
            n_dp, n_t, lambda p: sum_ref.at[pl.ds(0, 3 * shard), pl.ds(pl.multiple_of(p * LANES, LANES), LANES)], *take(size)
        )
        small_sum = Reduce(n_dp, n_t, lambda p: sum_ref.at[pl.ds(SMALL * shard, shard), pl.ds(0, LANES)], *take(size))
        sum_ref[SMALL * shard : (SMALL + 1) * shard, LANES:] = jnp.zeros((shard, width - LANES), F32)
        out_sum.put(0, 0, tn(mix[...], grad_attended))
        out_sum.to_core(0)
    else:
        sum_ref[OUT] = tn(mix[...], grad_attended)
    dq = mix
    dq[...] = nt(grad_attended, weights(OUT)).astype(BF16)

    def heads_back(j, carry):
        at = pl.ds(pl.multiple_of(j * LANES, LANES), LANES)
        query, key, value, grad = q_s[:, at], k_s[:, at], v_s[:, at], dq[:, at]
        for mask, mask_f in ((low, low_f), (high, high_f)):
            probs = soft_scores(query * mask, key, bias[...])
            grad_probs = nt(grad * mask, value)
            grad_scores = probs * (grad_probs - jnp.sum(probs * grad_probs, axis=1, keepdims=True))
            grad_scores = grad_scores.astype(BF16)
            part_v = tn(probs.astype(BF16), grad)
            part_q = nn(grad_scores, key) * scale
            part_k = tn(grad_scores, query) * scale
            if mask is low:
                sum_q, sum_k, sum_v = part_q * mask_f, part_k * mask_f, part_v * mask_f
            else:
                sum_q, sum_k, sum_v = sum_q + part_q * mask_f, sum_k + part_k * mask_f, sum_v + part_v * mask_f
        dq[:, at] = sum_q.astype(BF16)
        dk[:, at] = sum_k.astype(BF16)
        dv[:, at] = sum_v.astype(BF16)
        @pl.when(j == pairs // 2)
        def _():
            if n_t > 2:
                gi_collect.step(1, True)

        if inside:
            for spot, ref in enumerate((dq, dk, dv)):
                pair_sum.put(j, spot * shard, tn(norm[...], ref[:, at]))
            pair_sum.to_core(j)

            @pl.when(j == 0)
            def _():
                out_sum.to_chips(0)

            @pl.when(j > 0)
            def _():
                pair_sum.to_chips(j - 1)

        return carry

    lax.fori_loop(0, pairs, heads_back, 0)
    if inside:
        pair_sum.to_chips(pairs - 1)
    else:
        for spot, ref in enumerate((dq, dk, dv)):
            sum_ref[spot] = tn(norm[...], ref[...])
    grad_normed = nt(dq[...], weights(0)) + nt(dk[...], weights(1)) + nt(dv[...], weights(2))
    full[tail:, :] = jnp.zeros((padded - tail, width), F32)
    full[:rows, :] = x_ref[...].astype(F32)
    unit, inverse = centre(full[...])
    extra, gain_one, shift_one = norm_back(grad_normed, unit, inverse, norms[0:1])
    gx_ref[...] = (cot_full[...] + extra)[:rows].astype(BF16)
    small = small_grads(experts, grad_router, (gain_one, shift_one, gain_two, shift_two))
    lane = lax.broadcasted_iota(jnp.int32, small.shape, 1)
    small = jnp.where(lane == experts + 4, over[0:1, :], small)
    def combine():
        for half_copy in (r_first, r_second):
            half_copy.wait_all()
            half_copy.wait_sent()
        returned = ret_in[...].reshape(slot_count, width)
        lane = lax.broadcasted_iota(jnp.int32, (padded, slot_count), 1)
        first, second = ((lane == column(at)).astype(F32).astype(BF16) for at in (0, 1))
        first_rows, second_rows = nn(first, returned), nn(second, returned)
        first_gate, second_gate = place[:padded, 4:5], place[:padded, 5:6]
        outcome = res[...] + first_gate * first_rows + second_gate * second_rows
        out_ref[...] = outcome[:rows].astype(BF16)

    if inside:
        small_sum.put(0, 0, small)
        small_sum.to_core(0)
        small_sum.to_chips(0)
        r_second.start_all()
        out_sum.to_line(0)

        def line(p, carry):
            pair_sum.to_line(p)
            return carry

        lax.fori_loop(0, pairs, line, 0)
        small_sum.to_line(0)
        for e in range(2, n_t - 1):
            gi_collect.step(e, True)
        go_collect.finish(g_out_ref)
        combine()
        out_sum.finish(0)

        def last(p, carry):
            pair_sum.finish(p)
            return carry

        lax.fori_loop(0, pairs, last, 0)
        small_sum.finish(0)
        gather_a.drain()
        gather_s.drain()
        gather_b.drain()
    else:
        sum_ref[SMALL] = jnp.zeros((width, width), F32)
        sum_ref[SMALL, :, :LANES] = small
        r_second.start_all()
        for e in range(2, n_t - 1):
            gi_collect.step(e, True)
        go_collect.finish(g_out_ref)
        combine()
    gi_collect.finish(g_in_ref)
    wi_spread.drain()
    wo_spread.drain()


def run_step(cfg, cid, x, cot, routes, e_in, e_out, shared):
    n_dp, n_t, rows, padded, width, experts, rooms, shard, inside, hid = cfg
    rows_block = ceil_to(5 * shard, 16)
    total = (rows_block, width) if inside else (5, width, width)
    outs = [
        jax.ShapeDtypeStruct((rows, width), BF16),
        jax.ShapeDtypeStruct((rows, width), BF16),
        jax.ShapeDtypeStruct(total, F32),
        jax.ShapeDtypeStruct((width, hid), F32),
        jax.ShapeDtypeStruct((hid, width), F32),
    ]
    spread = (n_dp, n_t, rows_block, width) if inside else (1, 1, 16, LANES)
    wide, long = ceil_to(padded, LANES), ceil_to(rooms, LANES)
    rows_f, rows_b = VMEM((padded, width), F32), VMEM((padded, width), BF16)
    slots_b, units_b = VMEM((n_dp, rooms, width), BF16), VMEM((n_t, n_dp, rooms, hid), BF16)
    in_b, out_b = (VMEM((n_t,) + shape, BF16) for shape in ((width, hid), (hid, width)))
    in_more, out_more = (VMEM((n_t + 1,) + shape, BF16) for shape in ((width, hid), (hid, width)))
    given = [x, cot, routes, *shared]
    scratch = [VMEM(one.shape, one.dtype) for one in given] + [DMA((len(given),))]
    scratch += [VMEM((rows_block, width), BF16), VMEM(spread, BF16)]
    scratch += [rows_f, rows_f, VMEM((padded, padded), F32), rows_f, VMEM((padded, LANES), F32)]
    scratch += [VMEM((wide, LANES), F32), VMEM((LANES, wide), F32), VMEM((8, LANES), F32)]
    scratch += [VMEM((LANES, long), F32), VMEM((long, LANES), F32)] + [VMEM((n_dp, 8, long), F32)] * 4
    scratch += [rows_b] * 8 + [slots_b] * 6 + [units_b] * 2
    scratch += [in_b, out_b, in_b, out_b, in_more, out_more]
    scratch += [DMA, DMA((n_dp,))] + [DMA((2,))] * 4 + [DMA] * 6 + [DMA((2,))] + Spread.scratch(n_t) * 2 + Collect.scratch(n_t) * 2
    if inside:
        scratch += Gather.scratch(n_dp, n_t) * 3 + Reduce.scratch(n_dp, n_t, 1, (shard, width))
        scratch += Reduce.scratch(n_dp, n_t, width // LANES, (3 * shard, LANES))
        scratch += Reduce.scratch(n_dp, n_t, 1, (shard, LANES))
    whole, anywhere = pl.BlockSpec(memory_space=VMEM), pl.BlockSpec(memory_space=pl.ANY)
    return pl.pallas_call(
        partial(step_kernel, cfg),
        out_shape=outs,
        in_specs=[anywhere] * (5 + len(shared)),
        out_specs=[whole] * len(outs),
        scratch_shapes=scratch,
        compiler_params=pltpu.CompilerParams(
            collective_id=cid, has_side_effects=True, vmem_limit_bytes=57 * 2**20
        ),
        name="step_" + str(rooms),
    )(x, cot, routes, e_in, e_out, *shared)


def lay_kernel(shard, experts, out_ref, gx_ref, sum_ref, in_ref, outer_ref, *outs):
    outs[0][...] = out_ref[...]
    outs[1][...] = gx_ref[...]
    for at, spot in ((0, 4), (1, 5), (2, 6), (OUT, 7)):
        outs[spot][...] = sum_ref[at * shard : (at + 1) * shard, :]
    small = sum_ref[SMALL * shard : (SMALL + 1) * shard, :LANES]
    row, column = (lax.broadcasted_iota(jnp.int32, (shard, shard), axis) for axis in (0, 1))
    for at, spot in enumerate((2, 3, 8, 9)):
        upright = small[:, experts + at : experts + at + 1]
        outs[spot][...] = jnp.sum(jnp.where(row == column, upright, 0.0), axis=0, keepdims=True)
    for at in range(experts):
        outs[10][at : at + 1, :] = jnp.sum(jnp.where(row == column, small[:, at : at + 1], 0.0), axis=0, keepdims=True)
    outs[11][...] = in_ref[...]
    outs[12][...] = outer_ref[...]


def lay_out(shard, experts, *args):
    rows, width = args[0].shape
    line = jax.ShapeDtypeStruct((1, shard), F32)
    square = jax.ShapeDtypeStruct((shard, width), F32)
    outs = [jax.ShapeDtypeStruct((rows, width), BF16)] * 2 + [line] * 2 + [square] * 4 + [line] * 2
    outs += [jax.ShapeDtypeStruct((experts, shard), F32)]
    outs += [jax.ShapeDtypeStruct(arg.shape, F32) for arg in args[3:]]

    def full(shape):
        return pl.BlockSpec(shape, lambda i: (0,) * len(shape))

    return pl.pallas_call(
        partial(lay_kernel, shard, experts),
        grid=(1,),
        out_shape=outs,
        in_specs=[full(arg.shape) for arg in args],
        out_specs=[full(out.shape) for out in outs],
        compiler_params=pltpu.CompilerParams(vmem_limit_bytes=32 * 2**20),
        name="outputs",
    )(*args)


def route_pairs(routes, t, row_count, experts, capacity):
    tok_count = routes.shape[0]
    ids = jnp.arange(experts, dtype=jnp.int32)[None, :]
    start = t * row_count
    rows = lax.dynamic_slice_in_dim(routes, start, row_count, 0)
    before = (jnp.arange(tok_count, dtype=jnp.int32) < start)[:, None]
    all_first = routes[:, 0:1] == ids
    all_second = routes[:, 1:2] == ids
    base_first = jnp.sum((all_first & before).astype(jnp.int32), axis=0)
    total_first = jnp.sum(all_first.astype(jnp.int32), axis=0)
    base_second = jnp.sum((all_second & before).astype(jnp.int32), axis=0)
    hot_first = rows[:, 0:1] == ids
    hot_second = rows[:, 1:2] == ids
    at = jnp.arange(row_count, dtype=jnp.int32)
    lower = (at[:, None] > at[None, :]).astype(BF16)
    both = jnp.concatenate([hot_first, hot_second], axis=1).astype(BF16)
    earlier = nn(lower, both).astype(jnp.int32)
    own_first = jnp.sum(hot_first.astype(jnp.int32), axis=0)
    rank_first = earlier[:, :experts]
    rank_second = earlier[:, experts:] + own_first
    place_first = rank_first + base_first
    place_second = earlier[:, experts:] + total_first + base_second
    first = jnp.sum(jnp.where(hot_first & (place_first < capacity), rank_first + 1, 0), axis=1) - 1
    second = jnp.sum(jnp.where(hot_second & (place_second < capacity), rank_second + 1, 0), axis=1) - 1
    return rows, first, second


def per_device(
    n_dp,
    n_t,
    inputs,
    cotangent,
    routes,
    gain_attn,
    shift_attn,
    query_w,
    key_w,
    value_w,
    out_w,
    gain_moe,
    shift_moe,
    router_w,
    expert_in,
    expert_out,
):
    t = lax.axis_index("tensor")
    shard, width = query_w.shape
    experts = router_w.shape[1]
    tok_count = routes.shape[0]
    rows = inputs.shape[0]
    hid = expert_in.shape[2]
    padded = ceil_to(rows, 16)
    capacity = (5 * tok_count + 2 * experts - 1) // (2 * experts)
    inside = shard % 16 == 0
    every = ("dp", "tensor")
    lines = (gain_attn, shift_attn, gain_moe, shift_moe)

    def stack():
        small = jnp.concatenate([router_w] + [line[:, None] for line in lines], axis=1)
        small = jnp.pad(small, ((0, 0), (0, width - small.shape[1])))
        return jnp.stack([query_w, key_w, value_w, small, out_w]).astype(BF16)

    if inside:
        shared = [query_w, key_w, value_w, out_w, router_w.T] + [line[None, :] for line in lines]
    else:
        shared = [lax.all_gather(stack(), every, axis=1, tiled=True)]

    def finish(results):
        summed = results[2]
        if not inside:
            summed = lax.psum_scatter(summed, every, scatter_dimension=1, tiled=True).reshape(5 * shard, width)
        outs = lay_out(shard, experts, results[0], results[1], summed, *results[3:])
        return tuple(outs)

    def slow(_):
        rooms = ceil_to(rows, 16)
        cfg = (n_dp, n_t, rows, padded, width, experts, rooms, shard, inside)
        route_rows, first_rank, second_rank = route_pairs(routes, t, rows, experts, capacity)

        def slot(choice, rank):
            return jnp.where(rank >= 0, choice * rooms + rank, -1)

        slots = jnp.stack([slot(route_rows[:, 0], first_rank), slot(route_rows[:, 1], second_rank)])
        slots = jnp.pad(slots, ((0, 0), (0, padded - rows)), constant_values=-1)
        cols = jnp.concatenate([jnp.pad(route_rows, ((0, padded - rows), (0, 0))), slots.T], axis=1)
        block = stack().reshape(5 * shard, width) if inside else shared[0]
        kept = forward(cfg, 1, inputs, cotangent, cols, slots, block)

        def turn(k):
            return [(i, (i + k) % n_t) for i in range(n_t)]

        both = jnp.stack([expert_in[0].T, expert_out[0]]).astype(BF16)
        parts = [both] + [lax.ppermute(both, "tensor", turn(k)) for k in range(1, n_t)]
        w_in, w_out = (jnp.concatenate([part[i] for part in parts], axis=0) for i in range(2))
        returned, back, grad_inner, grad_outer = run_expert(
            kept[1].reshape(n_dp * rooms, width), kept[2].reshape(n_dp * rooms, width), w_in, w_out
        )
        both = jnp.stack([grad_inner.reshape(n_t, hid, width), grad_outer.reshape(n_t, hid, width)], axis=1)
        total = both[0].astype(F32)
        for k in range(1, n_t):
            total = total + lax.ppermute(both[k], "tensor", turn(-k)).astype(F32)
        results = backward(
            cfg,
            2,
            returned.reshape(n_dp, rooms, width),
            back.reshape(n_dp, rooms, width),
            inputs,
            cotangent,
            cols,
            kept[0] if inside else block,
            *kept[3:],
        )
        return finish((*results, total[0].T, total[1]))

    rooms = min(ceil_to((7 * rows + 2 * experts - 1) // (2 * experts), 16), ceil_to(rows, 16))
    cfg = (n_dp, n_t, rows, padded, width, experts, rooms, shard, inside, hid)
    fast = run_step(cfg, 0, inputs, cotangent, routes.T, expert_in[0], expert_out[0], shared)
    if inside:
        crowded = fast[2][SMALL * shard, experts + 4] > 0.5
    else:
        crowded = lax.psum(fast[2][SMALL, 0, experts + 4], every) > 0.5
    outs = lax.cond(crowded, slow, finish, tuple(fast))
    lined = [out.reshape(shard) if at in (2, 3, 8, 9) else out for at, out in enumerate(outs)]
    lined[10], lined[11], lined[12] = lined[10].T, lined[11][None], lined[12][None]
    return tuple(lined)


def solution(mesh):
    every = ("dp", "tensor")
    rows, line = P(every, None), P(every)
    w_in, w_out = P("dp", None, "tensor"), P("dp", "tensor", None)
    return jax.shard_map(
        partial(per_device, mesh.shape["dp"], mesh.shape["tensor"]),
        mesh=mesh,
        in_specs=(rows, rows, P("dp", None), line, line, rows, rows, rows, rows, line, line, rows, w_in, w_out),
        out_specs=(rows, rows, line, line, rows, rows, rows, rows, line, line, rows, w_in, w_out),
        check_vma=False,
    )
```

```python
from functools import partial

import jax
import jax.numpy as jnp
from jax import lax
from jax.experimental import pallas as pl
from jax.experimental.pallas import tpu as pltpu
from jax.sharding import PartitionSpec as P

SEQ = 197
HEAD_DIM = 64
LANES = 128
MESH = pl.DeviceIdType.MESH
F32 = jnp.float32
BF16 = jnp.bfloat16
VMEM = pltpu.VMEM
DMA = pltpu.SemaphoreType.DMA
SMALL, OUT = 3, 4


def ceil_to(value, unit):
    return (value + unit - 1) // unit * unit


def nn(left, right):
    return lax.dot_general(left, right, (((1,), (0,)), ((), ())), preferred_element_type=F32)


def nt(left, right):
    return lax.dot_general(left, right, (((1,), (1,)), ((), ())), preferred_element_type=F32)


def tn(left, right):
    return lax.dot_general(left, right, (((0,), (0,)), ((), ())), preferred_element_type=F32)


def remote(src, dst, send, recv, device):
    return pltpu.make_async_remote_copy(
        src_ref=src, dst_ref=dst, send_sem=send, recv_sem=recv, device_id=device, device_id_type=MESH
    )


def meet(n_dp, n_t, z_too):
    dp = lax.axis_index("dp")
    t = lax.axis_index("tensor")
    bar = pltpu.get_barrier_semaphore()
    for k in range(1, n_dp):
        pl.semaphore_signal(bar, inc=1, device_id={"dp": lax.rem(dp + k, n_dp)}, device_id_type=MESH)
    if z_too:
        for k in range(1, n_t):
            pl.semaphore_signal(bar, inc=1, device_id={"tensor": lax.rem(t + k, n_t)}, device_id_type=MESH)
    pl.semaphore_wait(bar, n_dp - 1 + (n_t - 1 if z_too else 0))


class Gather:
    def __init__(self, n_dp, n_t, first, count, lanes, block, out, own_sem, z_send, z_recv, c_send, c_recv, k_send, k_recv):
        self.n_t, self.n_chip = n_t, n_dp // 2
        self.rows, self.lanes = pl.ds(first, count), pl.ds(0, lanes)
        self.block, self.out, self.own_sem = block.at[self.rows, self.lanes], out, own_sem
        self.z_sems, self.c_sems, self.k_sems = (z_send, z_recv), (c_send, c_recv), (k_send, k_recv)
        self.dp, self.t = lax.axis_index("dp"), lax.axis_index("tensor")
        self.chip, self.core = self.dp // 2, lax.rem(self.dp, 2)
        self.other = self.chip * 2 + 1 - self.core

    @staticmethod
    def scratch(n_dp, n_t):
        n_chip = n_dp // 2
        return [DMA, DMA, DMA((n_t,)), DMA, DMA((n_chip, n_t)), DMA, DMA]

    def place(self, dp, t):
        return self.out.at[dp, t, self.rows, self.lanes]

    def z_copy(self, k):
        send, recv = self.z_sems
        to = lax.rem(self.t + k, self.n_t)
        return remote(self.block, self.place(self.dp, self.t), send, recv.at[k], {"tensor": to})

    def chip_copy(self, k, j):
        send, recv = self.c_sems
        here = self.place(self.dp, lax.rem(self.t + self.n_t - j, self.n_t))
        to = lax.rem(self.chip + k, self.n_chip) * 2 + self.core
        return remote(self.block if j == 0 else here, here, send, recv.at[k, j], {"dp": to})

    def core_copy(self, k, j):
        send, recv = self.k_sems
        src = lax.rem(self.chip + self.n_chip - k, self.n_chip) * 2 + self.core
        here = self.place(src, lax.rem(self.t + self.n_t - j, self.n_t))
        own = k == 0 and j == 0
        return remote(self.block if own else here, here, send, recv, {"dp": self.other})

    def own_copy(self):
        return pltpu.make_async_copy(self.block, self.place(self.dp, self.t), self.own_sem)

    def start(self):
        for k in range(1, self.n_t):
            self.z_copy(k).start()
        self.own_copy().start()
        for k in range(1, self.n_chip):
            self.chip_copy(k, 0).start()
        self.core_copy(0, 0).start()

    def pass_to_chips(self):
        for j in range(1, self.n_t):
            self.z_copy(j).wait_recv()
            for k in range(1, self.n_chip):
                self.chip_copy(k, j).start()
            self.core_copy(0, j).start()

    def pass_to_core(self):
        for j in range(self.n_t):
            for k in range(1, self.n_chip):
                self.chip_copy(k, j).wait_recv()
                self.core_copy(k, j).start()

    def arrive(self):
        self.own_copy().wait()
        self.wait_bytes(self.out.at[pl.ds(0, self.n_chip), :, self.rows, self.lanes], self.k_sems[1])

    @staticmethod
    def wait_bytes(part, sem):
        pltpu.make_async_copy(part, part, sem).wait()

    def drain(self):
        self.wait_bytes(self.out.at[0, pl.ds(0, self.n_t - 1), self.rows, self.lanes], self.z_sems[0])
        self.wait_bytes(self.out.at[pl.ds(0, self.n_chip - 1), :, self.rows, self.lanes], self.c_sems[0])
        self.wait_bytes(self.out.at[pl.ds(0, self.n_chip), :, self.rows, self.lanes], self.k_sems[0])


class Scatter:
    def __init__(
        self, n_dp, n_t, grads, out, core_in, half, chip_in, part, z_in, k_send, k_recv, c_send, c_recv, z_send, z_recv
    ):
        self.n_t, self.n_chip = n_t, n_dp // 2
        self.grads, self.out = grads, out
        self.core_in, self.half, self.chip_in, self.part, self.z_in = core_in, half, chip_in, part, z_in
        self.k_sems, self.c_sems, self.z_sems = (k_send, k_recv), (c_send, c_recv), (z_send, z_recv)
        self.dp, self.t = lax.axis_index("dp"), lax.axis_index("tensor")
        self.chip, self.core = self.dp // 2, lax.rem(self.dp, 2)
        self.other = self.chip * 2 + 1 - self.core

    @staticmethod
    def scratch(n_dp, n_t, block):
        n_chip = n_dp // 2
        buffers = [VMEM((n_chip, n_t) + block, BF16)] + [VMEM((n_chip - 1, n_t) + block, BF16)] * 2
        buffers += [VMEM((n_t - 1,) + block, BF16)] * 2
        return buffers + [DMA((n_chip,))] * 4 + [DMA((n_t,))] * 2

    def core_copy(self, k):
        to = lax.rem(self.chip + k, self.n_chip)
        src = self.grads.at[to * 2 + 1 - self.core]
        return remote(src, self.core_in.at[k], self.k_sems[0].at[k], self.k_sems[1].at[k], {"dp": self.other})

    def chip_copy(self, k):
        to = lax.rem(self.chip + k, self.n_chip) * 2 + self.core
        return remote(self.half.at[k - 1], self.chip_in.at[k - 1], self.c_sems[0].at[k], self.c_sems[1].at[k], {"dp": to})

    def z_copy(self, k):
        to = lax.rem(self.t + k, self.n_t)
        return remote(self.part.at[k - 1], self.z_in.at[k - 1], self.z_sems[0].at[k], self.z_sems[1].at[k], {"tensor": to})

    def run(self, between=None, after=None):
        n_chip, n_t = self.n_chip, self.n_t
        order = list(range(1, n_chip)) + [0]
        for k in order:
            self.core_copy(k).start()
        for k in order:
            self.core_copy(k).wait_recv()
            if k > 0:
                to = lax.rem(self.chip + k, n_chip) * 2 + self.core
                self.half[k - 1] = (self.grads[to].astype(F32) + self.core_in[k].astype(F32)).astype(BF16)
                self.chip_copy(k).start()
        if between is not None:
            between()
        for k in range(1, n_chip):
            self.chip_copy(k).wait_recv()
        for k in list(range(1, n_t)) + [0]:
            row = lax.rem(self.t + k, n_t)
            total = self.grads[self.dp, row].astype(F32) + self.core_in[0, row].astype(F32)
            for c in range(1, n_chip):
                total = total + self.chip_in[c - 1, row].astype(F32)
            if k > 0:
                self.part[k - 1] = total.astype(BF16)
                self.z_copy(k).start()
            else:
                self.out[...] = total
        if after is not None:
            after()
        for k in range(1, n_t):
            self.z_copy(k).wait_recv()
            self.out[...] += self.z_in[k - 1].astype(F32)
        for k in range(n_chip):
            self.core_copy(k).wait_send()
        for k in range(1, n_chip):
            self.chip_copy(k).wait_send()
        for k in range(1, n_t):
            self.z_copy(k).wait_send()


class Reduce:
    def __init__(self, n_dp, n_t, out, grads, core_in, half, chip_in, part, z_in, *sems):
        self.n_t, self.n_chip, self.out = n_t, n_dp // 2, out
        self.grads, self.core_in, self.half = grads, core_in, half
        self.chip_in, self.part, self.z_in = chip_in, part, z_in
        self.k_sems, self.c_sems, self.z_sems = sems[0:3], sems[3:5], sems[5:7]
        self.dp, self.t = lax.axis_index("dp"), lax.axis_index("tensor")
        self.chip, self.core = self.dp // 2, lax.rem(self.dp, 2)
        self.other = self.chip * 2 + 1 - self.core

    @staticmethod
    def scratch(n_dp, n_t, parts, block):
        n_chip = n_dp // 2
        sizes = [(n_dp, n_t), (n_chip, n_t), (n_chip - 1, n_t), (n_chip - 1, n_t), (n_t - 1,), (n_t - 1,)]
        return [VMEM((parts,) + size + block, BF16) for size in sizes] + [DMA((parts,))] * 7

    def put(self, p, first, value):
        n_dp, n_t = self.n_chip * 2, self.n_t
        count, lanes = value.shape[0] // (n_dp * n_t), value.shape[1]
        self.grads[p, :, :, first : first + count, :] = value.astype(BF16).reshape(n_dp, n_t, count, lanes)

    def core_copy(self, p, k):
        src = self.grads.at[p, lax.rem(self.chip + k, self.n_chip) * 2 + 1 - self.core]
        send, far, near = self.k_sems
        recv = near if isinstance(k, int) and k == 0 else far
        return remote(src, self.core_in.at[p, k], send.at[p], recv.at[p], {"dp": self.other})

    def chip_copy(self, p, k):
        to = lax.rem(self.chip + k, self.n_chip) * 2 + self.core
        send, recv = self.c_sems
        return remote(self.half.at[p, k - 1], self.chip_in.at[p, k - 1], send.at[p], recv.at[p], {"dp": to})

    def z_copy(self, p, k):
        to = lax.rem(self.t + k, self.n_t)
        send, recv = self.z_sems
        return remote(self.part.at[p, k - 1], self.z_in.at[p, k - 1], send.at[p], recv.at[p], {"tensor": to})

    def to_core(self, p):
        for k in list(range(1, self.n_chip)) + [0]:
            self.core_copy(p, k).start()

    def to_chips(self, p):
        Gather.wait_bytes(self.core_in.at[p, pl.ds(1, self.n_chip - 1)], self.k_sems[1].at[p])
        for k in range(1, self.n_chip):
            to = lax.rem(self.chip + k, self.n_chip) * 2 + self.core
            self.half[p, k - 1] = (self.grads[p, to].astype(F32) + self.core_in[p, k].astype(F32)).astype(BF16)
            self.chip_copy(p, k).start()

    def to_line(self, p):
        self.core_copy(p, 0).wait_recv()
        Gather.wait_bytes(self.chip_in.at[p], self.c_sems[1].at[p])
        for k in list(range(1, self.n_t)) + [0]:
            row = lax.rem(self.t + k, self.n_t)
            total = self.grads[p, self.dp, row].astype(F32) + self.core_in[p, 0, row].astype(F32)
            for c in range(1, self.n_chip):
                total = total + self.chip_in[p, c - 1, row].astype(F32)
            if k > 0:
                self.part[p, k - 1] = total.astype(BF16)
                self.z_copy(p, k).start()
            else:
                self.out(p)[...] = total

    def finish(self, p):
        Gather.wait_bytes(self.z_in.at[p], self.z_sems[1].at[p])
        for k in range(1, self.n_t):
            self.out(p)[...] += self.z_in[p, k - 1].astype(F32)
        Gather.wait_bytes(self.part.at[p], self.z_sems[0].at[p])
        Gather.wait_bytes(self.core_in.at[p], self.k_sems[0].at[p])
        Gather.wait_bytes(self.half.at[p], self.c_sems[0].at[p])


def greet(n_dp, n_t):
    dp, t = lax.axis_index("dp"), lax.axis_index("tensor")
    bar = pltpu.get_barrier_semaphore()
    for k in range(1, n_dp):
        pl.semaphore_signal(bar, inc=1, device_id={"dp": lax.rem(dp + k, n_dp)}, device_id_type=MESH)
    for k in range(1, n_t):
        pl.semaphore_signal(bar, inc=1, device_id={"tensor": lax.rem(t + k, n_t)}, device_id_type=MESH)


def greeted(n_dp, n_t):
    pl.semaphore_wait(pltpu.get_barrier_semaphore(), n_dp - 1 + n_t - 1)


class Exchange:
    def __init__(self, n_dp, src, dst, rows, send, recv, single):
        self.n_dp, self.src, self.dst, self.rows, self.send, self.recv = n_dp, src, dst, rows, send, recv
        self.dp, self.single = lax.axis_index("dp"), single

    def copy(self, k):
        to = lax.rem(self.dp + k, self.n_dp)
        recv = self.recv.at[k] if self.single else self.recv
        return remote(self.src.at[to, self.rows], self.dst.at[self.dp, self.rows], self.send, recv, {"dp": to})

    def start(self, k):
        self.copy(k).start()

    def start_all(self):
        for k in range(1, self.n_dp):
            self.start(k)

    def wait_from(self, k):
        self.copy(k).wait_recv()

    def wait_all(self):
        part = self.dst.at[pl.ds(0, self.n_dp - 1), self.rows]
        pltpu.make_async_copy(part, part, self.recv).wait()

    def wait_sent(self):
        part = self.src.at[pl.ds(0, self.n_dp - 1), self.rows]
        pltpu.make_async_copy(part, part, self.send).wait()


class Spread:
    def __init__(self, n_t, parts, send, recv):
        self.n_t, self.t, self.parts, self.send, self.recv = n_t, lax.axis_index("tensor"), parts, send, recv

    @staticmethod
    def scratch(n_t):
        return [DMA((2, n_t)), DMA((n_t,))]

    def hop(self, j, way):
        here = self.parts.at[j]
        return remote(here, here, self.send.at[way, j], self.recv.at[j], {"tensor": self.t + 1 - 2 * way})

    def step(self, s):
        for way, j, in_line, onward in (
            (0, self.t - s, self.t - s >= 0, self.t + 1 < self.n_t),
            (1, self.t + s, self.t + s < self.n_t, self.t > 0),
        ):
            if s > 0:

                @pl.when(in_line)
                def _():
                    self.hop(j, way).wait_recv()

            @pl.when(in_line & onward)
            def _():
                self.hop(j, way).start()

    def drain(self):
        for s in range(self.n_t):

            @pl.when((self.t - s >= 0) & (self.t + 1 < self.n_t))
            def _():
                self.hop(self.t - s, 0).wait_send()

            @pl.when((self.t + s < self.n_t) & (self.t > 0))
            def _():
                self.hop(self.t + s, 1).wait_send()


class Collect:
    def __init__(self, n_t, parts, came, send, recv):
        self.n_t, self.t, self.parts, self.came, self.send, self.recv = (
            n_t,
            lax.axis_index("tensor"),
            parts,
            came,
            send,
            recv,
        )

    @staticmethod
    def scratch(n_t):
        return [DMA((n_t,)), DMA((n_t + 1,))]

    def hop(self, j, way):
        slot = j if way == 0 else jnp.where(j == self.t - 1, self.n_t, j)
        to = self.t + 1 - 2 * way
        return remote(self.parts.at[j], self.came.at[slot], self.send.at[j], self.recv.at[slot], {"tensor": to})

    def wait_slot(self, slot):
        remote(self.parts.at[0], self.came.at[slot], self.send.at[0], self.recv.at[slot], {"tensor": self.t}).wait_recv()

    def begin(self, j):
        @pl.when((self.t == 0) & (j > 0))
        def _():
            self.hop(j, 0).start()

        @pl.when((self.t == self.n_t - 1) & (j < self.n_t - 1))
        def _():
            self.hop(j, 1).start()

    def step(self, e, far):
        if far:
            right, left = self.n_t - 1 - e + self.t, e - self.n_t + 1 + self.t
        else:
            right, left = e - self.t + 2, 2 * self.n_t - 4 - e - self.t
        for way, j, mine in (
            (0, right, (self.t >= 1) & (right <= self.n_t - 1) & (right > self.t)),
            (1, left, (self.t <= self.n_t - 2) & (left >= 0) & (left < self.t)),
        ):

            @pl.when(mine)
            def _():
                self.wait_slot(j)
                self.parts[j] = (self.parts[j].astype(F32) + self.came[j].astype(F32)).astype(BF16)
                self.hop(j, way).start()

    def finish(self, result):
        result[...] = self.parts[self.t].astype(F32)

        @pl.when(self.t > 0)
        def _():
            self.wait_slot(self.t)
            result[...] += self.came[self.t].astype(F32)

        @pl.when(self.t < self.n_t - 1)
        def _():
            self.wait_slot(self.n_t)
            result[...] += self.came[self.n_t].astype(F32)

        for j in range(self.n_t):

            @pl.when(self.t < j)
            def _():
                self.hop(j, 0).wait_send()

            @pl.when(self.t > j)
            def _():
                self.hop(j, 1).wait_send()


def centre(values):
    centred = values - jnp.mean(values, axis=1, keepdims=True)
    inverse = lax.rsqrt(jnp.mean(centred * centred, axis=1, keepdims=True) + 1e-06)
    return centred * inverse, inverse


def norm_back(grad, unit, inverse, gain):
    scaled = grad * gain
    back = inverse * (
        scaled
        - jnp.mean(scaled, axis=1, keepdims=True)
        - unit * jnp.mean(scaled * unit, axis=1, keepdims=True)
    )
    return back, jnp.sum(grad * unit, axis=0, keepdims=True), jnp.sum(grad, axis=0, keepdims=True)


def norm_picks(experts):
    row, lane = (lax.broadcasted_iota(jnp.int32, (8, LANES), axis) for axis in (0, 1))
    return (row + experts == lane).astype(F32).astype(BF16)


def norm_rows(small, experts):
    return nt(norm_picks(experts), small)


def small_grads(experts, grad_router, rows):
    line = lax.broadcasted_iota(jnp.int32, (8, rows[0].shape[1]), 0)
    stack = sum(jnp.where(line == at, row, 0.0) for at, row in enumerate(rows))
    return grad_router + tn(stack.astype(BF16), norm_picks(experts))


def image_bias(rows, padded):
    line = lax.broadcasted_iota(jnp.int32, (padded, padded), 0)
    column = lax.broadcasted_iota(jnp.int32, (padded, padded), 1)
    image_line, image_column = jnp.zeros_like(line), jnp.zeros_like(column)
    for at in range(SEQ, rows + 1, SEQ):
        image_line += (line >= at).astype(jnp.int32)
        image_column += (column >= at).astype(jnp.int32)
    return jnp.where((image_line == image_column) & (column < rows), 0.0, -1e30)


def half_masks():
    lane = lax.broadcasted_iota(jnp.int32, (1, LANES), 1)
    low = (lane < HEAD_DIM).astype(F32)
    return low.astype(BF16), (1.0 - low).astype(BF16)


def soft_scores(query, key, bias):
    scores = nt(query, key) * HEAD_DIM ** (-0.5) + bias
    power = jnp.exp(scores - jnp.max(scores, axis=1, keepdims=True))
    return power * (1.0 / jnp.sum(power, axis=1, keepdims=True))


def router_probs(logits, experts):
    lane = lax.broadcasted_iota(jnp.int32, logits.shape, 1)
    inside = lane < experts
    kept = jnp.where(inside, logits, -1e30)
    power = jnp.where(inside, jnp.exp(kept - jnp.max(kept, axis=1, keepdims=True)), 0.0)
    return power * (1.0 / jnp.sum(power, axis=1, keepdims=True))


def pick_gate(probs, choice):
    lane = lax.broadcasted_iota(jnp.int32, probs.shape, 1)
    return jnp.sum(jnp.where(lane == choice, probs, 0.0), axis=1, keepdims=True)


class Weights:
    def __init__(self, shard, width, gathered=None, whole=None):
        self.shard, self.width, self.gathered, self.whole = shard, width, gathered, whole

    def __call__(self, at):
        if self.whole is not None:
            return self.whole[at]
        part = self.gathered[:, :, at * self.shard : (at + 1) * self.shard, :]
        return part.reshape(self.width, self.width)

    def small(self):
        if self.whole is not None:
            return self.whole[SMALL, :, :LANES]
        part = self.gathered[:, :, SMALL * self.shard : (SMALL + 1) * self.shard, :LANES]
        return part.reshape(self.width, LANES)


def gelu_parts(hidden):
    bell = jnp.exp(-0.5 * hidden * hidden)
    near = 1.0 / (1.0 + 0.23164189 * jnp.abs(hidden))
    tail = near * (
        0.127414796 + near * (-0.142248368 + near * (0.7107068705 + near * (-0.7265760135 + near * 0.5307027145)))
    )
    tail = tail * bell
    share = jnp.where(hidden < 0.0, tail, 1.0 - tail)
    return hidden * share, share + hidden * bell * 0.3989422804014327


def forward_kernel(cfg, *refs):
    n_dp, n_t, rows, padded, width, experts, rooms, shard, inside = cfg
    refs = list(refs)

    def take(count):
        got = refs[:count]
        del refs[:count]
        return got

    x_ref, cot_ref, cols_ref, slots_ref, block_ref = take(5)
    gathered, recv_d, recv_s, res_ref, moe_ref, q_ref, k_ref, v_ref, mix_ref, norm_ref, probs_ref = take(11)
    full, cot_full, bias, send_d, send_s, d_send, d_recv, s_send, s_recv = take(9)
    dp = lax.axis_index("dp")
    meet(n_dp, n_t, inside)
    if inside:
        gather = Gather(n_dp, n_t, 0, block_ref.shape[0], width, block_ref, gathered, *refs)
        gather.start()
        weights = Weights(shard, width, gathered=gathered)
    else:
        gathered[...] = jnp.zeros_like(gathered)
        weights = Weights(shard, width, whole=block_ref)

    full[rows - rows % 8 :, :] = jnp.zeros((padded - rows + rows % 8, width), F32)
    full[:rows, :] = x_ref[...].astype(F32)
    cot_full[rows - rows % 8 :, :] = jnp.zeros((padded - rows + rows % 8, width), F32)
    cot_full[:rows, :] = cot_ref[...].astype(F32)
    bias[...] = image_bias(rows, padded)
    unit, _ = centre(full[...])
    norm_ref[...] = unit.astype(BF16)
    if inside:
        gather.pass_to_chips()
        gather.pass_to_core()
        gather.arrive()
        gather.drain()

    norms = norm_rows(weights.small(), experts)
    unit, _ = centre(full[...])
    normed = (unit * norms[0:1] + norms[1:2]).astype(BF16)
    norm_ref[...] = normed
    q_ref[...] = nn(normed, weights(0)).astype(BF16)
    k_ref[...] = nn(normed, weights(1)).astype(BF16)
    v_ref[...] = nn(normed, weights(2)).astype(BF16)
    low, high = half_masks()

    def heads(j, carry):
        at = pl.ds(pl.multiple_of(j * LANES, LANES), LANES)
        query, key, value = q_ref[:, at], k_ref[:, at], v_ref[:, at]
        first = nn(soft_scores(query * low, key, bias[...]).astype(BF16), value)
        second = nn(soft_scores(query * high, key, bias[...]).astype(BF16), value)
        mix_ref[:, at] = (first * low.astype(F32) + second * high.astype(F32)).astype(BF16)
        return carry

    lax.fori_loop(0, width // LANES, heads, 0)
    residual = full[...] + nn(mix_ref[...], weights(OUT))
    res_ref[...] = residual
    unit, _ = centre(residual)
    moe = (unit * norms[2:3] + norms[3:4]).astype(BF16)
    moe_ref[...] = moe
    probs = router_probs(nn(moe, weights.small()), experts)
    probs_ref[...] = probs
    cot = cot_full[...]
    full[...] = pick_gate(probs, cols_ref[:, 0:1]) * cot
    cot_full[...] = pick_gate(probs, cols_ref[:, 1:2]) * cot

    def selectors(p):
        slot = lax.broadcasted_iota(jnp.int32, (rooms, padded), 0) + p * rooms
        first = (slot == slots_ref[0:1, :]).astype(F32)
        second = (slot == slots_ref[1:2, :]).astype(F32)
        return first, second

    def d_copy(k):
        to = lax.rem(dp + k, n_dp)
        return remote(send_d.at[to], recv_d.at[dp], d_send.at[k], d_recv.at[k], {"dp": to})

    def s_copy(k):
        to = lax.rem(dp + k, n_dp)
        return remote(send_s.at[to], recv_s.at[dp], s_send.at[k], s_recv.at[k], {"dp": to})

    def dispatch(k, carry):
        to = lax.rem(dp + k, n_dp)
        first, second = selectors(to)
        send_d[to] = nn((first + second).astype(BF16), moe_ref[...]).astype(BF16)

        @pl.when(k > 0)
        def _():
            d_copy(k).start()

        return carry

    def dispatch_grad(k, carry):
        to = lax.rem(dp + k, n_dp)
        first, second = selectors(to)
        rows_grad = nn(first.astype(BF16), full[...].astype(BF16)) + nn(second.astype(BF16), cot_full[...].astype(BF16))
        send_s[to] = rows_grad.astype(BF16)

        @pl.when(k > 0)
        def _():
            s_copy(k).start()

        return carry

    lax.fori_loop(0, n_dp, dispatch, 0)
    lax.fori_loop(0, n_dp, dispatch_grad, 0)
    recv_d[dp] = send_d[dp]
    recv_s[dp] = send_s[dp]
    for k in range(1, n_dp):
        d_copy(k).wait()
    for k in range(1, n_dp):
        s_copy(k).wait()


def forward(cfg, cid, x, cot, cols, slots, block):
    n_dp, n_t, rows, padded, width, experts, rooms, shard, inside = cfg
    rows_block = ceil_to(5 * shard, 16)
    low = jax.ShapeDtypeStruct((padded, width), BF16)
    sent = jax.ShapeDtypeStruct((n_dp, rooms, width), BF16)
    gathered = (n_dp, n_t, rows_block, width) if inside else (1, 1, 16, LANES)
    outs = [jax.ShapeDtypeStruct(gathered, BF16), sent, sent, jax.ShapeDtypeStruct((padded, width), F32)]
    outs += [low] * 6 + [jax.ShapeDtypeStruct((padded, LANES), F32)]
    scratch = [
        VMEM((padded, width), F32),
        VMEM((padded, width), F32),
        VMEM((padded, padded), F32),
        VMEM((n_dp, rooms, width), BF16),
        VMEM((n_dp, rooms, width), BF16),
    ] + [DMA((n_dp,))] * 4
    if inside:
        scratch += Gather.scratch(n_dp, n_t)
    whole = pl.BlockSpec(memory_space=VMEM)
    return pl.pallas_call(
        partial(forward_kernel, cfg),
        out_shape=outs,
        in_specs=[whole] * 5,
        out_specs=[whole] * len(outs),
        scratch_shapes=scratch,
        compiler_params=pltpu.CompilerParams(
            collective_id=cid, has_side_effects=True, vmem_limit_bytes=56 * 2**20
        ),
        name="forward_" + str(rooms),
    )(x, cot, cols, slots, block)


def expert_kernel(chunks, d_ref, s_ref, w_in_ref, w_out_ref, ret_ref, back_ref, g_in_ref, g_out_ref, ret, back, g_in, g_out):
    step = pl.program_id(0)
    rows = d_ref.shape[0]
    chunk = rows // chunks

    @pl.when(step == 0)
    def _():
        ret[...] = jnp.zeros_like(ret)
        back[...] = jnp.zeros_like(back)

    g_in[...] = jnp.zeros_like(g_in)
    g_out[...] = jnp.zeros_like(g_out)
    w_in, w_out = w_in_ref[...], w_out_ref[...]

    def part(c, carry):
        at = pl.ds(pl.multiple_of(c * chunk, 16), chunk)
        took, slot_grad = d_ref[at, :], s_ref[at, :]
        active, slope = gelu_parts(nt(took, w_in))
        active = active.astype(BF16)
        grad_hidden = (nt(slot_grad, w_out) * slope).astype(BF16)
        ret[at, :] += nn(active, w_out)
        back[at, :] += nn(grad_hidden, w_in)
        g_out[...] += tn(active, slot_grad)
        g_in[...] += tn(grad_hidden, took)
        return carry

    lax.fori_loop(0, chunks, part, 0)
    g_in_ref[...] = g_in[...].astype(BF16)
    g_out_ref[...] = g_out[...].astype(BF16)

    @pl.when(step == pl.num_programs(0) - 1)
    def _():
        ret_ref[...] = ret[...].astype(BF16)
        back_ref[...] = back[...].astype(BF16)


def run_expert(took, slot_grad, w_in, w_out):
    rows, width = took.shape
    hidden = w_in.shape[0]
    block = 256
    chunks = next(c for c in range(max(1, rows // 400), rows + 1) if rows % c == 0 and (rows // c) % 16 == 0)
    whole = pl.BlockSpec((rows, width), lambda i: (0, 0))
    part = pl.BlockSpec((block, width), lambda i: (i, 0))
    low = jax.ShapeDtypeStruct((rows, width), BF16)
    grad = jax.ShapeDtypeStruct((hidden, width), BF16)
    return pl.pallas_call(
        partial(expert_kernel, chunks),
        grid=(hidden // block,),
        out_shape=[low, low, grad, grad],
        in_specs=[whole, whole, part, part],
        out_specs=[whole, whole, part, part],
        scratch_shapes=[
            VMEM((rows, width), F32),
            VMEM((rows, width), F32),
            VMEM((block, width), F32),
            VMEM((block, width), F32),
        ],
        compiler_params=pltpu.CompilerParams(vmem_limit_bytes=60 * 2**20),
        cost_estimate=pl.CostEstimate(
            flops=12 * rows * width * hidden, bytes_accessed=12 * rows * width + 8 * hidden * width, transcendentals=0
        ),
        name="expert_" + str(rows),
    )(took, slot_grad, w_in, w_out)


def backward_kernel(cfg, *refs):
    n_dp, n_t, rows, padded, width, experts, rooms, shard, inside = cfg
    refs = list(refs)

    def take(count):
        got = refs[:count]
        del refs[:count]
        return got

    ret_ref, back_ref, x_ref, cot_ref, cols_ref, weights_ref = take(6)
    res_ref, moe_ref, q_ref, k_ref, v_ref, mix_ref, norm_ref, probs_ref = take(8)
    out_ref, gx_ref, sum_ref = take(3)
    full, cot_full, bias, ret_in, back_in, grads, r_send, r_recv, b_send, b_recv = take(10)
    dq, dk, dv = take(3)
    dp = lax.axis_index("dp")
    meet(n_dp, n_t, inside)

    def r_copy(k):
        to = lax.rem(dp + k, n_dp)
        return remote(ret_ref.at[to], ret_in.at[dp], r_send.at[k], r_recv.at[k], {"dp": to})

    def b_copy(k):
        to = lax.rem(dp + k, n_dp)
        return remote(back_ref.at[to], back_in.at[dp], b_send.at[k], b_recv.at[k], {"dp": to})

    for k in range(1, n_dp):
        r_copy(k).start()
    for k in range(1, n_dp):
        b_copy(k).start()
    ret_in[dp] = ret_ref[dp]
    back_in[dp] = back_ref[dp]
    weights = Weights(shard, width, gathered=weights_ref) if inside else Weights(shard, width, whole=weights_ref)
    tail = rows - rows % 8
    full[tail:, :] = jnp.zeros((padded - tail, width), F32)
    full[:rows, :] = x_ref[...].astype(F32)
    cot_full[tail:, :] = jnp.zeros((padded - tail, width), F32)
    cot_full[:rows, :] = cot_ref[...].astype(F32)
    bias[...] = image_bias(rows, padded)
    norms = norm_rows(weights.small(), experts)

    def selectors(e):
        lane = lax.broadcasted_iota(jnp.int32, (padded, rooms), 1) + e * rooms
        return (lane == cols_ref[:, 2:3]).astype(F32), (lane == cols_ref[:, 3:4]).astype(F32)

    for k in range(1, n_dp):
        r_copy(k).wait()

    def pick(e, carry):
        return tuple(rows + nn(one.astype(BF16), ret_in[e]) for rows, one in zip(carry, selectors(e)))

    zero = jnp.zeros((padded, width), F32)
    first_rows, second_rows = lax.fori_loop(0, n_dp, pick, (zero, zero))
    probs = probs_ref[...]
    first_id, second_id = cols_ref[:, 0:1], cols_ref[:, 1:2]
    outcome = res_ref[...] + pick_gate(probs, first_id) * first_rows + pick_gate(probs, second_id) * second_rows
    out_ref[...] = outcome[:rows].astype(BF16)
    cot = cot_full[...]
    first_grad = jnp.sum(first_rows * cot, axis=1, keepdims=True)
    second_grad = jnp.sum(second_rows * cot, axis=1, keepdims=True)
    spot = lax.broadcasted_iota(jnp.int32, probs.shape, 1)
    grad_probs = jnp.where(spot == first_id, first_grad, 0.0) + jnp.where(spot == second_id, second_grad, 0.0)
    grad_logits = (probs * (grad_probs - jnp.sum(probs * grad_probs, axis=1, keepdims=True))).astype(BF16)
    grad_router = tn(moe_ref[...], grad_logits)

    for k in range(1, n_dp):
        b_copy(k).wait()

    def pick_both(e, rows):
        first, second = selectors(e)
        return rows + nn((first + second).astype(BF16), back_in[e])

    grad_moe = lax.fori_loop(0, n_dp, pick_both, nt(grad_logits, weights.small()))
    unit, inverse = centre(res_ref[...])
    extra, gain_two, shift_two = norm_back(grad_moe, unit, inverse, norms[2:3])
    grad_residual = cot + extra
    cot_full[...] = grad_residual
    grad_attended = grad_residual.astype(BF16)
    n_all = n_dp * n_t

    def keep(at, value):
        if inside:
            grads[:, :, at * shard : (at + 1) * shard, :] = value.astype(BF16).reshape(n_dp, n_t, shard, width)
        else:
            sum_ref[at] = value

    keep(OUT, tn(mix_ref[...], grad_attended))
    mix_ref_grad = nt(grad_attended, weights(OUT)).astype(BF16)
    dq[...] = mix_ref_grad
    low, high = half_masks()
    low_f, high_f = low.astype(F32), high.astype(F32)
    scale = HEAD_DIM ** (-0.5)

    def heads(j, carry):
        at = pl.ds(pl.multiple_of(j * LANES, LANES), LANES)
        query, key, value, grad = q_ref[:, at], k_ref[:, at], v_ref[:, at], dq[:, at]
        for mask, mask_f in ((low, low_f), (high, high_f)):
            probs = soft_scores(query * mask, key, bias[...])
            grad_probs = nt(grad * mask, value)
            grad_scores = probs * (grad_probs - jnp.sum(probs * grad_probs, axis=1, keepdims=True))
            grad_scores = grad_scores.astype(BF16)
            part_v = tn(probs.astype(BF16), grad)
            part_q = nn(grad_scores, key) * scale
            part_k = tn(grad_scores, query) * scale
            if mask is low:
                sum_q, sum_k, sum_v = part_q * mask_f, part_k * mask_f, part_v * mask_f
            else:
                sum_q, sum_k, sum_v = sum_q + part_q * mask_f, sum_k + part_k * mask_f, sum_v + part_v * mask_f
        dq[:, at] = sum_q.astype(BF16)
        dk[:, at] = sum_k.astype(BF16)
        dv[:, at] = sum_v.astype(BF16)
        return carry

    lax.fori_loop(0, width // LANES, heads, 0)
    keep(0, tn(norm_ref[...], dq[...]))
    keep(1, tn(norm_ref[...], dk[...]))
    keep(2, tn(norm_ref[...], dv[...]))
    grad_normed = nt(dq[...], weights(0)) + nt(dk[...], weights(1)) + nt(dv[...], weights(2))
    unit, inverse = centre(full[...])
    extra, gain_one, shift_one = norm_back(grad_normed, unit, inverse, norms[0:1])
    gx_ref[...] = (cot_full[...] + extra)[:rows].astype(BF16)
    small = small_grads(experts, grad_router, (gain_one, shift_one, gain_two, shift_two))
    if inside:
        at = slice(SMALL * shard, (SMALL + 1) * shard)
        grads[:, :, at, :LANES] = small.astype(BF16).reshape(n_dp, n_t, shard, LANES)
        grads[:, :, at, LANES:] = jnp.zeros((n_dp, n_t, shard, width - LANES), BF16)
        Scatter(n_dp, n_t, grads, sum_ref, *refs).run()
    else:
        sum_ref[SMALL] = jnp.zeros((width, width), F32)
        sum_ref[SMALL, :, :LANES] = small


def backward(cfg, cid, *args):
    n_dp, n_t, rows, padded, width, experts, rooms, shard, inside = cfg
    rows_block = ceil_to(5 * shard, 16)
    total = (rows_block, width) if inside else (5, width, width)
    outs = [jax.ShapeDtypeStruct((rows, width), BF16)] * 2 + [jax.ShapeDtypeStruct(total, F32)]
    scratch = [
        VMEM((padded, width), F32),
        VMEM((padded, width), F32),
        VMEM((padded, padded), F32),
        VMEM((n_dp, rooms, width), BF16),
        VMEM((n_dp, rooms, width), BF16),
        VMEM((n_dp, n_t, rows_block, width) if inside else (1, 1, 16, LANES), BF16),
    ]
    scratch += [DMA((n_dp,))] * 4 + [VMEM((padded, width), BF16)] * 3
    if inside:
        scratch += Scatter.scratch(n_dp, n_t, (rows_block, width))
    whole = pl.BlockSpec(memory_space=VMEM)
    return pl.pallas_call(
        partial(backward_kernel, cfg),
        out_shape=outs,
        in_specs=[whole] * len(args),
        out_specs=[whole] * len(outs),
        scratch_shapes=scratch,
        compiler_params=pltpu.CompilerParams(
            collective_id=cid, has_side_effects=True, vmem_limit_bytes=56 * 2**20
        ),
        name="backward_" + str(rooms),
    )(*args)


def image_blocks(rows):
    blocks = []
    for first in range(0, rows, SEQ):
        start = first // 16 * 16
        blocks.append((start, ceil_to(first - start + SEQ, 16), first - start))
    return blocks


def inside_image(size, first, axis):
    shape = (size, 1) if axis == 0 else (1, size)
    spot = lax.broadcasted_iota(jnp.int32, shape, axis)
    return (spot >= first) & (spot < first + SEQ)


def image_probs(query, key, size, first):
    scores = nt(query, key) * HEAD_DIM ** (-0.5) + jnp.where(inside_image(size, first, 1), 0.0, -1e30)
    power = jnp.exp(scores - jnp.max(scores, axis=1, keepdims=True))
    total = jnp.sum(power, axis=1, keepdims=True)
    return power * jnp.where(inside_image(size, first, 0), 1.0 / total, 0.0)


def join_images(parts, blocks):
    whole = parts[0]
    for (start, _, _), part in zip(blocks[1:], parts[1:]):
        shared = whole.shape[0] - start
        pieces = [whole[:start]]
        if shared > 0:
            pieces.append(whole[start:] + part[:shared])
        whole = jnp.concatenate(pieces + [part[shared:]], axis=0)
    return whole


def pack_block(refs, block, shard, width, experts):
    q_ref, k_ref, v_ref, o_ref, router_ref, *line_refs = refs
    for at, ref in ((0, q_ref), (1, k_ref), (2, v_ref), (OUT, o_ref)):
        block[at * shard : (at + 1) * shard, :] = ref[...].astype(BF16)
    here = slice(SMALL * shard, (SMALL + 1) * shard)
    block[here, :] = jnp.zeros((shard, width), BF16)
    row, column = (lax.broadcasted_iota(jnp.int32, (shard, shard), axis) for axis in (0, 1))
    lane = lax.broadcasted_iota(jnp.int32, (shard, LANES), 1)
    small = jnp.zeros((shard, LANES), F32)
    for at in range(experts + len(line_refs)):
        level = router_ref[at : at + 1, :] if at < experts else line_refs[at - experts][...]
        upright = jnp.sum(jnp.where(row == column, level, 0.0), axis=1, keepdims=True)
        small = jnp.where(lane == at, upright, small)
    block[here, :LANES] = small.astype(BF16)


def find_places(cfg, routes_ref, place, turned, over):
    n_dp, n_t, rows, padded, width, experts, rooms, shard, inside, hid = cfg
    t = lax.axis_index("tensor")
    tok_count = routes_ref.shape[1]
    capacity = (5 * tok_count + 2 * experts - 1) // (2 * experts)
    line = lax.broadcasted_iota(jnp.int32, (experts, tok_count), 0)
    lane = lax.broadcasted_iota(jnp.int32, (experts, tok_count), 1)

    def count(row, until):
        hot = (line == routes_ref[row : row + 1, :]) & (lane < until)
        return jnp.sum(hot.astype(F32), axis=1, keepdims=True)

    total = count(0, tok_count)
    before = (count(0, t * rows), count(1, t * rows))
    long = ceil_to(tok_count, LANES)
    wide = turned.shape[1]
    turned[...] = jnp.full(turned.shape, -1.0, F32)
    everyone = jnp.concatenate(
        [routes_ref[...], jnp.full((2, long - tok_count), experts, jnp.int32)], axis=1
    )
    everyone = jnp.concatenate([everyone, everyone, everyone, everyone], axis=0)
    mine = pltpu.roll(everyone, lax.rem(long - t * rows, long), 1)[:, :wide]
    spot = lax.broadcasted_iota(jnp.int32, (8, wide), 1)
    mine = jnp.where(spot < rows, mine, experts)
    line = lax.broadcasted_iota(jnp.int32, (experts, wide), 0)
    first, second = line == mine[0:1], line == mine[1:2]
    down, across = (lax.broadcasted_iota(jnp.int32, (wide, wide), axis) for axis in (0, 1))
    earlier = (down < across).astype(F32).astype(BF16)
    own = jnp.sum(first.astype(F32), axis=1, keepdims=True)
    first_rank = nn(first.astype(F32).astype(BF16), earlier)
    second_rank = nn(second.astype(F32).astype(BF16), earlier)

    def slot(choice, hot, rank, place):
        kept = hot & (place < capacity)
        here = jnp.sum(jnp.where(kept, rank + 1.0, 0.0), axis=0, keepdims=True) - 1.0
        good = (here >= 0.0) & (here < rooms)
        return jnp.where(good, choice.astype(F32) * rooms + here, -1.0), jnp.max(here, axis=1, keepdims=True)

    first_slot, first_most = slot(mine[0:1], first, first_rank, first_rank + before[0])
    second_slot, second_most = slot(mine[1:2], second, second_rank + own, second_rank + total + before[1])
    turned[0:1, :] = first_slot
    turned[1:2, :] = second_slot
    turned[2:3, :] = mine[0:1].astype(F32)
    turned[3:4, :] = mine[1:2].astype(F32)
    place[...] = turned[...].T
    most = jnp.maximum(first_most, second_most)
    over[...] = jnp.broadcast_to(jnp.where(most >= rooms, 1.0, 0.0), over.shape)


def step_kernel(cfg, *refs):
    n_dp, n_t, rows, padded, width, experts, rooms, shard, inside, hid = cfg
    refs = list(refs)

    def take(count):
        got = refs[:count]
        del refs[:count]
        return got

    here = take(3)
    e_in_ref, e_out_ref = take(2)
    here += take(9 if inside else 1)
    out_ref, gx_ref, sum_ref, g_in_ref, g_out_ref = take(5)
    held = take(len(here))
    x_ref, cot_ref, routes_ref, *shared = held
    here_sems = take(1)[0]
    block, gathered, full, cot_full, bias, res, probs_s = take(7)
    place, turned, over, gate_m, gate_c, gate_s, gate_r, rise_r = take(8)
    rise_s = gate_s
    moe, q_s, k_s, v_s, mix, norm, dk, dv = take(8)
    send_d, send_s, recv_d, recv_s, ret_in, back_in, act, slope = take(8)
    wi, wo, gi, go, gi_in, go_in = take(6)
    d_send, d_recv, s_send, s_recv, r_send, r_recv, b_send, b_recv = take(8)
    f_send, f_recv, e_send, e_recv, own_sems = take(5)
    wi_spread, wo_spread = Spread(n_t, wi, *take(2)), Spread(n_t, wo, *take(2))
    gi_collect, go_collect = Collect(n_t, gi, gi_in, *take(2)), Collect(n_t, go, go_in, *take(2))
    dp, t = lax.axis_index("dp"), lax.axis_index("tensor")
    scale = HEAD_DIM ** (-0.5)
    slot_count = n_dp * rooms
    half, wide = min(256, hid), min(256, width)
    long = gate_m.shape[1]
    early = 2 if hid == width and n_t > 2 else 0
    table = [sorted(range(n_t), key=lambda j: (abs(j - at), j)) for at in range(n_t)]

    def order(p):
        found = jnp.int32(0)
        for at in range(n_t):
            for spot in range(n_t):
                found = found + jnp.where((t == at) & (p == spot), table[at][spot], 0)
        return found

    every = pl.ds(0, rooms)
    cut = max(rooms // 2 // 16 * 16, 16)
    d_copy = Exchange(n_dp, send_d, recv_d, every, d_send, d_recv, True)
    s_first = Exchange(n_dp, send_s, recv_s, pl.ds(0, cut), s_send.at[0], s_recv.at[0], False)
    s_second = Exchange(n_dp, send_s, recv_s, pl.ds(cut, rooms - cut), s_send.at[1], s_recv.at[1], False)
    late = max(rooms * 2 // 5 // 16 * 16, 16)
    r_first = Exchange(n_dp, send_d, ret_in, pl.ds(late, rooms - late), r_send.at[0], r_recv.at[0], False)
    r_second = Exchange(n_dp, send_d, ret_in, pl.ds(0, late), r_send.at[1], r_recv.at[1], False)
    b_copy = Exchange(n_dp, send_s, back_in, every, b_send, b_recv, False)
    f_copy = Exchange(n_dp, gate_s, gate_r, pl.ds(0, 8), f_send, f_recv, False)
    e_copy = Exchange(n_dp, rise_s, rise_r, pl.ds(0, 8), e_send, e_recv, False)

    def column(at):
        return place[:padded, at : at + 1].astype(jnp.int32)

    greet(n_dp, n_t)
    load_in = pltpu.make_async_copy(e_in_ref, g_in_ref, own_sems.at[0])
    load_out = pltpu.make_async_copy(e_out_ref, g_out_ref, own_sems.at[1])
    loads = [pltpu.make_async_copy(src, dst, here_sems.at[at]) for at, (src, dst) in enumerate(zip(here, held))]
    for load in loads[3:]:
        load.start()
    load_in.start()
    for load in loads[:3]:
        load.start()
    load_out.start()
    for load in loads[3:]:
        load.wait()
    if inside:
        pack_block(shared, block, shard, width, experts)
        size = len(Gather.scratch(n_dp, n_t))
        gather_a = Gather(n_dp, n_t, 0, SMALL * shard, width, block, gathered, *take(size))
        gather_s = Gather(n_dp, n_t, SMALL * shard, shard, LANES, block, gathered, *take(size))
        gather_b = Gather(n_dp, n_t, OUT * shard, shard, width, block, gathered, *take(size))
        weights = Weights(shard, width, gathered=gathered)
    else:
        weights = Weights(shard, width, whole=shared[0])
    load_in.wait()
    wi[t] = g_in_ref[...].astype(BF16)
    greeted(n_dp, n_t)
    if inside:
        gather_a.start()
        gather_s.start()
        gather_b.start()
    wi_spread.step(0)
    for load in loads[:3]:
        load.wait()
    load_out.wait()
    wo[t] = g_out_ref[...].astype(BF16)
    tail = rows - rows % 8
    full[tail:, :] = jnp.zeros((padded - tail, width), F32)
    full[:rows, :] = x_ref[...].astype(F32)
    cot_full[tail:, :] = jnp.zeros((padded - tail, width), F32)
    cot_full[:rows, :] = cot_ref[...].astype(F32)
    bias[...] = image_bias(rows, padded)
    find_places(cfg, routes_ref, place, turned, over)

    def selectors(p):
        slot = lax.broadcasted_iota(jnp.int32, (rooms, padded), 0) + p * rooms
        first = (slot == turned[0:1, :padded].astype(jnp.int32)).astype(F32)
        second = (slot == turned[1:2, :padded].astype(jnp.int32)).astype(F32)
        return first, second

    dk[...] = cot_full[...].astype(BF16)

    def dispatch_grad(k, carry):
        to = lax.rem(dp + k, n_dp)
        first, second = selectors(to)
        got = nn((first + second).astype(BF16), dk[...]).astype(BF16)

        @pl.when(k > 0)
        def _():
            send_s[to] = got

        @pl.when(k == 0)
        def _():
            recv_s[to] = got

        return carry

    lax.fori_loop(0, n_dp, dispatch_grad, 0)
    if inside:
        gather_a.pass_to_chips()
        gather_s.pass_to_chips()
        gather_b.pass_to_chips()
        gather_a.pass_to_core()
        gather_s.pass_to_core()
    if inside:
        gather_a.arrive()
        gather_s.arrive()
    norms = norm_rows(weights.small(), experts)
    unit, _ = centre(full[...])
    norm[...] = (unit * norms[0:1] + norms[1:2]).astype(BF16)
    q_s[...] = nn(norm[...], weights(0)).astype(BF16)
    k_s[...] = nn(norm[...], weights(1)).astype(BF16)
    v_s[...] = nn(norm[...], weights(2)).astype(BF16)
    if inside:
        gather_b.pass_to_core()
    s_first.start_all()
    middle = (t > 0) & (t < n_t - 1)

    @pl.when(jnp.logical_not(middle))
    def _():
        wo_spread.step(0)

    low, high = half_masks()
    low_f, high_f = low.astype(F32), high.astype(F32)
    blocks = image_blocks(rows)

    def heads(j, carry):
        at = pl.ds(pl.multiple_of(j * LANES, LANES), LANES)
        parts = []
        for start, size, first in blocks:
            here = pl.ds(start, size)
            query, key, value = q_s[here, at], k_s[here, at], v_s[here, at]
            one = nn(image_probs(query * low, key, size, first).astype(BF16), value)
            two = nn(image_probs(query * high, key, size, first).astype(BF16), value)
            parts.append(one * low_f + two * high_f)
        mix[:, at] = join_images(parts, blocks).astype(BF16)
        return carry

    lax.fori_loop(0, width // LANES // 2, heads, 0)
    @pl.when(middle)
    def _():
        wi_spread.step(1)

    lax.fori_loop(width // LANES // 2, width // LANES, heads, 0)
    if inside:
        gather_b.arrive()
    residual = full[...] + nn(mix[...], weights(OUT))
    res[...] = residual
    unit, _ = centre(residual)
    moe[...] = (unit * norms[2:3] + norms[3:4]).astype(BF16)
    probs_s[...] = router_probs(nn(moe[...], weights.small()), experts)

    spot = lax.broadcasted_iota(jnp.int32, (padded, LANES), 1)
    first_gate, second_gate = pick_gate(probs_s[...], column(2)), pick_gate(probs_s[...], column(3))
    place[:padded, :] = jnp.where(spot == 4, first_gate, jnp.where(spot == 5, second_gate, place[:padded, :]))
    turned[...] = place[...].T
    gate_line = lax.broadcasted_iota(jnp.int32, (8, padded), 0)

    def terms(gate):
        one = gate.astype(BF16).astype(F32)
        two = (gate - one).astype(BF16).astype(F32)
        three = gate - one - two
        stack = jnp.where(gate_line == 0, one, jnp.where(gate_line == 1, two, jnp.where(gate_line == 2, three, 0.0)))
        return stack.astype(BF16)

    first_terms, second_terms = terms(turned[4:5, :padded]), terms(turned[5:6, :padded])
    def dispatch(k, carry):
        to = lax.rem(dp + k, n_dp)
        first, second = selectors(to)
        got = nn((first + second).astype(BF16), moe[...]).astype(BF16)

        @pl.when(k > 0)
        def _():
            send_d[to] = got
            d_copy.start(k)

        @pl.when(k == 0)
        def _():
            recv_d[to] = got

        return carry

    lax.fori_loop(0, n_dp, dispatch, 0)

    @pl.when(middle)
    def _():
        if n_t > 2:
            wi_spread.step(2)
        wo_spread.step(0)

    def dispatch_gates(k, carry):
        to = lax.rem(dp + k, n_dp)
        first, second = selectors(to)
        gate = nt(first_terms, first.astype(BF16)) + nt(second_terms, second.astype(BF16))
        gate = jnp.sum(gate, axis=0, keepdims=True)

        @pl.when(k > 0)
        def _():
            gate_s[to, :, :rooms] = jnp.broadcast_to(gate, (8, rooms))
            f_copy.start(k)

        @pl.when(k == 0)
        def _():
            gate_r[to, :, :rooms] = jnp.broadcast_to(gate, (8, rooms))

        return carry

    lax.fori_loop(0, n_dp, dispatch_gates, 0)

    def hidden_units(j, g):
        active, steep = gelu_parts(nn(recv_d[g], wi[j]))
        act[j, g] = active.astype(BF16)
        slope[j, g] = steep.astype(BF16)

    n_chip, chip = n_dp // 2, dp // 2

    def chip_rows(ref, c, *lead):
        value = ref[(*lead, pl.ds(2 * c, 2))]
        return value.reshape(2 * rooms, value.shape[-1])

    def chip_store(ref, c, value, *lead):
        ref[(*lead, pl.ds(2 * c, 2))] = value.reshape(2, rooms, value.shape[-1])

    def own_hidden(k, carry):
        @pl.when(k > 0)
        def _():
            d_copy.wait_from(k)

        hidden_units(t, lax.rem(dp + n_dp - k, n_dp))
        return carry

    lax.fori_loop(0, n_dp, own_hidden, 0)
    s_second.start_all()

    @pl.when(middle)
    def _():
        wo_spread.step(1)


    @pl.when(jnp.logical_not(middle))
    def _():
        wi_spread.step(1)
        if n_t > 2:
            wi_spread.step(2)

    slot_grads = send_s
    room_lane = lax.broadcasted_iota(jnp.int32, (rooms, LANES), 1)

    def slot_grad(g, carry):
        gate = jnp.sum(jnp.where(room_lane == g, gate_c[:rooms, :], 0.0), axis=1, keepdims=True)
        slot_grads[g] = (gate * recv_s[g].astype(F32)).astype(BF16)
        return carry

    def outer_grad(i, carry):
        j = order(n_t - 1 - i // (hid // half))
        at = pl.ds(pl.multiple_of(lax.rem(i, hid // half) * half, half), half)
        left = act[j, :, :, at].reshape(slot_count, half)
        go[j, at, :] = tn(left, slot_grads[...].reshape(slot_count, width)).astype(BF16)

        @pl.when(lax.rem(i, hid // half) == hid // half - 1)
        def _():
            go_collect.begin(j)

        return carry

    def cotangent_arrives():
        gate_m[...] = jnp.zeros_like(gate_m)
        f_copy.wait_all()
        f_copy.wait_sent()
        for g in range(n_dp):
            gate_m[g : g + 1, :rooms] = gate_r[g, 0:1, :rooms]
        gate_c[...] = gate_m[...].T
        for half_copy in (s_first, s_second):
            half_copy.wait_all()
            half_copy.wait_sent()
    def other_hidden(q, carry):
        p = jnp.where(q == 0, 1, jnp.where(q == 1, n_t - 1, q))

        @pl.when(q == 1)
        def _():
            for s in range(3, n_t):
                wi_spread.step(s)

        def one(g, inner):
            hidden_units(order(p), g)
            return inner

        lax.fori_loop(0, n_dp, one, 0, unroll=2)

        @pl.when(q == min(1, n_t - 2))
        def _():
            cotangent_arrives()
            lax.fori_loop(0, n_dp, slot_grad, 0)
            lax.fori_loop(0, hid // half, outer_grad, 0)

        return carry

    lax.fori_loop(0, n_t - 1, other_hidden, 0)
    @pl.when(jnp.logical_not(middle))
    def _():
        wo_spread.step(1)

    @pl.when(middle)
    def _():
        if n_t > 2:
            wo_spread.step(2)

    lax.fori_loop(hid // half, n_t * (hid // half), outer_grad, 0)

    def hidden_grads(p):
        j = order(p)

        def one(i, inner):
            grad = nt(chip_rows(slot_grads, i), wo[j]) * chip_rows(slope, i, j).astype(F32)
            chip_store(slope, i, grad.astype(BF16), j)
            return inner

        lax.fori_loop(0, n_chip, one, 0, unroll=2)

    def inner_grads(p):
        j = order(p)

        def one(i, inner):
            at = pl.ds(pl.multiple_of(i * wide, wide), wide)
            left = recv_d[:, :, at].reshape(slot_count, wide)
            gi[j, at, :] = tn(left, slope[j].reshape(slot_count, hid)).astype(BF16)
            return inner

        lax.fori_loop(0, width // wide, one, 0)

    def split(total):
        main = total.astype(BF16)
        return main, (total - main.astype(F32)).astype(BF16)

    def some_back(g, inner):
        near_a, near_b = order(0), order(1)
        total = nn(chip_rows(act, g, near_a), wo[near_a]) + nn(chip_rows(act, g, near_b), wo[near_b])
        for j, part in zip((near_a, near_b), split(total)):
            chip_store(act, g, part, j)
        return inner

    def hidden_step(p, carry):
        @pl.when(p == 1)
        def _():
            if n_t > 2:
                go_collect.step(1, True)

        @pl.when((p == 2) & jnp.logical_not(middle))
        def _():
            if n_t > 2:
                wo_spread.step(2)

        @pl.when(p == 3)
        def _():
            for s in range(3, n_t):
                wo_spread.step(s)

        hidden_grads(p)

        @pl.when((p < n_t - 1) & jnp.logical_not(middle))
        def _():
            inner_grads(p)

        if early:

            @pl.when((p == early) & jnp.logical_not(middle))
            def _():
                lax.fori_loop(0, n_chip, some_back, 0)

        return carry

    lax.fori_loop(0, n_t, hidden_step, 0)
    d_copy.wait_sent()

    def hand_out(c, value, buffer, own, copies):
        for q in range(2):
            to = 2 * c + q
            k = lax.rem(to - dp + n_dp, n_dp)
            part = value[q * rooms : (q + 1) * rooms]

            @pl.when(k > 0)
            def _():
                buffer[to] = part
                if copies is not None:
                    copies.start(k)

            @pl.when(k == 0)
            def _():
                own[to] = part

    def give_back_grad(i, carry):
        c = lax.rem(chip + 1 + i, n_chip)
        total = nt(chip_rows(slope, c, 0), wi[0])
        for j in range(1, n_t):
            total = total + nt(chip_rows(slope, c, j), wi[j])
        hand_out(c, total.astype(BF16), send_s, back_in, b_copy)
        return carry

    lax.fori_loop(0, n_chip, give_back_grad, 0)
    for e in range(2, n_t - 1):
        go_collect.step(e, True)

    gate_c[...] = jnp.zeros_like(gate_c)

    def give_back(c, total):
        rise = jnp.sum(total * chip_rows(recv_s, c).astype(F32), axis=1, keepdims=True)
        for q in range(2):
            found = rise[q * rooms : (q + 1) * rooms]
            gate_c[:rooms, :] = jnp.where(room_lane == 2 * c + q, found, gate_c[:rooms, :])
        hand_out(c, total.astype(BF16), send_d, ret_in, None)

    def give_back_whole(c, carry):
        total = nn(chip_rows(act, c, 0), wo[0])
        for j in range(1, n_t):
            total = total + nn(chip_rows(act, c, j), wo[j])
        give_back(c, total)
        return carry

    def give_back_rest(c, carry):
        near_a, near_b = order(0), order(1)
        total = chip_rows(act, c, near_a).astype(F32) + chip_rows(act, c, near_b).astype(F32)
        for p in range(early, n_t):
            j = order(p)
            total = total + nn(chip_rows(act, c, j), wo[j])
        give_back(c, total)
        return carry

    def last_inner():
        inner_grads(n_t - 1)

        def send_inner(p, carry):
            gi_collect.begin(order(n_t - 1 - p))
            return carry

        lax.fori_loop(0, n_t, send_inner, 0)

    if early:

        @pl.when(jnp.logical_not(middle))
        def _():
            last_inner()
            lax.fori_loop(0, n_chip, give_back_rest, 0)

        @pl.when(middle)
        def _():
            lax.fori_loop(0, n_chip, give_back_whole, 0)

    else:

        @pl.when(jnp.logical_not(middle))
        def _():
            last_inner()

        lax.fori_loop(0, n_chip, give_back_whole, 0)

    gate_m[...] = gate_c[...].T
    for g in range(n_dp):
        row = jnp.broadcast_to(gate_m[g : g + 1, :], (8, long))

        @pl.when(dp == g)
        def _():
            rise_r[g] = row

        @pl.when(dp != g)
        def _():
            rise_s[g] = row

    e_copy.start_all()

    @pl.when(middle)
    def _():
        def one(p, inner):
            inner_grads(p)
            return inner

        lax.fori_loop(0, n_t, one, 0)

    lane = lax.broadcasted_iota(jnp.int32, (padded, slot_count), 1)
    both = ((lane == column(0)).astype(F32) + (lane == column(1)).astype(F32)).astype(BF16)
    unit, inverse = centre(res[...])
    b_copy.wait_sent()
    r_first.start_all()
    b_copy.wait_all()
    e_copy.wait_all()
    e_copy.wait_sent()
    room = lax.broadcasted_iota(jnp.int32, (padded, long), 1)

    slots_of = (column(0), column(1))

    found = [jnp.zeros((padded, long), F32)] * 2
    for e in range(n_dp):
        row = jnp.where(room[0:1] < rooms, rise_r[e, 0:1, :], 0.0)
        for at, slot in enumerate(slots_of):
            here = jnp.where(slot < (e + 1) * rooms, slot - e * rooms, -1)
            found[at] = jnp.where(room == here, row, found[at])
    first_grad, second_grad = (jnp.sum(one, axis=1, keepdims=True) for one in found)
    probs = probs_s[...]
    spot = lax.broadcasted_iota(jnp.int32, probs.shape, 1)
    grad_probs = jnp.where(spot == column(2), first_grad, 0.0) + jnp.where(spot == column(3), second_grad, 0.0)
    grad_logits = (probs * (grad_probs - jnp.sum(probs * grad_probs, axis=1, keepdims=True))).astype(BF16)
    grad_router = tn(moe[...], grad_logits)
    grad_moe = nn(both, back_in[...].reshape(slot_count, width)) + nt(grad_logits, weights.small())
    extra, gain_two, shift_two = norm_back(grad_moe, unit, inverse, norms[2:3])
    grad_residual = cot_full[...] + extra
    cot_full[...] = grad_residual
    grad_attended = grad_residual.astype(BF16)

    pairs = width // LANES
    if inside:
        size = len(Reduce.scratch(n_dp, n_t, 1, (shard, LANES)))
        out_sum = Reduce(n_dp, n_t, lambda p: sum_ref.at[pl.ds(OUT * shard, shard)], *take(size))
        pair_sum = Reduce(
            n_dp, n_t, lambda p: sum_ref.at[pl.ds(0, 3 * shard), pl.ds(pl.multiple_of(p * LANES, LANES), LANES)], *take(size)
        )
        small_sum = Reduce(n_dp, n_t, lambda p: sum_ref.at[pl.ds(SMALL * shard, shard), pl.ds(0, LANES)], *take(size))
        sum_ref[SMALL * shard : (SMALL + 1) * shard, LANES:] = jnp.zeros((shard, width - LANES), F32)
        out_sum.put(0, 0, tn(mix[...], grad_attended))
        out_sum.to_core(0)
    else:
        sum_ref[OUT] = tn(mix[...], grad_attended)
    dq = mix
    dq[...] = nt(grad_attended, weights(OUT)).astype(BF16)

    def heads_back(j, carry):
        at = pl.ds(pl.multiple_of(j * LANES, LANES), LANES)
        query, key, value, grad = q_s[:, at], k_s[:, at], v_s[:, at], dq[:, at]
        for mask, mask_f in ((low, low_f), (high, high_f)):
            probs = soft_scores(query * mask, key, bias[...])
            grad_probs = nt(grad * mask, value)
            grad_scores = probs * (grad_probs - jnp.sum(probs * grad_probs, axis=1, keepdims=True))
            grad_scores = grad_scores.astype(BF16)
            part_v = tn(probs.astype(BF16), grad)
            part_q = nn(grad_scores, key) * scale
            part_k = tn(grad_scores, query) * scale
            if mask is low:
                sum_q, sum_k, sum_v = part_q * mask_f, part_k * mask_f, part_v * mask_f
            else:
                sum_q, sum_k, sum_v = sum_q + part_q * mask_f, sum_k + part_k * mask_f, sum_v + part_v * mask_f
        dq[:, at] = sum_q.astype(BF16)
        dk[:, at] = sum_k.astype(BF16)
        dv[:, at] = sum_v.astype(BF16)
        @pl.when(j == pairs // 2)
        def _():
            if n_t > 2:
                gi_collect.step(1, True)

        if inside:
            for spot, ref in enumerate((dq, dk, dv)):
                pair_sum.put(j, spot * shard, tn(norm[...], ref[:, at]))
            pair_sum.to_core(j)

            @pl.when(j == 0)
            def _():
                out_sum.to_chips(0)

            @pl.when(j > 0)
            def _():
                pair_sum.to_chips(j - 1)

        return carry

    lax.fori_loop(0, pairs, heads_back, 0)
    if inside:
        pair_sum.to_chips(pairs - 1)
    else:
        for spot, ref in enumerate((dq, dk, dv)):
            sum_ref[spot] = tn(norm[...], ref[...])
    grad_normed = nt(dq[...], weights(0)) + nt(dk[...], weights(1)) + nt(dv[...], weights(2))
    full[tail:, :] = jnp.zeros((padded - tail, width), F32)
    full[:rows, :] = x_ref[...].astype(F32)
    unit, inverse = centre(full[...])
    extra, gain_one, shift_one = norm_back(grad_normed, unit, inverse, norms[0:1])
    gx_ref[...] = (cot_full[...] + extra)[:rows].astype(BF16)
    small = small_grads(experts, grad_router, (gain_one, shift_one, gain_two, shift_two))
    lane = lax.broadcasted_iota(jnp.int32, small.shape, 1)
    small = jnp.where(lane == experts + 4, over[0:1, :], small)
    def combine():
        for half_copy in (r_first, r_second):
            half_copy.wait_all()
            half_copy.wait_sent()
        returned = ret_in[...].reshape(slot_count, width)
        lane = lax.broadcasted_iota(jnp.int32, (padded, slot_count), 1)
        first, second = ((lane == column(at)).astype(F32).astype(BF16) for at in (0, 1))
        first_rows, second_rows = nn(first, returned), nn(second, returned)
        first_gate, second_gate = place[:padded, 4:5], place[:padded, 5:6]
        outcome = res[...] + first_gate * first_rows + second_gate * second_rows
        out_ref[...] = outcome[:rows].astype(BF16)

    if inside:
        small_sum.put(0, 0, small)
        small_sum.to_core(0)
        small_sum.to_chips(0)
        r_second.start_all()
        out_sum.to_line(0)

        def line(p, carry):
            pair_sum.to_line(p)
            return carry

        lax.fori_loop(0, pairs, line, 0)
        small_sum.to_line(0)
        for e in range(2, n_t - 1):
            gi_collect.step(e, True)
        go_collect.finish(g_out_ref)
        combine()
        out_sum.finish(0)

        def last(p, carry):
            pair_sum.finish(p)
            return carry

        lax.fori_loop(0, pairs, last, 0)
        small_sum.finish(0)
        gather_a.drain()
        gather_s.drain()
        gather_b.drain()
    else:
        sum_ref[SMALL] = jnp.zeros((width, width), F32)
        sum_ref[SMALL, :, :LANES] = small
        r_second.start_all()
        for e in range(2, n_t - 1):
            gi_collect.step(e, True)
        go_collect.finish(g_out_ref)
        combine()
    gi_collect.finish(g_in_ref)
    wi_spread.drain()
    wo_spread.drain()


def run_step(cfg, cid, x, cot, routes, e_in, e_out, shared):
    n_dp, n_t, rows, padded, width, experts, rooms, shard, inside, hid = cfg
    rows_block = ceil_to(5 * shard, 16)
    total = (rows_block, width) if inside else (5, width, width)
    outs = [
        jax.ShapeDtypeStruct((rows, width), BF16),
        jax.ShapeDtypeStruct((rows, width), BF16),
        jax.ShapeDtypeStruct(total, F32),
        jax.ShapeDtypeStruct((width, hid), F32),
        jax.ShapeDtypeStruct((hid, width), F32),
    ]
    spread = (n_dp, n_t, rows_block, width) if inside else (1, 1, 16, LANES)
    wide, long = ceil_to(padded, LANES), ceil_to(rooms, LANES)
    rows_f, rows_b = VMEM((padded, width), F32), VMEM((padded, width), BF16)
    slots_b, units_b = VMEM((n_dp, rooms, width), BF16), VMEM((n_t, n_dp, rooms, hid), BF16)
    in_b, out_b = (VMEM((n_t,) + shape, BF16) for shape in ((width, hid), (hid, width)))
    in_more, out_more = (VMEM((n_t + 1,) + shape, BF16) for shape in ((width, hid), (hid, width)))
    given = [x, cot, routes, *shared]
    scratch = [VMEM(one.shape, one.dtype) for one in given] + [DMA((len(given),))]
    scratch += [VMEM((rows_block, width), BF16), VMEM(spread, BF16)]
    scratch += [rows_f, rows_f, VMEM((padded, padded), F32), rows_f, VMEM((padded, LANES), F32)]
    scratch += [VMEM((wide, LANES), F32), VMEM((LANES, wide), F32), VMEM((8, LANES), F32)]
    scratch += [VMEM((LANES, long), F32), VMEM((long, LANES), F32)] + [VMEM((n_dp, 8, long), F32)] * 3
    scratch += [rows_b] * 8 + [slots_b] * 6 + [units_b] * 2
    scratch += [in_b, out_b, in_b, out_b, in_more, out_more]
    scratch += [DMA, DMA((n_dp,))] + [DMA((2,))] * 4 + [DMA] * 6 + [DMA((2,))] + Spread.scratch(n_t) * 2 + Collect.scratch(n_t) * 2
    if inside:
        scratch += Gather.scratch(n_dp, n_t) * 3 + Reduce.scratch(n_dp, n_t, 1, (shard, width))
        scratch += Reduce.scratch(n_dp, n_t, width // LANES, (3 * shard, LANES))
        scratch += Reduce.scratch(n_dp, n_t, 1, (shard, LANES))
    whole, anywhere = pl.BlockSpec(memory_space=VMEM), pl.BlockSpec(memory_space=pl.ANY)
    return pl.pallas_call(
        partial(step_kernel, cfg),
        out_shape=outs,
        in_specs=[anywhere] * (5 + len(shared)),
        out_specs=[whole] * len(outs),
        scratch_shapes=scratch,
        compiler_params=pltpu.CompilerParams(
            collective_id=cid, has_side_effects=True, vmem_limit_bytes=57 * 2**20
        ),
        name="step_" + str(rooms),
    )(x, cot, routes, e_in, e_out, *shared)


def lay_kernel(shard, experts, out_ref, gx_ref, sum_ref, in_ref, outer_ref, *outs):
    outs[0][...] = out_ref[...]
    outs[1][...] = gx_ref[...]
    for at, spot in ((0, 4), (1, 5), (2, 6), (OUT, 7)):
        outs[spot][...] = sum_ref[at * shard : (at + 1) * shard, :]
    small = sum_ref[SMALL * shard : (SMALL + 1) * shard, :LANES]
    row, column = (lax.broadcasted_iota(jnp.int32, (shard, shard), axis) for axis in (0, 1))
    for at, spot in enumerate((2, 3, 8, 9)):
        upright = small[:, experts + at : experts + at + 1]
        outs[spot][...] = jnp.sum(jnp.where(row == column, upright, 0.0), axis=0, keepdims=True)
    for at in range(experts):
        outs[10][at : at + 1, :] = jnp.sum(jnp.where(row == column, small[:, at : at + 1], 0.0), axis=0, keepdims=True)
    outs[11][...] = in_ref[...]
    outs[12][...] = outer_ref[...]


def lay_out(shard, experts, *args):
    rows, width = args[0].shape
    line = jax.ShapeDtypeStruct((1, shard), F32)
    square = jax.ShapeDtypeStruct((shard, width), F32)
    outs = [jax.ShapeDtypeStruct((rows, width), BF16)] * 2 + [line] * 2 + [square] * 4 + [line] * 2
    outs += [jax.ShapeDtypeStruct((experts, shard), F32)]
    outs += [jax.ShapeDtypeStruct(arg.shape, F32) for arg in args[3:]]

    def full(shape):
        return pl.BlockSpec(shape, lambda i: (0,) * len(shape))

    return pl.pallas_call(
        partial(lay_kernel, shard, experts),
        grid=(1,),
        out_shape=outs,
        in_specs=[full(arg.shape) for arg in args],
        out_specs=[full(out.shape) for out in outs],
        compiler_params=pltpu.CompilerParams(vmem_limit_bytes=32 * 2**20),
        name="outputs",
    )(*args)


def route_pairs(routes, t, row_count, experts, capacity):
    tok_count = routes.shape[0]
    ids = jnp.arange(experts, dtype=jnp.int32)[None, :]
    start = t * row_count
    rows = lax.dynamic_slice_in_dim(routes, start, row_count, 0)
    before = (jnp.arange(tok_count, dtype=jnp.int32) < start)[:, None]
    all_first = routes[:, 0:1] == ids
    all_second = routes[:, 1:2] == ids
    base_first = jnp.sum((all_first & before).astype(jnp.int32), axis=0)
    total_first = jnp.sum(all_first.astype(jnp.int32), axis=0)
    base_second = jnp.sum((all_second & before).astype(jnp.int32), axis=0)
    hot_first = rows[:, 0:1] == ids
    hot_second = rows[:, 1:2] == ids
    at = jnp.arange(row_count, dtype=jnp.int32)
    lower = (at[:, None] > at[None, :]).astype(BF16)
    both = jnp.concatenate([hot_first, hot_second], axis=1).astype(BF16)
    earlier = nn(lower, both).astype(jnp.int32)
    own_first = jnp.sum(hot_first.astype(jnp.int32), axis=0)
    rank_first = earlier[:, :experts]
    rank_second = earlier[:, experts:] + own_first
    place_first = rank_first + base_first
    place_second = earlier[:, experts:] + total_first + base_second
    first = jnp.sum(jnp.where(hot_first & (place_first < capacity), rank_first + 1, 0), axis=1) - 1
    second = jnp.sum(jnp.where(hot_second & (place_second < capacity), rank_second + 1, 0), axis=1) - 1
    return rows, first, second


def per_device(
    n_dp,
    n_t,
    inputs,
    cotangent,
    routes,
    gain_attn,
    shift_attn,
    query_w,
    key_w,
    value_w,
    out_w,
    gain_moe,
    shift_moe,
    router_w,
    expert_in,
    expert_out,
):
    t = lax.axis_index("tensor")
    shard, width = query_w.shape
    experts = router_w.shape[1]
    tok_count = routes.shape[0]
    rows = inputs.shape[0]
    hid = expert_in.shape[2]
    padded = ceil_to(rows, 16)
    capacity = (5 * tok_count + 2 * experts - 1) // (2 * experts)
    inside = shard % 16 == 0
    every = ("dp", "tensor")
    lines = (gain_attn, shift_attn, gain_moe, shift_moe)

    def stack():
        small = jnp.concatenate([router_w] + [line[:, None] for line in lines], axis=1)
        small = jnp.pad(small, ((0, 0), (0, width - small.shape[1])))
        return jnp.stack([query_w, key_w, value_w, small, out_w]).astype(BF16)

    if inside:
        shared = [query_w, key_w, value_w, out_w, router_w.T] + [line[None, :] for line in lines]
    else:
        shared = [lax.all_gather(stack(), every, axis=1, tiled=True)]

    def finish(results):
        summed = results[2]
        if not inside:
            summed = lax.psum_scatter(summed, every, scatter_dimension=1, tiled=True).reshape(5 * shard, width)
        outs = lay_out(shard, experts, results[0], results[1], summed, *results[3:])
        return tuple(outs)

    def slow(_):
        rooms = ceil_to(rows, 16)
        cfg = (n_dp, n_t, rows, padded, width, experts, rooms, shard, inside)
        route_rows, first_rank, second_rank = route_pairs(routes, t, rows, experts, capacity)

        def slot(choice, rank):
            return jnp.where(rank >= 0, choice * rooms + rank, -1)

        slots = jnp.stack([slot(route_rows[:, 0], first_rank), slot(route_rows[:, 1], second_rank)])
        slots = jnp.pad(slots, ((0, 0), (0, padded - rows)), constant_values=-1)
        cols = jnp.concatenate([jnp.pad(route_rows, ((0, padded - rows), (0, 0))), slots.T], axis=1)
        block = stack().reshape(5 * shard, width) if inside else shared[0]
        kept = forward(cfg, 1, inputs, cotangent, cols, slots, block)

        def turn(k):
            return [(i, (i + k) % n_t) for i in range(n_t)]

        both = jnp.stack([expert_in[0].T, expert_out[0]]).astype(BF16)
        parts = [both] + [lax.ppermute(both, "tensor", turn(k)) for k in range(1, n_t)]
        w_in, w_out = (jnp.concatenate([part[i] for part in parts], axis=0) for i in range(2))
        returned, back, grad_inner, grad_outer = run_expert(
            kept[1].reshape(n_dp * rooms, width), kept[2].reshape(n_dp * rooms, width), w_in, w_out
        )
        both = jnp.stack([grad_inner.reshape(n_t, hid, width), grad_outer.reshape(n_t, hid, width)], axis=1)
        total = both[0].astype(F32)
        for k in range(1, n_t):
            total = total + lax.ppermute(both[k], "tensor", turn(-k)).astype(F32)
        results = backward(
            cfg,
            2,
            returned.reshape(n_dp, rooms, width),
            back.reshape(n_dp, rooms, width),
            inputs,
            cotangent,
            cols,
            kept[0] if inside else block,
            *kept[3:],
        )
        return finish((*results, total[0].T, total[1]))

    rooms = min(ceil_to((7 * rows + 2 * experts - 1) // (2 * experts), 16), ceil_to(rows, 16))
    cfg = (n_dp, n_t, rows, padded, width, experts, rooms, shard, inside, hid)
    fast = run_step(cfg, 0, inputs, cotangent, routes.T, expert_in[0], expert_out[0], shared)
    if inside:
        crowded = fast[2][SMALL * shard, experts + 4] > 0.5
    else:
        crowded = lax.psum(fast[2][SMALL, 0, experts + 4], every) > 0.5
    outs = lax.cond(crowded, slow, finish, tuple(fast))
    lined = [out.reshape(shard) if at in (2, 3, 8, 9) else out for at, out in enumerate(outs)]
    lined[10], lined[11], lined[12] = lined[10].T, lined[11][None], lined[12][None]
    return tuple(lined)


def solution(mesh):
    every = ("dp", "tensor")
    rows, line = P(every, None), P(every)
    w_in, w_out = P("dp", None, "tensor"), P("dp", "tensor", None)
    return jax.shard_map(
        partial(per_device, mesh.shape["dp"], mesh.shape["tensor"]),
        mesh=mesh,
        in_specs=(rows, rows, P("dp", None), line, line, rows, rows, rows, rows, line, line, rows, w_in, w_out),
        out_specs=(rows, rows, line, line, rows, rows, rows, rows, line, line, rows, w_in, w_out),
        check_vma=False,
    )
```
